32 devices in a mesh: items: 8 (over y, x, core), rows: 4 (over z).
Axes of the slice: x: 2, y: 2, z: 4, core: 2. Of those that a mesh axis runs over, the one named last changes fastest.
Arguments:
- latents: bfloat16 [8, 576, 1536], P('items', 'rows'), may hold values from -6 to 6
- clip_tokens: bfloat16 [8, 80, 1280], P('items', 'rows'), may hold values from -6 to 6
- time_embed: bfloat16 [8, 64], P('items'), may hold values from -6 to 6
- bucket_ids: int32 [8], P('items'), may hold values from 0 to 2, as said below
- heights: int32 [8], P('items'), may hold values from 9 to 32, as said below
- widths: int32 [8], P('items'), may hold values from 10 to 36, as said below
- text_mask: int32 [8, 80], P('items'), may hold values 0 or 1
- conv_weight: bfloat16 [9, 1536], P(None, ('items', 'rows')), may hold values from -2 to 2
- conv_bias: bfloat16 [1536], P(('items', 'rows')), may hold values from -3 to 3
- in_weight: bfloat16 [1536, 6144], P(('items', 'rows')), may hold values from -0.15625 to 0.15625
- in_bias: bfloat16 [6144], P(('items', 'rows')), may hold values from -3 to 3
- grn_gain: bfloat16 [6144], P(('items', 'rows')), may hold values from -3 to 3
- grn_bias: bfloat16 [6144], P(('items', 'rows')), may hold values from -2 to 2
- out_weight: bfloat16 [6144, 1536], P(('items', 'rows')), may hold values from -0.078125 to 0.078125
- out_bias: bfloat16 [1536], P(('items', 'rows')), may hold values from -2 to 2
- time_weight: bfloat16 [64, 3072], P(None, ('items', 'rows')), may hold values from -0.375 to 0.375
- time_bias: bfloat16 [3072], P(('items', 'rows')), may hold values from -2 to 2
- map_weight: bfloat16 [1280, 1536], P(('items', 'rows')), may hold values from -0.15625 to 0.15625
- map_bias: bfloat16 [1536], P(('items', 'rows')), may hold values from -2 to 2
- qkv_weight: bfloat16 [1536, 4608], P(('items', 'rows')), may hold values from -0.15625 to 0.15625
- qv_bias: bfloat16 [3072], P(('items', 'rows')), may hold values from -2 to 2
- proj_weight: bfloat16 [1536, 1536], P(('items', 'rows')), may hold values from -1.25 to 1.25
- proj_bias: bfloat16 [1536], P(('items', 'rows')), may hold values from -2 to 2
- cotangent: bfloat16 [8, 576, 1536], P('items', 'rows'), may hold values from -6 to 6
Outputs:
- output: bfloat16 [8, 576, 1536], P('items', 'rows')
- grad_latents: float32 [8, 576, 1536], P('items', 'rows')
- grad_conv_weight: float32 [9, 1536], P(None, ('items', 'rows'))
- grad_conv_bias: float32 [1536], P(('items', 'rows'))
- grad_in_weight: float32 [1536, 6144], P(('items', 'rows'))
- grad_in_bias: float32 [6144], P(('items', 'rows'))
- grad_grn_gain: float32 [6144], P(('items', 'rows'))
- grad_grn_bias: float32 [6144], P(('items', 'rows'))
- grad_out_weight: float32 [6144, 1536], P(('items', 'rows'))
- grad_out_bias: float32 [1536], P(('items', 'rows'))
- grad_time_weight: float32 [64, 3072], P(None, ('items', 'rows'))
- grad_time_bias: float32 [3072], P(('items', 'rows'))
- grad_map_weight: float32 [1280, 1536], P(('items', 'rows'))
- grad_map_bias: float32 [1536], P(('items', 'rows'))
- grad_qkv_weight: float32 [1536, 4608], P(('items', 'rows'))
- grad_qv_bias: float32 [3072], P(('items', 'rows'))
- grad_proj_weight: float32 [1536, 1536], P(('items', 'rows'))
- grad_proj_bias: float32 [1536], P(('items', 'rows'))
The draws below stay inside these ranges and needn't reach their ends.
Inputs may be any that keep to these rules, and one draw needn't show every extreme that they name: `bucket_ids`: items 0, 1 and 2 lie in buckets 0, 1 and 2. `heights`: an item's height is more than half of its bucket's rows and at most all of them; item 2 and every item whose index is a multiple of 16 have all rows of their bucket. `widths`: an item's width is more than half of its bucket's W and at most W; item 2 and every item whose index is a multiple of 16 have all columns of their bucket.
All inputs are finite; a program needn't handle non-finite values. No bound on the sum of `text_mask` on one device may be relied on, other than what follows from the above.
Results may differ from the reference program's by a relative error of at most 0.012.
Values may be sent and summed in bfloat16 or wider, within the bound.
A program may use at most 256 MiB of HBM per device.

```python
import jax
import jax.numpy as jnp
from jax import lax

C = 1536
FF = 6144
HEADS = 24
HEAD = 64
CCOND = 1280
RDIM = 64
TXT = 77
UNIT = 8
IPG = 1
TXT_PAD = 80
BPIX = 576
HALO = 36
ITEMS = 8


def geometry(key):
    position = jnp.arange(ITEMS, dtype=jnp.int32)
    drawn_ids = jax.random.randint(jax.random.fold_in(key, 11), (ITEMS,), 0, 3, dtype=jnp.int32)
    bucket = jnp.where(position < 3, position, drawn_ids)
    bucket_tall = (bucket + 2) * UNIT
    bucket_wide = jnp.where(bucket == 0, 9 * UNIT // 2, jnp.where(bucket == 1, 3 * UNIT, 9 * UNIT // 4))
    fill_all = (position % 16 == 0) | (position == 2)
    cut_rows = jax.random.randint(jax.random.fold_in(key, 12), (ITEMS,), 0, bucket_tall // 2, dtype=jnp.int32)
    cut_cols = jax.random.randint(jax.random.fold_in(key, 13), (ITEMS,), 0, bucket_wide // 2, dtype=jnp.int32)
    heights = jnp.where(fill_all, bucket_tall, bucket_tall - cut_rows)
    widths = jnp.where(fill_all, bucket_wide, bucket_wide - cut_cols)
    return (bucket, heights, widths)


def draw_bucket_ids(key, part):
    return geometry(key)[0]


def draw_heights(key, part):
    return geometry(key)[1]


def draw_widths(key, part):
    return geometry(key)[2]


def plant(values, rng, smallest, high):
    extent = values.shape
    place = [jax.random.randint(jax.random.fold_in(rng, axis), (), 0, extent[axis]) for axis in range(len(extent))]
    values = values.at[tuple(place)].set(smallest)
    longest = extent.index(max(extent))
    place[longest] = (place[longest] + 1) % extent[longest]
    return values.at[tuple(place)].set(high)


def shard_levels(own_key, extent, shards, least, top_value):
    loudness = 1.0
    for dim, shards_of in shards:
        steps = jax.random.uniform(jax.random.fold_in(jax.random.fold_in(own_key, 6), dim), (shards_of,), jnp.float32, least / len(shards), top_value / len(shards))
        loudness = loudness * jnp.repeat(jnp.exp(steps), extent[dim] // shards_of).reshape((-1,) + (1,) * (len(extent) - 1 - dim))
    return loudness


def normal_values(rng, extent, scale, bound, split=(), kind=jnp.bfloat16):
    drawn = jax.random.normal(rng, extent, jnp.float32) * scale
    if len(split) > 0:
        drawn = shard_levels(rng, extent, split, -0.22, 0.18) * drawn
    return jnp.clip(drawn, min=-bound, max=bound).astype(kind)


def setup_inputs(seed: int = 0) -> dict:
    streams_of = jax.random.split(jax.random.key(seed), 25)
    return {
        "latents": normal_values(streams_of[0], (ITEMS, BPIX, C), 1.0, 6.0, ((0, 8), (1, 4))),
        "clip_tokens": normal_values(streams_of[1], (ITEMS, TXT_PAD, CCOND), 1.0, 6.0, ((0, 8), (1, 4))),
        "time_embed": normal_values(streams_of[2], (ITEMS, RDIM), 1.0, 6.0, ((0, 8),)),
        "bucket_ids": draw_bucket_ids(jax.random.fold_in(streams_of[24], 71), 0),
        "heights": draw_heights(jax.random.fold_in(streams_of[24], 71), 0),
        "widths": draw_widths(jax.random.fold_in(streams_of[24], 71), 0),
        "text_mask": plant((jax.random.randint(streams_of[6], (ITEMS, TXT_PAD), 0, 4) < 3).astype(jnp.int32), jax.random.fold_in(streams_of[6], 1), 0, 1),
        "conv_weight": normal_values(streams_of[7], (9, C), 9 ** -0.5, 2.0, ((1, 32),)),
        "conv_bias": normal_values(streams_of[8], (C,), 0.5, 3.0, ((0, 32),)),
        "in_weight": normal_values(streams_of[9], (C, FF), C ** -0.5, 0.15625, ((0, 32),)),
        "in_bias": normal_values(streams_of[10], (FF,), 0.5, 3.0, ((0, 32),)),
        "grn_gain": normal_values(streams_of[11], (FF,), 0.5, 3.0, ((0, 32),)),
        "grn_bias": normal_values(streams_of[12], (FF,), 0.3, 2.0, ((0, 32),)),
        "out_weight": normal_values(streams_of[13], (FF, C), FF ** -0.5, 0.078125, ((0, 32),)),
        "out_bias": normal_values(streams_of[14], (C,), 0.3, 2.0, ((0, 32),)),
        "time_weight": normal_values(streams_of[15], (RDIM, 2 * C), (4 * RDIM) ** -0.5, 0.375, ((1, 32),)),
        "time_bias": normal_values(streams_of[16], (2 * C,), 0.3, 2.0, ((0, 32),)),
        "map_weight": normal_values(streams_of[17], (CCOND, C), CCOND ** -0.5, 0.15625, ((0, 32),)),
        "map_bias": normal_values(streams_of[18], (C,), 0.3, 2.0, ((0, 32),)),
        "qkv_weight": normal_values(streams_of[19], (C, 3 * C), C ** -0.5, 0.15625, ((0, 32),)),
        "qv_bias": normal_values(streams_of[20], (2 * C,), 0.3, 2.0, ((0, 32),)),
        "proj_weight": normal_values(streams_of[21], (C, C), (C // 64) ** -0.5, 1.25, ((0, 32),)),
        "proj_bias": normal_values(streams_of[22], (C,), 0.3, 2.0, ((0, 32),)),
        "cotangent": normal_values(streams_of[23], (ITEMS, BPIX, C), 1.0, 6.0, ((0, 8), (1, 4))),
    }


@jax.custom_vjp
def low(v):
    return lax.optimization_barrier(v.astype(jnp.bfloat16)).astype(jnp.float32)

@jax.custom_vjp
def low_back(v):
    return v

def low_keep(v):
    return (low(v), None)

def low_pass(kept, grad):
    return (grad,)

def back_keep(v):
    return (v, None)

def back_low(kept, grad):
    return (low(grad),)
low.defvjp(low_keep, low_pass)
low_back.defvjp(back_keep, back_low)
norm_eps = 1e-06
grn_eps = 1e-06
masked_score = -1000000000.0
highest = lax.Precision.HIGHEST

def bucket_shape(bucket_ids):
    bucket_rows = (bucket_ids + 2) * UNIT
    bucket_cols = jnp.where(bucket_ids == 0, 9 * UNIT // 2, jnp.where(bucket_ids == 1, 3 * UNIT, 9 * UNIT // 4))
    return (bucket_rows, bucket_cols)

def pixel_mask(start_pixel, pixel_count, heights, widths, bucket_cols):
    positions = start_pixel + jnp.arange(pixel_count, dtype=jnp.int32)
    row_at = positions[None, :] // bucket_cols[:, None]
    col_at = positions[None, :] % bucket_cols[:, None]
    inside = (row_at < heights[:, None]) & (col_at < widths[:, None])
    return inside.astype(jnp.float32)

def tap_values(extended, bucket_cols, pixel_count, tap_index):
    shift_y = tap_index // 3 - 1
    shift_x = tap_index % 3 - 1
    positions = jnp.arange(pixel_count, dtype=jnp.int32)
    column = positions[None, :] % bucket_cols[:, None]
    source = HALO + positions[None, :] + shift_y * bucket_cols[:, None] + shift_x
    source = jnp.clip(source, 0, extended.shape[1] - 1).astype(jnp.int32)
    picked = jax.vmap(lambda item_rows, item_index: item_rows[item_index])(extended, source).astype(jnp.float32)
    is_valid = (column + shift_x >= 0) & (column + shift_x < bucket_cols[:, None])
    return jnp.where(is_valid[:, :, None], picked, 0.0)

def depthwise(extended, kernel, bucket_cols, pixel_count):
    running = jnp.zeros((extended.shape[0], pixel_count, extended.shape[2]), jnp.float32)
    for tap_index in range(9):
        running = running + tap_values(extended, bucket_cols, pixel_count, tap_index) * kernel[tap_index]
    return running

def layer_norm(values):
    center = values - lax.optimization_barrier(jnp.mean(values, axis=-1, keepdims=True))
    spread = lax.optimization_barrier(jnp.mean(center * center, axis=-1, keepdims=True))
    return center * lax.rsqrt(spread + norm_eps)

def attend(pieces):
    queries, all_keys, all_values, key_keep = pieces
    queries = queries.reshape(queries.shape[0], HEADS, HEAD)
    all_keys = all_keys.reshape(all_keys.shape[0], HEADS, HEAD)
    all_values = all_values.reshape(all_values.shape[0], HEADS, HEAD)
    scores = jnp.einsum('qhd,khd->hqk', queries, all_keys, precision=highest) * HEAD ** (-0.5)
    scores = low_back(scores)
    scores = jnp.where(key_keep[None, None, :] > 0, scores, masked_score)
    biggest = lax.optimization_barrier(jnp.max(scores, axis=-1, keepdims=True))
    weights = jnp.exp(scores - biggest)
    weights = weights / lax.optimization_barrier(jnp.sum(weights, axis=-1, keepdims=True))
    mixed_heads = jnp.einsum('hqk,khd->qhd', low(weights), all_values, precision=highest)
    return mixed_heads.reshape(mixed_heads.shape[0], HEADS * HEAD)

def block(latents, params, clip_tokens, time_embed, bucket_cols, pixel_keep, key_keep):
    conv_weight, conv_bias, in_weight, in_bias, grn_gain, grn_bias, out_weight, out_bias, time_weight, time_bias, map_weight, map_bias, qkv_weight, qv_bias, proj_weight, proj_bias = params
    keep_col = pixel_keep[:, :, None]
    masked = latents * keep_col
    extended = jnp.pad(masked, ((0, 0), (HALO, HALO), (0, 0)))
    conv_out = depthwise(extended, conv_weight, bucket_cols, BPIX) + conv_bias
    normed = low(layer_norm(conv_out))
    hidden = low_back(jnp.einsum('gpc,cf->gpf', normed, in_weight, precision=highest) + in_bias)
    active = jax.nn.gelu(hidden, approximate=False)
    grn_norms = jnp.sqrt(lax.optimization_barrier(jnp.sum(keep_col * active * active, axis=1)))
    grn_ratio = grn_norms / (lax.optimization_barrier(jnp.mean(grn_norms, axis=-1, keepdims=True)) + grn_eps)
    grn_out = low(grn_gain * (active * grn_ratio[:, None, :]) + grn_bias + active)
    branch = low_back(jnp.einsum('gpf,fc->gpc', grn_out, out_weight, precision=highest) + out_bias)
    after_res = latents + keep_col * branch
    modulate = jnp.dot(time_embed, time_weight, precision=highest) + time_bias
    second = after_res * (1.0 + modulate[:, None, :C]) + modulate[:, None, C:]
    normed_two = low(layer_norm(second))
    projected = jnp.einsum('gpc,ce->gpe', normed_two, qkv_weight, precision=highest)
    queries = low(low_back(projected[:, :, :C] + qv_bias[:C]))
    pixel_keys = low(low_back(projected[:, :, C:2 * C]))
    pixel_values = low(low_back(projected[:, :, 2 * C:] + qv_bias[C:]))
    silu_text = low(jax.nn.silu(clip_tokens))
    mapped = low(low_back(jnp.einsum('gtc,ce->gte', silu_text, map_weight, precision=highest) + map_bias))
    text_kv = jnp.einsum('gtc,ce->gte', mapped, qkv_weight[:, C:], precision=highest)
    text_keys = low(low_back(text_kv[:, :, :C]))
    text_values = low(low_back(text_kv[:, :, C:] + qv_bias[C:]))
    all_keys = jnp.concatenate([pixel_keys, text_keys], axis=1)
    all_values = jnp.concatenate([pixel_values, text_values], axis=1)
    attended = lax.map(jax.checkpoint(attend), (queries, all_keys, all_values, key_keep))
    attended = low(low_back(attended))
    result = low_back(jnp.einsum('gpc,ce->gpe', attended, proj_weight, precision=highest) + proj_bias)
    return second + keep_col * result

def reference(latents, clip_tokens, time_embed, bucket_ids, heights, widths, text_mask, conv_weight, conv_bias, in_weight, in_bias, grn_gain, grn_bias, out_weight, out_bias, time_weight, time_bias, map_weight, map_bias, qkv_weight, qv_bias, proj_weight, proj_bias, cotangent):
    params = tuple((weight.astype(jnp.float32) for weight in (conv_weight, conv_bias, in_weight, in_bias, grn_gain, grn_bias, out_weight, out_bias, time_weight, time_bias, map_weight, map_bias, qkv_weight, qv_bias, proj_weight, proj_bias)))
    bucket_cols = bucket_shape(bucket_ids)[1]
    pixel_keep = pixel_mask(0, BPIX, heights, widths, bucket_cols)
    text_keep = text_mask.astype(jnp.float32) * (jnp.arange(TXT_PAD, dtype=jnp.int32) < TXT).astype(jnp.float32)[None, :]
    key_keep = jnp.concatenate([pixel_keep, text_keep], axis=1)
    groups = ITEMS // IPG

    def regroup(stacked):
        return stacked.reshape((groups, IPG) + stacked.shape[1:])
    inputs = tuple((regroup(stacked) for stacked in (latents, clip_tokens, time_embed, bucket_cols, pixel_keep, key_keep, cotangent)))

    def one_group(summed, pieces):
        latent_part, clip_part, embed_part, cols_part, keep_part, keys_part, grad_part = pieces

        def forward(latent_in, param_in):
            return block(latent_in, param_in, clip_part.astype(jnp.float32), embed_part.astype(jnp.float32), cols_part, keep_part, keys_part)
        produced, pullback = jax.vjp(forward, latent_part.astype(jnp.float32), params)
        grad_latent, grad_params = pullback(grad_part.astype(jnp.float32))
        summed = jax.tree.map(lambda running, adding: running + adding, summed, grad_params)
        return (summed, (produced.astype(jnp.bfloat16), grad_latent))
    zero_grads = tuple((jnp.zeros_like(weight) for weight in params))
    summed, (produced, grad_latents) = lax.scan(one_group, zero_grads, inputs)
    output = produced.reshape(ITEMS, BPIX, C)
    grad_latents = grad_latents.reshape(ITEMS, BPIX, C)
    return (output, grad_latents, summed[0], summed[1], summed[2], summed[3], summed[4], summed[5], summed[6], summed[7], summed[8], summed[9], summed[10], summed[11], summed[12], summed[13], summed[14], summed[15])
```

```python
import functools

import jax
import jax.numpy as jnp
from jax import lax
from jax.experimental import pallas as pl
from jax.experimental.pallas import tpu as pltpu
from jax.sharding import Mesh, PartitionSpec as P

HEAD = 64
TXT = 77
UNIT = 8
EDGE = 48

norm_eps = 1e-06
grn_eps = 1e-06
masked_score = -1000000000.0

AXES = ("grp", "duo", "rows")
MESH_ID = pl.DeviceIdType.MESH
F32 = jnp.float32
BF16 = jnp.bfloat16


class Place:
    def __init__(self):
        self.q, self.c, self.z = (lax.axis_index(axis) for axis in AXES)
        self.G, self.D, self.R = (lax.axis_size(axis) for axis in AXES)

    def team(self):
        for step in range(1, self.D * self.R):
            dc, dz = step // self.R, step % self.R
            yield lax.rem(self.c + dc, self.D), lax.rem(self.z + dz, self.R)

    def groups(self):
        for step in range(1, self.G):
            yield lax.rem(self.q + step, self.G)


def signal_all(barrier, targets):
    for target in targets:
        pl.semaphore_signal(barrier, inc=1, device_id=target, device_id_type=MESH_ID)


def run_plan(plan, count_in, count_out, *refs):
    ins, outs = refs[:count_in], refs[count_in : count_in + count_out]
    send_sem, recv_sem, local_sem = refs[count_in + count_out :]
    place = Place()
    greet, messages, local = plan(place, ins, outs)
    barrier = pltpu.get_barrier_semaphore()
    waits = 0
    for target, when in greet:
        if when is None:
            signal_all(barrier, [target])
            waits += 1
        else:

            @pl.when(when)
            def _():
                signal_all(barrier, [target])

    for _, when in greet:
        if when is not None:
            waits = waits + jnp.where(when, 1, 0).astype(jnp.int32)
    pl.semaphore_wait(barrier, waits)
    copies = []
    arrived = set()

    def guarded(when, act):
        if when is None:
            act()
        else:
            pl.when(when)(act)

    for number, (src, dst, target, after, when) in enumerate(messages):
        for earlier in after:
            if earlier not in arrived:
                arrived.add(earlier)
                guarded(copies[earlier][1], copies[earlier][0].wait_recv)
        copy = pltpu.make_async_remote_copy(
            src_ref=src,
            dst_ref=dst,
            send_sem=send_sem.at[number],
            recv_sem=recv_sem.at[number],
            device_id=target,
            device_id_type=MESH_ID,
        )
        guarded(when, copy.start)
        copies.append((copy, when))
    stays = []
    for number, (src, dst, when) in enumerate(local):
        copy = pltpu.make_async_copy(src, dst, local_sem.at[number])
        guarded(when, copy.start)
        stays.append((copy, when))
    for copy, when in stays:
        guarded(when, copy.wait)
    for number, (copy, when) in enumerate(copies):
        if number not in arrived:
            guarded(when, copy.wait_recv)
    for copy, when in copies:
        guarded(when, copy.wait_send)


def exchange(ident, name, plan, arrays, results, messages, local):
    spot = pl.BlockSpec(memory_space=pl.ANY)
    return pl.pallas_call(
        functools.partial(run_plan, plan, len(arrays), len(results)),
        out_shape=[jax.ShapeDtypeStruct(shape, kind) for shape, kind in results],
        in_specs=[spot] * len(arrays),
        out_specs=[spot] * len(results),
        scratch_shapes=[
            pltpu.SemaphoreType.DMA((messages,)),
            pltpu.SemaphoreType.DMA((messages,)),
            pltpu.SemaphoreType.DMA((max(local, 1),)),
        ],
        compiler_params=pltpu.CompilerParams(collective_id=ident, has_side_effects=True),
        name=name,
    )(*arrays)


def team_greet(p):
    return [({"duo": c, "rows": z}, None) for c, z in p.team()]


def group_greet(p):
    return [({"grp": q}, None) for q in p.groups()]


def rows_greet(p):
    return [({"rows": lax.rem(p.z + step, p.R)}, None) for step in range(1, p.R)]


def duo_greet(p):
    return [({"duo": lax.rem(p.c + step, p.D)}, None) for step in range(1, p.D)]


def team_swap(p, src, dst, slot=None):
    mine = p.c * p.R + p.z
    return (
        [
            (src.at[c * p.R + z], dst.at[mine], {"duo": c, "rows": z}, (), None)
            for c, z in p.team()
        ],
        [(src.at[mine], dst.at[mine], None)],
    )


def team_gather(p, src, dst):
    mine = p.c * p.R + p.z
    return (
        [(src, dst.at[mine], {"duo": c, "rows": z}, (), None) for c, z in p.team()],
        [(src, dst.at[mine], None)],
    )


def group_gather(p, src, dst):
    return (
        [(src, dst.at[p.q], {"grp": q}, (), None) for q in p.groups()],
        [(src, dst.at[p.q], None)],
    )


def group_swap(p, src, dst):
    return (
        [(src.at[q], dst.at[p.q], {"grp": q}, (), None) for q in p.groups()],
        [(src.at[p.q], dst.at[p.q], None)],
    )


def item_gather(p, src, dst, base):
    messages = []
    for step in range(1, p.R):
        messages.append((src, dst.at[p.c, p.z], {"rows": lax.rem(p.z + step, p.R)}, (), None))
    other = {"duo": lax.rem(p.c + 1, p.D)}
    messages.append((src, dst.at[p.c, p.z], other, (), None))
    for step in range(1, p.R):
        block = lax.rem(p.z - step + p.R, p.R)
        messages.append(
            (dst.at[p.c, block], dst.at[p.c, block], other, (base + step - 1,), None)
        )
    return messages, [(src, dst.at[p.c, p.z], None)]


def layer_stats(values):
    center = values - jnp.mean(values, axis=-1, keepdims=True)
    spread = jnp.mean(center * center, axis=-1, keepdims=True)
    inverse = lax.rsqrt(spread + norm_eps)
    return center * inverse, inverse


def layer_back(grad, hat, inverse):
    first = jnp.mean(grad, axis=-1, keepdims=True)
    second = jnp.mean(grad * hat, axis=-1, keepdims=True)
    return inverse * (grad - first - hat * second)


def mm(left, right):
    return jnp.dot(left, right, preferred_element_type=F32)


def mm_t(left, right):
    return lax.dot_general(left, right, (((1,), (1,)), ((), ())), preferred_element_type=F32)


def t_mm(left, right):
    return lax.dot_general(left, right, (((0,), (0,)), ((), ())), preferred_element_type=F32)


def columns_of(bucket_ids):
    return jnp.where(
        bucket_ids == 0, 9 * UNIT // 2, jnp.where(bucket_ids == 1, 3 * UNIT, 9 * UNIT // 4)
    )


def pixel_mask(positions, height, width, cols):
    row_at = positions // cols
    col_at = positions % cols
    return ((row_at < height) & (col_at < width)).astype(F32)


def reduce_items(p_kernel_id, name, part):
    duo, rows, count, width = part.shape

    def kernel(part_ref, out_ref, mate, passed, landed, s1, r1, s2, r2):
        p = Place()
        barrier = pltpu.get_barrier_semaphore()
        greet = [target for target, _ in duo_greet(p) + rows_greet(p)]
        signal_all(barrier, greet)
        pl.semaphore_wait(barrier, len(greet))
        other = lax.rem(p.c + 1, duo)
        order = list(range(1, rows)) + [0]
        first = []
        for step in order:
            block = lax.rem(p.z + step, rows)
            copy = pltpu.make_async_remote_copy(
                src_ref=part_ref.at[other, block],
                dst_ref=mate.at[block],
                send_sem=s1.at[step],
                recv_sem=r1.at[step],
                device_id={"duo": other},
                device_id_type=MESH_ID,
            )
            copy.start()
            first.append(copy)
        second = []
        for copy, step in zip(first, order):
            block = lax.rem(p.z + step, rows)
            copy.wait_recv()
            total = part_ref[p.c, block].astype(F32) + mate[block].astype(F32)
            if step == 0:
                out_ref[...] = total
            else:
                passed[block] = total.astype(BF16)
                onward = pltpu.make_async_remote_copy(
                    src_ref=passed.at[block],
                    dst_ref=landed.at[p.z],
                    send_sem=s2.at[step],
                    recv_sem=r2.at[step],
                    device_id={"rows": block},
                    device_id_type=MESH_ID,
                )
                onward.start()
                second.append((onward, step))
        for onward, step in second:
            onward.wait_recv()
            out_ref[...] += landed[lax.rem(p.z - step + rows, rows)].astype(F32)
        for copy in first:
            copy.wait_send()
        for onward, _ in second:
            onward.wait_send()

    spot = pl.BlockSpec(memory_space=pltpu.VMEM)
    block = (rows, count, width)
    return pl.pallas_call(
        kernel,
        out_shape=jax.ShapeDtypeStruct((count, width), F32),
        in_specs=[spot],
        out_specs=spot,
        scratch_shapes=[pltpu.VMEM(block, BF16)] * 3
        + [pltpu.SemaphoreType.DMA((rows,))] * 4,
        compiler_params=pltpu.CompilerParams(
            collective_id=p_kernel_id, has_side_effects=True, vmem_limit_bytes=48 * 2**20
        ),
        name=name,
    )(part)


def pad_rows(values, rows):
    return jnp.pad(values, ((0, rows - values.shape[0]),) + ((0, 0),) * (values.ndim - 1))


def pack_flat(pieces, rows, kind):
    flat = jnp.concatenate([piece.astype(kind).reshape(-1) for piece in pieces])
    return jnp.pad(flat, (0, rows * 128 - flat.shape[0])).reshape(rows, 128)


def body(
    latents,
    clip_tokens,
    time_embed,
    bucket_ids,
    heights,
    widths,
    text_mask,
    conv_weight,
    conv_bias,
    in_weight,
    in_bias,
    grn_gain,
    grn_bias,
    out_weight,
    out_bias,
    time_weight,
    time_bias,
    map_weight,
    map_bias,
    qkv_weight,
    qv_bias,
    proj_weight,
    proj_bias,
    cotangent,
):
    G, D, R = (lax.axis_size(axis) for axis in AXES)
    T = D * R
    q, c, z = (lax.axis_index(axis) for axis in AXES)
    N = latents.shape[1]
    C = latents.shape[2]
    pixels = R * N
    FFS = in_bias.shape[0]
    FL = G * FFS
    FF = in_weight.shape[1]
    cs = conv_bias.shape[0]
    ms = map_weight.shape[0]
    slots = clip_tokens.shape[1]
    text_all = R * slots
    HW = C // T
    even = G == R
    head_slice = R and (D * z + c)

    latents = latents[0]
    cotangent = cotangent[0]
    cols = columns_of(bucket_ids)[0]
    positions = z * N + jnp.arange(N, dtype=jnp.int32)
    keep = pixel_mask(positions, heights[0], widths[0], cols)[:, None]
    masked = latents * keep.astype(BF16)

    in_cut = in_weight.reshape(cs, G, T, FFS).transpose(2, 0, 1, 3).reshape(T, cs, FL)
    qkv_cut = qkv_weight.reshape(cs, 3, R, D, HW).transpose(3, 2, 0, 1, 4).reshape(T, cs, 3 * HW)
    mp = -(-ms // 16) * 16
    map_cut = jnp.pad(
        map_weight.reshape(ms, T, HW).transpose(1, 0, 2), ((0, 0), (0, mp - ms), (0, 0))
    )
    sp = -(-slots // 16) * 16
    clip_pad = pad_rows(clip_tokens[0], sp)
    meta = [
        conv_weight,
        conv_bias,
        out_bias,
        time_bias,
        map_bias,
        qv_bias,
        proj_bias,
        time_weight,
        time_embed,
        heights,
        widths,
        bucket_ids,
        text_mask,
    ]
    sizes = [piece.size for piece in meta]
    mrows = -(-sum(sizes) // 2048) * 16
    small = pack_flat(meta, mrows, BF16)
    frows = -(-3 * FFS // 2048) * 16
    fvec = pack_flat([in_bias, grn_gain, grn_bias], frows, BF16)

    def plan_start(p, ins, outs):
        edge_ref, small_ref, in_ref, qkv_ref, map_ref, clip_ref, fvec_ref = ins
        edge_out, small_out, in_out, qkv_out, map_out, clip_out, fvec_out = outs
        up, down = lax.rem(p.z + 1, R), lax.rem(p.z + R - 1, R)
        count = edge_ref.shape[0]
        messages = [
            (edge_ref.at[pl.ds(count - EDGE, EDGE)], edge_out.at[0], {"rows": up}, (), None),
            (edge_ref.at[pl.ds(0, EDGE)], edge_out.at[1], {"rows": down}, (), None),
        ]
        local = []
        mine = p.c * R + p.z
        stage, kept = group_gather(p, small_ref, small_out.at[mine])
        base = len(messages)
        messages += stage
        local += kept
        for c2, z2 in p.team():
            messages.append(
                (small_ref, small_out.at[mine, p.q], {"duo": c2, "rows": z2}, (), None)
            )
        for step, q2 in enumerate(range(1, G)):
            block = lax.rem(p.q - q2 + G, G)
            for c2, z2 in p.team():
                messages.append(
                    (
                        small_out.at[mine, block],
                        small_out.at[mine, block],
                        {"duo": c2, "rows": z2},
                        (base + step,),
                        None,
                    )
                )
        for ref, out in ((in_ref, in_out), (qkv_ref, qkv_out), (map_ref, map_out)):
            stage, kept = team_swap(p, ref, out)
            messages += stage
            local += kept
        stage, kept = team_gather(p, clip_ref, clip_out)
        messages += stage
        local += kept
        stage, kept = group_gather(p, fvec_ref, fvec_out)
        messages += stage
        local += kept
        return team_greet(p) + group_greet(p), messages, local

    count = 2 + (G - 1) + (T - 1) * G + 4 * (T - 1) + (G - 1)
    edges, small_all, in_rows, qkv_rows, map_rows, clip_all, fvec_all = exchange(
        0,
        "exchange_start",
        plan_start,
        [masked, small, in_cut, qkv_cut, map_cut, clip_pad, fvec],
        [
            ((2, EDGE, C), BF16),
            ((T, G, mrows, 128), BF16),
            ((T, cs, FL), BF16),
            ((T, cs, 3 * HW), BF16),
            ((T, mp, HW), BF16),
            ((T, sp, clip_tokens.shape[2]), BF16),
            ((G, frows, 128), BF16),
        ],
        count,
        6,
    )
    flat = small_all.reshape(D, R, G, mrows * 128).transpose(2, 0, 1, 3).reshape(T * G, -1)
    parts = []
    at = 0
    for size in sizes:
        parts.append(flat[:, at : at + size])
        at += size
    shards = T * G

    def whole(part):
        return part.reshape(-1)

    kernel_full = parts[0].reshape(shards, 9, cs).transpose(1, 0, 2).reshape(9, C).astype(F32)
    conv_bias_full = whole(parts[1]).astype(F32)
    out_bias_full = whole(parts[2]).astype(F32)
    time_bias_full = whole(parts[3]).astype(F32)
    map_bias_full = whole(parts[4]).astype(F32)
    qv_full = whole(parts[5]).astype(F32)
    proj_bias_full = whole(parts[6]).astype(F32)
    time_full = parts[7].reshape(shards, time_weight.shape[0], -1).transpose(1, 0, 2)
    time_full = time_full.reshape(time_weight.shape[0], -1)
    per_item = [part.reshape(G, D, R, -1)[:, :, 0] for part in parts[8:]]
    embed_all = per_item[0].reshape(G * D, -1).astype(F32)
    pair = [lax.dynamic_index_in_dim(part, q, 0, keepdims=False) for part in per_item[1:]]
    pair_height, pair_width, pair_bucket = (part.astype(jnp.int32) for part in pair[:3])
    pair_cols = columns_of(pair_bucket)
    pair_keep = pixel_mask(
        jnp.arange(pixels, dtype=jnp.int32)[None, :], pair_height, pair_width, pair_cols
    )
    text_keep = pair[3].astype(F32) * (jnp.arange(text_all) < TXT).astype(F32)[None, :]
    key_keep = jnp.concatenate([pair_keep, text_keep], axis=1)
    fv = fvec_all.reshape(G, -1)[:, : 3 * FFS].reshape(G, 3, FFS).transpose(1, 0, 2)
    in_bias_s, gain_s, grn_bias_s = fv.reshape(3, FL).astype(F32)

    def extend(low, mid, high):
        return jnp.concatenate(
            [
                jnp.where(z > 0, low, jnp.zeros_like(low)),
                mid,
                jnp.where(z < R - 1, high, jnp.zeros_like(high)),
            ],
            axis=0,
        )

    column = (positions % cols)[:, None]

    def tap(extended, dy, dx):
        piece = lax.dynamic_slice_in_dim(extended, EDGE + dy * cols + dx, N, axis=0).astype(F32)
        ok = (column + dx >= 0) & (column + dx < cols)
        return jnp.where(ok, piece, 0.0)

    extended = extend(edges[0], masked, edges[1])
    conv_out = jnp.zeros((N, C), F32) + conv_bias_full
    for index in range(9):
        conv_out = conv_out + tap(extended, index // 3 - 1, index % 3 - 1) * kernel_full[index]
    norm_hat, norm_inv = layer_stats(conv_out)
    normed = norm_hat.astype(BF16)

    def plan_first(p, ins, outs):
        messages, local = item_gather(p, ins[0], outs[0], 0)
        for ref, out in zip(ins[1:], outs[1:]):
            stage, kept = group_gather(p, ref, out)
            messages += stage
            local += kept
        return rows_greet(p) + duo_greet(p) + group_greet(p), messages, local

    normed_all, in_full, out_full, map_full = exchange(
        1,
        "exchange_normed",
        plan_first,
        [normed, in_rows, out_weight, map_rows],
        [
            ((D, R, N, C), BF16),
            ((G,) + in_rows.shape, BF16),
            ((G,) + out_weight.shape, BF16),
            ((G,) + map_rows.shape, BF16),
        ],
        2 * R - 1 + 3 * (G - 1),
        4,
    )
    normed_all = normed_all.reshape(D * pixels, C)
    in_full = in_full.reshape(C, FL)
    out_full = out_full.reshape(FL, C)
    map_full = map_full[:, :, :ms].reshape(G * T * ms, HW)
    keep_all = pair_keep.reshape(D, pixels, 1)

    hidden = mm(normed_all, in_full) + in_bias_s
    gate = 0.5 * lax.erfc(-hidden * (0.5**0.5))
    active = hidden * gate
    active3 = active.reshape(D, pixels, FL)
    squares = jnp.sum(keep_all * active3 * active3, axis=1)
    grn_norms = jnp.sqrt(squares)

    def team_total(ident, name, values):
        block = jnp.zeros((8, 128), F32).at[0, :D].set(values)

        def plan(p, ins, outs):
            messages, local = team_gather(p, ins[0], outs[0])
            return team_greet(p), messages, local

        (everyone,) = exchange(
            ident, name, plan, [block], [((T, 8, 128), F32)], T - 1, 1
        )
        return jnp.sum(everyone[:, 0, :D], axis=0)

    norm_mean = (team_total(2, "total_norms", jnp.sum(grn_norms, axis=1)) / FF + grn_eps)[:, None]
    grn_ratio = grn_norms / norm_mean
    grn_out = (
        (gain_s * (active3 * grn_ratio[:, None, :]) + grn_bias_s + active3)
        .astype(BF16)
        .reshape(D * pixels, FL)
    )
    branch = reduce_items(
        3, "reduce_branch", mm(grn_out, out_full).astype(BF16).reshape(D, R, N, C)
    )
    branch = branch + out_bias_full
    after_res = latents.astype(F32) + keep * branch
    modulate = mm(time_embed, time_full) + time_bias_full
    scale_by = 1.0 + modulate[:, :C]
    second = after_res * scale_by + modulate[:, C:]
    two_hat, two_inv = layer_stats(second)
    normed_two = two_hat.astype(BF16)

    silu_text = jax.nn.silu(clip_all[:, :slots].astype(F32)).astype(BF16)
    silu_text = silu_text.reshape(D * text_all, -1)
    map_bias_s = lax.dynamic_slice_in_dim(map_bias_full, (c * R + z) * HW, HW)
    mapped_s = (mm(silu_text, map_full) + map_bias_s).astype(BF16)
    grad_result = (keep * cotangent.astype(F32)).astype(BF16)

    def plan_second(p, ins, outs):
        two, grad, text, qkv = ins[:4]
        messages, local = item_gather(p, two, outs[0], 0)
        stage, kept = team_gather(p, text, outs[2])
        messages += stage
        local += kept
        stage, kept = item_gather(p, grad, outs[1], len(messages))
        messages += stage
        local += kept
        stage, kept = group_gather(p, qkv, outs[3])
        messages += stage
        local += kept
        greet = team_greet(p) + group_greet(p)
        if even:
            proj, proj_out = ins[4], outs[4]
            selfish = p.q == p.z
            for step in range(G):
                to = lax.rem(p.z + step, G)
                where = {"grp": to, "duo": p.c, "rows": p.q}
                when = None if step else p.q != p.z
                messages.append((proj, proj_out.at[p.z], where, (), when))
                source = {"grp": p.z, "duo": p.c, "rows": lax.rem(p.q - step + G, G)}
                greet.append((source, when))
            local.append((proj, proj_out.at[p.z], selfish))
        return greet, messages, local

    arrays = [normed_two, grad_result, mapped_s, qkv_rows]
    results = [
        ((D, R, N, C), BF16),
        ((D, R, N, C), BF16),
        ((T,) + mapped_s.shape, BF16),
        ((G,) + qkv_rows.shape, BF16),
    ]
    if even:
        arrays.append(proj_weight)
        results.append(((R,) + proj_weight.shape, BF16))
    gathered = exchange(
        4,
        "exchange_second",
        plan_second,
        arrays,
        results,
        2 * (2 * R - 1) + T - 1 + G - 1 + (G if even else 0),
        5,
    )
    two_all = gathered[0].reshape(D * pixels, C)
    gres_all = gathered[1].reshape(D * pixels, C)
    mapped = gathered[2].transpose(1, 0, 2).reshape(D * text_all, C)
    qkv_full = gathered[3].reshape(C, 3 * HW)
    if even:
        proj_s = gathered[4].reshape(HW, C)
    else:
        proj_whole = lax.all_gather(proj_weight, AXES, axis=0, tiled=True)
        proj_s = lax.dynamic_slice_in_dim(proj_whole, head_slice * HW, HW, axis=0)

    q_bias = lax.dynamic_slice_in_dim(qv_full, head_slice * HW, HW)
    v_bias = lax.dynamic_slice_in_dim(qv_full, C + head_slice * HW, HW)
    projected = mm(two_all, qkv_full)
    heads = HW // HEAD

    def split(values):
        return values.astype(BF16).reshape(D, -1, heads, HEAD)

    queries = split(projected[:, :HW] + q_bias)
    text_kv = mm(mapped, qkv_full[:, HW:])
    keys = jnp.concatenate([split(projected[:, HW : 2 * HW]), split(text_kv[:, :HW])], axis=1)
    values = jnp.concatenate(
        [split(projected[:, 2 * HW :] + v_bias), split(text_kv[:, HW:] + v_bias)], axis=1
    )
    score_scale = HEAD ** (-0.5)

    def dots(spec, left, right):
        return jnp.einsum(spec, left, right, preferred_element_type=F32)

    scores = dots("iqhd,ikhd->ihqk", queries, keys) * score_scale
    scores = jnp.where(key_keep[:, None, None, :] > 0, scores, masked_score)
    weights = jnp.exp(scores - jnp.max(scores, axis=-1, keepdims=True))
    probs = weights / jnp.sum(weights, axis=-1, keepdims=True)
    probs_low = probs.astype(BF16)
    attended = dots("ihqk,ikhd->iqhd", probs_low, values).astype(BF16).reshape(D * pixels, HW)
    result_part = mm(attended, proj_s).astype(BF16).reshape(D, R, N, C)
    grad_att = split(mm_t(gres_all, proj_s))
    grad_probs = dots("iqhd,ikhd->ihqk", grad_att, values)
    grad_values = dots("ihqk,iqhd->ikhd", probs_low, grad_att).astype(BF16)
    row_sums = jnp.sum(probs * grad_probs, axis=-1, keepdims=True)
    grad_scores = (probs * (grad_probs - row_sums)).astype(BF16)
    grad_queries = (dots("ihqk,ikhd->iqhd", grad_scores, keys) * score_scale).astype(BF16)
    grad_keys = (dots("ihqk,iqhd->ikhd", grad_scores, queries) * score_scale).astype(BF16)
    grad_pixel = jnp.concatenate(
        [
            piece.reshape(D * pixels, HW)
            for piece in (grad_queries, grad_keys[:, :pixels], grad_values[:, :pixels])
        ],
        axis=1,
    )
    grad_text = jnp.concatenate(
        [
            piece.reshape(D * text_all, HW)
            for piece in (grad_keys[:, pixels:], grad_values[:, pixels:])
        ],
        axis=1,
    )
    grad_qkv = t_mm(two_all, grad_pixel) + jnp.pad(t_mm(mapped, grad_text), ((0, 0), (HW, 0)))
    q_bias_grad = jnp.sum(grad_pixel[:, :HW].astype(F32), axis=0)
    v_bias_grad = jnp.sum(grad_pixel[:, 2 * HW :].astype(F32), axis=0) + jnp.sum(
        grad_text[:, HW:].astype(F32), axis=0
    )
    grad_proj = t_mm(attended, gres_all)
    mapped_part = mm_t(grad_text, qkv_full[:, HW:]).astype(BF16)
    mapped_part = mapped_part.reshape(D * text_all, T, HW).transpose(1, 0, 2)
    two_part = mm_t(grad_pixel, qkv_full).astype(BF16).reshape(D, R, N, C)

    result = reduce_items(5, "reduce_result", result_part) + proj_bias_full
    output = (second + keep * result).astype(BF16)
    grad_two = reduce_items(6, "reduce_two", two_part)

    grad_output = cotangent.astype(F32)
    grad_second = grad_output + layer_back(grad_two, two_hat, two_inv)
    grad_modulate = jnp.concatenate(
        [jnp.sum(grad_second * after_res, axis=0), jnp.sum(grad_second, axis=0)]
    )
    grad_after = grad_second * scale_by
    grad_branch = (keep * grad_after).astype(BF16)

    def plan_third(p, ins, outs):
        messages, local = item_gather(p, ins[0], outs[0], 0)
        stage, kept = team_swap(p, ins[1], outs[1])
        messages += stage
        local += kept
        stage, kept = group_swap(p, ins[2], outs[2])
        messages += stage
        local += kept
        greet = team_greet(p) + group_greet(p)
        if even:
            proj, proj_out = ins[3], outs[3]
            for step in range(G):
                to = lax.rem(p.q + step, G)
                where = {"grp": p.z, "duo": p.c, "rows": to}
                when = None if step else p.q != p.z
                messages.append((proj.at[to], proj_out.at[p.q], where, (), when))
                source = {"grp": lax.rem(p.z - step + G, G), "duo": p.c, "rows": p.q}
                greet.append((source, when))
            local.append((proj.at[p.z], proj_out.at[p.q], p.q == p.z))
        return greet, messages, local

    arrays = [grad_branch, mapped_part, grad_qkv.astype(BF16).reshape(G, T * cs, 3 * HW)]
    results = [
        ((D, R, N, C), BF16),
        (mapped_part.shape, BF16),
        ((G, T * cs, 3 * HW), BF16),
    ]
    if even:
        arrays.append(grad_proj.astype(BF16).reshape(R, cs, C))
        results.append(((R, cs, C), BF16))
    gathered = exchange(
        7,
        "exchange_branch",
        plan_third,
        arrays,
        results,
        2 * R - 1 + T - 1 + G - 1 + (G if even else 0),
        4,
    )
    gb_all = gathered[0].reshape(D * pixels, C)
    grad_mapped = jnp.sum(gathered[1].astype(F32), axis=0).astype(BF16)
    qkv_sum = jnp.sum(gathered[2].astype(F32), axis=0).astype(BF16).reshape(T, cs, 3 * HW)
    if even:
        grad_proj_out = jnp.sum(gathered[3].astype(F32), axis=0)
    else:
        spread = jnp.zeros((C, C), F32)
        spread = lax.dynamic_update_slice_in_dim(spread, grad_proj, head_slice * HW, axis=0)
        grad_proj_out = lax.psum_scatter(spread, AXES, scatter_dimension=0, tiled=True)
    grad_map = t_mm(silu_text, grad_mapped).astype(BF16)
    grad_map = jnp.pad(
        grad_map.reshape(G, T, ms, HW), ((0, 0), (0, 0), (0, mp - ms), (0, 0))
    )
    map_bias_grad = jnp.sum(grad_mapped.astype(F32), axis=0)

    grad_out = t_mm(grn_out, gb_all).astype(BF16).reshape(G, FFS, C)
    grad_grn = mm_t(gb_all, out_full)
    grad_grn3 = grad_grn.reshape(D, pixels, FL)
    moment = jnp.sum(grad_grn3 * active3, axis=1)
    grad_gain = jnp.sum(moment * grn_ratio, axis=0)
    grad_grn_bias = jnp.sum(grad_grn, axis=0)
    ratio_grad = moment * gain_s
    cross = team_total(8, "total_cross", jnp.sum(ratio_grad * grn_norms, axis=1))[:, None]
    grad_norms = ratio_grad / norm_mean - cross / (FF * norm_mean * norm_mean)
    grad_active = (
        grad_grn3 * (gain_s * grn_ratio[:, None, :] + 1.0)
        + keep_all * active3 * (grad_norms / grn_norms)[:, None, :]
    ).reshape(D * pixels, FL)
    density = jnp.exp(-0.5 * hidden * hidden) * 0.3989422804014327
    grad_hidden = (grad_active * (gate + hidden * density)).astype(BF16)
    grad_in_bias = jnp.sum(grad_hidden.astype(F32), axis=0)
    grad_in = t_mm(normed_all, grad_hidden).astype(BF16).reshape(G, T * cs, FL)
    back_part = mm_t(grad_hidden, in_full).astype(BF16).reshape(D, R, N, C)

    def plan_fourth(p, ins, outs):
        messages, local = [], []
        for ref, out in zip(ins[:3], outs[:3]):
            stage, kept = group_swap(p, ref, out)
            messages += stage
            local += kept
        stage, kept = team_swap(p, ins[3], outs[3])
        messages += stage
        local += kept
        return team_greet(p) + group_greet(p), messages, local

    fgrads = jnp.stack([grad_in_bias, grad_gain, grad_grn_bias]).reshape(3, G, FFS)
    fgrads = fgrads.transpose(1, 0, 2).reshape(G, -1)
    grows = -(-fgrads.shape[1] // 1024) * 8
    fgrads = jnp.pad(fgrads, ((0, 0), (0, grows * 128 - fgrads.shape[1]))).reshape(G, grows, 128)

    grad_conv_in = reduce_items(9, "reduce_back", back_part)
    out_sum, in_sum, map_sum, qkv_team = exchange(
        10,
        "exchange_grads",
        plan_fourth,
        [grad_out, grad_in, grad_map.reshape(G, T * mp, HW), qkv_sum],
        [
            (grad_out.shape, BF16),
            (grad_in.shape, BF16),
            ((G, T * mp, HW), BF16),
            (qkv_sum.shape, BF16),
        ],
        3 * (G - 1) + T - 1,
        4,
    )
    grad_out_shard = jnp.sum(out_sum.astype(F32), axis=0)
    grad_conv = layer_back(grad_conv_in, norm_hat, norm_inv)
    taps = [
        jnp.sum(tap(extended, index // 3 - 1, index % 3 - 1) * grad_conv, axis=0)
        for index in range(9)
    ]
    in_back = jnp.sum(in_sum.astype(F32), axis=0).astype(BF16).reshape(T, cs, FL)
    map_back = jnp.sum(map_sum.astype(F32), axis=0).astype(BF16).reshape(T, mp, HW)

    def by_shard(values):
        return values.reshape(shards, -1)

    def placed(values, start, size):
        return lax.dynamic_update_slice_in_dim(jnp.zeros((size,), F32), values, start, axis=0)

    map_bias_vec = placed(map_bias_grad, (c * R + z) * HW, C)
    qv_vec = jnp.concatenate(
        [
            placed(q_bias_grad, head_slice * HW, C),
            placed(v_bias_grad, head_slice * HW, C),
        ]
    )
    pieces = [
        jnp.stack(taps).reshape(9, shards, cs).transpose(1, 0, 2).reshape(shards, -1),
        by_shard(jnp.sum(grad_conv, axis=0)),
        by_shard(jnp.sum(grad_branch.astype(F32), axis=0)),
        by_shard(jnp.sum(grad_result.astype(F32), axis=0)),
        by_shard(map_bias_vec),
        by_shard(qv_vec),
        by_shard(grad_modulate),
    ]
    widths_of = [piece.shape[1] for piece in pieces]
    tiny = jnp.concatenate(pieces, axis=1)
    trows = -(-tiny.shape[1] // 1024) * 8
    tiny = jnp.pad(tiny, ((0, 0), (0, trows * 128 - tiny.shape[1])))
    tiny = tiny.reshape(G, T, trows, 128).transpose(1, 0, 2, 3)

    def plan_fifth(p, ins, outs):
        up, down = lax.rem(p.z + 1, R), lax.rem(p.z + R - 1, R)
        conv_ref = ins[0]
        count = conv_ref.shape[0]
        messages = [
            (conv_ref.at[pl.ds(count - EDGE, EDGE)], outs[0].at[0], {"rows": up}, (), None),
            (conv_ref.at[pl.ds(0, EDGE)], outs[0].at[1], {"rows": down}, (), None),
        ]
        local = []
        for ref, out in zip(ins[1:4], outs[1:4]):
            stage, kept = team_swap(p, ref, out)
            messages += stage
            local += kept
        stage, kept = group_swap(p, ins[4], outs[4])
        messages += stage
        local += kept
        return team_greet(p) + group_greet(p), messages, local

    conv_low = grad_conv.astype(BF16)
    conv_edges, tiny_team, in_team, map_team, f_sum = exchange(
        11,
        "exchange_tail",
        plan_fifth,
        [conv_low, tiny, in_back, map_back, fgrads],
        [
            ((2, EDGE, C), BF16),
            (tiny.shape, F32),
            (in_back.shape, BF16),
            (map_back.shape, BF16),
            (fgrads.shape, F32),
        ],
        2 + 3 * (T - 1) + G - 1,
        4,
    )
    tiny_items = jnp.sum(tiny_team.reshape(D, R, G, trows, 128), axis=1).transpose(1, 0, 2, 3)

    def plan_sixth(p, ins, outs):
        messages, local = group_swap(p, ins[0], outs[0])
        return group_greet(p), messages, local

    (tiny_all,) = exchange(
        12,
        "exchange_tiny",
        plan_sixth,
        [tiny_items],
        [((G, D, trows, 128), F32)],
        G - 1,
        1,
    )
    tiny_all = tiny_all.reshape(G * D, -1)
    tiny_sum = jnp.sum(tiny_all, axis=0)
    outs = []
    at = 0
    for width in widths_of[:-1]:
        outs.append(tiny_sum[at : at + width])
        at += width
    modulate_items = tiny_all[:, at : at + widths_of[-1]]
    grad_time = lax.dot_general(
        embed_all,
        modulate_items,
        (((0,), (0,)), ((), ())),
        precision=lax.Precision.HIGHEST,
    )
    grad_time_bias = jnp.sum(modulate_items, axis=0)

    grad_extended = extend(conv_edges[0], conv_low, conv_edges[1])
    spread = jnp.zeros((N, C), F32)
    for index in range(9):
        spread = spread + tap(grad_extended, 1 - index // 3, 1 - index % 3) * kernel_full[index]
    grad_latents = grad_after + keep * spread

    grad_in_shard = in_team.astype(F32).reshape(T, cs, G, FFS).transpose(1, 2, 0, 3).reshape(cs, FF)
    grad_map_shard = map_team[:, :ms].astype(F32).transpose(1, 0, 2).reshape(ms, C)
    grad_qkv_shard = (
        qkv_team.astype(F32)
        .reshape(D, R, cs, 3, HW)
        .transpose(2, 3, 1, 0, 4)
        .reshape(cs, 3 * C)
    )
    f_total = jnp.sum(f_sum, axis=0).reshape(-1)
    return (
        output[None],
        grad_latents[None],
        outs[0].reshape(9, cs),
        outs[1],
        grad_in_shard,
        f_total[:FFS],
        f_total[FFS : 2 * FFS],
        f_total[2 * FFS : 3 * FFS],
        grad_out_shard,
        outs[2],
        grad_time,
        grad_time_bias,
        grad_map_shard,
        outs[4],
        grad_qkv_shard,
        outs[5],
        grad_proj_out,
        outs[3],
    )


def solution(mesh):
    items, rows = mesh.devices.shape
    fine = Mesh(mesh.devices.reshape(items // 2, 2, rows), AXES)
    item = ("grp", "duo")
    full = AXES
    ins = (
        P(item, "rows", None),
        P(item, "rows", None),
        P(item, None),
        P(item),
        P(item),
        P(item),
        P(item, None),
        P(None, full),
        P(full),
        P(full, None),
        P(full),
        P(full),
        P(full),
        P(full, None),
        P(full),
        P(None, full),
        P(full),
        P(full, None),
        P(full),
        P(full, None),
        P(full),
        P(full, None),
        P(full),
        P(item, "rows", None),
    )
    outs = (
        P(item, "rows", None),
        P(item, "rows", None),
        P(None, full),
        P(full),
        P(full, None),
        P(full),
        P(full),
        P(full),
        P(full, None),
        P(full),
        P(None, full),
        P(full),
        P(full, None),
        P(full),
        P(full, None),
        P(full),
        P(full, None),
        P(full),
    )
    return jax.shard_map(body, mesh=fine, in_specs=ins, out_specs=outs, check_vma=False)
```

```python
import functools

import jax
import jax.numpy as jnp
from jax import lax
from jax.experimental import pallas as pl
from jax.experimental.pallas import tpu as pltpu
from jax.sharding import Mesh, PartitionSpec as P

HEAD = 64
TXT = 77
UNIT = 8
EDGE = 48

norm_eps = 1e-06
grn_eps = 1e-06
masked_score = -1000000000.0

AXES = ("grp", "duo", "rows")
MESH_ID = pl.DeviceIdType.MESH
F32 = jnp.float32
BF16 = jnp.bfloat16


class Place:
    def __init__(self):
        self.q, self.c, self.z = (lax.axis_index(axis) for axis in AXES)
        self.G, self.D, self.R = (lax.axis_size(axis) for axis in AXES)

    def team(self):
        for step in range(1, self.D * self.R):
            dc, dz = step // self.R, step % self.R
            yield lax.rem(self.c + dc, self.D), lax.rem(self.z + dz, self.R)

    def groups(self):
        for step in range(1, self.G):
            yield lax.rem(self.q + step, self.G)


def signal_all(barrier, targets):
    for target in targets:
        pl.semaphore_signal(barrier, inc=1, device_id=target, device_id_type=MESH_ID)


def guarded(when, act):
    if when is None:
        act()
    else:
        pl.when(when)(act)


class Flow:
    def __init__(self, send_sem, recv_sem):
        self.send_sem, self.recv_sem = send_sem, recv_sem
        self.used = 0
        self.open = []

    def take(self, count=1):
        at = self.used
        self.used += count
        return at

    def copy(self, src, dst, target, at):
        return pltpu.make_async_remote_copy(
            src_ref=src,
            dst_ref=dst,
            send_sem=self.send_sem.at[at],
            recv_sem=self.recv_sem.at[at],
            device_id=target,
            device_id_type=MESH_ID,
        )

    def finish(self):
        for act, when in self.open:
            guarded(when, act)


class LineGather:
    def __init__(self, flow, place, src, dst):
        self.flow, self.p, self.src, self.dst = flow, place, src, dst
        self.up = flow.take(place.R - 1)
        self.down = flow.take(place.R - 1)
        self.side = flow.take(2 * place.R - 1)

    def send(self, block, hop, direction):
        p, dst = self.p, self.dst
        src = self.src if hop == 0 else dst.at[p.c, block]
        at = (self.up if direction > 0 else self.down) + hop
        return self.flow.copy(src, dst.at[p.c, block], {"rows": p.z + direction}, at)

    def across(self, block, number):
        p, dst = self.p, self.dst
        src = self.src if number == 0 else dst.at[p.c, block]
        other = {"duo": lax.rem(p.c + 1, p.D)}
        return self.flow.copy(src, dst.at[p.c, block], other, self.side + number)

    def start(self):
        p = self.p
        for direction, ok in ((1, p.z < p.R - 1), (-1, p.z > 0)):
            copy = self.send(p.z, 0, direction)
            guarded(ok, copy.start)
            self.flow.open.append((copy.wait_send, ok))
        copy = self.across(p.z, 0)
        copy.start()
        self.flow.open += [(copy.wait_recv, None), (copy.wait_send, None)]

    def hop(self, step):
        p = self.p
        for direction, number in ((1, step), (-1, p.R - 1 + step)):
            block = p.z - direction * step
            ok = (block >= 0) if direction > 0 else (block < p.R)
            last = (p.z < p.R - 1) if direction > 0 else (p.z > 0)
            arrived = self.send(block, step - 1, direction)
            side = self.across(block, number)

            def relay(arrived=arrived, side=side, block=block, direction=direction, last=last):
                arrived.wait_recv()
                if step < p.R - 1:
                    pl.when(last)(self.send(block, step, direction).start)
                side.start()

            pl.when(ok)(relay)
            if step < p.R - 1:
                self.flow.open.append((self.send(block, step, direction).wait_send, ok & last))
            self.flow.open += [(side.wait_recv, ok), (side.wait_send, ok)]


class LineReduce:
    def __init__(self, flow, place, part, total_ref, mate, passed, landed):
        self.flow, self.p, self.part, self.total = flow, place, part, total_ref
        self.mate, self.passed, self.landed = mate, passed, landed
        self.side = flow.take(place.R)
        self.line = flow.take(2 * place.R)

    def across(self, block):
        p = self.p
        other = lax.rem(p.c + 1, p.D)
        return self.flow.copy(
            self.part.at[other, block], self.mate.at[block], {"duo": other}, self.side + block
        )

    def along(self, upward, block):
        p = self.p
        way = jnp.where(upward, 1, 0)
        target = {"rows": jnp.where(upward, p.z + 1, p.z - 1)}
        return self.flow.copy(
            self.passed.at[way, block],
            self.landed.at[way, block],
            target,
            self.line + way * p.R + block,
        )

    def steps(self):
        p = self.p
        low = p.z < p.R // 2
        for k in range(p.R - 1):
            for first in (True, False):
                upward = low if first else jnp.logical_not(low)
                block = jnp.where(upward, p.R - 1 - k, k)
                yield upward, block, jnp.where(upward, block > p.z, block < p.z)

    def start(self):
        p = self.p
        for k in range(p.R):
            block = jnp.where(p.z < p.R // 2, p.R - 1 - k, k)
            copy = self.across(block)
            copy.start()
            self.flow.open.append((copy.wait_send, None))

    def rows_of(self, act):
        count = self.part.shape[2]
        step = 16

        @pl.loop(0, count // step)
        def _(number):
            act(pl.ds(pl.multiple_of(number * step, step), step))

    def run(self):
        p = self.p
        for number, (upward, block, ok) in enumerate(self.steps()):
            way = jnp.where(upward, 1, 0)
            behind = jnp.where(upward, p.z > 0, p.z < p.R - 1)

            def act(upward=upward, block=block, way=way, behind=behind):
                self.across(block).wait_recv()

                @pl.when(behind)
                def _():
                    self.along(upward, block).wait_recv()

                    def add(rows):
                        self.passed[way, block, rows] = (
                            self.part[p.c, block, rows].astype(F32)
                            + self.mate[block, rows].astype(F32)
                            + self.landed[way, block, rows].astype(F32)
                        ).astype(BF16)

                    self.rows_of(add)

                @pl.when(jnp.logical_not(behind))
                def _():
                    def add(rows):
                        self.passed[way, block, rows] = (
                            self.part[p.c, block, rows].astype(F32)
                            + self.mate[block, rows].astype(F32)
                        ).astype(BF16)

                    self.rows_of(add)

                self.along(upward, block).start()

            pl.when(ok)(act)
            self.flow.open.append((self.along(upward, block).wait_send, ok))
        self.across(p.z).wait_recv()

        def base(rows):
            self.total[rows] = self.part[p.c, p.z, rows].astype(F32) + self.mate[
                p.z, rows
            ].astype(F32)

        self.rows_of(base)
        for way, ok in ((1, p.z > 0), (0, p.z < p.R - 1)):

            def more(way=way):
                self.along(way == 1, p.z).wait_recv()

                def add(rows):
                    self.total[rows] += self.landed[way, p.z, rows].astype(F32)

                self.rows_of(add)

            pl.when(ok)(more)


def team_kernel(
    ident, name, plan, arrays, results, gathers=(), reduces=(), messages=0, local=1, late=None
):
    D, R = lax.axis_size("duo"), lax.axis_size("rows")
    count_a, count_g, count_r = len(arrays), len(gathers), len(reduces)
    extra = 0 if late is None else 1
    total_sems = messages + (count_g + extra) * (4 * R - 3) + count_r * 3 * R

    def kernel(*refs):
        refs = list(refs)
        ins = refs[:count_a]
        g_in = refs[count_a : count_a + count_g]
        r_in = refs[count_a + count_g : count_a + count_g + count_r]
        refs = refs[count_a + count_g + count_r :]
        outs = refs[: len(results)]
        refs = refs[len(results) :]
        late_out = refs[:extra]
        g_out = refs[extra : extra + count_g]
        r_out = refs[extra + count_g : extra + count_g + count_r]
        refs = refs[extra + count_g + count_r :]
        send_sem, recv_sem, local_sem = refs[:3]
        buffers = refs[3:]
        p = Place()
        flow = Flow(send_sem, recv_sem)
        greet, direct, stay = plan(p, ins, outs)
        barrier = pltpu.get_barrier_semaphore()
        waits = 0
        for target, when in greet:
            if when is None:
                waits = waits + 1
            else:
                waits = waits + jnp.where(when, 1, 0).astype(jnp.int32)
            guarded(when, lambda target=target: signal_all(barrier, [target]))
        pl.semaphore_wait(barrier, waits)
        lines = [LineGather(flow, p, src, dst) for src, dst in zip(g_in, g_out)]
        sums = [
            LineReduce(flow, p, src, dst, *buffers[3 * n : 3 * n + 3])
            for n, (src, dst) in enumerate(zip(r_in, r_out))
        ]
        base = flow.take(messages)
        copies = {}
        arrived = set()

        stays = []

        def landed(number):
            if number not in arrived:
                arrived.add(number)
                guarded(copies[number][2], copies[number][0].wait_recv)

        def run_stage(stage):
            for number, (src, dst, target, after, when, when_stage, lands) in enumerate(direct):
                if when_stage != stage:
                    continue
                for earlier in after:
                    landed(earlier)
                copy = flow.copy(src, dst, target, base + number)
                guarded(when, copy.start)
                copies[number] = (copy, when, lands)
            if late is not None and late[1] == stage:
                for number in range(late[2]):
                    landed(number)
                stays[0][0].wait()
                line = LineGather(flow, p, outs[late[0]], late_out[0])
                line.start()
                own = pltpu.make_async_copy(
                    outs[late[0]], late_out[0].at[p.c, p.z], local_sem.at[local + count_g]
                )
                own.start()
                stays[0] = (own, None)
                if stage:
                    for earlier in range(1, stage + 1):
                        line.hop(earlier)
                lines.append(line)

        for item in sums:
            item.start()
        for line in lines:
            line.start()
        for number, (src, dst, when) in enumerate(
            list(stay) + [(src, dst.at[p.c, p.z], None) for src, dst in zip(g_in, g_out)]
        ):
            copy = pltpu.make_async_copy(src, dst, local_sem.at[number])
            guarded(when, copy.start)
            stays.append((copy, when))
        run_stage(0)
        for step in range(1, R):
            for line in lines:
                line.hop(step)
            run_stage(step)
        for item in sums:
            item.run()
        for copy, when in stays:
            guarded(when, copy.wait)
        for number in copies:
            landed(number)
        for copy, when, _ in copies.values():
            guarded(when, copy.wait_send)
        flow.finish()

    spot = pl.BlockSpec(memory_space=pl.ANY)
    near = pl.BlockSpec(memory_space=pltpu.VMEM)
    out_shape = [jax.ShapeDtypeStruct(shape, kind) for shape, kind in results]
    if late is not None:
        shape, kind = results[late[0]]
        out_shape.append(jax.ShapeDtypeStruct((D, R) + shape, kind))
    out_shape += [jax.ShapeDtypeStruct((D, R) + g.shape, g.dtype) for g in gathers]
    out_shape += [jax.ShapeDtypeStruct(r.shape[2:], F32) for r in reduces]
    scratch = [
        pltpu.SemaphoreType.DMA((total_sems,)),
        pltpu.SemaphoreType.DMA((total_sems,)),
        pltpu.SemaphoreType.DMA((local + count_g + extra,)),
    ]
    for r in reduces:
        block = r.shape[1:]
        scratch += [
            pltpu.VMEM(block, BF16),
            pltpu.VMEM((2,) + block, BF16),
            pltpu.VMEM((2,) + block, BF16),
        ]
    return pl.pallas_call(
        kernel,
        out_shape=out_shape,
        in_specs=[spot] * (count_a + count_g) + [near] * count_r,
        out_specs=[spot] * (len(results) + extra + count_g) + [near] * count_r,
        scratch_shapes=scratch,
        compiler_params=pltpu.CompilerParams(
            collective_id=ident, has_side_effects=True, vmem_limit_bytes=56 * 2**20
        ),
        name=name,
    )(*arrays, *gathers, *reduces)


def team_greet(p):
    return [({"duo": c, "rows": z}, None) for c, z in p.team()]


def group_greet(p):
    return [({"grp": q}, None) for q in p.groups()]


class Plan:
    def __init__(self, p):
        self.p = p
        self.messages, self.local, self.greet = [], [], []

    def add(self, src, dst, target, after=(), when=None, stage=0, lands=None):
        self.messages.append((src, dst, target, after, when, stage, when if lands is None else lands))
        return len(self.messages) - 1

    def team_swap(self, src, dst, stage=0):
        p = self.p
        mine = p.c * p.R + p.z
        for c, z in p.team():
            self.add(src.at[c * p.R + z], dst.at[mine], {"duo": c, "rows": z}, stage=stage)
        self.local.append((src.at[mine], dst.at[mine], None))

    def team_gather(self, src, dst, stage=0):
        p = self.p
        mine = p.c * p.R + p.z
        for c, z in p.team():
            self.add(src, dst.at[mine], {"duo": c, "rows": z}, stage=stage)
        self.local.append((src, dst.at[mine], None))

    def group_gather(self, src, dst, late=None):
        p = self.p
        self.local.append((src, dst.at[p.q], None))
        if late is None or p.G != 4:
            for q in p.groups():
                self.add(src, dst.at[p.q], {"grp": q})
            return
        across = p.q + 1 - 2 * lax.rem(p.q, 2)
        along = lax.rem(p.q + 2, 4)
        one = self.add(src, dst.at[p.q], {"grp": across})
        two = self.add(src, dst.at[p.q], {"grp": along})
        half = src.shape[0] // 2
        top, bottom = pl.ds(0, half), pl.ds(half, half)
        self.add(
            dst.at[across, top], dst.at[across, top], {"grp": along}, after=(one,), stage=late
        )
        self.add(
            dst.at[along, bottom],
            dst.at[along, bottom],
            {"grp": across},
            after=(two,),
            stage=late,
        )

    def group_swap(self, src, dst, stage=0):
        p = self.p
        for q in p.groups():
            self.add(src.at[q], dst.at[p.q], {"grp": q}, stage=stage)
        self.local.append((src.at[p.q], dst.at[p.q], None))

    def done(self):
        p = self.p
        return team_greet(p) + group_greet(p) + self.greet, self.messages, self.local


def layer_stats(values):
    center = values - jnp.mean(values, axis=-1, keepdims=True)
    spread = jnp.mean(center * center, axis=-1, keepdims=True)
    inverse = lax.rsqrt(spread + norm_eps)
    return center * inverse, inverse


def layer_back(grad, hat, inverse):
    first = jnp.mean(grad, axis=-1, keepdims=True)
    second = jnp.mean(grad * hat, axis=-1, keepdims=True)
    return inverse * (grad - first - hat * second)


def mm(left, right):
    return jnp.dot(left, right, preferred_element_type=F32)


def mm_t(left, right):
    return lax.dot_general(left, right, (((1,), (1,)), ((), ())), preferred_element_type=F32)


def t_mm(left, right):
    return lax.dot_general(left, right, (((0,), (0,)), ((), ())), preferred_element_type=F32)


def columns_of(bucket_ids):
    return jnp.where(
        bucket_ids == 0, 9 * UNIT // 2, jnp.where(bucket_ids == 1, 3 * UNIT, 9 * UNIT // 4)
    )


def pixel_mask(positions, height, width, cols):
    row_at = positions // cols
    col_at = positions % cols
    return ((row_at < height) & (col_at < width)).astype(F32)


def attention(queries, text_kv, key_keep, grad_att):
    D, pixels, width = queries.shape
    HW = width // 3
    texts = text_kv.shape[1]
    keys = pixels + texts
    heads = HW // HEAD
    scale = HEAD ** (-0.5)

    def kernel(q_ref, t_ref, keep_ref, g_ref, att_ref, dq_ref, dt_ref, k_all, v_all, dk, dv, o_t, dq_t):
        k_all[pl.ds(0, pixels)] = q_ref[0, :, HW : 2 * HW]
        k_all[pl.ds(pixels, texts)] = t_ref[0, :, :HW]
        v_all[pl.ds(0, pixels)] = q_ref[0, :, 2 * HW :]
        v_all[pl.ds(pixels, texts)] = t_ref[0, :, HW:]
        k_t = k_all[...].T
        v_t = v_all[...].T
        dk[...] = jnp.zeros_like(dk)
        dv[...] = jnp.zeros_like(dv)
        o_t[...] = jnp.zeros_like(o_t)
        dq_t[...] = jnp.zeros_like(dq_t)
        lane = lax.broadcasted_iota(jnp.int32, (1, HW), 1)
        line = lax.broadcasted_iota(jnp.int32, (HW, 1), 0)
        alive = keep_ref[0] > 0

        @pl.loop(0, heads)
        def _(head):
            low = head * HEAD
            in_head = (lane >= low) & (lane < low + HEAD)
            in_line = (line >= low) & (line < low + HEAD)
            q_h = jnp.where(in_head, q_ref[0, :, :HW], 0).astype(BF16)
            g_h = jnp.where(in_head, g_ref[0], 0).astype(BF16)
            scores = mm_t(k_all[...], q_h) * scale
            scores = jnp.where(alive, scores, masked_score)
            top = jnp.max(scores, axis=0, keepdims=True)
            weights = jnp.exp(scores - top)
            probs = weights / jnp.sum(weights, axis=0, keepdims=True)
            probs_low = probs.astype(BF16)
            v_h = jnp.where(in_line, v_t, 0).astype(BF16)
            o_t[...] += mm(v_h, probs_low)
            dv[...] += mm(probs_low, g_h)
            grad_probs = mm_t(v_all[...], g_h)
            sums = jnp.sum(probs * grad_probs, axis=0, keepdims=True)
            grad_scores = (probs * (grad_probs - sums)).astype(BF16)
            k_h = jnp.where(in_line, k_t, 0).astype(BF16)
            dq_t[...] += mm(k_h, grad_scores)
            dk[...] += mm(grad_scores, q_h)

        att_ref[0] = o_t[...].T.astype(BF16)
        dq_ref[0, :, :HW] = (dq_t[...].T * scale).astype(BF16)
        dq_ref[0, :, HW : 2 * HW] = (dk[pl.ds(0, pixels)] * scale).astype(BF16)
        dq_ref[0, :, 2 * HW :] = dv[pl.ds(0, pixels)].astype(BF16)
        dt_ref[0, :, :HW] = (dk[pl.ds(pixels, texts)] * scale).astype(BF16)
        dt_ref[0, :, HW:] = dv[pl.ds(pixels, texts)].astype(BF16)

    def one(shape):
        return pl.BlockSpec((1,) + shape, lambda i: (i, 0, 0))

    return pl.pallas_call(
        kernel,
        grid=(D,),
        out_shape=[
            jax.ShapeDtypeStruct((D, pixels, HW), BF16),
            jax.ShapeDtypeStruct((D, pixels, width), BF16),
            jax.ShapeDtypeStruct((D, texts, 2 * HW), BF16),
        ],
        in_specs=[
            one((pixels, width)),
            one((texts, 2 * HW)),
            one((keys, 1)),
            one((pixels, HW)),
        ],
        out_specs=[one((pixels, HW)), one((pixels, width)), one((texts, 2 * HW))],
        scratch_shapes=[
            pltpu.VMEM((keys, HW), BF16),
            pltpu.VMEM((keys, HW), BF16),
            pltpu.VMEM((keys, HW), F32),
            pltpu.VMEM((keys, HW), F32),
            pltpu.VMEM((HW, pixels), F32),
            pltpu.VMEM((HW, pixels), F32),
        ],
        compiler_params=pltpu.CompilerParams(vmem_limit_bytes=56 * 2**20),
        name="attention",
    )(queries, text_kv, key_keep, grad_att)


def pad_rows(values, rows):
    return jnp.pad(values, ((0, rows - values.shape[0]),) + ((0, 0),) * (values.ndim - 1))


def pack_flat(pieces, rows, kind):
    flat = jnp.concatenate([piece.astype(kind).reshape(-1) for piece in pieces])
    return jnp.pad(flat, (0, rows * 128 - flat.shape[0])).reshape(rows, 128)


def body(
    latents,
    clip_tokens,
    time_embed,
    bucket_ids,
    heights,
    widths,
    text_mask,
    conv_weight,
    conv_bias,
    in_weight,
    in_bias,
    grn_gain,
    grn_bias,
    out_weight,
    out_bias,
    time_weight,
    time_bias,
    map_weight,
    map_bias,
    qkv_weight,
    qv_bias,
    proj_weight,
    proj_bias,
    cotangent,
):
    G, D, R = (lax.axis_size(axis) for axis in AXES)
    T = D * R
    q, c, z = (lax.axis_index(axis) for axis in AXES)
    N = latents.shape[1]
    C = latents.shape[2]
    pixels = R * N
    FFS = in_bias.shape[0]
    FL = G * FFS
    FF = in_weight.shape[1]
    cs = conv_bias.shape[0]
    ms = map_weight.shape[0]
    slots = clip_tokens.shape[1]
    text_all = R * slots
    HW = C // T
    even = G == R
    head_slice = R and (D * z + c)

    latents = latents[0]
    cotangent = cotangent[0]
    cols = columns_of(bucket_ids)[0]
    positions = z * N + jnp.arange(N, dtype=jnp.int32)
    keep = pixel_mask(positions, heights[0], widths[0], cols)[:, None]
    masked = latents * keep.astype(BF16)
    grad_result = (keep * cotangent.astype(F32)).astype(BF16)
    gres_all = lax.all_gather(grad_result, ("duo", "rows"), axis=0, tiled=True)

    in_cut = in_weight.reshape(cs, G, T, FFS).transpose(2, 0, 1, 3).reshape(T, cs, FL)
    qkv_cut = qkv_weight.reshape(cs, 3, R, D, HW).transpose(3, 2, 0, 1, 4).reshape(T, cs, 3 * HW)
    mp = -(-ms // 16) * 16
    map_cut = jnp.pad(
        map_weight.reshape(ms, T, HW).transpose(1, 0, 2), ((0, 0), (0, mp - ms), (0, 0))
    )
    sp = -(-slots // 16) * 16
    clip_pad = pad_rows(clip_tokens[0], sp)

    def lanes(piece):
        piece = piece.astype(BF16).reshape(-1, piece.shape[-1])
        return jnp.pad(piece, ((0, 0), (0, 128 - piece.shape[1])))

    numbers = jnp.stack([heights[0], widths[0], bucket_ids[0]]).astype(BF16)[None]
    small = jnp.concatenate(
        [
            lanes(piece)
            for piece in (
                conv_weight,
                conv_bias,
                out_bias,
                map_bias,
                proj_bias,
                qv_bias,
                time_embed,
                numbers,
                text_mask,
            )
        ]
    )
    mrows = 32
    small = pad_rows(small, mrows)
    fvec = pad_rows(jnp.stack([in_bias, grn_gain, grn_bias]), 16)

    def swap_edges(plan, src, dst):
        p = plan.p
        for block, to, sends, lands in (
            (src.at[pl.ds(src.shape[0] - EDGE, EDGE)], p.z + 1, p.z < R - 1, p.z > 0),
            (src.at[pl.ds(0, EDGE)], p.z - 1, p.z > 0, p.z < R - 1),
        ):
            slot = jnp.where(to > p.z, 0, 1)
            plan.add(block, dst.at[slot], {"rows": to}, when=sends, lands=lands)

    def plan_start(p, ins, outs):
        plan = Plan(p)
        plan.group_gather(ins[1], outs[1])
        swap_edges(plan, ins[0], outs[0])
        plan.team_swap(ins[2], outs[2])
        plan.group_gather(ins[3], outs[3])
        return plan.done()

    edges, _, in_rows, fvec_all, small_all = team_kernel(
        0,
        "exchange_start",
        plan_start,
        [masked, small, in_cut, fvec],
        [
            ((2, EDGE, C), BF16),
            ((G, mrows, 128), BF16),
            ((T, cs, FL), BF16),
            ((G, 16, FFS), BF16),
        ],
        messages=2 + 2 * (G - 1) + (T - 1),
        local=3,
        late=(1, 0, G - 1),
    )
    shards = T * G
    by_place = small_all.reshape(D, R, G, mrows, 128).transpose(2, 0, 1, 3, 4)
    by_place = by_place.reshape(shards, mrows, 128)

    def whole(row, width):
        return by_place[:, row, :width].reshape(-1).astype(F32)

    kernel_full = by_place[:, :9, :cs].transpose(1, 0, 2).reshape(9, C).astype(F32)
    conv_bias_full, out_bias_full, map_bias_full, proj_bias_full = (
        whole(9 + row, cs) for row in range(4)
    )
    qv_full = whole(13, 2 * cs)
    per_item = by_place.reshape(G * D, R, mrows, 128)[:, 0]
    embed_all = per_item[:, 14, : time_embed.shape[1]]
    pair = lax.dynamic_slice_in_dim(per_item, q * D, D, axis=0)
    facts = pair[:, 15, :3].astype(jnp.int32)
    pair_height, pair_width, pair_bucket = (facts[:, n : n + 1] for n in range(3))
    pair_cols = columns_of(pair_bucket)
    pair_keep = pixel_mask(
        jnp.arange(pixels, dtype=jnp.int32)[None, :], pair_height, pair_width, pair_cols
    )
    text_keep = (
        pair[:, 16, :text_all].astype(F32) * (jnp.arange(text_all) < TXT).astype(F32)[None, :]
    )
    key_keep = jnp.concatenate([pair_keep, text_keep], axis=1)
    in_bias_s, gain_s, grn_bias_s = (
        fvec_all[:, row].reshape(FL).astype(F32) for row in range(3)
    )
    mod_rows = -(-G * D // 8) * 8
    mod_part = mm(embed_all, time_weight) + time_bias.astype(F32)
    mod_part = pad_rows(jnp.pad(mod_part, ((0, 0), (0, 128 - 2 * cs))), mod_rows)

    def extend(low, mid, high):
        return jnp.concatenate(
            [
                jnp.where(z > 0, low, jnp.zeros_like(low)),
                mid,
                jnp.where(z < R - 1, high, jnp.zeros_like(high)),
            ],
            axis=0,
        )

    column = (positions % cols)[:, None]

    def tap(extended, dy, dx):
        piece = lax.dynamic_slice_in_dim(extended, EDGE + dy * cols + dx, N, axis=0).astype(F32)
        ok = (column + dx >= 0) & (column + dx < cols)
        return jnp.where(ok, piece, 0.0)

    extended = extend(edges[0], masked, edges[1])
    conv_out = jnp.zeros((N, C), F32) + conv_bias_full
    for index in range(9):
        conv_out = conv_out + tap(extended, index // 3 - 1, index % 3 - 1) * kernel_full[index]
    norm_hat, norm_inv = layer_stats(conv_out)
    normed = norm_hat.astype(BF16)

    def plan_first(p, ins, outs):
        plan = Plan(p)
        plan.group_gather(ins[4], outs[4])
        plan.group_gather(ins[0], outs[0], late=1)
        plan.group_gather(ins[1], outs[1], late=2)
        plan.team_swap(ins[2], outs[2])
        plan.team_swap(ins[3], outs[3])
        if even:
            wide = C // G
            for step in range(G):
                to = lax.rem(p.z + step, G)
                when = None if step else p.q != p.z
                piece = ins[5].at[:, pl.ds(pl.multiple_of(to * wide, 128), wide)]
                plan.add(
                    piece, outs[5].at[p.z], {"grp": to, "duo": p.c, "rows": p.q}, when=when
                )
                source = {"grp": p.z, "duo": p.c, "rows": lax.rem(p.q - step + G, G)}
                plan.greet.append((source, when))
            piece = ins[5].at[:, pl.ds(pl.multiple_of(p.z * wide, 128), wide)]
            plan.local.append((piece, outs[5].at[p.z], p.q == p.z))
        return plan.done()

    group_count = 4 if G == 4 else G - 1
    arrays = [in_rows.reshape(T * cs, FL), out_weight, qkv_cut, map_cut, mod_part]
    results = [
        ((G, T * cs, FL), BF16),
        ((G,) + out_weight.shape, BF16),
        ((T, cs, 3 * HW), BF16),
        ((T, mp, HW), BF16),
        ((G,) + mod_part.shape, F32),
    ]
    if even:
        arrays.append(proj_weight)
        results.append(((R, cs, C // G), BF16))
    gathered = team_kernel(
        1,
        "exchange_normed",
        plan_first,
        arrays,
        results,
        gathers=[normed, clip_pad],
        messages=2 * group_count + 2 * (T - 1) + G - 1 + (G if even else 0),
        local=5 + (1 if even else 0),
        late=(4, 1, G - 1),
    )
    in_full, out_full, qkv_rows, map_rows = gathered[:4]
    mod_all, normed_all, clip_all = gathered[-3:]
    clip_all = clip_all.reshape(T, sp, -1)
    modulate = lax.dynamic_index_in_dim(mod_all, q * D + c, 3, keepdims=False)[..., : 2 * cs]
    modulate = modulate.transpose(2, 0, 1, 3).reshape(1, 2 * C)
    normed_all = normed_all.reshape(D * pixels, C)
    in_full = in_full.reshape(C, FL)
    out_full = out_full.reshape(FL, C)
    keep_all = pair_keep.reshape(D, pixels, 1)

    hidden = mm(normed_all, in_full) + in_bias_s
    gate = 0.5 * lax.erfc(-hidden * (0.5**0.5))
    active = hidden * gate
    active3 = active.reshape(D, pixels, FL)
    squares = jnp.sum(keep_all * active3 * active3, axis=1)
    grn_norms = jnp.sqrt(squares)

    def team_total(ident, name, values):
        block = jnp.zeros((8, 128), F32).at[0, :D].set(values)

        def plan(p, ins, outs):
            plan = Plan(p)
            plan.team_gather(ins[0], outs[0])
            return team_greet(p), plan.messages, plan.local

        (everyone,) = team_kernel(
            ident, name, plan, [block], [((T, 8, 128), F32)], messages=T - 1
        )
        return jnp.sum(everyone[:, 0, :D], axis=0)

    norm_mean = (team_total(2, "total_norms", jnp.sum(grn_norms, axis=1)) / FF + grn_eps)[:, None]
    grn_ratio = grn_norms / norm_mean
    grn_out = (
        (gain_s * (active3 * grn_ratio[:, None, :]) + grn_bias_s + active3)
        .astype(BF16)
        .reshape(D * pixels, FL)
    )

    def plan_branch(p, ins, outs):
        plan = Plan(p)
        plan.group_gather(ins[0], outs[0])
        plan.group_gather(ins[1], outs[1])
        if even:
            plan.group_gather(ins[2], outs[2])
        return plan.done()

    arrays = [qkv_rows.reshape(T * cs, 3 * HW), map_rows.reshape(T * mp, HW)]
    results = [((G, T * cs, 3 * HW), BF16), ((G, T * mp, HW), BF16)]
    if even:
        arrays.append(gathered[5].reshape(HW, C // G))
        results.append(((G, HW, C // G), BF16))
    gathered = team_kernel(
        3,
        "reduce_branch",
        plan_branch,
        arrays,
        results,
        reduces=[mm(grn_out, out_full).astype(BF16).reshape(D, R, N, C)],
        messages=(3 if even else 2) * (G - 1),
        local=3,
    )
    qkv_full = gathered[0].reshape(C, 3 * HW)
    map_full = gathered[1].reshape(G * T, mp, HW)[:, :ms].reshape(G * T * ms, HW)
    if even:
        proj_s = gathered[2].transpose(1, 0, 2).reshape(HW, C)
    else:
        proj_whole = lax.all_gather(proj_weight, AXES, axis=0, tiled=True)
        proj_s = lax.dynamic_slice_in_dim(proj_whole, head_slice * HW, HW, axis=0)
    branch = gathered[-1] + out_bias_full
    after_res = latents.astype(F32) + keep * branch
    scale_by = 1.0 + modulate[:, :C]
    second = after_res * scale_by + modulate[:, C:]
    two_hat, two_inv = layer_stats(second)
    normed_two = two_hat.astype(BF16)

    silu_text = jax.nn.silu(clip_all[:, :slots].astype(F32)).astype(BF16)
    silu_text = silu_text.reshape(D * text_all, -1)
    map_bias_s = lax.dynamic_slice_in_dim(map_bias_full, (c * R + z) * HW, HW)
    mapped_s = (mm(silu_text, map_full) + map_bias_s).astype(BF16)

    def plan_none(p, ins, outs):
        return team_greet(p), [], []

    two_all, mapped = team_kernel(
        4, "exchange_second", plan_none, [], [], gathers=[normed_two, mapped_s]
    )
    two_all = two_all.reshape(D * pixels, C)
    mapped = mapped.reshape(T, D * text_all, HW).transpose(1, 0, 2).reshape(D * text_all, C)

    q_bias = lax.dynamic_slice_in_dim(qv_full, head_slice * HW, HW)
    v_bias = lax.dynamic_slice_in_dim(qv_full, C + head_slice * HW, HW)
    projected = mm(two_all, qkv_full)
    bias = jnp.concatenate([q_bias, jnp.zeros_like(q_bias), v_bias])
    queries = (projected + bias).astype(BF16).reshape(D, pixels, 3 * HW)
    text_kv = (mm(mapped, qkv_full[:, HW:]) + bias[HW:]).astype(BF16)
    text_kv = text_kv.reshape(D, text_all, 2 * HW)
    grad_att = mm_t(gres_all, proj_s).astype(BF16).reshape(D, pixels, HW)
    attended, grad_pixel, grad_text = attention(queries, text_kv, key_keep[:, :, None], grad_att)
    attended = attended.reshape(D * pixels, HW)
    grad_pixel = grad_pixel.reshape(D * pixels, 3 * HW)
    grad_text = grad_text.reshape(D * text_all, 2 * HW)
    result_part = mm(attended, proj_s).astype(BF16)
    result = lax.psum_scatter(result_part, ("duo", "rows"), scatter_dimension=0, tiled=True)
    grad_qkv = t_mm(two_all, grad_pixel) + jnp.pad(t_mm(mapped, grad_text), ((0, 0), (HW, 0)))
    q_bias_grad = jnp.sum(grad_pixel[:, :HW].astype(F32), axis=0)
    v_bias_grad = jnp.sum(grad_pixel[:, 2 * HW :].astype(F32), axis=0) + jnp.sum(
        grad_text[:, HW:].astype(F32), axis=0
    )
    grad_proj = t_mm(attended, gres_all)
    mapped_part = mm_t(grad_text, qkv_full[:, HW:]).astype(BF16)
    mapped_part = mapped_part.reshape(D * text_all, T, HW).transpose(1, 0, 2)
    two_part = mm_t(grad_pixel, qkv_full).astype(BF16).reshape(D, R, N, C)


    grad_two, mapped_sum = team_kernel(
        5,
        "reduce_attended",
        plan_none,
        [],
        [],
        reduces=[two_part, mapped_part.reshape(D, R, D * text_all, HW)],
    )
    output = (second + keep * (result.astype(F32) + proj_bias_full)).astype(BF16)
    grad_mapped = mapped_sum.astype(BF16)
    grad_map = t_mm(silu_text, grad_mapped).astype(BF16)
    grad_map = jnp.pad(grad_map.reshape(G, T, ms, HW), ((0, 0), (0, 0), (0, mp - ms), (0, 0)))
    map_bias_grad = jnp.sum(grad_mapped.astype(F32), axis=0)

    grad_output = cotangent.astype(F32)
    grad_second = grad_output + layer_back(grad_two, two_hat, two_inv)
    grad_modulate = jnp.concatenate(
        [jnp.sum(grad_second * after_res, axis=0), jnp.sum(grad_second, axis=0)]
    )
    grad_after = grad_second * scale_by
    grad_branch = (keep * grad_after).astype(BF16)

    def plan_third(p, ins, outs):
        plan = Plan(p)
        plan.group_swap(ins[0], outs[0])
        plan.group_swap(ins[1], outs[1])
        if even:
            plan.group_swap(ins[2], outs[2])
        return plan.done()

    arrays = [grad_qkv.astype(BF16).reshape(G, T * cs, 3 * HW), grad_map.reshape(G, T * mp, HW)]
    if even:
        arrays.append(grad_proj.astype(BF16).reshape(HW, G, C // G).transpose(1, 0, 2))
    gathered = team_kernel(
        7,
        "exchange_branch",
        plan_third,
        arrays,
        [(array.shape, BF16) for array in arrays],
        gathers=[grad_branch],
        messages=(3 if even else 2) * (G - 1),
        local=3,
    )
    gb_all = gathered[-1].reshape(D * pixels, C)
    qkv_sum = jnp.sum(gathered[0].astype(F32), axis=0).astype(BF16).reshape(T, cs, 3 * HW)
    map_back = jnp.sum(gathered[1].astype(F32), axis=0).astype(BF16).reshape(T, mp, HW)
    if even:
        proj_back = jnp.sum(gathered[2].astype(F32), axis=0).astype(BF16).reshape(R, cs, C // G)
    else:
        spread = jnp.zeros((C, C), F32)
        spread = lax.dynamic_update_slice_in_dim(spread, grad_proj, head_slice * HW, axis=0)
        grad_proj_out = lax.psum_scatter(spread, AXES, scatter_dimension=0, tiled=True)

    grad_out = t_mm(grn_out, gb_all).astype(BF16)
    grad_out_shard = lax.psum_scatter(grad_out, "grp", scatter_dimension=0, tiled=True).astype(F32)
    grad_grn = mm_t(gb_all, out_full)
    grad_grn3 = grad_grn.reshape(D, pixels, FL)
    moment = jnp.sum(grad_grn3 * active3, axis=1)
    grad_gain = jnp.sum(moment * grn_ratio, axis=0)
    grad_grn_bias = jnp.sum(grad_grn, axis=0)
    ratio_grad = moment * gain_s
    cross = team_total(8, "total_cross", jnp.sum(ratio_grad * grn_norms, axis=1))[:, None]
    grad_norms = ratio_grad / norm_mean - cross / (FF * norm_mean * norm_mean)
    grad_active = (
        grad_grn3 * (gain_s * grn_ratio[:, None, :] + 1.0)
        + keep_all * active3 * (grad_norms / grn_norms)[:, None, :]
    ).reshape(D * pixels, FL)
    density = jnp.exp(-0.5 * hidden * hidden) * 0.3989422804014327
    grad_hidden = (grad_active * (gate + hidden * density)).astype(BF16)
    grad_in_bias = jnp.sum(grad_hidden.astype(F32), axis=0)
    grad_in = t_mm(normed_all, grad_hidden).astype(BF16).reshape(G, T * cs, FL)
    back_part = mm_t(grad_hidden, in_full).astype(BF16).reshape(D, R, N, C)

    def plan_fourth(p, ins, outs):
        plan = Plan(p)
        plan.group_swap(ins[0], outs[0])
        plan.team_swap(ins[1], outs[1])
        plan.team_swap(ins[2], outs[2])
        plan.group_swap(ins[3], outs[3])
        if even:
            for step in range(G):
                to = lax.rem(p.q + step, G)
                when = None if step else p.q != p.z
                plan.add(
                    ins[4].at[to],
                    outs[4].at[p.q],
                    {"grp": p.z, "duo": p.c, "rows": to},
                    when=when,
                )
                source = {"grp": lax.rem(p.z - step + G, G), "duo": p.c, "rows": p.q}
                plan.greet.append((source, when))
            plan.local.append((ins[4].at[p.z], outs[4].at[p.q], p.q == p.z))
        return plan.done()

    fgrads = jnp.stack([grad_in_bias, grad_gain, grad_grn_bias]).reshape(3, G, FFS)
    fgrads = fgrads.transpose(1, 0, 2).reshape(G, -1)
    grows = -(-fgrads.shape[1] // 1024) * 8
    fgrads = jnp.pad(fgrads, ((0, 0), (0, grows * 128 - fgrads.shape[1]))).reshape(G, grows, 128)

    arrays = [grad_in, qkv_sum, map_back, fgrads]
    results = [(array.shape, array.dtype) for array in arrays]
    if even:
        arrays.append(proj_back)
        results.append(((G, cs, C // G), BF16))
    gathered = team_kernel(
        9,
        "reduce_back",
        plan_fourth,
        arrays,
        results,
        reduces=[back_part],
        messages=2 * (G - 1) + 2 * (T - 1) + (G if even else 0),
        local=5,
    )
    in_sum, qkv_team, map_team, f_sum = gathered[:4]
    if even:
        grad_proj_out = gathered[4].transpose(1, 0, 2).reshape(cs, C).astype(F32)
    grad_conv_in = gathered[-1]
    grad_conv = layer_back(grad_conv_in, norm_hat, norm_inv)
    taps = [
        jnp.sum(tap(extended, index // 3 - 1, index % 3 - 1) * grad_conv, axis=0)
        for index in range(9)
    ]
    in_back = jnp.sum(in_sum.astype(F32), axis=0).astype(BF16).reshape(T, cs, FL)

    def by_shard(values):
        return values.reshape(shards, -1)

    def placed(values, start, size):
        return lax.dynamic_update_slice_in_dim(jnp.zeros((size,), F32), values, start, axis=0)

    map_bias_vec = placed(map_bias_grad, (c * R + z) * HW, C)
    qv_vec = jnp.concatenate(
        [
            placed(q_bias_grad, head_slice * HW, C),
            placed(v_bias_grad, head_slice * HW, C),
        ]
    )
    pieces = [
        jnp.stack(taps).reshape(9, shards, cs).transpose(1, 0, 2).reshape(shards, -1),
        by_shard(jnp.sum(grad_conv, axis=0)),
        by_shard(jnp.sum(grad_branch.astype(F32), axis=0)),
        by_shard(jnp.sum(grad_result.astype(F32), axis=0)),
        by_shard(map_bias_vec),
        by_shard(qv_vec),
        by_shard(grad_modulate),
    ]
    widths_of = [piece.shape[1] for piece in pieces]
    tiny = jnp.concatenate(pieces, axis=1)
    trows = -(-tiny.shape[1] // 1024) * 8
    tiny = jnp.pad(tiny, ((0, 0), (0, trows * 128 - tiny.shape[1])))
    tiny = tiny.reshape(G, T, trows, 128).transpose(1, 0, 2, 3)

    def plan_fifth(p, ins, outs):
        plan = Plan(p)
        swap_edges(plan, ins[0], outs[0])
        plan.team_swap(ins[1], outs[1])
        plan.team_swap(ins[2], outs[2])
        return plan.done()

    conv_low = grad_conv.astype(BF16)
    conv_edges, tiny_team, in_team = team_kernel(
        11,
        "exchange_tail",
        plan_fifth,
        [conv_low, tiny, in_back],
        [((2, EDGE, C), BF16), (tiny.shape, F32), (in_back.shape, BF16)],
        messages=2 + 2 * (T - 1),
        local=2,
    )
    tiny_items = jnp.sum(tiny_team.reshape(D, R, G, trows, 128), axis=1).transpose(1, 0, 2, 3)

    def plan_sixth(p, ins, outs):
        plan = Plan(p)
        plan.group_swap(ins[0], outs[0])
        return group_greet(p), plan.messages, plan.local

    (tiny_all,) = team_kernel(
        12,
        "exchange_tiny",
        plan_sixth,
        [tiny_items],
        [((G, D, trows, 128), F32)],
        messages=G - 1,
    )
    tiny_all = tiny_all.reshape(G * D, -1)
    tiny_sum = jnp.sum(tiny_all, axis=0)
    outs = []
    at = 0
    for width in widths_of[:-1]:
        outs.append(tiny_sum[at : at + width])
        at += width
    modulate_items = tiny_all[:, at : at + widths_of[-1]]
    grad_time = lax.dot_general(
        embed_all.astype(F32),
        modulate_items,
        (((0,), (0,)), ((), ())),
        precision=lax.Precision.HIGHEST,
    )
    grad_time_bias = jnp.sum(modulate_items, axis=0)

    grad_extended = extend(conv_edges[0], conv_low, conv_edges[1])
    spread = jnp.zeros((N, C), F32)
    for index in range(9):
        spread = spread + tap(grad_extended, 1 - index // 3, 1 - index % 3) * kernel_full[index]
    grad_latents = grad_after + keep * spread

    grad_in_shard = in_team.astype(F32).reshape(T, cs, G, FFS).transpose(1, 2, 0, 3).reshape(cs, FF)
    grad_map_shard = map_team[:, :ms].astype(F32).transpose(1, 0, 2).reshape(ms, C)
    grad_qkv_shard = (
        qkv_team.astype(F32)
        .reshape(D, R, cs, 3, HW)
        .transpose(2, 3, 1, 0, 4)
        .reshape(cs, 3 * C)
    )
    f_total = jnp.sum(f_sum, axis=0).reshape(-1)
    return (
        output[None],
        grad_latents[None],
        outs[0].reshape(9, cs),
        outs[1],
        grad_in_shard,
        f_total[:FFS],
        f_total[FFS : 2 * FFS],
        f_total[2 * FFS : 3 * FFS],
        grad_out_shard,
        outs[2],
        grad_time,
        grad_time_bias,
        grad_map_shard,
        outs[4],
        grad_qkv_shard,
        outs[5],
        grad_proj_out,
        outs[3],
    )


def solution(mesh):
    items, rows = mesh.devices.shape
    fine = Mesh(mesh.devices.reshape(items // 2, 2, rows), AXES)
    item = ("grp", "duo")
    full = AXES
    ins = (
        P(item, "rows", None),
        P(item, "rows", None),
        P(item, None),
        P(item),
        P(item),
        P(item),
        P(item, None),
        P(None, full),
        P(full),
        P(full, None),
        P(full),
        P(full),
        P(full),
        P(full, None),
        P(full),
        P(None, full),
        P(full),
        P(full, None),
        P(full),
        P(full, None),
        P(full),
        P(full, None),
        P(full),
        P(item, "rows", None),
    )
    outs = (
        P(item, "rows", None),
        P(item, "rows", None),
        P(None, full),
        P(full),
        P(full, None),
        P(full),
        P(full),
        P(full),
        P(full, None),
        P(full),
        P(None, full),
        P(full),
        P(full, None),
        P(full),
        P(full, None),
        P(full),
        P(full, None),
        P(full),
    )
    return jax.shard_map(body, mesh=fine, in_specs=ins, out_specs=outs, check_vma=False)
```

```python
import functools

import jax
import jax.numpy as jnp
from jax import lax
from jax.experimental import pallas as pl
from jax.experimental.pallas import tpu as pltpu
from jax.sharding import Mesh, PartitionSpec as P

HEAD = 64
TXT = 77
UNIT = 8
EDGE = 48

norm_eps = 1e-06
grn_eps = 1e-06
masked_score = -1000000000.0

AXES = ("grp", "duo", "rows")
MESH_ID = pl.DeviceIdType.MESH
F32 = jnp.float32
BF16 = jnp.bfloat16


class Place:
    def __init__(self):
        self.q, self.c, self.z = (lax.axis_index(axis) for axis in AXES)
        self.G, self.D, self.R = (lax.axis_size(axis) for axis in AXES)

    def team(self):
        for step in range(1, self.D * self.R):
            dc, dz = step // self.R, step % self.R
            yield lax.rem(self.c + dc, self.D), lax.rem(self.z + dz, self.R)

    def groups(self):
        for step in range(1, self.G):
            yield lax.rem(self.q + step, self.G)


def signal_all(barrier, targets):
    for target in targets:
        pl.semaphore_signal(barrier, inc=1, device_id=target, device_id_type=MESH_ID)


def guarded(when, act):
    if when is None:
        act()
    else:
        pl.when(when)(act)


class Flow:
    def __init__(self, send_sem, recv_sem, local_sem=None):
        self.send_sem, self.recv_sem, self.local_sem = send_sem, recv_sem, local_sem
        self.used = 0
        self.kept = 0
        self.open = []
        self.posted = []

    def take(self, count=1):
        at = self.used
        self.used += count
        return at

    def copy(self, src, dst, target, at):
        return pltpu.make_async_remote_copy(
            src_ref=src,
            dst_ref=dst,
            send_sem=self.send_sem.at[at],
            recv_sem=self.recv_sem.at[at],
            device_id=target,
            device_id_type=MESH_ID,
        )

    def post(self, src, dst, target, when=None, lands=None):
        copy = self.copy(src, dst, target, self.take())
        guarded(when, copy.start)
        item = Posted(copy, when if lands is None else lands)
        self.posted.append(item)
        self.open.append((copy.wait_send, when))
        return item

    def land(self, item):
        if not item.landed:
            item.landed = True
            guarded(item.lands, item.copy.wait_recv)

    def keep(self, src, dst, when=None):
        copy = pltpu.make_async_copy(src, dst, self.local_sem.at[self.kept])
        self.kept += 1
        guarded(when, copy.start)
        self.open.append((copy.wait, when))

    def gather_group(self, p, src, dst):
        self.keep(src, dst.at[p.q])
        for q in p.groups():
            self.post(src, dst.at[p.q], {"grp": q})

    def swap_group(self, p, src, dst):
        self.keep(src.at[p.q], dst.at[p.q])
        for q in p.groups():
            self.post(src.at[q], dst.at[p.q], {"grp": q})

    def swap_team(self, p, src, dst):
        mine = p.c * p.R + p.z
        self.keep(src.at[mine], dst.at[mine])
        for c, z in p.team():
            self.post(src.at[c * p.R + z], dst.at[mine], {"duo": c, "rows": z})

    def finish(self):
        for item in self.posted:
            self.land(item)
        for act, when in self.open:
            guarded(when, act)


class LineGather:
    def __init__(self, flow, place, src, dst):
        self.flow, self.p, self.src, self.dst = flow, place, src, dst
        self.up = flow.take(place.R - 1)
        self.down = flow.take(place.R - 1)
        self.side = flow.take(2 * place.R - 1)

    def send(self, block, hop, direction):
        p, dst = self.p, self.dst
        src = self.src if hop == 0 else dst.at[p.c, block]
        at = (self.up if direction > 0 else self.down) + hop
        return self.flow.copy(src, dst.at[p.c, block], {"rows": p.z + direction}, at)

    def across(self, block, number):
        p, dst = self.p, self.dst
        src = self.src if number == 0 else dst.at[p.c, block]
        other = {"duo": lax.rem(p.c + 1, p.D)}
        return self.flow.copy(src, dst.at[p.c, block], other, self.side + number)

    def start(self):
        p = self.p
        for direction, ok in ((1, p.z < p.R - 1), (-1, p.z > 0)):
            copy = self.send(p.z, 0, direction)
            guarded(ok, copy.start)
            self.flow.open.append((copy.wait_send, ok))
        copy = self.across(p.z, 0)
        copy.start()
        self.flow.open += [(copy.wait_recv, None), (copy.wait_send, None)]

    def hop(self, step):
        p = self.p
        for direction, number in ((1, step), (-1, p.R - 1 + step)):
            block = p.z - direction * step
            ok = (block >= 0) if direction > 0 else (block < p.R)
            last = (p.z < p.R - 1) if direction > 0 else (p.z > 0)
            arrived = self.send(block, step - 1, direction)
            side = self.across(block, number)

            def relay(arrived=arrived, side=side, block=block, direction=direction, last=last):
                arrived.wait_recv()
                if step < p.R - 1:
                    pl.when(last)(self.send(block, step, direction).start)
                side.start()

            pl.when(ok)(relay)
            if step < p.R - 1:
                self.flow.open.append((self.send(block, step, direction).wait_send, ok & last))
            self.flow.open += [(side.wait_recv, ok), (side.wait_send, ok)]


class LineReduce:
    def __init__(self, flow, place, part, total_ref, mate, passed, landed):
        self.flow, self.p, self.part, self.total = flow, place, part, total_ref
        self.mate, self.passed, self.landed = mate, passed, landed
        self.side = flow.take(place.R)
        self.line = flow.take(2 * place.R)

    def across(self, block):
        p = self.p
        other = lax.rem(p.c + 1, p.D)
        return self.flow.copy(
            self.part.at[other, block], self.mate.at[block], {"duo": other}, self.side + block
        )

    def along(self, upward, block):
        p = self.p
        way = jnp.where(upward, 1, 0)
        target = {"rows": jnp.where(upward, p.z + 1, p.z - 1)}
        return self.flow.copy(
            self.passed.at[way, block],
            self.landed.at[way, block],
            target,
            self.line + way * p.R + block,
        )

    def steps(self):
        p = self.p
        low = p.z < p.R // 2
        for k in range(p.R - 1):
            for first in (True, False):
                upward = low if first else jnp.logical_not(low)
                block = jnp.where(upward, p.R - 1 - k, k)
                yield upward, block, jnp.where(upward, block > p.z, block < p.z)

    def start(self):
        p = self.p
        for k in range(p.R):
            block = jnp.where(p.z < p.R // 2, p.R - 1 - k, k)
            copy = self.across(block)
            copy.start()
            self.flow.open.append((copy.wait_send, None))

    def rows_of(self, act):
        count = self.part.shape[2]
        step = 16

        @pl.loop(0, count // step)
        def _(number):
            act(pl.ds(pl.multiple_of(number * step, step), step))

    def step(self, upward, block, ok):
        p = self.p
        way = jnp.where(upward, 1, 0)
        behind = jnp.where(upward, p.z > 0, p.z < p.R - 1)

        def act():
            self.across(block).wait_recv()

            @pl.when(behind)
            def _():
                self.along(upward, block).wait_recv()

                def add(rows):
                    self.passed[way, block, rows] = (
                        self.part[p.c, block, rows].astype(F32)
                        + self.mate[block, rows].astype(F32)
                        + self.landed[way, block, rows].astype(F32)
                    ).astype(BF16)

                self.rows_of(add)

            @pl.when(jnp.logical_not(behind))
            def _():
                def add(rows):
                    self.passed[way, block, rows] = (
                        self.part[p.c, block, rows].astype(F32) + self.mate[block, rows].astype(F32)
                    ).astype(BF16)

                self.rows_of(add)

            self.along(upward, block).start()

        pl.when(ok)(act)
        self.flow.open.append((self.along(upward, block).wait_send, ok))

    def close(self):
        p = self.p
        self.across(p.z).wait_recv()

        def base(rows):
            self.total[rows] = self.part[p.c, p.z, rows].astype(F32) + self.mate[
                p.z, rows
            ].astype(F32)

        self.rows_of(base)
        for way, ok in ((1, p.z > 0), (0, p.z < p.R - 1)):

            def more(way=way):
                self.along(way == 1, p.z).wait_recv()

                def add(rows):
                    self.total[rows] += self.landed[way, p.z, rows].astype(F32)

                self.rows_of(add)

            pl.when(ok)(more)

    def steps_all(self):
        for upward, block, ok in self.steps():
            self.step(upward, block, ok)
        self.close()

    def run(self, produce=None, between=None):
        p = self.p
        if produce is None:
            self.steps_all()
            return
        ready = 0

        def more():
            block = line_order(p, ready)
            produce(block)
            copy = self.across(block)
            copy.start()
            self.flow.open.append((copy.wait_send, None))

        for number, (upward, block, ok) in enumerate(self.steps()):
            while ready < min(number + 2, p.R):
                more()
                ready += 1
            self.step(upward, block, ok)
            if between is not None:
                between(number)
        self.close()


def team_kernel(
    ident, name, plan, arrays, results, gathers=(), reduces=(), messages=0, local=1, late=None
):
    D, R = lax.axis_size("duo"), lax.axis_size("rows")
    count_a, count_g, count_r = len(arrays), len(gathers), len(reduces)
    extra = 0 if late is None else 1
    total_sems = messages + (count_g + extra) * (4 * R - 3) + count_r * 3 * R

    def kernel(*refs):
        refs = list(refs)
        ins = refs[:count_a]
        g_in = refs[count_a : count_a + count_g]
        r_in = refs[count_a + count_g : count_a + count_g + count_r]
        refs = refs[count_a + count_g + count_r :]
        outs = refs[: len(results)]
        refs = refs[len(results) :]
        late_out = refs[:extra]
        g_out = refs[extra : extra + count_g]
        r_out = refs[extra + count_g : extra + count_g + count_r]
        refs = refs[extra + count_g + count_r :]
        send_sem, recv_sem, local_sem = refs[:3]
        buffers = refs[3:]
        p = Place()
        flow = Flow(send_sem, recv_sem)
        greet, direct, stay = plan(p, ins, outs)
        barrier = pltpu.get_barrier_semaphore()
        waits = 0
        for target, when in greet:
            if when is None:
                waits = waits + 1
            else:
                waits = waits + jnp.where(when, 1, 0).astype(jnp.int32)
            guarded(when, lambda target=target: signal_all(barrier, [target]))
        pl.semaphore_wait(barrier, waits)
        lines = [LineGather(flow, p, src, dst) for src, dst in zip(g_in, g_out)]
        sums = [
            LineReduce(flow, p, src, dst, *buffers[3 * n : 3 * n + 3])
            for n, (src, dst) in enumerate(zip(r_in, r_out))
        ]
        base = flow.take(messages)
        copies = {}
        arrived = set()

        stays = []

        def landed(number):
            if number not in arrived:
                arrived.add(number)
                guarded(copies[number][2], copies[number][0].wait_recv)

        def run_stage(stage):
            for number, (src, dst, target, after, when, when_stage, lands) in enumerate(direct):
                if when_stage != stage:
                    continue
                for earlier in after:
                    landed(earlier)
                copy = flow.copy(src, dst, target, base + number)
                guarded(when, copy.start)
                copies[number] = (copy, when, lands)
            if late is not None and late[1] == stage:
                for number in range(late[2]):
                    landed(number)
                stays[0][0].wait()
                line = LineGather(flow, p, outs[late[0]], late_out[0])
                line.start()
                own = pltpu.make_async_copy(
                    outs[late[0]], late_out[0].at[p.c, p.z], local_sem.at[local + count_g]
                )
                own.start()
                stays[0] = (own, None)
                if stage:
                    for earlier in range(1, stage + 1):
                        line.hop(earlier)
                lines.append(line)

        for item in sums:
            item.start()
        for line in lines:
            line.start()
        for number, (src, dst, when) in enumerate(
            list(stay) + [(src, dst.at[p.c, p.z], None) for src, dst in zip(g_in, g_out)]
        ):
            copy = pltpu.make_async_copy(src, dst, local_sem.at[number])
            guarded(when, copy.start)
            stays.append((copy, when))
        run_stage(0)
        for step in range(1, R):
            for line in lines:
                line.hop(step)
            run_stage(step)
        for item in sums:
            item.run()
        for copy, when in stays:
            guarded(when, copy.wait)
        for number in copies:
            landed(number)
        for copy, when, _ in copies.values():
            guarded(when, copy.wait_send)
        flow.finish()

    spot = pl.BlockSpec(memory_space=pl.ANY)
    near = pl.BlockSpec(memory_space=pltpu.VMEM)
    out_shape = [jax.ShapeDtypeStruct(shape, kind) for shape, kind in results]
    if late is not None:
        shape, kind = results[late[0]]
        out_shape.append(jax.ShapeDtypeStruct((D, R) + shape, kind))
    out_shape += [jax.ShapeDtypeStruct((D, R) + g.shape, g.dtype) for g in gathers]
    out_shape += [jax.ShapeDtypeStruct(r.shape[2:], F32) for r in reduces]
    scratch = [
        pltpu.SemaphoreType.DMA((total_sems,)),
        pltpu.SemaphoreType.DMA((total_sems,)),
        pltpu.SemaphoreType.DMA((local + count_g + extra,)),
    ]
    for r in reduces:
        block = r.shape[1:]
        scratch += [
            pltpu.VMEM(block, BF16),
            pltpu.VMEM((2,) + block, BF16),
            pltpu.VMEM((2,) + block, BF16),
        ]
    return pl.pallas_call(
        kernel,
        out_shape=out_shape,
        in_specs=[spot] * (count_a + count_g) + [near] * count_r,
        out_specs=[spot] * (len(results) + extra + count_g) + [near] * count_r,
        scratch_shapes=scratch,
        compiler_params=pltpu.CompilerParams(
            collective_id=ident, has_side_effects=True, vmem_limit_bytes=56 * 2**20
        ),
        name=name,
    )(*arrays, *gathers, *reduces)


def team_greet(p):
    return [({"duo": c, "rows": z}, None) for c, z in p.team()]


def group_greet(p):
    return [({"grp": q}, None) for q in p.groups()]


class Plan:
    def __init__(self, p):
        self.p = p
        self.messages, self.local, self.greet = [], [], []

    def add(self, src, dst, target, after=(), when=None, stage=0, lands=None):
        self.messages.append((src, dst, target, after, when, stage, when if lands is None else lands))
        return len(self.messages) - 1

    def team_swap(self, src, dst, stage=0):
        p = self.p
        mine = p.c * p.R + p.z
        for c, z in p.team():
            self.add(src.at[c * p.R + z], dst.at[mine], {"duo": c, "rows": z}, stage=stage)
        self.local.append((src.at[mine], dst.at[mine], None))

    def team_gather(self, src, dst, stage=0):
        p = self.p
        mine = p.c * p.R + p.z
        for c, z in p.team():
            self.add(src, dst.at[mine], {"duo": c, "rows": z}, stage=stage)
        self.local.append((src, dst.at[mine], None))

    def group_gather(self, src, dst, late=None):
        p = self.p
        self.local.append((src, dst.at[p.q], None))
        if late is None or p.G != 4:
            for q in p.groups():
                self.add(src, dst.at[p.q], {"grp": q})
            return
        across = p.q + 1 - 2 * lax.rem(p.q, 2)
        along = lax.rem(p.q + 2, 4)
        one = self.add(src, dst.at[p.q], {"grp": across})
        two = self.add(src, dst.at[p.q], {"grp": along})
        half = src.shape[0] // 2
        top, bottom = pl.ds(0, half), pl.ds(half, half)
        self.add(
            dst.at[across, top], dst.at[across, top], {"grp": along}, after=(one,), stage=late
        )
        self.add(
            dst.at[along, bottom],
            dst.at[along, bottom],
            {"grp": across},
            after=(two,),
            stage=late,
        )

    def group_swap(self, src, dst, stage=0):
        p = self.p
        for q in p.groups():
            self.add(src.at[q], dst.at[p.q], {"grp": q}, stage=stage)
        self.local.append((src.at[p.q], dst.at[p.q], None))

    def done(self):
        p = self.p
        return team_greet(p) + group_greet(p) + self.greet, self.messages, self.local


def layer_stats(values):
    center = values - jnp.mean(values, axis=-1, keepdims=True)
    spread = jnp.mean(center * center, axis=-1, keepdims=True)
    inverse = lax.rsqrt(spread + norm_eps)
    return center * inverse, inverse


def layer_back(grad, hat, inverse):
    first = jnp.mean(grad, axis=-1, keepdims=True)
    second = jnp.mean(grad * hat, axis=-1, keepdims=True)
    return inverse * (grad - first - hat * second)


def mm(left, right):
    return jnp.dot(left, right, preferred_element_type=F32)


def mm_t(left, right):
    return lax.dot_general(left, right, (((1,), (1,)), ((), ())), preferred_element_type=F32)


def t_mm(left, right):
    return lax.dot_general(left, right, (((0,), (0,)), ((), ())), preferred_element_type=F32)


def columns_of(bucket_ids):
    return jnp.where(
        bucket_ids == 0, 9 * UNIT // 2, jnp.where(bucket_ids == 1, 3 * UNIT, 9 * UNIT // 4)
    )


def pixel_mask(positions, height, width, cols):
    row_at = positions // cols
    col_at = positions % cols
    return ((row_at < height) & (col_at < width)).astype(F32)


def spots(shapes):
    return [jax.ShapeDtypeStruct(shape, kind) for shape, kind in shapes]


def local_kernel(name, kernel, arrays, results, scratch=(), scalars=0):
    near = pl.BlockSpec(memory_space=pltpu.VMEM)
    numbers = pl.BlockSpec(memory_space=pltpu.SMEM)
    return pl.pallas_call(
        kernel,
        out_shape=spots(results),
        in_specs=[numbers] * scalars + [near] * (len(arrays) - scalars),
        out_specs=[near] * len(results),
        scratch_shapes=list(scratch),
        compiler_params=pltpu.CompilerParams(vmem_limit_bytes=56 * 2**20),
        name=name,
    )(*arrays)


class Sizes:
    def __init__(self, latents, clip_tokens, in_weight, in_bias, conv_bias, map_weight):
        self.G, self.D, self.R = (lax.axis_size(axis) for axis in AXES)
        self.T = self.D * self.R
        self.S = self.T * self.G
        self.N, self.C = latents.shape[1:]
        self.pixels = self.R * self.N
        self.FFS = in_bias.shape[0]
        self.FL = self.G * self.FFS
        self.FF = in_weight.shape[1]
        self.cs = conv_bias.shape[0]
        self.ms = map_weight.shape[0]
        self.mp = -(-self.ms // 16) * 16
        self.slots = clip_tokens.shape[1]
        self.sp = -(-self.slots // 16) * 16
        self.texts = self.R * self.slots
        self.HW = self.C // self.T
        self.even = self.G == self.R
        self.Q = self.G if self.even else 1
        self.places = [(g, d, r) for g in range(self.G) for d in range(self.D) for r in range(self.R)]


def rows_cols(first, count, cols):
    position = (first + lax.broadcasted_iota(jnp.int32, (count, 1), 0)).astype(F32)
    row = jnp.floor((position + 0.5) / cols)
    return row, position - row * cols


def float_cols(bucket):
    return jnp.where(bucket == 0, 9.0 * UNIT / 2, jnp.where(bucket == 1, 3.0 * UNIT, 9.0 * UNIT / 4))


WIDTHS = (9 * UNIT // 2, 3 * UNIT, 9 * UNIT // 4)
SMALL = 32
VEC = 16


def cut_kernel(m, arrays):
    def kernel(h_ref, w_ref, b_ref, in_ref, qkv_ref, map_ref, clip_ref, lat_ref, cot_ref, cw_ref, *refs):
        vectors, refs = refs[:5], refs[5:]
        te_ref, tm_ref, f0, f1, f2 = refs[:5]
        in_out, qkv_out, map_out, clip_out, masked_out, gres_out, small_out, f_out, small, fv = refs[5:]
        for g in range(m.G):
            for t in range(m.T):
                start = m.FFS * (g * m.T + t)
                in_out[t, :, pl.ds(g * m.FFS, m.FFS)] = in_ref[:, pl.ds(start, m.FFS)]
        for d in range(m.D):
            for r in range(m.R):
                for j in range(3):
                    start = m.C * j + m.HW * (m.D * r + d)
                    qkv_out[d * m.R + r, :, pl.ds(j * m.HW, m.HW)] = qkv_ref[:, pl.ds(start, m.HW)]
        map_out[...] = jnp.zeros_like(map_out)
        for t in range(m.T):
            map_out[t, pl.ds(0, m.ms)] = map_ref[:, pl.ds(t * m.HW, m.HW)]
        clip_out[...] = jnp.zeros_like(clip_out)
        clip_out[pl.ds(0, m.slots)] = clip_ref[0]
        z = lax.axis_index("rows")
        row, col = rows_cols(z * m.N, m.N, float_cols(b_ref[0]))
        keep = (row < h_ref[0].astype(F32)) & (col < w_ref[0].astype(F32))
        masked_out[...] = jnp.where(keep, lat_ref[0].astype(F32), 0.0).astype(BF16)
        gres_out[...] = jnp.where(keep, cot_ref[0].astype(F32), 0.0).astype(BF16)
        small[...] = jnp.zeros_like(small)
        small[pl.ds(0, 9), pl.ds(0, m.cs)] = cw_ref[...].astype(F32)
        for number, ref in enumerate(vectors):
            small[pl.ds(9 + number, 1), pl.ds(0, ref.shape[1])] = ref[...].astype(F32)
        small[pl.ds(14, 1), pl.ds(0, te_ref.shape[1])] = te_ref[...].astype(F32)
        lane = lax.broadcasted_iota(jnp.int32, (1, 128), 1)
        facts = jnp.where(lane == 0, h_ref[0], jnp.where(lane == 1, w_ref[0], b_ref[0]))
        small[pl.ds(15, 1)] = facts.astype(F32)
        small[pl.ds(16, 1), pl.ds(0, m.texts)] = tm_ref[...].astype(F32)
        small_out[...] = small[...].astype(BF16)
        fv[...] = jnp.zeros_like(fv)
        for number, ref in enumerate((f0, f1, f2)):
            fv[pl.ds(number, 1)] = ref[...].astype(F32)
        f_out[...] = fv[...].astype(BF16)

    return local_kernel(
        "cut_weights",
        kernel,
        arrays,
        [
            ((m.T, m.cs, m.FL), BF16),
            ((m.T, m.cs, 3 * m.HW), BF16),
            ((m.T, m.mp, m.HW), BF16),
            ((m.sp, arrays[6].shape[2]), BF16),
            ((m.N, m.C), BF16),
            ((m.N, m.C), BF16),
            ((SMALL, 128), BF16),
            ((16, m.FFS), BF16),
        ],
        [pltpu.VMEM((SMALL, 128), F32), pltpu.VMEM((16, m.FFS), F32)],
        scalars=3,
    )


def fill_extended(m, extended, edges_ref, mid_ref):
    z = lax.axis_index("rows")
    extended[pl.ds(0, EDGE)] = jnp.where(z > 0, edges_ref[0].astype(F32), 0.0)
    extended[pl.ds(EDGE, m.N)] = mid_ref[...].astype(F32)
    extended[pl.ds(EDGE + m.N, EDGE)] = jnp.where(z < m.R - 1, edges_ref[1].astype(F32), 0.0)


def each_bucket(bucket, act):
    for number, width in enumerate(WIDTHS):
        pl.when(bucket == number)(functools.partial(act, width))


def each_column_block(m, act):
    @pl.loop(0, m.C // 128)
    def _(number):
        act(pl.ds(pl.multiple_of(number * 128, 128), 128))


def tap_steps():
    return [(index, index // 3 - 1, index % 3 - 1) for index in range(9)]


def conv_kernel(m, b_ref, edges, masked, small_all, time_weight, time_bias):
    def kernel(b_ref, edges_ref, mid_ref, small_ref, tw_ref, tb_ref, normed, hat, inv, vec, mod, keys, pix, extended, conv, item, te):
        vec[...] = jnp.zeros_like(vec)
        for s, (g, d, r) in enumerate(m.places):
            piece = small_ref[d, r, g].astype(F32)
            vec[pl.ds(0, 13), pl.ds(s * m.cs, m.cs)] = piece[:13, : m.cs]
            half = m.S // 2
            vec[pl.ds(13 + s // half, 1), pl.ds(2 * m.cs * (s % half), 2 * m.cs)] = piece[
                13:14, : 2 * m.cs
            ]
            if r == 0:
                item[pl.ds(m.D * g + d, 1)] = piece[14:15]
        te[...] = item[...][:, : te.shape[1]].astype(BF16)
        mod[...] = jnp.zeros_like(mod)
        mod[pl.ds(0, te.shape[0]), pl.ds(0, 2 * m.cs)] = mm(te[...], tw_ref[...]) + tb_ref[...].astype(F32)
        q = lax.axis_index("grp")
        for d in range(m.D):
            facts = small_ref[d, 0, q].astype(F32)
            row, col = rows_cols(0, m.pixels, float_cols(facts[15:16, 2:3]))
            inside = (row < facts[15:16, 0:1]) & (col < facts[15:16, 1:2])
            keys[d, pl.ds(0, m.pixels)] = jnp.where(inside, 1.0, 0.0)
            text = facts.T[: m.texts, 16:17]
            slot = lax.broadcasted_iota(jnp.int32, (m.texts, 1), 0)
            keys[d, pl.ds(m.pixels, m.texts)] = jnp.where(slot < TXT, text, 0.0)
        fill_extended(m, extended, edges_ref, mid_ref)
        z = lax.axis_index("rows")

        def taps(width):
            _, col = rows_cols(z * m.N, m.N, float(width))

            def block(lanes):
                total = jnp.zeros((m.N, 128), F32) + vec[pl.ds(9, 1), lanes]
                for index, dy, dx in tap_steps():
                    piece = extended[pl.ds(EDGE + dy * width + dx, m.N), lanes]
                    ok = (col + dx >= 0) & (col + dx < width)
                    total = total + jnp.where(ok, piece, 0.0) * vec[pl.ds(index, 1), lanes]
                conv[:, lanes] = total

            each_column_block(m, block)

        each_bucket(b_ref[0], taps)
        values, inverse = layer_stats(conv[...])
        hat[...] = values
        normed[...] = values.astype(BF16)
        inv[...] = inverse
        pix[...] = keys[lax.axis_index("duo"), pl.ds(pl.multiple_of(z * m.N, 8), m.N)]

    items = m.G * m.D
    return local_kernel(
        "convolve",
        kernel,
        [b_ref, edges, masked, small_all, time_weight, time_bias],
        [
            ((m.N, m.C), BF16),
            ((m.N, m.C), F32),
            ((m.N, 1), F32),
            ((VEC, m.C), F32),
            ((-(-items // 8) * 8, 128), F32),
            ((m.D, m.pixels + m.texts, 1), F32),
            ((m.N, 1), F32),
        ],
        [
            pltpu.VMEM((m.N + 2 * EDGE, m.C), F32),
            pltpu.VMEM((m.N, m.C), F32),
            pltpu.VMEM((items, 128), F32),
            pltpu.VMEM((items, time_weight.shape[0]), BF16),
        ],
        scalars=1,
    )


def attention_kernel(m, two_all, gres_all, mapped_all, weight, proj, bias, key_keep):
    heads = m.HW // HEAD
    keys = m.pixels + m.texts
    scale = HEAD ** (-0.5)
    HW, C, pixels, texts = m.HW, m.C, m.pixels, m.texts
    wide = C // m.Q

    def kernel(two_ref, gres_ref, map_ref, w_ref, p_ref, bias_ref, keep_ref, res_out, two_out, map_out, gw_out, gp_out, gb_out,
               qkv, k_all, v_all, dk, dv, o_t, dq_t, g_all, dqkv, dtext, att, gw, gp):
        step = pl.program_id(0)

        @pl.when(step == 0)
        def _():
            gw[...] = jnp.zeros_like(gw)
            gp[...] = jnp.zeros_like(gp)
            gb_out[...] = jnp.zeros_like(gb_out)

        qkv[...] = (mm(two_ref[0], w_ref[...]) + bias_ref[...]).astype(BF16)
        text = jnp.zeros((texts, 3 * HW), F32) + bias_ref[...]
        for t in range(m.T):
            text = text + mm(map_ref[t], w_ref[pl.ds(t * HW, HW)])
        text = text.astype(BF16)
        g = jnp.zeros((pixels, HW), F32)
        for n in range(m.Q):
            g = g + mm_t(gres_ref[0, :, pl.ds(n * wide, wide)], p_ref[n])
        g_all[...] = g.astype(BF16)
        k_all[pl.ds(0, pixels)] = qkv[:, HW : 2 * HW]
        k_all[pl.ds(pixels, texts)] = text[:, HW : 2 * HW]
        v_all[pl.ds(0, pixels)] = qkv[:, 2 * HW :]
        v_all[pl.ds(pixels, texts)] = text[:, 2 * HW :]
        k_t = k_all[...].T
        v_t = v_all[...].T
        dk[...] = jnp.zeros_like(dk)
        dv[...] = jnp.zeros_like(dv)
        o_t[...] = jnp.zeros_like(o_t)
        dq_t[...] = jnp.zeros_like(dq_t)
        lane = lax.broadcasted_iota(jnp.int32, (1, HW), 1)
        line = lax.broadcasted_iota(jnp.int32, (HW, 1), 0)
        alive = keep_ref[0] > 0

        @pl.loop(0, heads)
        def _(head):
            low = head * HEAD
            in_head = (lane >= low) & (lane < low + HEAD)
            in_line = (line >= low) & (line < low + HEAD)
            q_h = jnp.where(in_head, qkv[:, :HW], 0).astype(BF16)
            g_h = jnp.where(in_head, g_all[...], 0).astype(BF16)
            scores = mm_t(k_all[...], q_h) * scale
            scores = jnp.where(alive, scores, masked_score)
            top = jnp.max(scores, axis=0, keepdims=True)
            weights = jnp.exp(scores - top)
            probs = weights / jnp.sum(weights, axis=0, keepdims=True)
            probs_low = probs.astype(BF16)
            v_h = jnp.where(in_line, v_t, 0).astype(BF16)
            o_t[...] += mm(v_h, probs_low)
            dv[...] += mm(probs_low, g_h)
            grad_probs = mm_t(v_all[...], g_h)
            sums = jnp.sum(probs * grad_probs, axis=0, keepdims=True)
            grad_scores = (probs * (grad_probs - sums)).astype(BF16)
            k_h = jnp.where(in_line, k_t, 0).astype(BF16)
            dq_t[...] += mm(k_h, grad_scores)
            dk[...] += mm(grad_scores, q_h)

        o_low = o_t[...].astype(BF16)
        att[...] = o_t[...].T.astype(BF16)
        dqkv[:, :HW] = (dq_t[...].T * scale).astype(BF16)
        dqkv[:, HW : 2 * HW] = (dk[pl.ds(0, pixels)] * scale).astype(BF16)
        dqkv[:, 2 * HW :] = dv[pl.ds(0, pixels)].astype(BF16)
        dtext[:, :HW] = jnp.zeros((texts, HW), BF16)
        dtext[:, HW : 2 * HW] = (dk[pl.ds(pixels, texts)] * scale).astype(BF16)
        dtext[:, 2 * HW :] = dv[pl.ds(pixels, texts)].astype(BF16)
        gb_out[pl.ds(0, 1)] += jnp.sum(dqkv[...].astype(F32), axis=0, keepdims=True) + jnp.sum(
            dtext[...].astype(F32), axis=0, keepdims=True
        )
        for n in range(m.Q):
            block = pl.ds(n * wide, wide)
            res_out[0, :, block] = mm(att[...], p_ref[n]).astype(BF16)
            gp[n] += mm(o_low, gres_ref[0, :, block])
        two_out[0] = mm_t(dqkv[...], w_ref[...]).astype(BF16)
        gw[...] += t_mm(two_ref[0], dqkv[...])
        for t in range(m.T):
            rows = pl.ds(t * HW, HW)
            map_out[t] = mm_t(dtext[...], w_ref[rows]).astype(BF16)
            gw[rows] += t_mm(map_ref[t], dtext[...])

        @pl.when(step == m.D - 1)
        def _():
            gw_out[...] = gw[...].astype(BF16)
            gp_out[...] = gp[...].astype(BF16)

    def item(shape):
        return pl.BlockSpec((1,) + shape, lambda i: (i, 0, 0))

    def fixed(shape):
        return pl.BlockSpec(shape, lambda i: (0,) * len(shape))

    slots = pl.BlockSpec((m.T, texts, HW), lambda i: (0, i, 0))
    return pl.pallas_call(
        kernel,
        grid=(m.D,),
        out_shape=spots(
            [
                ((m.D, pixels, C), BF16),
                ((m.D, pixels, C), BF16),
                ((m.T, m.D * texts, HW), BF16),
                ((C, 3 * HW), BF16),
                ((m.Q, HW, wide), BF16),
                ((8, 3 * HW), F32),
            ]
        ),
        in_specs=[
            item((pixels, C)),
            item((pixels, C)),
            slots,
            fixed((C, 3 * HW)),
            fixed((m.Q, HW, wide)),
            fixed((1, 3 * HW)),
            item((keys, 1)),
        ],
        out_specs=[
            item((pixels, C)),
            item((pixels, C)),
            slots,
            fixed((C, 3 * HW)),
            fixed((m.Q, HW, wide)),
            fixed((8, 3 * HW)),
        ],
        scratch_shapes=[
            pltpu.VMEM((pixels, 3 * HW), BF16),
            pltpu.VMEM((keys, HW), BF16),
            pltpu.VMEM((keys, HW), BF16),
            pltpu.VMEM((keys, HW), F32),
            pltpu.VMEM((keys, HW), F32),
            pltpu.VMEM((HW, pixels), F32),
            pltpu.VMEM((HW, pixels), F32),
            pltpu.VMEM((pixels, HW), BF16),
            pltpu.VMEM((pixels, 3 * HW), BF16),
            pltpu.VMEM((texts, 3 * HW), BF16),
            pltpu.VMEM((pixels, HW), BF16),
            pltpu.VMEM((C, 3 * HW), F32),
            pltpu.VMEM((m.Q, HW, wide), F32),
        ],
        compiler_params=pltpu.CompilerParams(vmem_limit_bytes=60 * 2**20),
        name="attention_block",
    )(two_all, gres_all, mapped_all, weight, proj, bias, key_keep)


def conv_back_kernel(m, b_ref, grad_in, hat, inv, edges, masked, vec_grads, qv_grads, modulate_grads):
    def kernel(b_ref, g_ref, hat_ref, inv_ref, edges_ref, mid_ref, vec_ref, qv_ref, gm_ref, grad, low, tiny, extended, vec):
        values = layer_back(g_ref[...], hat_ref[...], inv_ref[...])
        grad[...] = values
        low[...] = values.astype(BF16)
        fill_extended(m, extended, edges_ref, mid_ref)
        vec[pl.ds(9, 1)] = jnp.sum(values, axis=0, keepdims=True)
        vec[pl.ds(10, 3)] = vec_ref[pl.ds(0, 3)]
        vec[pl.ds(13, 3)] = jnp.zeros((3, m.C), F32)
        z = lax.axis_index("rows")

        def taps(width):
            _, col = rows_cols(z * m.N, m.N, float(width))

            def block(lanes):
                value = grad[:, lanes]
                for index, dy, dx in tap_steps():
                    piece = extended[pl.ds(EDGE + dy * width + dx, m.N), lanes]
                    ok = (col + dx >= 0) & (col + dx < width)
                    vec[pl.ds(index, 1), lanes] = jnp.sum(
                        jnp.where(ok, piece, 0.0) * value, axis=0, keepdims=True
                    )

            each_column_block(m, block)

        each_bucket(b_ref[0], taps)
        tiny[...] = jnp.zeros_like(tiny)
        half = m.S // 2
        pair = 2 * m.cs
        for s, (g, d, r) in enumerate(m.places):
            t = d * m.R + r
            tiny[t, g, pl.ds(0, 13), pl.ds(0, m.cs)] = vec[pl.ds(0, 13), pl.ds(s * m.cs, m.cs)]
            side, at = pl.ds(s // half, 1), pl.ds(pair * (s % half), pair)
            tiny[t, g, pl.ds(13, 1), pl.ds(0, pair)] = qv_ref[side, at]
            tiny[t, g, pl.ds(14, 1), pl.ds(0, pair)] = gm_ref[side, at]

    return local_kernel(
        "convolve_back",
        kernel,
        [b_ref, grad_in, hat, inv, edges, masked, vec_grads, qv_grads, modulate_grads],
        [((m.N, m.C), F32), ((m.N, m.C), BF16), ((m.T, m.G, 16, 128), F32)],
        [pltpu.VMEM((m.N + 2 * EDGE, m.C), F32), pltpu.VMEM((VEC, m.C), F32)],
        scalars=1,
    )


def finish_kernel(m, b_ref, edges, low, after, pix, vec, in_team, qkv_team, map_team, proj_team):
    def kernel(b_ref, edges_ref, low_ref, after_ref, pix_ref, vec_ref, in_ref, qkv_ref, map_ref, proj_ref,
               lat_out, in_out, qkv_out, map_out, proj_out, extended):
        fill_extended(m, extended, edges_ref, low_ref)
        z = lax.axis_index("rows")
        keep = pix_ref[...] > 0

        def taps(width):
            _, col = rows_cols(z * m.N, m.N, float(width))

            def block(lanes):
                total = jnp.zeros((m.N, 128), F32)
                for index, dy, dx in tap_steps():
                    piece = extended[pl.ds(EDGE - dy * width - dx, m.N), lanes]
                    ok = (col - dx >= 0) & (col - dx < width)
                    total = total + jnp.where(ok, piece, 0.0) * vec_ref[pl.ds(index, 1), lanes]
                lat_out[0, :, lanes] = after_ref[:, lanes] + jnp.where(keep, total, 0.0)

            each_column_block(m, block)

        each_bucket(b_ref[0], taps)
        for g in range(m.G):
            for t in range(m.T):
                start = m.FFS * (g * m.T + t)
                in_out[:, pl.ds(start, m.FFS)] = in_ref[t, :, pl.ds(g * m.FFS, m.FFS)].astype(F32)
        for d in range(m.D):
            for r in range(m.R):
                for j in range(3):
                    start = m.C * j + m.HW * (m.D * r + d)
                    qkv_out[:, pl.ds(start, m.HW)] = qkv_ref[
                        d * m.R + r, :, pl.ds(j * m.HW, m.HW)
                    ].astype(F32)
        for t in range(m.T):
            map_out[:, pl.ds(t * m.HW, m.HW)] = map_ref[t].astype(F32)[: m.ms]
        wide = m.C // m.Q
        for n in range(m.Q):
            proj_out[:, pl.ds(n * wide, wide)] = proj_ref[n].astype(F32)

    return local_kernel(
        "finish",
        kernel,
        [b_ref, edges, low, after, pix, vec, in_team, qkv_team, map_team, proj_team],
        [
            ((1, m.N, m.C), F32),
            ((m.cs, m.FF), F32),
            ((m.cs, 3 * m.C), F32),
            ((m.ms, m.C), F32),
            ((m.cs, m.C), F32),
        ],
        [pltpu.VMEM((m.N + 2 * EDGE, m.C), F32)],
        scalars=1,
    )


class Posted:
    def __init__(self, copy, lands):
        self.copy, self.lands, self.landed = copy, lands, False


def line_order(p, number):
    low = p.z < p.R // 2
    far, near = p.R - 1 - number // 2, number // 2
    if number % 2:
        far, near = near, far
    return jnp.where(low, far, near)


def chunks(count, act, step=16):
    @pl.loop(0, count // step)
    def _(number):
        act(pl.ds(pl.multiple_of(number * step, step), step))


def greet_all(p, targets):
    barrier = pltpu.get_barrier_semaphore()
    waits = 0
    for target, when in targets:
        if when is None:
            waits = waits + 1
        else:
            waits = waits + jnp.where(when, 1, 0).astype(jnp.int32)
        guarded(when, lambda target=target: signal_all(barrier, [target]))
    pl.semaphore_wait(barrier, waits)


def fused_kernel(ident, name, greet, act, near, loads, far, near_out, far_out, scratch, sems, local):
    close = pl.BlockSpec(memory_space=pltpu.VMEM)
    spot = pl.BlockSpec(memory_space=pl.ANY)
    counts = [len(near), len(loads), len(far), len(near_out), len(far_out), len(scratch), len(loads)]

    def kernel(*refs):
        groups = []
        for count in counts:
            groups.append(refs[:count])
            refs = refs[count:]
        send_sem, recv_sem, local_sem, load_sem = refs
        near, sources, far, near_out, far_out, scratch, held = groups
        brought = []
        for number, (source, place) in enumerate(zip(sources, held)):
            copy = pltpu.make_async_copy(source, place, load_sem.at[number])
            copy.start()
            brought.append(Brought(copy, place))
        p = Place()
        flow = Flow(send_sem, recv_sem, local_sem)
        greet_all(p, greet(p))
        act(p, flow, near, brought, far, near_out, far_out, scratch)
        flow.finish()

    return pl.pallas_call(
        kernel,
        out_shape=spots(near_out + far_out),
        in_specs=[close] * len(near) + [spot] * (len(loads) + len(far)),
        out_specs=[close] * len(near_out) + [spot] * len(far_out),
        scratch_shapes=list(scratch)
        + [pltpu.VMEM(array.shape, array.dtype) for array in loads]
        + [
            pltpu.SemaphoreType.DMA((sems,)),
            pltpu.SemaphoreType.DMA((sems,)),
            pltpu.SemaphoreType.DMA((local,)),
            pltpu.SemaphoreType.DMA((max(len(loads), 1),)),
        ],
        compiler_params=pltpu.CompilerParams(
            collective_id=ident, has_side_effects=True, vmem_limit_bytes=63 * 2**20
        ),
        name=name,
    )(*near, *loads, *far)


class Brought:
    def __init__(self, copy, place):
        self.copy, self.place, self.here = copy, place, False

    def get(self):
        if not self.here:
            self.copy.wait()
            self.here = True
        return self.place


def gather_sems(m):
    return 4 * m.R - 3


def reduce_sems(m):
    return 3 * m.R


def reduce_buffers(m, count, width, part=True):
    block = (m.R, count, width)
    mine = [pltpu.VMEM((m.D,) + block, BF16)] if part else []
    return mine + [
        pltpu.VMEM(block, BF16),
        pltpu.VMEM((2,) + block, BF16),
        pltpu.VMEM((2,) + block, BF16),
    ]


def spread_greet(m, p):
    greet = []
    for step in range(m.G):
        source = {"grp": p.z, "duo": p.c, "rows": lax.rem(p.q - step + m.G, m.G)}
        greet.append((source, None if step else p.q != p.z))
    return greet


def common_greet(p):
    return team_greet(p) + group_greet(p)


def up_kernel(m, normed_all, in_full, in_bias, key_keep, clip_all, map_full, vec):
    step = m.N
    per = m.pixels // step
    root = 0.5**0.5

    def kernel(x_ref, w_ref, b_ref, keep_ref, clip_ref, map_ref, vec_ref,
               active, slope, norms, total, silu, mapped, squares, weight, text):
        squares[...] = jnp.zeros_like(squares)

        @pl.loop(0, m.D * per)
        def _(number):
            rows = pl.ds(pl.multiple_of(number * step, 16), step)
            hidden = mm(x_ref[rows], w_ref[...]) + b_ref[...]
            gate = 0.5 * (1.0 + lax.erf(hidden * root))
            value = hidden * gate
            active[rows] = value
            slope[rows] = gate + hidden * (jnp.exp(-0.5 * hidden * hidden) * 0.3989422804014327)
            item = number // per
            inside = pl.ds(pl.multiple_of((number - item * per) * step, 16), step)
            squares[pl.ds(item, 1)] += jnp.sum(
                keep_ref[item, inside] * value * value, axis=0, keepdims=True
            )

        norms[...] = jnp.sqrt(squares[...])
        total[...] = jnp.broadcast_to(jnp.sum(norms[...], axis=1, keepdims=True), total.shape)
        for t in range(m.T):
            piece = clip_ref[t].astype(F32)[: m.slots]
            text[pl.ds(t * m.slots, m.slots)] = piece / (1.0 + jnp.exp(-piece))
        silu[...] = text[...].astype(BF16)
        for g in range(m.G):
            for t in range(m.T):
                at = m.ms * (g * m.T + t)
                piece = map_ref[g, pl.ds(t * m.mp, m.mp)].astype(F32)
                weight[pl.ds(at, m.ms)] = piece[: m.ms]
        for t in range(m.T):
            @pl.when(lax.axis_index("duo") * m.R + lax.axis_index("rows") == t)
            def _():
                bias = vec_ref[pl.ds(11, 1), pl.ds(t * m.HW, m.HW)]
                mapped[...] = (mm(silu[...], weight[...].astype(BF16)) + bias).astype(BF16)

    texts = m.D * m.texts
    cond = clip_all.shape[2]
    return local_kernel(
        "hidden_units",
        kernel,
        [normed_all, in_full, in_bias, key_keep, clip_all, map_full, vec],
        [
            ((m.D * m.pixels, m.FL), F32),
            ((m.D * m.pixels, m.FL), F32),
            ((8, m.FL), F32),
            ((8, 128), F32),
            ((texts, cond), BF16),
            ((texts, m.HW), BF16),
        ],
        [
            pltpu.VMEM((8, m.FL), F32),
            pltpu.VMEM((cond, m.HW), F32),
            pltpu.VMEM((texts, cond), F32),
        ],
    )


def team_sum(m, p, flow, own, everyone):
    mine = p.c * m.R + p.z
    posted = [
        flow.post(own, everyone.at[mine], {"duo": c, "rows": z}) for c, z in p.team()
    ]

    def total():
        for item in posted:
            flow.land(item)
        result = own[...]
        for step, (c, z) in enumerate(p.team()):
            result = result + everyone[c * m.R + z]
        return result

    return total


def branch_kernel(m, active, norms, total, out_full, gain, grn_bias, latents, keep, vec, mod_all, qkv_rows, mapped, gres, proj_part):
    near = [norms, total, gain, grn_bias, keep, mod_all]
    loads = [active, out_full, latents, vec]
    far = [qkv_rows, mapped, gres] + ([proj_part] if m.even else [])
    N, C = m.N, m.C
    rows_all = m.D * m.pixels

    def act(p, flow, near, loads, far, near_out, far_out, scratch):
        norms, total, gain, grn_bias, keep, mod_all = near
        grn, after, hat, inv, two, ratio, means, mods = near_out
        two_all, mapped_all, gres_all, qkv_all = far_out[:4]
        everyone, part, mate, passed, landed, branch, slopes = scratch
        add_up = team_sum(m, p, flow, total, everyone)
        flow.gather_group(p, far[0], qkv_all)
        if m.even:
            flow.gather_group(p, far[3], far_out[4])
        text_line = LineGather(flow, p, far[1], mapped_all)
        grad_line = LineGather(flow, p, far[2], gres_all)
        two_line = LineGather(flow, p, two, two_all)
        half = m.S // 2
        pair = 2 * m.cs
        for s, (g, d, r) in enumerate(m.places):
            item = pl.ds(m.D * p.q + p.c, 1)
            mods[pl.ds(s // half, 1), pl.ds(pair * (s % half), pair)] = mod_all[d, r, g, item, pl.ds(0, pair)]
        mean = add_up() / m.FF + grn_eps
        means[...] = mean
        ratio[...] = norms[...] / mean[:, :1]
        slopes[...] = gain[...] * ratio[...] + 1.0
        line = LineReduce(flow, p, part, branch, mate, passed, landed)
        active, out_w, lat, vec = (load.get() for load in loads)

        def produce(block):
            for d in range(m.D):
                rows = pl.ds(pl.multiple_of(d * m.pixels + block * N, 16), N)
                low = (active[rows] * slopes[pl.ds(d, 1)] + grn_bias[...]).astype(BF16)
                grn[rows] = low
                part[d, block] = mm(low, out_w[...]).astype(BF16)

        line.run(produce)
        text_line.start()

        def tail(rows):
            value = lat[rows].astype(F32) + keep[rows] * (branch[rows] + vec[pl.ds(10, 1)])
            after[rows] = value
            second = value * (1.0 + mods[pl.ds(0, 1)]) + mods[pl.ds(1, 1)]
            normal, inverse = layer_stats(second)
            hat[rows] = normal
            inv[rows] = inverse
            two[rows] = normal.astype(BF16)

        chunks(N, tail)
        two_line.start()
        grad_line.start()
        flow.keep(far[1], mapped_all.at[p.c, p.z])
        flow.keep(two, two_all.at[p.c, p.z])
        flow.keep(far[2], gres_all.at[p.c, p.z])
        for step in range(1, m.R):
            text_line.hop(step)
            two_line.hop(step)
            grad_line.hop(step)

    near_out = [
        ((rows_all, m.FL), BF16),
        ((N, C), F32),
        ((N, C), F32),
        ((N, 1), F32),
        ((N, C), BF16),
        ((8, m.FL), F32),
        ((8, 128), F32),
        ((8, C), F32),
    ]
    far_out = [
        ((m.D, m.R, N, C), BF16),
        ((m.D, m.R) + mapped.shape, BF16),
        ((m.D, m.R, N, C), BF16),
        ((m.G,) + qkv_rows.shape, BF16),
    ]
    if m.even:
        far_out.append(((m.G,) + proj_part.shape, BF16))
    scratch = (
        [pltpu.VMEM((m.T, 8, 128), F32)]
        + reduce_buffers(m, N, C)
        + [pltpu.VMEM((N, C), F32), pltpu.VMEM((8, m.FL), F32)]
    )
    return fused_kernel(
        3,
        "branch",
        common_greet,
        act,
        near,
        loads,
        far,
        near_out,
        far_out,
        scratch,
        (m.T - 1) + 2 * (m.G - 1) + 3 * gather_sems(m) + reduce_sems(m),
        5,
    )


def attended_kernel(m, two_part, text_part, result_part, cot, gres, hat, inv, after, mods, keep, vec, grad_qkv, grad_proj):
    near = [inv, mods, keep]
    loads = [two_part, hat, after, cot, gres, text_part, result_part, vec]
    far = [grad_qkv] + ([grad_proj] if m.even else [])
    N, C = m.N, m.C
    texts = m.D * m.texts

    def act(p, flow, near, loads, far, near_out, far_out, scratch):
        inv, mods, keep = near
        two_part, hat, after, cot, gres, text_part, result_part, vec = (load.get() for load in loads)
        output, grad_after, branch, gm, vecg, text = near_out
        gb_all = far_out[0]
        two_sum, result_sum, text_sum = scratch[:3]
        two_red = LineReduce(flow, p, two_part, two_sum, *scratch[3:6])
        text_red = LineReduce(flow, p, text_part, text_sum, *scratch[6:9])
        result_red = LineReduce(flow, p, result_part, result_sum, *scratch[9:12])
        line = LineGather(flow, p, branch, gb_all)
        two_red.start()
        flow.swap_group(p, far[0], far_out[1])
        if m.even:
            flow.swap_group(p, far[1], far_out[2])
        two_red.steps_all()
        gm[...] = jnp.zeros_like(gm)
        vecg[...] = jnp.zeros_like(vecg)

        def back(rows):
            grad = cot[rows].astype(F32) + layer_back(two_sum[rows], hat[rows], inv[rows])
            gm[pl.ds(0, 1)] += jnp.sum(grad * after[rows], axis=0, keepdims=True)
            gm[pl.ds(1, 1)] += jnp.sum(grad, axis=0, keepdims=True)
            scaled = grad * (1.0 + mods[pl.ds(0, 1)])
            grad_after[rows] = scaled
            low = (keep[rows] * scaled).astype(BF16)
            branch[rows] = low
            vecg[pl.ds(0, 1)] += jnp.sum(low.astype(F32), axis=0, keepdims=True)
            vecg[pl.ds(1, 1)] += jnp.sum(gres[rows].astype(F32), axis=0, keepdims=True)

        chunks(N, back)
        line.start()
        flow.keep(branch, gb_all.at[p.c, p.z])
        text_red.start()
        result_red.start()
        for step in range(1, m.R):
            line.hop(step)
        text_red.steps_all()
        text[...] = text_sum[...].astype(BF16)
        result_red.steps_all()

        def out(rows):
            second = after[rows] * (1.0 + mods[pl.ds(0, 1)]) + mods[pl.ds(1, 1)]
            value = keep[rows] * (result_sum[rows] + vec[pl.ds(12, 1)])
            output[rows] = (second + value).astype(BF16)

        chunks(N, out)

    near_out = [
        ((N, C), BF16),
        ((N, C), F32),
        ((N, C), BF16),
        ((8, C), F32),
        ((8, C), F32),
        ((texts, m.HW), BF16),
    ]
    far_out = [((m.D, m.R, N, C), BF16), (grad_qkv.shape, BF16)]
    if m.even:
        far_out.append((grad_proj.shape, BF16))
    scratch = (
        [pltpu.VMEM((N, C), F32), pltpu.VMEM((N, C), F32), pltpu.VMEM((texts, m.HW), F32)]
        + reduce_buffers(m, N, C, False)
        + reduce_buffers(m, texts, m.HW, False)
        + reduce_buffers(m, N, C, False)
    )
    return fused_kernel(
        5,
        "attended",
        common_greet,
        act,
        near,
        loads,
        far,
        near_out,
        far_out,
        scratch,
        2 * (m.G - 1) + gather_sems(m) + 3 * reduce_sems(m),
        4,
    )


def text_back_kernel(m, silu, grad_mapped):
    def kernel(s_ref, g_ref, out, bias, weight):
        weight[...] = t_mm(s_ref[...], g_ref[...])
        out[...] = jnp.zeros_like(out)
        for g in range(m.G):
            for t in range(m.T):
                at = m.ms * (g * m.T + t)
                out[g, pl.ds(t * m.mp, m.ms)] = weight[pl.ds(at, m.ms)].astype(BF16)
        bias[...] = jnp.sum(g_ref[...].astype(F32), axis=0, keepdims=True)

    return local_kernel(
        "text_back",
        kernel,
        [silu, grad_mapped],
        [((m.G, m.T * m.mp, m.HW), BF16), ((1, m.HW), F32)],
        [pltpu.VMEM((silu.shape[1], m.HW), F32)],
    )


def back_kernel(m, gb_all, out_full, active, slope, grn_out, normed_all, in_full, norms, ratio, means, gain, key_keep,
                hat, inv, qkv_parts, proj_parts, grad_map):
    near = [norms, ratio, means, gain, key_keep]
    loads = [gb_all, out_full, active, grn_out, slope, normed_all, in_full, qkv_parts]
    loads += [proj_parts] if m.even else []
    far = [grad_map]
    N, C, FL, G = m.N, m.C, m.FL, m.G
    rows_in = C // G
    wide = C // m.Q
    per = m.pixels // N

    def act(p, flow, near, loads, far, near_out, far_out, scratch):
        norms, ratio, means, gain, keep = near
        (back,) = near_out
        out_parts, in_parts, f_parts, map_parts, qkv_team = far_out[:5]
        everyone, mine, moments, slopes, shifts, grads, hidden, part, mate, passed, landed = scratch[:11]
        g_out, g_in, f_own, qkv_own = scratch[11:15]
        flow.swap_group(p, far[0], map_parts)
        gb, out_w, active, grn = (load.get() for load in loads[:4])
        moments[...] = jnp.zeros_like(moments)

        @pl.loop(0, m.D * per)
        def _(number):
            rows = pl.ds(pl.multiple_of(number * N, 16), N)
            item = number // per
            grad = mm_t(gb[rows], out_w[...])
            grads[rows] = grad
            moments[pl.ds(item, 1)] += jnp.sum(grad * active[rows], axis=0, keepdims=True)
            moments[pl.ds(m.D, 1)] += jnp.sum(grad, axis=0, keepdims=True)

        scaled = moments[...] * gain[...]
        cross = jnp.sum(scaled * norms[...], axis=1, keepdims=True)
        mine[...] = jnp.broadcast_to(cross, mine.shape)
        add_up = team_sum(m, p, flow, mine, everyone)
        for g in range(G):
            g_out[g] = t_mm(grn[:, g * m.FFS : (g + 1) * m.FFS], gb[...]).astype(BF16)
        slope, x, in_w, qkv_parts = (load.get() for load in loads[4:8])
        step = m.cs

        def add_parts(parts, own, count):
            for t in range(count):
                rows = pl.ds(t * step, step)
                total = parts[0, rows].astype(F32)
                for g in range(1, G):
                    total = total + parts[g, rows].astype(F32)
                own[t] = total.astype(BF16)

        add_parts(qkv_parts, qkv_own, m.T)
        if m.even:
            proj_own = scratch[15]
            add_parts(loads[8].get(), proj_own, m.R)
        flow.swap_group(p, g_out, out_parts)
        mean = means[...][:, :1]
        cross = add_up()[:, :1]
        slopes[...] = gain[...] * ratio[...] + 1.0
        shifts[...] = (scaled / mean - cross / (m.FF * mean * mean)) / norms[...]
        gains = jnp.sum(moments[pl.ds(0, m.D)] * ratio[pl.ds(0, m.D)], axis=0, keepdims=True)
        biases = moments[pl.ds(m.D, 1)]
        moments[pl.ds(m.D + 1, 1)] = jnp.zeros((1, FL), F32)
        flow.swap_team(p, qkv_own, qkv_team)
        if m.even:
            for number in range(G):
                to = lax.rem(p.q + number, G)
                flow.post(
                    proj_own.at[to],
                    far_out[5].at[p.q],
                    {"grp": p.z, "duo": p.c, "rows": to},
                    when=None if number else p.q != p.z,
                )
            flow.keep(proj_own.at[p.z], far_out[5].at[p.q], p.q == p.z)

        @pl.loop(0, m.D * per)
        def _(number):
            rows = pl.ds(pl.multiple_of(number * N, 16), N)
            item = number // per
            inside = pl.ds(pl.multiple_of((number - item * per) * N, 16), N)
            one = pl.ds(item, 1)
            grad = grads[rows] * slopes[one] + keep[item, inside] * (active[rows] * shifts[one])
            low = (grad * slope[rows]).astype(BF16)
            hidden[rows] = low
            moments[pl.ds(m.D + 1, 1)] += jnp.sum(low.astype(F32), axis=0, keepdims=True)

        inner = moments[pl.ds(m.D + 1, 1)]
        f_own[...] = jnp.zeros_like(f_own)
        for g in range(G):
            lanes = slice(g * m.FFS, (g + 1) * m.FFS)
            for row, values in enumerate((inner, gains, biases)):
                f_own[g, pl.ds(row, 1)] = values[:, lanes]
        flow.swap_group(p, f_own, f_parts)
        line = LineReduce(flow, p, part, back, mate, passed, landed)

        def produce(block):
            for d in range(m.D):
                rows = pl.ds(pl.multiple_of(d * m.pixels + block * N, 16), N)
                part[d, block] = mm_t(hidden[rows], in_w[...]).astype(BF16)

        def between(number):
            if number < G:
                g = lax.rem(p.q + 1 + number, G)
                lanes = pl.ds(pl.multiple_of(g * rows_in, 128), rows_in)
                g_in[g] = t_mm(x[:, lanes], hidden[...]).astype(BF16)
                if number < G - 1:
                    flow.post(g_in.at[g], in_parts.at[p.q], {"grp": g})
                else:
                    flow.keep(g_in.at[p.q], in_parts.at[p.q])

        line.run(produce, between)

    near_out = [((N, C), F32)]
    far_out = [
        ((G, m.FFS, C), BF16),
        ((G, rows_in, FL), BF16),
        ((G, 8, m.FFS), F32),
        (grad_map.shape, BF16),
        ((m.T, m.cs, 3 * m.HW), BF16),
    ]
    scratch = [
        pltpu.VMEM((m.T, 8, 128), F32),
        pltpu.VMEM((8, 128), F32),
        pltpu.VMEM((8, FL), F32),
        pltpu.VMEM((8, FL), F32),
        pltpu.VMEM((8, FL), F32),
        pltpu.VMEM((m.D * m.pixels, FL), F32),
        pltpu.VMEM((m.D * m.pixels, FL), BF16),
    ]
    scratch += reduce_buffers(m, N, C)
    scratch += [
        pltpu.VMEM((G, m.FFS, C), BF16),
        pltpu.VMEM((G, rows_in, FL), BF16),
        pltpu.VMEM((G, 8, m.FFS), F32),
        pltpu.VMEM((m.T, m.cs, 3 * m.HW), BF16),
    ]
    if m.even:
        far_out.append(((G, m.cs, wide), BF16))
        scratch.append(pltpu.VMEM((m.R, m.cs, wide), BF16))
    return fused_kernel(
        9,
        "feed_forward_back",
        lambda p: common_greet(p) + (spread_greet(m, p) if m.even else []),
        act,
        near,
        loads,
        far,
        near_out,
        far_out,
        scratch,
        2 * (m.T - 1) + 4 * (G - 1) + reduce_sems(m) + (G if m.even else 0),
        7,
    )


def pad_rows(values, rows):
    return jnp.pad(values, ((0, rows - values.shape[0]),) + ((0, 0),) * (values.ndim - 1))


def body(
    latents,
    clip_tokens,
    time_embed,
    bucket_ids,
    heights,
    widths,
    text_mask,
    conv_weight,
    conv_bias,
    in_weight,
    in_bias,
    grn_gain,
    grn_bias,
    out_weight,
    out_bias,
    time_weight,
    time_bias,
    map_weight,
    map_bias,
    qkv_weight,
    qv_bias,
    proj_weight,
    proj_bias,
    cotangent,
):
    m = Sizes(latents, clip_tokens, in_weight, in_bias, conv_bias, map_weight)
    G, D, R, T, N, C = m.G, m.D, m.R, m.T, m.N, m.C
    pixels, texts, FFS, FL, FF, HW = m.pixels, m.texts, m.FFS, m.FL, m.FF, m.HW
    cs, ms, mp, sp, even, Q = m.cs, m.ms, m.mp, m.sp, m.even, m.Q
    q, c, z = (lax.axis_index(axis) for axis in AXES)
    head_slice = D * z + c

    vectors = [conv_bias, out_bias, map_bias, proj_bias, qv_bias]
    fvectors = [in_bias, grn_gain, grn_bias]
    in_cut, qkv_cut, map_cut, clip_pad, masked, grad_result, small, fvec = cut_kernel(
        m,
        [heights, widths, bucket_ids, in_weight, qkv_weight, map_weight, clip_tokens, latents]
        + [cotangent, conv_weight]
        + [vector[None] for vector in vectors]
        + [time_embed, text_mask]
        + [vector[None] for vector in fvectors],
    )
    latents = latents[0]
    cotangent = cotangent[0]

    def swap_edges(plan, src, dst):
        p = plan.p
        for block, to, sends, lands in (
            (src.at[pl.ds(src.shape[0] - EDGE, EDGE)], p.z + 1, p.z < R - 1, p.z > 0),
            (src.at[pl.ds(0, EDGE)], p.z - 1, p.z > 0, p.z < R - 1),
        ):
            slot = jnp.where(to > p.z, 0, 1)
            plan.add(block, dst.at[slot], {"rows": to}, when=sends, lands=lands)

    def plan_start(p, ins, outs):
        plan = Plan(p)
        plan.group_gather(ins[1], outs[1])
        swap_edges(plan, ins[0], outs[0])
        plan.team_swap(ins[2], outs[2])
        plan.group_gather(ins[3], outs[3])
        plan.team_swap(ins[4], outs[4])
        return plan.done()

    edges, _, in_rows, fvec_all, map_rows, small_all, clip_all = team_kernel(
        0,
        "exchange_start",
        plan_start,
        [masked, small, in_cut, fvec, map_cut],
        [
            ((2, EDGE, C), BF16),
            ((G, SMALL, 128), BF16),
            ((T, cs, FL), BF16),
            ((G, 16, FFS), BF16),
            ((T, mp, HW), BF16),
        ],
        gathers=[clip_pad],
        messages=2 + 2 * (G - 1) + 2 * (T - 1),
        local=4,
        late=(1, 0, G - 1),
    )
    normed, norm_hat, norm_inv, vec, mod_part, key_keep, keep = conv_kernel(
        m, bucket_ids, edges, masked, small_all, time_weight, time_bias[None]
    )
    in_bias_s, gain_s, grn_bias_s = (
        fvec_all[:, row].reshape(1, FL).astype(F32) for row in range(3)
    )

    def plan_first(p, ins, outs):
        plan = Plan(p)
        plan.group_gather(ins[4], outs[4])
        plan.group_gather(ins[0], outs[0], late=1)
        plan.group_gather(ins[1], outs[1], late=2)
        plan.team_swap(ins[2], outs[2])
        plan.group_gather(ins[3], outs[3])
        if even:
            wide = C // G
            for step in range(G):
                to = lax.rem(p.z + step, G)
                when = None if step else p.q != p.z
                piece = ins[5].at[:, pl.ds(pl.multiple_of(to * wide, 128), wide)]
                plan.add(
                    piece, outs[5].at[p.z], {"grp": to, "duo": p.c, "rows": p.q}, when=when
                )
                source = {"grp": p.z, "duo": p.c, "rows": lax.rem(p.q - step + G, G)}
                plan.greet.append((source, when))
            piece = ins[5].at[:, pl.ds(pl.multiple_of(p.z * wide, 128), wide)]
            plan.local.append((piece, outs[5].at[p.z], p.q == p.z))
        return plan.done()

    group_count = 4 if G == 4 else G - 1
    arrays = [in_rows.reshape(T * cs, FL), out_weight, qkv_cut, map_rows.reshape(T * mp, HW)]
    arrays.append(mod_part)
    results = [
        ((G, T * cs, FL), BF16),
        ((G,) + out_weight.shape, BF16),
        ((T, cs, 3 * HW), BF16),
        ((G, T * mp, HW), BF16),
        ((G,) + mod_part.shape, F32),
    ]
    if even:
        arrays.append(proj_weight)
        results.append(((R, cs, C // G), BF16))
    gathered = team_kernel(
        1,
        "exchange_normed",
        plan_first,
        arrays,
        results,
        gathers=[normed],
        messages=2 * group_count + (T - 1) + 2 * (G - 1) + (G if even else 0),
        local=5 + (1 if even else 0),
        late=(4, 1, G - 1),
    )
    in_full, out_full, qkv_rows, map_full = gathered[:4]
    proj_part = gathered[5].reshape(HW, C // G) if even else None
    mod_all, normed_all = gathered[-2:]
    normed_all = normed_all.reshape(D * pixels, C)
    in_full = in_full.reshape(C, FL)
    out_full = out_full.reshape(FL, C)
    active, slope, norms, total, silu, mapped_s = up_kernel(
        m,
        normed_all,
        in_full,
        in_bias_s,
        key_keep,
        clip_all.reshape(T, sp, -1),
        map_full,
        vec,
    )
    outs = branch_kernel(
        m,
        active,
        norms,
        total,
        out_full,
        gain_s,
        grn_bias_s,
        latents,
        keep,
        vec,
        mod_all,
        qkv_rows.reshape(T * cs, 3 * HW),
        mapped_s,
        grad_result,
        proj_part,
    )
    grn_out, after_res, two_hat, two_inv, _, ratio, means, mods, two_all, mapped, gres_all = outs[:11]
    qkv_full = outs[11].reshape(C, 3 * HW)
    if even:
        proj_s = outs[12]
    else:
        proj_whole = lax.all_gather(proj_weight, AXES, axis=0, tiled=True)
        proj_s = lax.dynamic_slice_in_dim(proj_whole, head_slice * HW, HW, axis=0)[None]
    q_bias = lax.dynamic_slice_in_dim(vec[13], head_slice * HW, HW)
    v_bias = lax.dynamic_slice_in_dim(vec[14], head_slice * HW, HW)
    bias = jnp.concatenate([q_bias, jnp.zeros_like(q_bias), v_bias])[None]
    result_part, two_part, mapped_part, grad_qkv, grad_proj, qkv_bias_grad = attention_kernel(
        m,
        two_all.reshape(D, pixels, C),
        gres_all.reshape(D, pixels, C),
        mapped.reshape(T, D * texts, HW),
        qkv_full,
        proj_s,
        bias,
        key_keep,
    )
    outs = attended_kernel(
        m,
        two_part.reshape(D, R, N, C),
        mapped_part.reshape(D, R, D * texts, HW),
        result_part.reshape(D, R, N, C),
        cotangent,
        grad_result,
        two_hat,
        two_inv,
        after_res,
        mods,
        keep,
        vec,
        grad_qkv.reshape(G, T * cs, 3 * HW),
        grad_proj,
    )
    output, grad_after, _, grad_modulate, vec_sums, grad_mapped, gb_all, qkv_parts = outs[:8]
    if even:
        proj_parts = outs[8]
    else:
        proj_parts = None
        spread = jnp.zeros((C, C), F32)
        spread = lax.dynamic_update_slice_in_dim(
            spread, grad_proj[0].astype(F32), head_slice * HW, axis=0
        )
        proj_team = lax.psum_scatter(spread, AXES, scatter_dimension=0, tiled=True)[None]
    grad_map, map_bias_grad = text_back_kernel(m, silu, grad_mapped)
    outs = back_kernel(
        m,
        gb_all.reshape(D * pixels, C),
        out_full,
        active,
        slope,
        grn_out,
        normed_all,
        in_full,
        norms,
        ratio,
        means,
        gain_s,
        key_keep,
        norm_hat,
        norm_inv,
        qkv_parts,
        proj_parts,
        grad_map,
    )
    grad_conv_in, out_sum, in_sum, f_sum, map_sum, qkv_team = outs[:6]
    if even:
        proj_team = outs[6]
    grad_out_shard = jnp.sum(out_sum.astype(F32), axis=0)
    in_back = jnp.sum(in_sum.astype(F32), axis=0).astype(BF16).reshape(T, cs, FL)
    map_back = jnp.sum(map_sum.astype(F32), axis=0).astype(BF16).reshape(T, mp, HW)

    def placed(values, start):
        return lax.dynamic_update_slice_in_dim(jnp.zeros((C,), F32), values, start, axis=0)

    vec_grads = jnp.concatenate(
        [vec_sums[:2], placed(map_bias_grad[0], (c * R + z) * HW)[None]], axis=0
    )
    qv_grads = jnp.stack(
        [
            placed(qkv_bias_grad[0, :HW], head_slice * HW),
            placed(qkv_bias_grad[0, 2 * HW :], head_slice * HW),
        ]
    )
    grad_conv, conv_low, tiny = conv_back_kernel(
        m,
        bucket_ids,
        grad_conv_in,
        norm_hat,
        norm_inv,
        edges,
        masked,
        vec_grads,
        qv_grads,
        grad_modulate,
    )
    trows = 16

    def plan_fifth(p, ins, outs):
        plan = Plan(p)
        swap_edges(plan, ins[0], outs[0])
        plan.team_swap(ins[1], outs[1])
        plan.team_swap(ins[2], outs[2])
        plan.team_swap(ins[3], outs[3])
        return plan.done()

    conv_edges, tiny_team, in_team, map_team = team_kernel(
        11,
        "exchange_tail",
        plan_fifth,
        [conv_low, tiny, in_back, map_back],
        [((2, EDGE, C), BF16), (tiny.shape, F32), (in_back.shape, BF16), (map_back.shape, BF16)],
        messages=2 + 3 * (T - 1),
        local=3,
    )
    tiny_items = jnp.sum(tiny_team.reshape(D, R, G, trows, 128), axis=1).transpose(1, 0, 2, 3)

    def plan_sixth(p, ins, outs):
        plan = Plan(p)
        plan.group_swap(ins[0], outs[0])
        return group_greet(p), plan.messages, plan.local

    (tiny_all,) = team_kernel(
        12,
        "exchange_tiny",
        plan_sixth,
        [tiny_items],
        [((G, D, trows, 128), F32)],
        messages=G - 1,
    )
    tiny_all = tiny_all.reshape(G * D, trows, 128)
    tiny_sum = jnp.sum(tiny_all, axis=0)
    modulate_items = tiny_all[:, 14, : 2 * cs]
    embed_all = small_all.reshape(D, R, G, SMALL, 128)[:, 0, :, 14, : time_embed.shape[1]]
    embed_all = embed_all.transpose(1, 0, 2).reshape(G * D, -1)
    grad_time = lax.dot_general(
        embed_all.astype(F32),
        modulate_items,
        (((0,), (0,)), ((), ())),
        precision=lax.Precision.HIGHEST,
    )
    grad_time_bias = jnp.sum(modulate_items, axis=0)
    grad_latents, grad_in_shard, grad_qkv_shard, grad_map_shard, grad_proj_shard = finish_kernel(
        m,
        bucket_ids,
        conv_edges,
        conv_low,
        grad_after,
        keep,
        vec,
        in_team,
        qkv_team,
        map_team,
        proj_team,
    )
    f_total = jnp.sum(f_sum, axis=0)
    return (
        output[None],
        grad_latents,
        tiny_sum[:9, :cs],
        tiny_sum[9, :cs],
        grad_in_shard,
        f_total[0],
        f_total[1],
        f_total[2],
        grad_out_shard,
        tiny_sum[10, :cs],
        grad_time,
        grad_time_bias,
        grad_map_shard,
        tiny_sum[12, :cs],
        grad_qkv_shard,
        tiny_sum[13, : 2 * cs],
        grad_proj_shard,
        tiny_sum[11, :cs],
    )


def solution(mesh):
    items, rows = mesh.devices.shape
    fine = Mesh(mesh.devices.reshape(items // 2, 2, rows), AXES)
    item = ("grp", "duo")
    full = AXES
    ins = (
        P(item, "rows", None),
        P(item, "rows", None),
        P(item, None),
        P(item),
        P(item),
        P(item),
        P(item, None),
        P(None, full),
        P(full),
        P(full, None),
        P(full),
        P(full),
        P(full),
        P(full, None),
        P(full),
        P(None, full),
        P(full),
        P(full, None),
        P(full),
        P(full, None),
        P(full),
        P(full, None),
        P(full),
        P(item, "rows", None),
    )
    outs = (
        P(item, "rows", None),
        P(item, "rows", None),
        P(None, full),
        P(full),
        P(full, None),
        P(full),
        P(full),
        P(full),
        P(full, None),
        P(full),
        P(None, full),
        P(full),
        P(full, None),
        P(full),
        P(full, None),
        P(full),
        P(full, None),
        P(full),
    )
    return jax.shard_map(body, mesh=fine, in_specs=ins, out_specs=outs, check_vma=False)
```

```python
import functools

import jax
import jax.numpy as jnp
from jax import lax
from jax.experimental import pallas as pl
from jax.experimental.pallas import tpu as pltpu
from jax.sharding import Mesh, PartitionSpec as P

HEAD = 64
TXT = 77
UNIT = 8
EDGE = 48

norm_eps = 1e-06
grn_eps = 1e-06
masked_score = -1000000000.0

AXES = ("grp", "duo", "rows")
MESH_ID = pl.DeviceIdType.MESH
F32 = jnp.float32
BF16 = jnp.bfloat16


class Place:
    def __init__(self):
        self.q, self.c, self.z = (lax.axis_index(axis) for axis in AXES)
        self.G, self.D, self.R = (lax.axis_size(axis) for axis in AXES)

    def team(self):
        for step in range(1, self.D * self.R):
            dc, dz = step // self.R, step % self.R
            yield lax.rem(self.c + dc, self.D), lax.rem(self.z + dz, self.R)

    def groups(self):
        for step in range(1, self.G):
            yield lax.rem(self.q + step, self.G)


def signal_all(barrier, targets):
    for target in targets:
        pl.semaphore_signal(barrier, inc=1, device_id=target, device_id_type=MESH_ID)


def guarded(when, act):
    if when is None:
        act()
    else:
        pl.when(when)(act)


class Flow:
    def __init__(self, send_sem, recv_sem, local_sem=None):
        self.send_sem, self.recv_sem, self.local_sem = send_sem, recv_sem, local_sem
        self.used = 0
        self.kept = 0
        self.open = []
        self.posted = []
        self.lines = []
        self.stays = []

    def take(self, count=1):
        at = self.used
        self.used += count
        return at

    def copy(self, src, dst, target, at):
        return pltpu.make_async_remote_copy(
            src_ref=src,
            dst_ref=dst,
            send_sem=self.send_sem.at[at],
            recv_sem=self.recv_sem.at[at],
            device_id=target,
            device_id_type=MESH_ID,
        )

    def post(self, src, dst, target, when=None, lands=None):
        copy = self.copy(src, dst, target, self.take())
        guarded(when, copy.start)
        item = Posted(copy, when if lands is None else lands)
        self.posted.append(item)
        self.open.append((copy.wait_send, when))
        return item

    def land(self, item):
        if not item.landed:
            item.landed = True
            guarded(item.lands, item.copy.wait_recv)

    def keep(self, src, dst, when=None, now=False):
        copy = pltpu.make_async_copy(src, dst, self.local_sem.at[self.kept])
        self.kept += 1
        guarded(when, copy.start)
        if now:
            guarded(when, copy.wait)
        else:
            self.stays.append((copy.wait, when))

    def square(self, p, src, dst):
        across = p.q + 1 - 2 * lax.rem(p.q, 2)
        along = lax.rem(p.q + 2, 4)
        one = self.post(src, dst.at[p.q], {"grp": across})
        two = self.post(src, dst.at[p.q], {"grp": along})
        half = dst.shape[1] // 2
        top, bottom = pl.ds(0, half), pl.ds(half, half)

        def relay():
            self.land(one)
            block = dst.at[across, top]
            first = self.post(block, block, {"grp": along})
            self.land(two)
            block = dst.at[along, bottom]
            second = self.post(block, block, {"grp": across})
            return first, second

        return relay

    def settle_kept(self):
        for act, when in self.stays:
            guarded(when, act)
        self.stays = []

    def gather_team(self, p, src, dst):
        mine = p.c * p.R + p.z
        self.keep(src, dst.at[mine])
        return [self.post(src, dst.at[mine], {"duo": c, "rows": z}) for c, z in p.team()]

    def gather_group(self, p, src, dst):
        self.keep(src, dst.at[p.q])
        return [self.post(src, dst.at[p.q], {"grp": q}) for q in p.groups()]

    def swap_group(self, p, src, dst):
        self.keep(src.at[p.q], dst.at[p.q])
        for q in p.groups():
            self.post(src.at[q], dst.at[p.q], {"grp": q})

    def swap_team(self, p, src, dst):
        mine = p.c * p.R + p.z
        self.keep(src.at[mine], dst.at[mine])
        return [
            self.post(src.at[c * p.R + z], dst.at[mine], {"duo": c, "rows": z}) for c, z in p.team()
        ]

    def finish(self):
        self.settle_kept()
        for line in self.lines:
            line.settle(line.p.R)
        for item in self.posted:
            self.land(item)
        for act, when in self.open:
            guarded(when, act)


class LineGather:
    def __init__(self, flow, place, src, dst):
        self.flow, self.p, self.src, self.dst = flow, place, src, dst
        self.up = flow.take(place.R - 1)
        self.down = flow.take(place.R - 1)
        self.side = flow.take(2 * place.R - 1)

    def send(self, block, hop, direction):
        p, dst = self.p, self.dst
        src = self.src if hop == 0 else dst.at[p.c, block]
        at = (self.up if direction > 0 else self.down) + hop
        return self.flow.copy(src, dst.at[p.c, block], {"rows": p.z + direction}, at)

    def across(self, block, number):
        p, dst = self.p, self.dst
        src = self.src if isinstance(number, int) and number == 0 else dst.at[p.c, block]
        other = {"duo": lax.rem(p.c + 1, p.D)}
        return self.flow.copy(src, dst.at[p.c, block], other, self.side + number)

    def start(self):
        p = self.p
        for direction, ok in ((1, p.z < p.R - 1), (-1, p.z > 0)):
            copy = self.send(p.z, 0, direction)
            guarded(ok, copy.start)
            self.flow.open.append((copy.wait_send, ok))
        copy = self.across(p.z, 0)
        copy.start()
        self.flow.open.append((copy.wait_send, None))
        self.flow.lines.append(self)
        self.settled = 0

    def hop(self, step):
        p = self.p
        for direction, number in ((1, step), (-1, p.R - 1 + step)):
            block = p.z - direction * step
            ok = (block >= 0) if direction > 0 else (block < p.R)
            last = (p.z < p.R - 1) if direction > 0 else (p.z > 0)
            arrived = self.send(block, step - 1, direction)
            side = self.across(block, number)

            def relay(arrived=arrived, side=side, block=block, direction=direction, last=last):
                arrived.wait_recv()
                if step < p.R - 1:
                    pl.when(last)(self.send(block, step, direction).start)
                side.start()

            pl.when(ok)(relay)
            if step < p.R - 1:
                self.flow.open.append((self.send(block, step, direction).wait_send, ok & last))
            self.flow.open.append((side.wait_send, ok))


    def nth(self, number):
        p = self.p
        reach = [p.z]
        for step in range(1, p.R):
            reach += [p.z - step, p.z + step]
        seen, found = 0, jnp.int32(0)
        for block in reach:
            ok = (block >= 0) & (block < p.R)
            found = jnp.where(ok & (seen == number), block, found)
            seen = seen + jnp.where(ok, 1, 0)
        return found

    def settle(self, upto):
        p = self.p
        while self.settled < upto:
            block = self.nth(self.settled)
            number = jnp.where(block <= p.z, p.z - block, p.R - 1 + block - p.z)
            self.across(block, number).wait_recv()
            self.settled += 1


class LineReduce:
    def __init__(self, flow, place, part, total_ref, mate, passed, landed):
        self.flow, self.p, self.part, self.total = flow, place, part, total_ref
        self.mate, self.passed, self.landed = mate, passed, landed
        self.side = flow.take(place.R)
        self.line = flow.take(2 * place.R)

    def across(self, block):
        p = self.p
        other = lax.rem(p.c + 1, p.D)
        return self.flow.copy(
            self.part.at[other, block], self.mate.at[block], {"duo": other}, self.side + block
        )

    def along(self, upward, block):
        p = self.p
        way = jnp.where(upward, 1, 0)
        target = {"rows": jnp.where(upward, p.z + 1, p.z - 1)}
        return self.flow.copy(
            self.passed.at[way, block],
            self.landed.at[way, block],
            target,
            self.line + way * p.R + block,
        )

    def steps(self):
        p = self.p
        low = p.z < p.R // 2
        for k in range(p.R - 1):
            for first in (True, False):
                upward = low if first else jnp.logical_not(low)
                block = jnp.where(upward, p.R - 1 - k, k)
                yield upward, block, jnp.where(upward, block > p.z, block < p.z)

    def start(self):
        p = self.p
        for k in range(p.R):
            block = jnp.where(p.z < p.R // 2, p.R - 1 - k, k)
            copy = self.across(block)
            copy.start()
            self.flow.open.append((copy.wait_send, None))

    def rows_of(self, act):
        count = self.part.shape[2]
        step = 16

        @pl.loop(0, count // step)
        def _(number):
            act(pl.ds(pl.multiple_of(number * step, step), step))

    def early(self):
        for upward, block, ok in self.steps():
            behind = jnp.where(upward, self.p.z > 0, self.p.z < self.p.R - 1)
            self.step(upward, block, ok & jnp.logical_not(behind), False)

    def later(self):
        for upward, block, ok in self.steps():
            behind = jnp.where(upward, self.p.z > 0, self.p.z < self.p.R - 1)
            yield functools.partial(self.step, upward, block, ok & behind, True)

    def step(self, upward, block, ok, relays=None):
        p = self.p
        way = jnp.where(upward, 1, 0)
        behind = jnp.where(upward, p.z > 0, p.z < p.R - 1)

        def act():
            self.across(block).wait_recv()
            if relays is False:

                def add(rows):
                    self.passed[way, block, rows] = (
                        self.part[p.c, block, rows].astype(F32) + self.mate[block, rows].astype(F32)
                    ).astype(BF16)

                self.rows_of(add)
                self.along(upward, block).start()
                return

            @pl.when(behind)
            def _():
                self.along(upward, block).wait_recv()

                def add(rows):
                    self.passed[way, block, rows] = (
                        self.part[p.c, block, rows].astype(F32)
                        + self.mate[block, rows].astype(F32)
                        + self.landed[way, block, rows].astype(F32)
                    ).astype(BF16)

                self.rows_of(add)

            if relays is None:

                @pl.when(jnp.logical_not(behind))
                def _():
                    def add(rows):
                        self.passed[way, block, rows] = (
                            self.part[p.c, block, rows].astype(F32)
                            + self.mate[block, rows].astype(F32)
                        ).astype(BF16)

                    self.rows_of(add)

            self.along(upward, block).start()

        pl.when(ok)(act)
        self.flow.open.append((self.along(upward, block).wait_send, ok))

    def close(self):
        p = self.p
        self.across(p.z).wait_recv()

        def base(rows):
            self.total[rows] = self.part[p.c, p.z, rows].astype(F32) + self.mate[
                p.z, rows
            ].astype(F32)

        self.rows_of(base)
        for way, ok in ((1, p.z > 0), (0, p.z < p.R - 1)):

            def more(way=way):
                self.along(way == 1, p.z).wait_recv()

                def add(rows):
                    self.total[rows] += self.landed[way, p.z, rows].astype(F32)

                self.rows_of(add)

            pl.when(ok)(more)

    def steps_all(self):
        self.early()
        for act in self.later():
            act()
        self.close()

    def run(self, produce=None, between=None):
        p = self.p
        if produce is None:
            self.steps_all()
            return
        ready = 0

        def more():
            block = line_order(p, ready)
            produce(block)
            copy = self.across(block)
            copy.start()
            self.flow.open.append((copy.wait_send, None))

        for number, (upward, block, ok) in enumerate(self.steps()):
            while ready < min(number + 2, p.R):
                more()
                ready += 1
            self.step(upward, block, ok)
            if between is not None:
                between(number)
        self.close()


def team_kernel(
    ident, name, plan, arrays, results, gathers=(), reduces=(), messages=0, local=1, late=None
):
    D, R = lax.axis_size("duo"), lax.axis_size("rows")
    count_a, count_g, count_r = len(arrays), len(gathers), len(reduces)
    extra = 0 if late is None else 1
    total_sems = messages + (count_g + extra) * (4 * R - 3) + count_r * 3 * R

    def kernel(*refs):
        refs = list(refs)
        ins = refs[:count_a]
        g_in = refs[count_a : count_a + count_g]
        r_in = refs[count_a + count_g : count_a + count_g + count_r]
        refs = refs[count_a + count_g + count_r :]
        outs = refs[: len(results)]
        refs = refs[len(results) :]
        late_out = refs[:extra]
        g_out = refs[extra : extra + count_g]
        r_out = refs[extra + count_g : extra + count_g + count_r]
        refs = refs[extra + count_g + count_r :]
        send_sem, recv_sem, local_sem = refs[:3]
        buffers = refs[3:]
        p = Place()
        flow = Flow(send_sem, recv_sem)
        greet, direct, stay = plan(p, ins, outs)
        barrier = pltpu.get_barrier_semaphore()
        waits = 0
        for target, when in greet:
            if when is None:
                waits = waits + 1
            else:
                waits = waits + jnp.where(when, 1, 0).astype(jnp.int32)
            guarded(when, lambda target=target: signal_all(barrier, [target]))
        pl.semaphore_wait(barrier, waits)
        lines = [LineGather(flow, p, src, dst) for src, dst in zip(g_in, g_out)]
        sums = [
            LineReduce(flow, p, src, dst, *buffers[3 * n : 3 * n + 3])
            for n, (src, dst) in enumerate(zip(r_in, r_out))
        ]
        base = flow.take(messages)
        copies = {}
        arrived = set()

        stays = []

        def landed(number):
            if number not in arrived:
                arrived.add(number)
                guarded(copies[number][2], copies[number][0].wait_recv)

        def run_stage(stage):
            for number, (src, dst, target, after, when, when_stage, lands) in enumerate(direct):
                if when_stage != stage:
                    continue
                for earlier in after:
                    landed(earlier)
                copy = flow.copy(src, dst, target, base + number)
                guarded(when, copy.start)
                copies[number] = (copy, when, lands)
            if late is not None and late[1] == stage:
                for number in range(late[2]):
                    landed(number)
                stays[0][0].wait()
                line = LineGather(flow, p, outs[late[0]], late_out[0])
                line.start()
                own = pltpu.make_async_copy(
                    outs[late[0]], late_out[0].at[p.c, p.z], local_sem.at[local + count_g]
                )
                own.start()
                stays[0] = (own, None)
                if stage:
                    for earlier in range(1, stage + 1):
                        line.hop(earlier)
                lines.append(line)

        for item in sums:
            item.start()
        for line in lines:
            line.start()
        for number, (src, dst, when) in enumerate(
            list(stay) + [(src, dst.at[p.c, p.z], None) for src, dst in zip(g_in, g_out)]
        ):
            copy = pltpu.make_async_copy(src, dst, local_sem.at[number])
            guarded(when, copy.start)
            stays.append((copy, when))
        run_stage(0)
        for step in range(1, R):
            for line in lines:
                line.hop(step)
            run_stage(step)
        for item in sums:
            item.run()
        for copy, when in stays:
            guarded(when, copy.wait)
        for number in copies:
            landed(number)
        for copy, when, _ in copies.values():
            guarded(when, copy.wait_send)
        flow.finish()

    spot = pl.BlockSpec(memory_space=pl.ANY)
    near = pl.BlockSpec(memory_space=pltpu.VMEM)
    out_shape = [jax.ShapeDtypeStruct(shape, kind) for shape, kind in results]
    if late is not None:
        shape, kind = results[late[0]]
        out_shape.append(jax.ShapeDtypeStruct((D, R) + shape, kind))
    out_shape += [jax.ShapeDtypeStruct((D, R) + g.shape, g.dtype) for g in gathers]
    out_shape += [jax.ShapeDtypeStruct(r.shape[2:], F32) for r in reduces]
    scratch = [
        pltpu.SemaphoreType.DMA((total_sems,)),
        pltpu.SemaphoreType.DMA((total_sems,)),
        pltpu.SemaphoreType.DMA((local + count_g + extra,)),
    ]
    for r in reduces:
        block = r.shape[1:]
        scratch += [
            pltpu.VMEM(block, BF16),
            pltpu.VMEM((2,) + block, BF16),
            pltpu.VMEM((2,) + block, BF16),
        ]
    return pl.pallas_call(
        kernel,
        out_shape=out_shape,
        in_specs=[spot] * (count_a + count_g) + [near] * count_r,
        out_specs=[spot] * (len(results) + extra + count_g) + [near] * count_r,
        scratch_shapes=scratch,
        compiler_params=pltpu.CompilerParams(
            collective_id=ident, has_side_effects=True, vmem_limit_bytes=56 * 2**20
        ),
        name=name,
    )(*arrays, *gathers, *reduces)


def team_greet(p):
    return [({"duo": c, "rows": z}, None) for c, z in p.team()]


def group_greet(p):
    return [({"grp": q}, None) for q in p.groups()]


class Plan:
    def __init__(self, p):
        self.p = p
        self.messages, self.local, self.greet = [], [], []

    def add(self, src, dst, target, after=(), when=None, stage=0, lands=None):
        self.messages.append((src, dst, target, after, when, stage, when if lands is None else lands))
        return len(self.messages) - 1

    def team_swap(self, src, dst, stage=0):
        p = self.p
        mine = p.c * p.R + p.z
        for c, z in p.team():
            self.add(src.at[c * p.R + z], dst.at[mine], {"duo": c, "rows": z}, stage=stage)
        self.local.append((src.at[mine], dst.at[mine], None))

    def team_gather(self, src, dst, stage=0):
        p = self.p
        mine = p.c * p.R + p.z
        for c, z in p.team():
            self.add(src, dst.at[mine], {"duo": c, "rows": z}, stage=stage)
        self.local.append((src, dst.at[mine], None))

    def group_gather(self, src, dst, late=None):
        p = self.p
        self.local.append((src, dst.at[p.q], None))
        if late is None or p.G != 4:
            for q in p.groups():
                self.add(src, dst.at[p.q], {"grp": q})
            return
        across = p.q + 1 - 2 * lax.rem(p.q, 2)
        along = lax.rem(p.q + 2, 4)
        one = self.add(src, dst.at[p.q], {"grp": across})
        two = self.add(src, dst.at[p.q], {"grp": along})
        half = src.shape[0] // 2
        top, bottom = pl.ds(0, half), pl.ds(half, half)
        self.add(
            dst.at[across, top], dst.at[across, top], {"grp": along}, after=(one,), stage=late
        )
        self.add(
            dst.at[along, bottom],
            dst.at[along, bottom],
            {"grp": across},
            after=(two,),
            stage=late,
        )

    def group_swap(self, src, dst, stage=0):
        p = self.p
        for q in p.groups():
            self.add(src.at[q], dst.at[p.q], {"grp": q}, stage=stage)
        self.local.append((src.at[p.q], dst.at[p.q], None))

    def done(self):
        p = self.p
        return team_greet(p) + group_greet(p) + self.greet, self.messages, self.local


def layer_stats(values):
    center = values - jnp.mean(values, axis=-1, keepdims=True)
    spread = jnp.mean(center * center, axis=-1, keepdims=True)
    inverse = lax.rsqrt(spread + norm_eps)
    return center * inverse, inverse


def layer_back(grad, hat, inverse):
    first = jnp.mean(grad, axis=-1, keepdims=True)
    second = jnp.mean(grad * hat, axis=-1, keepdims=True)
    return inverse * (grad - first - hat * second)


def mm(left, right):
    return jnp.dot(left, right, preferred_element_type=F32)


def mm_t(left, right):
    return lax.dot_general(left, right, (((1,), (1,)), ((), ())), preferred_element_type=F32)


def t_mm(left, right):
    return lax.dot_general(left, right, (((0,), (0,)), ((), ())), preferred_element_type=F32)


def columns_of(bucket_ids):
    return jnp.where(
        bucket_ids == 0, 9 * UNIT // 2, jnp.where(bucket_ids == 1, 3 * UNIT, 9 * UNIT // 4)
    )


def pixel_mask(positions, height, width, cols):
    row_at = positions // cols
    col_at = positions % cols
    return ((row_at < height) & (col_at < width)).astype(F32)


def spots(shapes):
    return [jax.ShapeDtypeStruct(shape, kind) for shape, kind in shapes]


def local_kernel(name, kernel, arrays, results, scratch=(), scalars=0):
    near = pl.BlockSpec(memory_space=pltpu.VMEM)
    numbers = pl.BlockSpec(memory_space=pltpu.SMEM)
    return pl.pallas_call(
        kernel,
        out_shape=spots(results),
        in_specs=[numbers] * scalars + [near] * (len(arrays) - scalars),
        out_specs=[near] * len(results),
        scratch_shapes=list(scratch),
        compiler_params=pltpu.CompilerParams(vmem_limit_bytes=56 * 2**20),
        name=name,
    )(*arrays)


class Sizes:
    def __init__(self, latents, clip_tokens, in_weight, in_bias, conv_bias, map_weight):
        self.G, self.D, self.R = (lax.axis_size(axis) for axis in AXES)
        self.T = self.D * self.R
        self.S = self.T * self.G
        self.N, self.C = latents.shape[1:]
        self.pixels = self.R * self.N
        self.FFS = in_bias.shape[0]
        self.FL = self.G * self.FFS
        self.FF = in_weight.shape[1]
        self.cs = conv_bias.shape[0]
        self.ms = map_weight.shape[0]
        self.mp = -(-self.ms // 16) * 16
        self.slots = clip_tokens.shape[1]
        self.sp = -(-self.slots // 16) * 16
        self.texts = self.R * self.slots
        self.HW = self.C // self.T
        self.even = self.G == self.R
        self.Q = self.G if self.even else 1
        self.places = [(g, d, r) for g in range(self.G) for d in range(self.D) for r in range(self.R)]


def rows_cols(first, count, cols):
    position = (first + lax.broadcasted_iota(jnp.int32, (count, 1), 0)).astype(F32)
    row = jnp.floor((position + 0.5) / cols)
    return row, position - row * cols


def float_cols(bucket):
    return jnp.where(bucket == 0, 9.0 * UNIT / 2, jnp.where(bucket == 1, 3.0 * UNIT, 9.0 * UNIT / 4))


WIDTHS = (9 * UNIT // 2, 3 * UNIT, 9 * UNIT // 4)
SMALL = 16
VEC = 16
FACTS = 96


def cut_kernel(m, arrays):
    def kernel(h_ref, w_ref, b_ref, in_ref, qkv_ref, map_ref, clip_ref, lat_ref, cot_ref, cw_ref, *refs):
        vectors, refs = refs[:5], refs[5:]
        te_ref, tm_ref, f0, f1, f2 = refs[:5]
        in_out, qkv_out, map_out, clip_out, masked_out, gres_out, small_out, f_out, small, fv = refs[5:]
        for g in range(m.G):
            for t in range(m.T):
                start = m.FFS * (g * m.T + t)
                in_out[t, :, pl.ds(g * m.FFS, m.FFS)] = in_ref[:, pl.ds(start, m.FFS)]
        for d in range(m.D):
            for r in range(m.R):
                for j in range(3):
                    start = m.C * j + m.HW * (m.D * r + d)
                    qkv_out[d * m.R + r, :, pl.ds(j * m.HW, m.HW)] = qkv_ref[:, pl.ds(start, m.HW)]
        map_out[...] = jnp.zeros_like(map_out)
        for t in range(m.T):
            map_out[t, pl.ds(0, m.ms)] = map_ref[:, pl.ds(t * m.HW, m.HW)]
        clip_out[...] = jnp.zeros_like(clip_out)
        clip_out[pl.ds(0, m.slots)] = clip_ref[0]
        z = lax.axis_index("rows")
        row, col = rows_cols(z * m.N, m.N, float_cols(b_ref[0]))
        keep = (row < h_ref[0].astype(F32)) & (col < w_ref[0].astype(F32))
        masked_out[...] = jnp.where(keep, lat_ref[0].astype(F32), 0.0).astype(BF16)
        gres_out[...] = jnp.where(keep, cot_ref[0].astype(F32), 0.0).astype(BF16)
        small[...] = jnp.zeros_like(small)
        small[pl.ds(0, 9), pl.ds(0, m.cs)] = cw_ref[...].astype(F32)
        for number, ref in enumerate(vectors):
            small[pl.ds(9 + number, 1), pl.ds(0, ref.shape[0])] = ref[...].astype(F32).reshape(1, -1)
        small[pl.ds(14, 1), pl.ds(0, te_ref.shape[1])] = te_ref[...].astype(F32)
        lane = lax.broadcasted_iota(jnp.int32, (1, 128), 1)
        for number, ref in enumerate((h_ref, w_ref, b_ref)):
            fact = jnp.full((1, 128), ref[0]).astype(F32)
            row = small[pl.ds(14, 1)]
            small[pl.ds(14, 1)] = jnp.where(lane == FACTS + number, fact, row)
        small[pl.ds(15, 1), pl.ds(0, m.texts)] = tm_ref[...].astype(F32)
        small_out[...] = small[...].astype(BF16)
        fv[...] = jnp.zeros_like(fv)
        for number, ref in enumerate((f0, f1, f2)):
            fv[pl.ds(number, 1)] = ref[...].astype(F32).reshape(1, -1)
        f_out[...] = fv[...].astype(BF16)

    return local_kernel(
        "cut_weights",
        kernel,
        arrays,
        [
            ((m.T, m.cs, m.FL), BF16),
            ((m.T, m.cs, 3 * m.HW), BF16),
            ((m.T, m.mp, m.HW), BF16),
            ((m.sp, arrays[6].shape[2]), BF16),
            ((m.N, m.C), BF16),
            ((m.N, m.C), BF16),
            ((SMALL, 128), BF16),
            ((16, m.FFS), BF16),
        ],
        [pltpu.VMEM((SMALL, 128), F32), pltpu.VMEM((16, m.FFS), F32)],
        scalars=3,
    )


def fill_extended(m, extended, edges_ref, mid_ref):
    z = lax.axis_index("rows")
    extended[pl.ds(0, EDGE)] = jnp.where(z > 0, edges_ref[0].astype(F32), 0.0)
    extended[pl.ds(EDGE, m.N)] = mid_ref[...].astype(F32)
    extended[pl.ds(EDGE + m.N, EDGE)] = jnp.where(z < m.R - 1, edges_ref[1].astype(F32), 0.0)


def width_of(bucket):
    return jnp.where(bucket == 0, WIDTHS[0], jnp.where(bucket == 1, WIDTHS[1], WIDTHS[2]))


def shifted_rows(ref, count, shift, lanes):
    start = EDGE + shift
    whole = start // 8
    tall = count + 8
    block = ref[pl.ds(pl.multiple_of(whole * 8, 8), tall), lanes]
    extra = start - whole * 8
    return pltpu.roll(block, jnp.where(extra == 0, 0, tall - extra), 0)[:count]


def each_column_block(m, act):
    @pl.loop(0, m.C // 128)
    def _(number):
        act(pl.ds(pl.multiple_of(number * 128, 128), 128))


def tap_steps():
    return [(index, index // 3 - 1, index % 3 - 1) for index in range(9)]


def conv_back_kernel(m, b_ref, grad_in, hat, inv, edges, masked, vec_grads, qv_grads, modulate_grads):
    def kernel(b_ref, g_ref, hat_ref, inv_ref, edges_ref, mid_ref, vec_ref, qv_ref, gm_ref, grad, low, tiny, extended, vec):
        values = layer_back(g_ref[...], hat_ref[...], inv_ref[...])
        grad[...] = values
        low[...] = values.astype(BF16)
        fill_extended(m, extended, edges_ref, mid_ref)
        vec[pl.ds(9, 1)] = jnp.sum(values, axis=0, keepdims=True)
        vec[pl.ds(10, 3)] = vec_ref[pl.ds(0, 3)]
        vec[pl.ds(13, 3)] = jnp.zeros((3, m.C), F32)
        z = lax.axis_index("rows")

        def taps(width):
            _, col = rows_cols(z * m.N, m.N, width.astype(F32))

            def block(lanes):
                value = grad[:, lanes]
                for index, dy, dx in tap_steps():
                    piece = shifted_rows(extended, m.N, dy * width + dx, lanes)
                    ok = (col + dx >= 0) & (col + dx < width)
                    vec[pl.ds(index, 1), lanes] = jnp.sum(
                        jnp.where(ok, piece, 0.0) * value, axis=0, keepdims=True
                    )

            each_column_block(m, block)

        taps(width_of(b_ref[0]))
        tiny[...] = jnp.zeros_like(tiny)
        half = m.S // 2
        pair = 2 * m.cs
        for s, (g, d, r) in enumerate(m.places):
            t = d * m.R + r
            tiny[t, g, pl.ds(0, 13), pl.ds(0, m.cs)] = vec[pl.ds(0, 13), pl.ds(s * m.cs, m.cs)]
            side, at = pl.ds(s // half, 1), pl.ds(pair * (s % half), pair)
            tiny[t, g, pl.ds(13, 1), pl.ds(0, pair)] = qv_ref[side, at]
            tiny[t, g, pl.ds(14, 1), pl.ds(0, pair)] = gm_ref[side, at]

    return local_kernel(
        "convolve_back",
        kernel,
        [b_ref, grad_in, hat, inv, edges, masked, vec_grads, qv_grads, modulate_grads],
        [((m.N, m.C), F32), ((m.N, m.C), BF16), ((m.T, m.G, 16, 128), F32)],
        [pltpu.VMEM((m.N + 2 * EDGE, m.C), F32), pltpu.VMEM((VEC, m.C), F32)],
        scalars=1,
    )


def finish_kernel(m, b_ref, edges, low, after, pix, vec, in_team, qkv_team, map_team, proj_team, out_parts):
    def kernel(b_ref, edges_ref, low_ref, after_ref, pix_ref, vec_ref, in_ref, qkv_ref, map_ref, proj_ref, parts_ref,
               lat_out, in_out, qkv_out, map_out, proj_out, out_out, extended):
        fill_extended(m, extended, edges_ref, low_ref)
        z = lax.axis_index("rows")
        keep = pix_ref[...] > 0

        def taps(width):
            _, col = rows_cols(z * m.N, m.N, width.astype(F32))

            def block(lanes):
                total = jnp.zeros((m.N, 128), F32)
                for index, dy, dx in tap_steps():
                    piece = shifted_rows(extended, m.N, -dy * width - dx, lanes)
                    ok = (col - dx >= 0) & (col - dx < width)
                    total = total + jnp.where(ok, piece, 0.0) * vec_ref[pl.ds(index, 1), lanes]
                lat_out[0, :, lanes] = after_ref[:, lanes] + jnp.where(keep, total, 0.0)

            each_column_block(m, block)

        taps(width_of(b_ref[0]))
        for g in range(m.G):
            for t in range(m.T):
                start = m.FFS * (g * m.T + t)
                in_out[:, pl.ds(start, m.FFS)] = in_ref[t, :, pl.ds(g * m.FFS, m.FFS)].astype(F32)
        for d in range(m.D):
            for r in range(m.R):
                for j in range(3):
                    start = m.C * j + m.HW * (m.D * r + d)
                    qkv_out[:, pl.ds(start, m.HW)] = qkv_ref[
                        d * m.R + r, :, pl.ds(j * m.HW, m.HW)
                    ].astype(F32)
        for t in range(m.T):
            map_out[:, pl.ds(t * m.HW, m.HW)] = map_ref[t].astype(F32)[: m.ms]
        total = parts_ref[0].astype(F32)
        for g in range(1, m.G):
            total = total + parts_ref[g].astype(F32)
        out_out[...] = total
        wide = m.C // m.Q
        for n in range(m.Q):
            proj_out[:, pl.ds(n * wide, wide)] = proj_ref[n].astype(F32)

    return local_kernel(
        "finish",
        kernel,
        [b_ref, edges, low, after, pix, vec, in_team, qkv_team, map_team, proj_team, out_parts],
        [
            ((1, m.N, m.C), F32),
            ((m.cs, m.FF), F32),
            ((m.cs, 3 * m.C), F32),
            ((m.ms, m.C), F32),
            ((m.cs, m.C), F32),
            ((m.FFS, m.C), F32),
        ],
        [pltpu.VMEM((m.N + 2 * EDGE, m.C), F32)],
        scalars=1,
    )


class Posted:
    def __init__(self, copy, lands):
        self.copy, self.lands, self.landed = copy, lands, False


def line_order(p, number):
    low = p.z < p.R // 2
    far, near = p.R - 1 - number // 2, number // 2
    if number % 2:
        far, near = near, far
    return jnp.where(low, far, near)


def chunks(count, act, step=16):
    @pl.loop(0, count // step)
    def _(number):
        act(pl.ds(pl.multiple_of(number * step, step), step))


def each_rows(count, step, act):
    if step % 16:
        for number in range(count):
            act(number, pl.ds(number * step, step))
    else:

        @pl.loop(0, count)
        def _(number):
            act(number, pl.ds(pl.multiple_of(number * step, 16), step))


def greet_all(p, targets):
    barrier = pltpu.get_barrier_semaphore()
    waits = 0
    for target, when in targets:
        if when is None:
            waits = waits + 1
        else:
            waits = waits + jnp.where(when, 1, 0).astype(jnp.int32)
        guarded(when, lambda target=target: signal_all(barrier, [target]))
    pl.semaphore_wait(barrier, waits)


def fused_kernel(
    ident, name, greet, act, near, loads, far, near_out, far_out, scratch, sems, local, numbers=0
):
    close = pl.BlockSpec(memory_space=pltpu.VMEM)
    spot = pl.BlockSpec(memory_space=pl.ANY)
    counts = [len(near), len(loads), len(far), len(near_out), len(far_out), len(scratch), len(loads)]

    def kernel(*refs):
        groups = []
        for count in counts:
            groups.append(refs[:count])
            refs = refs[count:]
        send_sem, recv_sem, local_sem, load_sem = refs
        near, sources, far, near_out, far_out, scratch, held = groups
        brought = []
        for number, (source, place) in enumerate(zip(sources, held)):
            copy = pltpu.make_async_copy(source, place, load_sem.at[number])
            copy.start()
            brought.append(Brought(copy, place))
        p = Place()
        flow = Flow(send_sem, recv_sem, local_sem)
        greet_all(p, greet(p))
        act(p, flow, near, brought, far, near_out, far_out, scratch)
        flow.finish()
        if flow.used > sems or flow.kept > local:
            raise ValueError(f"{name}: {flow.used} {flow.kept}")

    return pl.pallas_call(
        kernel,
        out_shape=spots(near_out + far_out),
        in_specs=[pl.BlockSpec(memory_space=pltpu.SMEM)] * numbers
        + [close] * (len(near) - numbers)
        + [spot] * (len(loads) + len(far)),
        out_specs=[close] * len(near_out) + [spot] * len(far_out),
        scratch_shapes=list(scratch)
        + [pltpu.VMEM(array.shape, array.dtype) for array in loads]
        + [
            pltpu.SemaphoreType.DMA((sems,)),
            pltpu.SemaphoreType.DMA((sems,)),
            pltpu.SemaphoreType.DMA((local,)),
            pltpu.SemaphoreType.DMA((max(len(loads), 1),)),
        ],
        compiler_params=pltpu.CompilerParams(
            collective_id=ident, has_side_effects=True, vmem_limit_bytes=63 * 2**20
        ),
        name=name,
    )(*near, *loads, *far)


class Brought:
    def __init__(self, copy, place):
        self.copy, self.place, self.here = copy, place, False

    def get(self):
        if not self.here:
            self.copy.wait()
            self.here = True
        return self.place


def gather_sems(m):
    return 4 * m.R - 3


def reduce_sems(m):
    return 3 * m.R


def reduce_buffers(m, count, width, part=True):
    block = (m.R, count, width)
    mine = [pltpu.VMEM((m.D,) + block, BF16)] if part else []
    return mine + [
        pltpu.VMEM(block, BF16),
        pltpu.VMEM((2,) + block, BF16),
        pltpu.VMEM((2,) + block, BF16),
    ]


def spread_greet(m, p):
    greet = []
    for step in range(m.G):
        source = {"grp": p.z, "duo": p.c, "rows": lax.rem(p.q - step + m.G, m.G)}
        greet.append((source, None if step else p.q != p.z))
    return greet


def common_greet(p):
    return team_greet(p) + group_greet(p)


def front_kernel(m, time_weight, time_bias, masked, small, fvec, in_cut, out_weight, map_cut, qkv_cut, clip_pad, proj_weight):
    near = [time_weight, time_bias]
    loads = [masked]
    far = [masked, small, fvec, in_cut, out_weight, map_cut, qkv_cut, clip_pad]
    far += [proj_weight] if m.even else []
    N, C, FL, G, T = m.N, m.C, m.FL, m.G, m.T
    root = 0.5**0.5
    texts = m.D * m.texts
    cond = clip_pad.shape[1]
    wide = C // m.Q
    square = G == 4
    items = m.G * m.D
    mod_rows = -(-items // 8) * 8
    pair = 2 * m.cs

    def act(p, flow, near, loads, far, near_out, far_out, scratch):
        tw_ref, tb_ref = near
        norms, total, silu, mapped, x_all, in_all, active, slope = near_out[:8]
        hat, inv, vec, fv, keep, pix, qkv_bias, embed, edges, normed = near_out[8:]
        out_all, qkv_rows, mod_all, mod_line = far_out[:4]
        map_all, clip_all, squares, weight, text, small_all, f_all, extended, conv, te, mod = scratch
        mid, small_ref, fvec_ref, in_cut, out_own, map_cut, qkv_cut, clip = far[:8]
        mine = p.c * p.R + p.z
        own_in = in_all.at[p.q]
        small_posts = [
            flow.post(small_ref, small_all.at[mine, p.q], {"grp": to}) for to in p.groups()
        ]
        edge_posts = []
        for block, to, sends, lands in (
            (mid.at[pl.ds(N - EDGE, EDGE)], p.z + 1, p.z < p.R - 1, p.z > 0),
            (mid.at[pl.ds(0, EDGE)], p.z - 1, p.z > 0, p.z < p.R - 1),
        ):
            slot = jnp.where(to > p.z, 0, 1)
            edge_posts.append(
                flow.post(block, edges.at[slot], {"rows": to}, when=sends, lands=lands)
            )
        f_posts = [flow.post(fvec_ref, f_all.at[p.q], {"grp": to}) for to in p.groups()]
        flow.keep(small_ref, small_all.at[mine, p.q], now=True)
        for item in small_posts:
            flow.land(item)
        spread = [
            flow.post(small_all.at[mine], small_all.at[mine], {"duo": c, "rows": z})
            for c, z in p.team()
        ]
        in_team = [
            flow.post(in_cut.at[c * p.R + z], own_in.at[mine], {"duo": c, "rows": z})
            for c, z in p.team()
        ]
        if square:
            out_relay = flow.square(p, out_own, out_all)
            flow.keep(out_own, out_all.at[p.q])
        else:
            flow.gather_group(p, out_own, out_all)
        own_map = map_all.at[p.q]
        map_team = [
            flow.post(map_cut.at[c * p.R + z], own_map.at[mine], {"duo": c, "rows": z})
            for c, z in p.team()
        ]
        clip_line = LineGather(flow, p, clip, clip_all)
        clip_line.start()
        if m.even:
            for number in range(G):
                to = lax.rem(p.z + number, G)
                piece = far[8].at[:, pl.ds(pl.multiple_of(to * wide, 128), wide)]
                flow.post(
                    piece,
                    far_out[4].at[p.z],
                    {"grp": to, "duo": p.c, "rows": p.q},
                    when=None if number else p.q != p.z,
                )
            piece = far[8].at[:, pl.ds(pl.multiple_of(p.z * wide, 128), wide)]
            flow.keep(piece, far_out[4].at[p.z], p.q == p.z)
        flow.keep(in_cut.at[mine], own_in.at[mine], now=True)
        flow.keep(map_cut.at[mine], own_map.at[mine], now=True)
        flow.keep(clip, clip_all.at[p.c, p.z], now=True)
        flow.keep(fvec_ref, f_all.at[p.q], now=True)
        for item in spread + edge_posts:
            flow.land(item)
        half = m.S // 2
        vec[...] = jnp.zeros_like(vec)
        for s, (g, d, r) in enumerate(m.places):
            piece = small_all[d * m.R + r, g].astype(F32)
            vec[pl.ds(0, 13), pl.ds(s * m.cs, m.cs)] = piece[:13, : m.cs]
            vec[pl.ds(13 + s // half, 1), pl.ds(pair * (s % half), pair)] = piece[13:14, :pair]
            if r == 0:
                embed[pl.ds(m.D * g + d, 1)] = piece[14:15]
        extended[pl.ds(0, EDGE)] = jnp.where(p.z > 0, edges[0].astype(F32), 0.0)
        extended[pl.ds(EDGE, N)] = loads[0].get()[...].astype(F32)
        extended[pl.ds(EDGE + N, EDGE)] = jnp.where(p.z < m.R - 1, edges[1].astype(F32), 0.0)
        kind = small_all[mine, p.q].astype(F32)[14:15, FACTS + 2 : FACTS + 3]
        real = float_cols(kind)
        _, col = rows_cols(p.z * N, N, real)

        def taps(lanes):
            sum_of = jnp.zeros((N, 128), F32) + vec[pl.ds(9, 1), lanes]
            for index, dy, dx in tap_steps():
                pieces = [
                    extended[pl.ds(EDGE + dy * width + dx, N), lanes]
                    for width in (WIDTHS if dy else WIDTHS[:1])
                ]
                piece = pieces[0]
                if dy:
                    piece = jnp.where(kind == 0, piece, jnp.where(kind == 1, pieces[1], pieces[2]))
                ok = (col + dx >= 0) & (col + dx < real)
                sum_of = sum_of + jnp.where(ok, piece, 0.0) * vec[pl.ds(index, 1), lanes]
            conv[:, lanes] = sum_of

        each_column_block(m, taps)
        values, inverse = layer_stats(conv[...])
        hat[...] = values
        normed[...] = values.astype(BF16)
        inv[...] = inverse
        line = LineGather(flow, p, normed, x_all)
        line.start()
        flow.keep(normed, x_all.at[p.c, p.z], now=True)
        te[...] = embed[...][:items, : te.shape[1]].astype(BF16)
        mod[...] = jnp.zeros_like(mod)
        mod[pl.ds(0, items), pl.ds(0, pair)] = mm(te[...], tw_ref[...]) + tb_ref[...].astype(F32)
        mod_posts = flow.gather_group(p, mod, mod_all)
        for item in in_team:
            flow.land(item)
        if square:
            in_relay = flow.square(p, own_in, in_all)
        else:
            in_posts = [flow.post(own_in, in_all.at[p.q], {"grp": q}) for q in p.groups()]
        for d in range(m.D):
            facts = small_all[d * m.R, p.q].astype(F32)
            row, col_all = rows_cols(0, m.pixels, float_cols(facts[14:15, FACTS + 2 : FACTS + 3]))
            inside = (row < facts[14:15, FACTS : FACTS + 1]) & (
                col_all < facts[14:15, FACTS + 1 : FACTS + 2]
            )
            keep[d, pl.ds(0, m.pixels)] = jnp.where(inside, 1.0, 0.0)
            shown = facts.T[: m.texts, 15:16]
            slot = lax.broadcasted_iota(jnp.int32, (m.texts, 1), 0)
            keep[d, pl.ds(m.pixels, m.texts)] = jnp.where(slot < TXT, shown, 0.0)
        pix[...] = keep[p.c, pl.ds(pl.multiple_of(p.z * N, 8), N)]
        for item in f_posts:
            flow.land(item)
        for g in range(G):
            fv[:, pl.ds(g * m.FFS, m.FFS)] = f_all[g].astype(F32)[:8]
        qkv_bias[...] = jnp.zeros_like(qkv_bias)
        for h in range(T):

            @pl.when(p.D * p.z + p.c == h)
            def _():
                at = pl.ds(h * m.HW, m.HW)
                qkv_bias[:, : m.HW] = vec[pl.ds(13, 1), at]
                qkv_bias[:, 2 * m.HW :] = vec[pl.ds(14, 1), at]

        line.hop(1)
        if square:
            out_relay()
        line.hop(2)
        for item in map_team:
            flow.land(item)
        map_posts = [flow.post(own_map, map_all.at[p.q], {"grp": q}) for q in p.groups()]
        flow.swap_team(p, qkv_cut, qkv_rows)
        if square:
            in_posts = in_relay()
        for item in mod_posts:
            flow.land(item)
        flow.settle_kept()
        mods = LineGather(flow, p, mod_all, mod_line)
        mods.start()
        flow.keep(mod_all, mod_line.at[p.c, p.z])
        squares[...] = jnp.zeros_like(squares)
        for item in in_posts:
            flow.land(item)

        def multiply(first, count):
            line.settle(first + count)

            @pl.loop(0, count * m.D)
            def _(number):
                d = number // count
                block = jnp.where(
                    number - d * count == 0, line.nth(first), line.nth(first + count - 1)
                )
                base = pl.multiple_of(block * N, 16)
                hidden = mm(x_all[d, block], in_all[...].reshape(C, FL)) + fv[pl.ds(0, 1)]
                gate = 0.5 * (1.0 + lax.erf(hidden * root))
                value = hidden * gate
                rows = pl.ds(pl.multiple_of(d * m.pixels + base, 16), N)
                active[rows] = value
                slope[rows] = gate + hidden * (
                    jnp.exp(-0.5 * hidden * hidden) * 0.3989422804014327
                )
                squares[pl.ds(d, 1)] += jnp.sum(
                    keep[d, pl.ds(base, N)] * value * value, axis=0, keepdims=True
                )

        first = m.R // 2
        multiply(0, first)
        line.hop(3)
        for step in range(4, m.R):
            line.hop(step)
        multiply(first, m.R - first)
        norms[...] = jnp.sqrt(squares[...])
        total[...] = jnp.broadcast_to(jnp.sum(norms[...], axis=1, keepdims=True), total.shape)
        for step in range(1, m.R):
            clip_line.hop(step)
            mods.hop(step)
        clip_line.settle(m.R)
        for item in map_posts:
            flow.land(item)
        for d in range(m.D):
            for r in range(m.R):
                piece = clip_all[d, r].astype(F32)[: m.slots]
                text[pl.ds((d * m.R + r) * m.slots, m.slots)] = piece / (1.0 + jnp.exp(-piece))
        silu[...] = text[...].astype(BF16)
        for g in range(G):
            for t in range(T):
                piece = map_all[g, t].astype(F32)
                weight[pl.ds(m.ms * (g * T + t), m.ms)] = piece[: m.ms]
        product = mm(silu[...], weight[...].astype(BF16))
        for t in range(T):

            @pl.when(mine == t)
            def _():
                mapped[...] = (product + vec[pl.ds(11, 1), pl.ds(t * m.HW, m.HW)]).astype(BF16)

    near_out = [
        ((8, FL), F32),
        ((8, 128), F32),
        ((texts, cond), BF16),
        ((texts, m.HW), BF16),
        ((m.D, m.R, N, C), BF16),
        ((G, T, m.cs, FL), BF16),
        ((m.D * m.pixels, FL), F32),
        ((m.D * m.pixels, FL), F32),
        ((N, C), F32),
        ((N, 1), F32),
        ((VEC, C), F32),
        ((8, FL), F32),
        ((m.D, m.pixels + m.texts, 1), F32),
        ((N, 1), F32),
        ((1, 3 * m.HW), F32),
        ((mod_rows, 128), F32),
        ((2, EDGE, C), BF16),
        ((N, C), BF16),
    ]
    far_out = [
        ((G,) + out_weight.shape, BF16),
        (qkv_cut.shape, BF16),
        ((G, mod_rows, 128), F32),
        ((m.D, m.R, G, mod_rows, 128), F32),
    ]
    if m.even:
        far_out.append(((m.R, m.cs, wide), BF16))
    scratch = [
        pltpu.VMEM((G, T, m.mp, m.HW), BF16),
        pltpu.VMEM((m.D, m.R) + clip_pad.shape, BF16),
        pltpu.VMEM((8, FL), F32),
        pltpu.VMEM((cond, m.HW), F32),
        pltpu.VMEM((texts, cond), F32),
        pltpu.VMEM((T, G, SMALL, 128), BF16),
        pltpu.VMEM((G,) + fvec.shape, BF16),
        pltpu.VMEM((N + 2 * EDGE, C), F32),
        pltpu.VMEM((N, C), F32),
        pltpu.VMEM((items, time_weight.shape[0]), BF16),
        pltpu.VMEM((mod_rows, 128), F32),
    ]
    columns = 4 if square else G - 1
    return fused_kernel(
        1,
        "front",
        lambda p: common_greet(p) + (sources_greet(m, p) if m.even else []),
        act,
        near,
        loads,
        far,
        near_out,
        far_out,
        scratch,
        4 * (T - 1) + 2 + 2 * columns + 4 * (G - 1) + (G if m.even else 0) + 3 * gather_sems(m),
        12,
    )


def sources_greet(m, p):
    greet = []
    for step in range(m.G):
        source = {"grp": p.z, "duo": p.c, "rows": lax.rem(p.q - step + m.G, m.G)}
        greet.append((source, None if step else p.q != p.z))
    return greet


def team_sum(m, p, flow, own, everyone):
    mine = p.c * m.R + p.z
    posted = [
        flow.post(own, everyone.at[mine], {"duo": c, "rows": z}) for c, z in p.team()
    ]

    def total():
        for item in posted:
            flow.land(item)
        result = own[...]
        for step, (c, z) in enumerate(p.team()):
            result = result + everyone[c * m.R + z]
        return result

    return total


def branch_kernel(m, active, norms, total, out_full, fv, latents, keep, vec, mod_all, qkv_rows, mapped, proj_part):
    near = [norms, total, fv, keep, mod_all]
    loads = [active, out_full, latents, vec]
    far = [qkv_rows, mapped] + ([proj_part] if m.even else [])
    N, C = m.N, m.C
    rows_all = m.D * m.pixels

    def act(p, flow, near, loads, far, near_out, far_out, scratch):
        norms, total, fv, keep, mod_all = near
        gain, grn_bias = fv[pl.ds(1, 1)], fv[pl.ds(2, 1)]
        grn, after, hat, inv, two, ratio, means, mods = near_out
        two_all, mapped_all, qkv_all = far_out[:3]
        everyone, part, mate, passed, landed, branch, slopes = scratch
        add_up = team_sum(m, p, flow, total, everyone)
        flow.gather_group(p, far[0], qkv_all)
        if m.even:
            flow.gather_group(p, far[2], far_out[3])
        text_line = LineGather(flow, p, far[1], mapped_all)
        two_line = LineGather(flow, p, two, two_all)
        half = m.S // 2
        pair = 2 * m.cs
        for s, (g, d, r) in enumerate(m.places):
            item = pl.ds(m.D * p.q + p.c, 1)
            mods[pl.ds(s // half, 1), pl.ds(pair * (s % half), pair)] = mod_all[d, r, g, item, pl.ds(0, pair)]
        mean = add_up() / m.FF + grn_eps
        means[...] = mean
        ratio[...] = norms[...] / mean[:, :1]
        slopes[...] = gain * ratio[...] + 1.0
        line = LineReduce(flow, p, part, branch, mate, passed, landed)
        active, out_w, lat, vec = (load.get() for load in loads)

        def produce(block):
            @pl.loop(0, m.D)
            def _(d):
                rows = pl.ds(pl.multiple_of(d * m.pixels + block * N, 16), N)
                low = (active[rows] * slopes[pl.ds(d, 1)] + grn_bias).astype(BF16)
                grn[rows] = low
                part[d, block] = mm(low, out_w[...]).astype(BF16)

        line.run(produce)
        text_line.start()

        def tail(rows):
            value = lat[rows].astype(F32) + keep[rows] * (branch[rows] + vec[pl.ds(10, 1)])
            after[rows] = value
            second = value * (1.0 + mods[pl.ds(0, 1)]) + mods[pl.ds(1, 1)]
            normal, inverse = layer_stats(second)
            hat[rows] = normal
            inv[rows] = inverse
            two[rows] = normal.astype(BF16)

        chunks(N, tail)
        two_line.start()
        flow.keep(far[1], mapped_all.at[p.c, p.z])
        flow.keep(two, two_all.at[p.c, p.z])
        for step in range(1, m.R):
            text_line.hop(step)
            two_line.hop(step)

    near_out = [
        ((rows_all, m.FL), BF16),
        ((N, C), F32),
        ((N, C), F32),
        ((N, 1), F32),
        ((N, C), BF16),
        ((8, m.FL), F32),
        ((8, 128), F32),
        ((8, C), F32),
    ]
    far_out = [
        ((m.D, m.R, N, C), BF16),
        ((m.D, m.R) + mapped.shape, BF16),
        ((m.G,) + qkv_rows.shape, BF16),
    ]
    if m.even:
        far_out.append(((m.G,) + proj_part.shape, BF16))
    scratch = (
        [pltpu.VMEM((m.T, 8, 128), F32)]
        + reduce_buffers(m, N, C)
        + [pltpu.VMEM((N, C), F32), pltpu.VMEM((8, m.FL), F32)]
    )
    return fused_kernel(
        3,
        "branch",
        common_greet,
        act,
        near,
        loads,
        far,
        near_out,
        far_out,
        scratch,
        (m.T - 1) + 2 * (m.G - 1) + 2 * gather_sems(m) + reduce_sems(m),
        5,
    )


def attention_kernel(m, two_all, gres, mapped_all, weight, proj, bias, key_keep):
    near = [bias, key_keep]
    loads = [two_all, weight, proj, mapped_all]
    far = [gres]
    heads = m.HW // HEAD
    keys = m.pixels + m.texts
    scale = HEAD ** (-0.5)
    HW, C, N, D, R, G, pixels, texts = m.HW, m.C, m.N, m.D, m.R, m.G, m.pixels, m.texts
    wide = C // m.Q
    block_rows = 2 * HW

    def act(p, flow, near, loads, far, near_out, far_out, scratch):
        bias, keep = near
        result, two_out, map_out, gw_out, gp_out, gb_out = near_out
        (gres_all, part, mate, passed, landed, qkv, k_all, v_all, k_t, v_t, dk, dv, o_t, dq_t, o_low, att, g_all, probs, dqkv,
         dtext, piece, words) = scratch
        line = LineGather(flow, p, far[0], gres_all)
        line.start()
        flow.keep(far[0], gres_all.at[p.c, p.z], now=True)
        two, w, proj, mapped = (load.get() for load in loads)
        red = LineReduce(flow, p, part, result, mate, passed, landed)

        @pl.loop(0, D)
        def _(d):
            qkv[d] = (mm(two[d], w[...]) + bias[...]).astype(BF16)
            words[...] = jnp.zeros((texts, 3 * HW), F32) + bias[...]

            @pl.loop(0, m.T)
            def _(t):
                words[...] += mm(mapped[t, d], w[pl.ds(pl.multiple_of(t * HW, 16), HW)])

            text = words[...].astype(BF16)
            k_all[d, pl.ds(0, pixels)] = qkv[d, :, HW : 2 * HW]
            k_all[d, pl.ds(pixels, texts)] = text[:, HW : 2 * HW]
            v_all[d, pl.ds(0, pixels)] = qkv[d, :, 2 * HW :]
            v_all[d, pl.ds(pixels, texts)] = text[:, 2 * HW :]
            k_t[d] = k_all[d].T
            v_t[d] = v_all[d].T
            dk[d] = jnp.zeros_like(dk[d])
            dv[d] = jnp.zeros_like(dv[d])
            o_t[d] = jnp.zeros_like(o_t[d])
            dq_t[d] = jnp.zeros_like(dq_t[d])

        lane = lax.broadcasted_iota(jnp.int32, (1, HW), 1)
        row = lax.broadcasted_iota(jnp.int32, (HW, 1), 0)

        def masks(number):
            d = number // heads
            low = (number - d * heads) * HEAD
            return d, (lane >= low) & (lane < low + HEAD), (row >= low) & (row < low + HEAD)

        def forward(number):
            d, in_head, in_row = masks(number)
            q_h = jnp.where(in_head, qkv[d, :, :HW], 0).astype(BF16)
            scores = mm_t(k_all[d], q_h) * scale
            scores = jnp.where(keep[d] > 0, scores, masked_score)
            weights = jnp.exp(scores - jnp.max(scores, axis=0, keepdims=True))
            low = (weights / jnp.sum(weights, axis=0, keepdims=True)).astype(BF16)
            probs[number] = low
            o_t[d] += mm(jnp.where(in_row, v_t[d], 0).astype(BF16), low)

        pl.loop(0, D * heads // 2)(forward)
        line.hop(1)
        pl.loop(D * heads // 2, D * heads)(forward)

        @pl.loop(0, D)
        def _(d):
            o_low[d] = o_t[d].astype(BF16)
            att[d] = o_t[d].T.astype(BF16)

        def lanes_of(n):
            return pl.ds(pl.multiple_of(n * wide, 128), wide)

        @pl.loop(0, D * R)
        def _(number):
            d = number // R
            block = number - d * R
            mine = att[d, pl.ds(pl.multiple_of(block * N, 16), N)]
            for n in range(m.Q):
                part[d, block, :, pl.ds(n * wide, wide)] = mm(mine, proj[n]).astype(BF16)

        red.start()
        line.hop(2)
        red.early()
        steps = list(red.later())
        for number in range(3, R):
            line.hop(number)
        line.settle(R)

        @pl.loop(0, D * R)
        def _(number):
            d = number // R
            block = number - d * R
            total = jnp.zeros((N, HW), F32)
            for n in range(m.Q):
                total = total + mm_t(gres_all[d, block, :, pl.ds(n * wide, wide)], proj[n])
            g_all[d, pl.ds(pl.multiple_of(block * N, 16), N)] = total.astype(BF16)

        def back(first, last):
            @pl.loop(first, last)
            def _(number):
                d, in_head, in_row = masks(number)
                q_h = jnp.where(in_head, qkv[d, :, :HW], 0).astype(BF16)
                g_h = jnp.where(in_head, g_all[d], 0).astype(BF16)
                low = probs[number]
                dv[d] += mm(low, g_h)
                grad_probs = mm_t(v_all[d], g_h)
                high = low.astype(F32)
                sums = jnp.sum(high * grad_probs, axis=0, keepdims=True)
                grad_scores = (high * (grad_probs - sums)).astype(BF16)
                dq_t[d] += mm(jnp.where(in_row, k_t[d], 0).astype(BF16), grad_scores)
                dk[d] += mm(grad_scores, q_h)

        cut = D * heads // 2
        steps[0]()
        back(0, cut)
        for step in steps[1:3]:
            step()
        back(cut, D * heads)
        for step in steps[3:]:
            step()
        gb_out[...] = jnp.zeros_like(gb_out)

        @pl.loop(0, D)
        def _(d):
            dqkv[d, :, :HW] = (dq_t[d].T * scale).astype(BF16)
            dqkv[d, :, HW : 2 * HW] = (dk[d, pl.ds(0, pixels)] * scale).astype(BF16)
            dqkv[d, :, 2 * HW :] = dv[d, pl.ds(0, pixels)].astype(BF16)
            dtext[d, :, :HW] = jnp.zeros((texts, HW), BF16)
            dtext[d, :, HW : 2 * HW] = (dk[d, pl.ds(pixels, texts)] * scale).astype(BF16)
            dtext[d, :, 2 * HW :] = dv[d, pl.ds(pixels, texts)].astype(BF16)
            gb_out[pl.ds(0, 1)] += jnp.sum(dqkv[d].astype(F32), axis=0, keepdims=True) + jnp.sum(
                dtext[d].astype(F32), axis=0, keepdims=True
            )
            two_out[d] = mm_t(dqkv[d], w[...]).astype(BF16)
            @pl.loop(0, m.T)
            def _(t):
                rows = pl.ds(pl.multiple_of(t * HW, 16), HW)
                map_out[t, d] = mm_t(dtext[d], w[rows]).astype(BF16)

        @pl.loop(0, C // block_rows)
        def _(g):
            lanes = pl.ds(pl.multiple_of(g * block_rows, 128), block_rows)
            piece[...] = t_mm(two[0, :, lanes], dqkv[0])
            for d in range(1, D):
                piece[...] += t_mm(two[d, :, lanes], dqkv[d])
            for side in range(2):
                rows = pl.ds(side * HW, HW)
                for d in range(D):
                    piece[rows] += t_mm(mapped[2 * g + side, d], dtext[d])
            gw_out[pl.ds(pl.multiple_of(g * block_rows, 16), block_rows)] = piece[...].astype(BF16)

        @pl.loop(0, m.Q)
        def _(n):
            total = jnp.zeros((HW, wide), F32)
            for d in range(D):
                columns = gres_all[d, :, :, lanes_of(n)].reshape(pixels, wide)
                total = total + mm(o_low[d], columns)
            gp_out[n] = total.astype(BF16)
        red.close()

    near_out = [
        ((N, C), F32),
        ((D, pixels, C), BF16),
        ((m.T, D, texts, HW), BF16),
        ((C, 3 * HW), BF16),
        ((m.Q, HW, wide), BF16),
        ((8, 3 * HW), F32),
    ]
    scratch = [pltpu.VMEM((D, R, N, C), BF16)] + reduce_buffers(m, N, C)
    scratch += [
        pltpu.VMEM((D, pixels, 3 * HW), BF16),
        pltpu.VMEM((D, keys, HW), BF16),
        pltpu.VMEM((D, keys, HW), BF16),
        pltpu.VMEM((D, HW, keys), BF16),
        pltpu.VMEM((D, HW, keys), BF16),
        pltpu.VMEM((D, keys, HW), F32),
        pltpu.VMEM((D, keys, HW), F32),
        pltpu.VMEM((D, HW, pixels), F32),
        pltpu.VMEM((D, HW, pixels), F32),
        pltpu.VMEM((D, HW, pixels), BF16),
        pltpu.VMEM((D, pixels, HW), BF16),
        pltpu.VMEM((D, pixels, HW), BF16),
        pltpu.VMEM((D * heads, keys, pixels), BF16),
        pltpu.VMEM((D, pixels, 3 * HW), BF16),
        pltpu.VMEM((D, texts, 3 * HW), BF16),
        pltpu.VMEM((block_rows, 3 * HW), F32),
        pltpu.VMEM((texts, 3 * HW), F32),
    ]
    return fused_kernel(
        4,
        "attention_block",
        team_greet,
        act,
        near,
        loads,
        far,
        near_out,
        [],
        scratch,
        gather_sems(m) + reduce_sems(m),
        1,
    )


def attended_kernel(m, two_part, text_part, result, cot, gres, hat, inv, after, mods, keep, vec, grad_qkv, grad_proj):
    near = [inv, mods, keep]
    loads = [two_part, hat, after, cot, gres, text_part, result, vec]
    far = [grad_qkv] + ([grad_proj] if m.even else [])
    N, C = m.N, m.C
    texts = m.D * m.texts

    def act(p, flow, near, loads, far, near_out, far_out, scratch):
        inv, mods, keep = near
        two_part, hat, after, cot, gres, text_part, result, vec = (load.get() for load in loads)
        output, grad_after, branch, gm, vecg, text = near_out
        gb_all = far_out[0]
        two_sum, text_sum = scratch[:2]
        two_red = LineReduce(flow, p, two_part, two_sum, *scratch[2:5])
        text_red = LineReduce(flow, p, text_part, text_sum, *scratch[5:8])
        line = LineGather(flow, p, branch, gb_all)
        two_red.start()
        flow.swap_group(p, far[0], far_out[1])
        if m.even:
            flow.swap_group(p, far[1], far_out[2])
        two_red.steps_all()
        gm[...] = jnp.zeros_like(gm)
        vecg[...] = jnp.zeros_like(vecg)

        def back(rows):
            grad = cot[rows].astype(F32) + layer_back(two_sum[rows], hat[rows], inv[rows])
            gm[pl.ds(0, 1)] += jnp.sum(grad * after[rows], axis=0, keepdims=True)
            gm[pl.ds(1, 1)] += jnp.sum(grad, axis=0, keepdims=True)
            scaled = grad * (1.0 + mods[pl.ds(0, 1)])
            grad_after[rows] = scaled
            low = (keep[rows] * scaled).astype(BF16)
            branch[rows] = low
            vecg[pl.ds(0, 1)] += jnp.sum(low.astype(F32), axis=0, keepdims=True)
            vecg[pl.ds(1, 1)] += jnp.sum(gres[rows].astype(F32), axis=0, keepdims=True)

        chunks(N, back)
        line.start()
        flow.keep(branch, gb_all.at[p.c, p.z])
        text_red.start()
        line.hop(1)

        def out(rows):
            second = after[rows] * (1.0 + mods[pl.ds(0, 1)]) + mods[pl.ds(1, 1)]
            value = keep[rows] * (result[rows] + vec[pl.ds(12, 1)])
            output[rows] = (second + value).astype(BF16)

        chunks(N, out)
        for step in range(2, m.R):
            line.hop(step)
        text_red.steps_all()
        text[...] = text_sum[...].astype(BF16)

    near_out = [
        ((N, C), BF16),
        ((N, C), F32),
        ((N, C), BF16),
        ((8, C), F32),
        ((8, C), F32),
        ((texts, m.HW), BF16),
    ]
    far_out = [((m.D, m.R, N, C), BF16), (grad_qkv.shape, BF16)]
    if m.even:
        far_out.append((grad_proj.shape, BF16))
    scratch = (
        [pltpu.VMEM((N, C), F32), pltpu.VMEM((texts, m.HW), F32)]
        + reduce_buffers(m, N, C, False)
        + reduce_buffers(m, texts, m.HW, False)
    )
    return fused_kernel(
        5,
        "attended",
        common_greet,
        act,
        near,
        loads,
        far,
        near_out,
        far_out,
        scratch,
        2 * (m.G - 1) + gather_sems(m) + 2 * reduce_sems(m),
        4,
    )


def text_back_kernel(m, silu, grad_mapped):
    def kernel(s_ref, g_ref, out, bias, weight):
        weight[...] = t_mm(s_ref[...], g_ref[...])
        out[...] = jnp.zeros_like(out)
        for g in range(m.G):
            for t in range(m.T):
                at = m.ms * (g * m.T + t)
                out[g, pl.ds(t * m.mp, m.ms)] = weight[pl.ds(at, m.ms)].astype(BF16)
        bias[...] = jnp.sum(g_ref[...].astype(F32), axis=0, keepdims=True)

    return local_kernel(
        "text_back",
        kernel,
        [silu, grad_mapped],
        [((m.G, m.T * m.mp, m.HW), BF16), ((1, m.HW), F32)],
        [pltpu.VMEM((silu.shape[1], m.HW), F32)],
    )


def back_kernel(m, gb_all, out_full, active, slope, grn_out, normed_all, in_full, norms, ratio, means, fv, key_keep,
                qkv_parts, proj_parts, grad_map):
    near = [norms, ratio, means, fv, key_keep]
    loads = [gb_all, out_full, active, grn_out, slope, normed_all, in_full, qkv_parts]
    loads += [proj_parts] if m.even else []
    far = [grad_map]
    N, C, FL, G = m.N, m.C, m.FL, m.G
    rows_in = C // G
    wide = C // m.Q
    per = m.pixels // N

    def act(p, flow, near, loads, far, near_out, far_out, scratch):
        norms, ratio, means, fv, keep = near
        gain = fv[pl.ds(1, 1)]
        back, g_out = near_out
        in_parts, f_parts, map_parts, qkv_team = far_out[:4]
        everyone, mine, moments, slopes, shifts, grads, hidden, part, mate, passed, landed = scratch[:11]
        turned_g, turned_x, g_in, f_own, qkv_own = scratch[11:16]
        flow.swap_group(p, far[0], map_parts)
        gb, out_w, active, grn = (load.get() for load in loads[:4])
        moments[...] = jnp.zeros_like(moments)

        @pl.loop(0, m.D * per)
        def _(number):
            rows = pl.ds(pl.multiple_of(number * N, 16), N)
            item = number // per
            grad = mm_t(gb[rows], out_w[...])
            grads[rows] = grad
            moments[pl.ds(item, 1)] += jnp.sum(grad * active[rows], axis=0, keepdims=True)
            moments[pl.ds(m.D, 1)] += jnp.sum(grad, axis=0, keepdims=True)

        scaled = moments[...] * gain
        cross = jnp.sum(scaled * norms[...], axis=1, keepdims=True)
        mine[...] = jnp.broadcast_to(cross, mine.shape)
        add_up = team_sum(m, p, flow, mine, everyone)
        turned_g[...] = grn[...].T

        def multiply_out(g, rows):
            g_out[g] = mm(turned_g[rows], gb[...]).astype(BF16)

        each_rows(G, m.FFS, multiply_out)

        slope, x, in_w, qkv_parts = (load.get() for load in loads[4:8])
        step = m.cs

        def add_parts(parts, own, count):
            for t in range(count):
                rows = pl.ds(t * step, step)
                total = parts[0, rows].astype(F32)
                for g in range(1, G):
                    total = total + parts[g, rows].astype(F32)
                own[t] = total.astype(BF16)

        add_parts(qkv_parts, qkv_own, m.T)
        if m.even:
            proj_own = scratch[16]
            add_parts(loads[8].get(), proj_own, m.R)
        mean = means[...][:, :1]
        cross = add_up()[:, :1]
        slopes[...] = gain * ratio[...] + 1.0
        shifts[...] = (scaled / mean - cross / (m.FF * mean * mean)) / norms[...]
        gains = jnp.sum(moments[pl.ds(0, m.D)] * ratio[pl.ds(0, m.D)], axis=0, keepdims=True)
        biases = moments[pl.ds(m.D, 1)]
        moments[pl.ds(m.D + 1, 1)] = jnp.zeros((1, FL), F32)
        flow.swap_team(p, qkv_own, qkv_team)
        if m.even:
            for number in range(G):
                to = lax.rem(p.q + number, G)
                flow.post(
                    proj_own.at[to],
                    far_out[4].at[p.q],
                    {"grp": p.z, "duo": p.c, "rows": to},
                    when=None if number else p.q != p.z,
                )
            flow.keep(proj_own.at[p.z], far_out[4].at[p.q], p.q == p.z)

        @pl.loop(0, m.D * per)
        def _(number):
            rows = pl.ds(pl.multiple_of(number * N, 16), N)
            item = number // per
            inside = pl.ds(pl.multiple_of((number - item * per) * N, 16), N)
            one = pl.ds(item, 1)
            grad = grads[rows] * slopes[one] + keep[item, inside] * (active[rows] * shifts[one])
            low = (grad * slope[rows]).astype(BF16)
            hidden[rows] = low
            moments[pl.ds(m.D + 1, 1)] += jnp.sum(low.astype(F32), axis=0, keepdims=True)

        inner = moments[pl.ds(m.D + 1, 1)]
        f_own[...] = jnp.zeros_like(f_own)
        for g in range(G):
            lanes = slice(g * m.FFS, (g + 1) * m.FFS)
            for row, values in enumerate((inner, gains, biases)):
                f_own[g, pl.ds(row, 1)] = values[:, lanes]
        flow.swap_group(p, f_own, f_parts)
        line = LineReduce(flow, p, part, back, mate, passed, landed)

        def produce(block):
            @pl.loop(0, m.D)
            def _(d):
                rows = pl.ds(pl.multiple_of(d * m.pixels + block * N, 16), N)
                part[d, block] = mm_t(hidden[rows], in_w[...]).astype(BF16)

        turned_x[...] = x[...].T
        first = flow.take(G - 1)

        def send_in(number):
            g = lax.rem(p.q + 1 + number, G)
            return flow.copy(g_in.at[g], in_parts.at[p.q], {"grp": g}, first + number)

        def between(number):
            if number != 1:
                return

            @pl.loop(0, G)
            def _(number):
                g = lax.rem(p.q + 1 + number, G)
                rows = pl.ds(pl.multiple_of(g * rows_in, 16), rows_in)
                g_in[g] = mm(turned_x[rows], hidden[...]).astype(BF16)
                pl.when(number < G - 1)(lambda: send_in(number).start())

            flow.keep(g_in.at[p.q], in_parts.at[p.q])

        line.run(produce, between)
        for number in range(G - 1):
            send_in(number).wait_recv()
            send_in(number).wait_send()

    near_out = [((N, C), F32), ((G, m.FFS, C), BF16)]
    far_out = [
        ((G, rows_in, FL), BF16),
        ((G, 8, m.FFS), F32),
        (grad_map.shape, BF16),
        ((m.T, m.cs, 3 * m.HW), BF16),
    ]
    scratch = [
        pltpu.VMEM((m.T, 8, 128), F32),
        pltpu.VMEM((8, 128), F32),
        pltpu.VMEM((8, FL), F32),
        pltpu.VMEM((8, FL), F32),
        pltpu.VMEM((8, FL), F32),
        pltpu.VMEM((m.D * m.pixels, FL), F32),
        pltpu.VMEM((m.D * m.pixels, FL), BF16),
    ]
    scratch += reduce_buffers(m, N, C)
    scratch += [
        pltpu.VMEM((FL, m.D * m.pixels), BF16),
        pltpu.VMEM((C, m.D * m.pixels), BF16),
        pltpu.VMEM((G, rows_in, FL), BF16),
        pltpu.VMEM((G, 8, m.FFS), F32),
        pltpu.VMEM((m.T, m.cs, 3 * m.HW), BF16),
    ]
    if m.even:
        far_out.append(((G, m.cs, wide), BF16))
        scratch.append(pltpu.VMEM((m.R, m.cs, wide), BF16))
    return fused_kernel(
        9,
        "feed_forward_back",
        lambda p: common_greet(p) + (spread_greet(m, p) if m.even else []),
        act,
        near,
        loads,
        far,
        near_out,
        far_out,
        scratch,
        2 * (m.T - 1) + 4 * (G - 1) + reduce_sems(m) + (G if m.even else 0),
        7,
    )


def tail_kernel(m, grad_low, tiny, g_out, in_parts, map_parts):
    loads = [in_parts, map_parts]
    far = [grad_low, tiny, g_out]
    N, C, G, T = m.N, m.C, m.G, m.T

    def act(p, flow, near, loads, far, near_out, far_out, scratch):
        low, tiny, g_out = far
        edges, tiny_all, in_team, map_team, out_parts = far_out
        in_own, map_own, tiny_in, tiny_own = scratch
        for block, to, sends, lands in (
            (low.at[pl.ds(N - EDGE, EDGE)], p.z + 1, p.z < p.R - 1, p.z > 0),
            (low.at[pl.ds(0, EDGE)], p.z - 1, p.z > 0, p.z < p.R - 1),
        ):
            slot = jnp.where(to > p.z, 0, 1)
            flow.post(block, edges.at[slot], {"rows": to}, when=sends, lands=lands)
        posts = flow.swap_team(p, tiny, tiny_in)
        flow.swap_group(p, g_out, out_parts)
        for load, own, step in ((loads[0], in_own, m.cs), (loads[1], map_own, m.mp)):
            parts = load.get()

            def add(t, rows, parts=parts, own=own):
                total = parts[0, rows].astype(F32)
                for g in range(1, G):
                    total = total + parts[g, rows].astype(F32)
                own[t] = total.astype(BF16)

            each_rows(T, step, add)

        flow.swap_team(p, in_own, in_team)
        flow.swap_team(p, map_own, map_team)
        for item in posts:
            flow.land(item)
        flow.settle_kept()
        for d in range(m.D):
            for g in range(G):
                total = tiny_in[d * m.R, g]
                for r in range(1, m.R):
                    total = total + tiny_in[d * m.R + r, g]
                tiny_own[g, d] = total
        flow.swap_group(p, tiny_own, tiny_all)

    return fused_kernel(
        11,
        "tail",
        common_greet,
        act,
        [],
        loads,
        far,
        [],
        [
            ((2, EDGE, C), BF16),
            ((G, m.D) + tiny.shape[2:], F32),
            ((T, m.cs, m.FL), BF16),
            ((T, m.mp, m.HW), BF16),
            (g_out.shape, BF16),
        ],
        [
            pltpu.VMEM((T, m.cs, m.FL), BF16),
            pltpu.VMEM((T, m.mp, m.HW), BF16),
            pltpu.VMEM(tiny.shape, F32),
            pltpu.VMEM((G, m.D) + tiny.shape[2:], F32),
        ],
        2 + 3 * (T - 1) + 2 * (G - 1),
        5,
    )


def pad_rows(values, rows):
    return jnp.pad(values, ((0, rows - values.shape[0]),) + ((0, 0),) * (values.ndim - 1))


def body(
    latents,
    clip_tokens,
    time_embed,
    bucket_ids,
    heights,
    widths,
    text_mask,
    conv_weight,
    conv_bias,
    in_weight,
    in_bias,
    grn_gain,
    grn_bias,
    out_weight,
    out_bias,
    time_weight,
    time_bias,
    map_weight,
    map_bias,
    qkv_weight,
    qv_bias,
    proj_weight,
    proj_bias,
    cotangent,
):
    m = Sizes(latents, clip_tokens, in_weight, in_bias, conv_bias, map_weight)
    G, D, R, T, N, C = m.G, m.D, m.R, m.T, m.N, m.C
    pixels, texts, FFS, FL, FF, HW = m.pixels, m.texts, m.FFS, m.FL, m.FF, m.HW
    cs, ms, mp, sp, even, Q = m.cs, m.ms, m.mp, m.sp, m.even, m.Q
    q, c, z = (lax.axis_index(axis) for axis in AXES)
    head_slice = D * z + c

    vectors = [conv_bias, out_bias, map_bias, proj_bias, qv_bias]
    fvectors = [in_bias, grn_gain, grn_bias]
    in_cut, qkv_cut, map_cut, clip_pad, masked, grad_result, small, fvec = cut_kernel(
        m,
        [heights, widths, bucket_ids, in_weight, qkv_weight, map_weight, clip_tokens, latents]
        + [cotangent, conv_weight]
        + vectors
        + [time_embed, text_mask]
        + fvectors,
    )
    latents = latents[0]
    cotangent = cotangent[0]

    def swap_edges(plan, src, dst):
        p = plan.p
        for block, to, sends, lands in (
            (src.at[pl.ds(src.shape[0] - EDGE, EDGE)], p.z + 1, p.z < R - 1, p.z > 0),
            (src.at[pl.ds(0, EDGE)], p.z - 1, p.z > 0, p.z < R - 1),
        ):
            slot = jnp.where(to > p.z, 0, 1)
            plan.add(block, dst.at[slot], {"rows": to}, when=sends, lands=lands)

    outs = front_kernel(
        m,
        time_weight,
        time_bias[None],
        masked,
        small,
        fvec,
        in_cut,
        out_weight,
        map_cut,
        qkv_cut,
        clip_pad,
        proj_weight,
    )
    norms, total, silu, mapped_s, normed_all, in_full, active, slope = outs[:8]
    norm_hat, norm_inv, vec, fv, key_keep, keep, bias, embed, edges, _ = outs[8:18]
    out_full, qkv_rows, _, mod_all = outs[18:22]
    proj_part = outs[22].reshape(HW, C // G) if even else None
    normed_all = normed_all.reshape(D * pixels, C)
    in_full = in_full.reshape(C, FL)
    out_full = out_full.reshape(FL, C)
    outs = branch_kernel(
        m,
        active,
        norms,
        total,
        out_full,
        fv,
        latents,
        keep,
        vec,
        mod_all,
        qkv_rows.reshape(T * cs, 3 * HW),
        mapped_s,
        proj_part,
    )
    grn_out, after_res, two_hat, two_inv, _, ratio, means, mods, two_all, mapped = outs[:10]
    qkv_full = outs[10].reshape(C, 3 * HW)
    if even:
        proj_s = outs[11]
    else:
        proj_whole = lax.all_gather(proj_weight, AXES, axis=0, tiled=True)
        proj_s = lax.dynamic_slice_in_dim(proj_whole, head_slice * HW, HW, axis=0)[None]
    result, two_part, mapped_part, grad_qkv, grad_proj, qkv_bias_grad = attention_kernel(
        m,
        two_all.reshape(D, pixels, C),
        grad_result,
        mapped.reshape(T, D, texts, HW),
        qkv_full,
        proj_s,
        bias,
        key_keep,
    )
    outs = attended_kernel(
        m,
        two_part.reshape(D, R, N, C),
        mapped_part.reshape(D, R, D * texts, HW),
        result,
        cotangent,
        grad_result,
        two_hat,
        two_inv,
        after_res,
        mods,
        keep,
        vec,
        grad_qkv.reshape(G, T * cs, 3 * HW),
        grad_proj,
    )
    output, grad_after, _, grad_modulate, vec_sums, grad_mapped, gb_all, qkv_parts = outs[:8]
    if even:
        proj_parts = outs[8]
    else:
        proj_parts = None
        spread = jnp.zeros((C, C), F32)
        spread = lax.dynamic_update_slice_in_dim(
            spread, grad_proj[0].astype(F32), head_slice * HW, axis=0
        )
        proj_team = lax.psum_scatter(spread, AXES, scatter_dimension=0, tiled=True)[None]
    grad_map, map_bias_grad = text_back_kernel(m, silu, grad_mapped)
    outs = back_kernel(
        m,
        gb_all.reshape(D * pixels, C),
        out_full,
        active,
        slope,
        grn_out,
        normed_all,
        in_full,
        norms,
        ratio,
        means,
        fv,
        key_keep,
        qkv_parts,
        proj_parts,
        grad_map,
    )
    grad_conv_in, grad_out, in_parts, f_sum, map_parts, qkv_team = outs[:6]
    if even:
        proj_team = outs[6]

    def placed(values, start):
        return lax.dynamic_update_slice_in_dim(jnp.zeros((C,), F32), values, start, axis=0)

    vec_grads = jnp.concatenate(
        [vec_sums[:2], placed(map_bias_grad[0], (c * R + z) * HW)[None]], axis=0
    )
    qv_grads = jnp.stack(
        [
            placed(qkv_bias_grad[0, :HW], head_slice * HW),
            placed(qkv_bias_grad[0, 2 * HW :], head_slice * HW),
        ]
    )
    grad_conv, conv_low, tiny = conv_back_kernel(
        m,
        bucket_ids,
        grad_conv_in,
        norm_hat,
        norm_inv,
        edges,
        masked,
        vec_grads,
        qv_grads,
        grad_modulate,
    )
    conv_edges, tiny_all, in_team, map_team, out_parts = tail_kernel(
        m, conv_low, tiny, grad_out, in_parts, map_parts
    )
    trows = 16
    tiny_all = tiny_all.reshape(G * D, trows, 128)
    tiny_sum = jnp.sum(tiny_all, axis=0)
    modulate_items = tiny_all[:, 14, : 2 * cs]
    embed_all = embed[: G * D, : time_embed.shape[1]]
    grad_time = lax.dot_general(
        embed_all,
        modulate_items,
        (((0,), (0,)), ((), ())),
        precision=lax.Precision.HIGHEST,
    )
    grad_time_bias = jnp.sum(modulate_items, axis=0)
    outs = finish_kernel(
        m,
        bucket_ids,
        conv_edges,
        conv_low,
        grad_after,
        keep,
        vec,
        in_team,
        qkv_team,
        map_team,
        proj_team,
        out_parts,
    )
    grad_latents, grad_in_shard, grad_qkv_shard, grad_map_shard, grad_proj_shard = outs[:5]
    grad_out_shard = outs[5]
    f_total = jnp.sum(f_sum, axis=0)
    return (
        output[None],
        grad_latents,
        tiny_sum[:9, :cs],
        tiny_sum[9, :cs],
        grad_in_shard,
        f_total[0],
        f_total[1],
        f_total[2],
        grad_out_shard,
        tiny_sum[10, :cs],
        grad_time,
        grad_time_bias,
        grad_map_shard,
        tiny_sum[12, :cs],
        grad_qkv_shard,
        tiny_sum[13, : 2 * cs],
        grad_proj_shard,
        tiny_sum[11, :cs],
    )


def solution(mesh):
    items, rows = mesh.devices.shape
    fine = Mesh(mesh.devices.reshape(items // 2, 2, rows), AXES)
    item = ("grp", "duo")
    full = AXES
    ins = (
        P(item, "rows", None),
        P(item, "rows", None),
        P(item, None),
        P(item),
        P(item),
        P(item),
        P(item, None),
        P(None, full),
        P(full),
        P(full, None),
        P(full),
        P(full),
        P(full),
        P(full, None),
        P(full),
        P(None, full),
        P(full),
        P(full, None),
        P(full),
        P(full, None),
        P(full),
        P(full, None),
        P(full),
        P(item, "rows", None),
    )
    outs = (
        P(item, "rows", None),
        P(item, "rows", None),
        P(None, full),
        P(full),
        P(full, None),
        P(full),
        P(full),
        P(full),
        P(full, None),
        P(full),
        P(None, full),
        P(full),
        P(full, None),
        P(full),
        P(full, None),
        P(full),
        P(full, None),
        P(full),
    )
    return jax.shard_map(body, mesh=fine, in_specs=ins, out_specs=outs, check_vma=False)
```

```python
import functools

import jax
import jax.numpy as jnp
from jax import lax
from jax.experimental import pallas as pl
from jax.experimental.pallas import tpu as pltpu
from jax.sharding import Mesh, PartitionSpec as P

HEAD = 64
TXT = 77
UNIT = 8
EDGE = 48

norm_eps = 1e-06
grn_eps = 1e-06
masked_score = -1000000000.0

AXES = ("grp", "duo", "rows")
MESH_ID = pl.DeviceIdType.MESH
F32 = jnp.float32
BF16 = jnp.bfloat16


class Place:
    def __init__(self):
        self.q, self.c, self.z = (lax.axis_index(axis) for axis in AXES)
        self.G, self.D, self.R = (lax.axis_size(axis) for axis in AXES)

    def team(self):
        for step in range(1, self.D * self.R):
            dc, dz = step // self.R, step % self.R
            yield lax.rem(self.c + dc, self.D), lax.rem(self.z + dz, self.R)

    def groups(self):
        for step in range(1, self.G):
            yield lax.rem(self.q + step, self.G)


def signal_all(barrier, targets):
    for target in targets:
        pl.semaphore_signal(barrier, inc=1, device_id=target, device_id_type=MESH_ID)


def guarded(when, act):
    if when is None:
        act()
    else:
        pl.when(when)(act)


class Flow:
    def __init__(self, send_sem, recv_sem, local_sem=None):
        self.send_sem, self.recv_sem, self.local_sem = send_sem, recv_sem, local_sem
        self.used = 0
        self.kept = 0
        self.open = []
        self.posted = []
        self.lines = []
        self.stays = []

    def take(self, count=1):
        at = self.used
        self.used += count
        return at

    def copy(self, src, dst, target, at):
        return pltpu.make_async_remote_copy(
            src_ref=src,
            dst_ref=dst,
            send_sem=self.send_sem.at[at],
            recv_sem=self.recv_sem.at[at],
            device_id=target,
            device_id_type=MESH_ID,
        )

    def post(self, src, dst, target, when=None, lands=None):
        copy = self.copy(src, dst, target, self.take())
        guarded(when, copy.start)
        item = Posted(copy, when if lands is None else lands)
        self.posted.append(item)
        self.open.append((copy.wait_send, when))
        return item

    def land(self, item):
        if not item.landed:
            item.landed = True
            guarded(item.lands, item.copy.wait_recv)

    def keep(self, src, dst, when=None, now=False):
        copy = pltpu.make_async_copy(src, dst, self.local_sem.at[self.kept])
        self.kept += 1
        guarded(when, copy.start)
        if now:
            guarded(when, copy.wait)
        else:
            self.stays.append((copy.wait, when))

    def square(self, p, src, dst):
        across = p.q + 1 - 2 * lax.rem(p.q, 2)
        along = lax.rem(p.q + 2, 4)
        one = self.post(src, dst.at[p.q], {"grp": across})
        two = self.post(src, dst.at[p.q], {"grp": along})
        half = dst.shape[1] // 2
        top, bottom = pl.ds(0, half), pl.ds(half, half)

        def relay():
            self.land(one)
            block = dst.at[across, top]
            first = self.post(block, block, {"grp": along})
            self.land(two)
            block = dst.at[along, bottom]
            second = self.post(block, block, {"grp": across})
            return first, second

        return relay

    def settle_kept(self):
        for act, when in self.stays:
            guarded(when, act)
        self.stays = []

    def gather_team(self, p, src, dst):
        mine = p.c * p.R + p.z
        self.keep(src, dst.at[mine])
        return [self.post(src, dst.at[mine], {"duo": c, "rows": z}) for c, z in p.team()]

    def gather_group(self, p, src, dst):
        self.keep(src, dst.at[p.q])
        return [self.post(src, dst.at[p.q], {"grp": q}) for q in p.groups()]

    def swap_group(self, p, src, dst):
        self.keep(src.at[p.q], dst.at[p.q])
        for q in p.groups():
            self.post(src.at[q], dst.at[p.q], {"grp": q})

    def swap_team(self, p, src, dst):
        mine = p.c * p.R + p.z
        self.keep(src.at[mine], dst.at[mine])
        return [
            self.post(src.at[c * p.R + z], dst.at[mine], {"duo": c, "rows": z}) for c, z in p.team()
        ]

    def finish(self):
        self.settle_kept()
        for line in self.lines:
            line.settle(line.p.R)
        for item in self.posted:
            self.land(item)
        for act, when in self.open:
            guarded(when, act)


class LineGather:
    def __init__(self, flow, place, src, dst):
        self.flow, self.p, self.src, self.dst = flow, place, src, dst
        self.up = flow.take(place.R - 1)
        self.down = flow.take(place.R - 1)
        self.side = flow.take(2 * place.R - 1)

    def send(self, block, hop, direction):
        p, dst = self.p, self.dst
        src = self.src if hop == 0 else dst.at[p.c, block]
        at = (self.up if direction > 0 else self.down) + hop
        return self.flow.copy(src, dst.at[p.c, block], {"rows": p.z + direction}, at)

    def across(self, block, number):
        p, dst = self.p, self.dst
        src = self.src if isinstance(number, int) and number == 0 else dst.at[p.c, block]
        other = {"duo": lax.rem(p.c + 1, p.D)}
        return self.flow.copy(src, dst.at[p.c, block], other, self.side + number)

    def start(self):
        p = self.p
        for direction, ok in ((1, p.z < p.R - 1), (-1, p.z > 0)):
            copy = self.send(p.z, 0, direction)
            guarded(ok, copy.start)
            self.flow.open.append((copy.wait_send, ok))
        copy = self.across(p.z, 0)
        copy.start()
        self.flow.open.append((copy.wait_send, None))
        self.flow.lines.append(self)
        self.settled = 0

    def hop(self, step):
        p = self.p
        for direction, number in ((1, step), (-1, p.R - 1 + step)):
            block = p.z - direction * step
            ok = (block >= 0) if direction > 0 else (block < p.R)
            last = (p.z < p.R - 1) if direction > 0 else (p.z > 0)
            arrived = self.send(block, step - 1, direction)
            side = self.across(block, number)

            def relay(arrived=arrived, side=side, block=block, direction=direction, last=last):
                arrived.wait_recv()
                if step < p.R - 1:
                    pl.when(last)(self.send(block, step, direction).start)
                side.start()

            pl.when(ok)(relay)
            if step < p.R - 1:
                self.flow.open.append((self.send(block, step, direction).wait_send, ok & last))
            self.flow.open.append((side.wait_send, ok))


    def nth(self, number):
        p = self.p
        reach = [p.z]
        for step in range(1, p.R):
            reach += [p.z - step, p.z + step]
        seen, found = 0, jnp.int32(0)
        for block in reach:
            ok = (block >= 0) & (block < p.R)
            found = jnp.where(ok & (seen == number), block, found)
            seen = seen + jnp.where(ok, 1, 0)
        return found

    def settle(self, upto):
        p = self.p
        while self.settled < upto:
            block = self.nth(self.settled)
            number = jnp.where(block <= p.z, p.z - block, p.R - 1 + block - p.z)
            self.across(block, number).wait_recv()
            self.settled += 1


class LineReduce:
    def __init__(self, flow, place, part, total_ref, mate, passed, landed):
        self.flow, self.p, self.part, self.total = flow, place, part, total_ref
        self.mate, self.passed, self.landed = mate, passed, landed
        self.side = flow.take(place.R)
        self.line = flow.take(2 * place.R)

    def across(self, block):
        p = self.p
        other = lax.rem(p.c + 1, p.D)
        return self.flow.copy(
            self.part.at[other, block], self.mate.at[block], {"duo": other}, self.side + block
        )

    def along(self, upward, block):
        p = self.p
        way = jnp.where(upward, 1, 0)
        target = {"rows": jnp.where(upward, p.z + 1, p.z - 1)}
        return self.flow.copy(
            self.passed.at[way, block],
            self.landed.at[way, block],
            target,
            self.line + way * p.R + block,
        )

    def steps(self):
        p = self.p
        low = p.z < p.R // 2
        for k in range(p.R - 1):
            for first in (True, False):
                upward = low if first else jnp.logical_not(low)
                block = jnp.where(upward, p.R - 1 - k, k)
                yield upward, block, jnp.where(upward, block > p.z, block < p.z)

    def start(self):
        p = self.p
        for k in range(p.R):
            block = jnp.where(p.z < p.R // 2, p.R - 1 - k, k)
            copy = self.across(block)
            copy.start()
            self.flow.open.append((copy.wait_send, None))

    def rows_of(self, act):
        count = self.part.shape[2]
        step = 16

        @pl.loop(0, count // step)
        def _(number):
            act(pl.ds(pl.multiple_of(number * step, step), step))

    def offer(self, block):
        copy = self.across(block)
        copy.start()
        self.flow.open.append((copy.wait_send, None))

    def early(self):
        for upward, block, ok in self.steps():
            behind = jnp.where(upward, self.p.z > 0, self.p.z < self.p.R - 1)
            self.step(upward, block, ok & jnp.logical_not(behind), False)

    def later(self):
        for upward, block, ok in self.steps():
            behind = jnp.where(upward, self.p.z > 0, self.p.z < self.p.R - 1)
            yield functools.partial(self.step, upward, block, ok & behind, True)

    def step(self, upward, block, ok, relays=None):
        p = self.p
        way = jnp.where(upward, 1, 0)
        behind = jnp.where(upward, p.z > 0, p.z < p.R - 1)

        def act():
            self.across(block).wait_recv()
            if relays is False:

                def add(rows):
                    self.passed[way, block, rows] = (
                        self.part[p.c, block, rows].astype(F32) + self.mate[block, rows].astype(F32)
                    ).astype(BF16)

                self.rows_of(add)
                self.along(upward, block).start()
                return

            @pl.when(behind)
            def _():
                self.along(upward, block).wait_recv()

                def add(rows):
                    self.passed[way, block, rows] = (
                        self.part[p.c, block, rows].astype(F32)
                        + self.mate[block, rows].astype(F32)
                        + self.landed[way, block, rows].astype(F32)
                    ).astype(BF16)

                self.rows_of(add)

            if relays is None:

                @pl.when(jnp.logical_not(behind))
                def _():
                    def add(rows):
                        self.passed[way, block, rows] = (
                            self.part[p.c, block, rows].astype(F32)
                            + self.mate[block, rows].astype(F32)
                        ).astype(BF16)

                    self.rows_of(add)

            self.along(upward, block).start()

        pl.when(ok)(act)
        self.flow.open.append((self.along(upward, block).wait_send, ok))

    def close(self):
        p = self.p
        self.across(p.z).wait_recv()

        def base(rows):
            self.total[rows] = self.part[p.c, p.z, rows].astype(F32) + self.mate[
                p.z, rows
            ].astype(F32)

        self.rows_of(base)
        for way, ok in ((1, p.z > 0), (0, p.z < p.R - 1)):

            def more(way=way):
                self.along(way == 1, p.z).wait_recv()

                def add(rows):
                    self.total[rows] += self.landed[way, p.z, rows].astype(F32)

                self.rows_of(add)

            pl.when(ok)(more)

    def steps_all(self):
        self.early()
        for act in self.later():
            act()
        self.close()

    def run(self, produce=None, between=None):
        p = self.p
        if produce is None:
            self.steps_all()
            return
        ready = 0

        def more():
            block = line_order(p, ready)
            produce(block)
            copy = self.across(block)
            copy.start()
            self.flow.open.append((copy.wait_send, None))

        for number, (upward, block, ok) in enumerate(self.steps()):
            while ready < min(number + 2, p.R):
                more()
                ready += 1
            self.step(upward, block, ok)
            if between is not None:
                between(number)
        self.close()


def team_kernel(
    ident, name, plan, arrays, results, gathers=(), reduces=(), messages=0, local=1, late=None
):
    D, R = lax.axis_size("duo"), lax.axis_size("rows")
    count_a, count_g, count_r = len(arrays), len(gathers), len(reduces)
    extra = 0 if late is None else 1
    total_sems = messages + (count_g + extra) * (4 * R - 3) + count_r * 3 * R

    def kernel(*refs):
        refs = list(refs)
        ins = refs[:count_a]
        g_in = refs[count_a : count_a + count_g]
        r_in = refs[count_a + count_g : count_a + count_g + count_r]
        refs = refs[count_a + count_g + count_r :]
        outs = refs[: len(results)]
        refs = refs[len(results) :]
        late_out = refs[:extra]
        g_out = refs[extra : extra + count_g]
        r_out = refs[extra + count_g : extra + count_g + count_r]
        refs = refs[extra + count_g + count_r :]
        send_sem, recv_sem, local_sem = refs[:3]
        buffers = refs[3:]
        p = Place()
        flow = Flow(send_sem, recv_sem)
        greet, direct, stay = plan(p, ins, outs)
        barrier = pltpu.get_barrier_semaphore()
        waits = 0
        for target, when in greet:
            if when is None:
                waits = waits + 1
            else:
                waits = waits + jnp.where(when, 1, 0).astype(jnp.int32)
            guarded(when, lambda target=target: signal_all(barrier, [target]))
        pl.semaphore_wait(barrier, waits)
        lines = [LineGather(flow, p, src, dst) for src, dst in zip(g_in, g_out)]
        sums = [
            LineReduce(flow, p, src, dst, *buffers[3 * n : 3 * n + 3])
            for n, (src, dst) in enumerate(zip(r_in, r_out))
        ]
        base = flow.take(messages)
        copies = {}
        arrived = set()

        stays = []

        def landed(number):
            if number not in arrived:
                arrived.add(number)
                guarded(copies[number][2], copies[number][0].wait_recv)

        def run_stage(stage):
            for number, (src, dst, target, after, when, when_stage, lands) in enumerate(direct):
                if when_stage != stage:
                    continue
                for earlier in after:
                    landed(earlier)
                copy = flow.copy(src, dst, target, base + number)
                guarded(when, copy.start)
                copies[number] = (copy, when, lands)
            if late is not None and late[1] == stage:
                for number in range(late[2]):
                    landed(number)
                stays[0][0].wait()
                line = LineGather(flow, p, outs[late[0]], late_out[0])
                line.start()
                own = pltpu.make_async_copy(
                    outs[late[0]], late_out[0].at[p.c, p.z], local_sem.at[local + count_g]
                )
                own.start()
                stays[0] = (own, None)
                if stage:
                    for earlier in range(1, stage + 1):
                        line.hop(earlier)
                lines.append(line)

        for item in sums:
            item.start()
        for line in lines:
            line.start()
        for number, (src, dst, when) in enumerate(
            list(stay) + [(src, dst.at[p.c, p.z], None) for src, dst in zip(g_in, g_out)]
        ):
            copy = pltpu.make_async_copy(src, dst, local_sem.at[number])
            guarded(when, copy.start)
            stays.append((copy, when))
        run_stage(0)
        for step in range(1, R):
            for line in lines:
                line.hop(step)
            run_stage(step)
        for item in sums:
            item.run()
        for copy, when in stays:
            guarded(when, copy.wait)
        for number in copies:
            landed(number)
        for copy, when, _ in copies.values():
            guarded(when, copy.wait_send)
        flow.finish()

    spot = pl.BlockSpec(memory_space=pl.ANY)
    near = pl.BlockSpec(memory_space=pltpu.VMEM)
    out_shape = [jax.ShapeDtypeStruct(shape, kind) for shape, kind in results]
    if late is not None:
        shape, kind = results[late[0]]
        out_shape.append(jax.ShapeDtypeStruct((D, R) + shape, kind))
    out_shape += [jax.ShapeDtypeStruct((D, R) + g.shape, g.dtype) for g in gathers]
    out_shape += [jax.ShapeDtypeStruct(r.shape[2:], F32) for r in reduces]
    scratch = [
        pltpu.SemaphoreType.DMA((total_sems,)),
        pltpu.SemaphoreType.DMA((total_sems,)),
        pltpu.SemaphoreType.DMA((local + count_g + extra,)),
    ]
    for r in reduces:
        block = r.shape[1:]
        scratch += [
            pltpu.VMEM(block, BF16),
            pltpu.VMEM((2,) + block, BF16),
            pltpu.VMEM((2,) + block, BF16),
        ]
    return pl.pallas_call(
        kernel,
        out_shape=out_shape,
        in_specs=[spot] * (count_a + count_g) + [near] * count_r,
        out_specs=[spot] * (len(results) + extra + count_g) + [near] * count_r,
        scratch_shapes=scratch,
        compiler_params=pltpu.CompilerParams(
            collective_id=ident, has_side_effects=True, vmem_limit_bytes=56 * 2**20
        ),
        name=name,
    )(*arrays, *gathers, *reduces)


def team_greet(p):
    return [({"duo": c, "rows": z}, None) for c, z in p.team()]


def group_greet(p):
    return [({"grp": q}, None) for q in p.groups()]


class Plan:
    def __init__(self, p):
        self.p = p
        self.messages, self.local, self.greet = [], [], []

    def add(self, src, dst, target, after=(), when=None, stage=0, lands=None):
        self.messages.append((src, dst, target, after, when, stage, when if lands is None else lands))
        return len(self.messages) - 1

    def team_swap(self, src, dst, stage=0):
        p = self.p
        mine = p.c * p.R + p.z
        for c, z in p.team():
            self.add(src.at[c * p.R + z], dst.at[mine], {"duo": c, "rows": z}, stage=stage)
        self.local.append((src.at[mine], dst.at[mine], None))

    def team_gather(self, src, dst, stage=0):
        p = self.p
        mine = p.c * p.R + p.z
        for c, z in p.team():
            self.add(src, dst.at[mine], {"duo": c, "rows": z}, stage=stage)
        self.local.append((src, dst.at[mine], None))

    def group_gather(self, src, dst, late=None):
        p = self.p
        self.local.append((src, dst.at[p.q], None))
        if late is None or p.G != 4:
            for q in p.groups():
                self.add(src, dst.at[p.q], {"grp": q})
            return
        across = p.q + 1 - 2 * lax.rem(p.q, 2)
        along = lax.rem(p.q + 2, 4)
        one = self.add(src, dst.at[p.q], {"grp": across})
        two = self.add(src, dst.at[p.q], {"grp": along})
        half = src.shape[0] // 2
        top, bottom = pl.ds(0, half), pl.ds(half, half)
        self.add(
            dst.at[across, top], dst.at[across, top], {"grp": along}, after=(one,), stage=late
        )
        self.add(
            dst.at[along, bottom],
            dst.at[along, bottom],
            {"grp": across},
            after=(two,),
            stage=late,
        )

    def group_swap(self, src, dst, stage=0):
        p = self.p
        for q in p.groups():
            self.add(src.at[q], dst.at[p.q], {"grp": q}, stage=stage)
        self.local.append((src.at[p.q], dst.at[p.q], None))

    def done(self):
        p = self.p
        return team_greet(p) + group_greet(p) + self.greet, self.messages, self.local


def layer_stats(values):
    center = values - jnp.mean(values, axis=-1, keepdims=True)
    spread = jnp.mean(center * center, axis=-1, keepdims=True)
    inverse = lax.rsqrt(spread + norm_eps)
    return center * inverse, inverse


def layer_back(grad, hat, inverse):
    first = jnp.mean(grad, axis=-1, keepdims=True)
    second = jnp.mean(grad * hat, axis=-1, keepdims=True)
    return inverse * (grad - first - hat * second)


def mm(left, right):
    return jnp.dot(left, right, preferred_element_type=F32)


def mm_t(left, right):
    return lax.dot_general(left, right, (((1,), (1,)), ((), ())), preferred_element_type=F32)


def t_mm(left, right):
    return lax.dot_general(left, right, (((0,), (0,)), ((), ())), preferred_element_type=F32)


def columns_of(bucket_ids):
    return jnp.where(
        bucket_ids == 0, 9 * UNIT // 2, jnp.where(bucket_ids == 1, 3 * UNIT, 9 * UNIT // 4)
    )


def pixel_mask(positions, height, width, cols):
    row_at = positions // cols
    col_at = positions % cols
    return ((row_at < height) & (col_at < width)).astype(F32)


def spots(shapes):
    return [jax.ShapeDtypeStruct(shape, kind) for shape, kind in shapes]


def local_kernel(name, kernel, arrays, results, scratch=(), scalars=0):
    near = pl.BlockSpec(memory_space=pltpu.VMEM)
    numbers = pl.BlockSpec(memory_space=pltpu.SMEM)
    return pl.pallas_call(
        kernel,
        out_shape=spots(results),
        in_specs=[numbers] * scalars + [near] * (len(arrays) - scalars),
        out_specs=[near] * len(results),
        scratch_shapes=list(scratch),
        compiler_params=pltpu.CompilerParams(vmem_limit_bytes=56 * 2**20),
        name=name,
    )(*arrays)


class Sizes:
    def __init__(self, latents, clip_tokens, in_weight, in_bias, conv_bias, map_weight):
        self.G, self.D, self.R = (lax.axis_size(axis) for axis in AXES)
        self.T = self.D * self.R
        self.S = self.T * self.G
        self.N, self.C = latents.shape[1:]
        self.pixels = self.R * self.N
        self.FFS = in_bias.shape[0]
        self.FL = self.G * self.FFS
        self.FF = in_weight.shape[1]
        self.cs = conv_bias.shape[0]
        self.ms = map_weight.shape[0]
        self.mp = -(-self.ms // 16) * 16
        self.slots = clip_tokens.shape[1]
        self.sp = -(-self.slots // 16) * 16
        self.texts = self.R * self.slots
        self.HW = self.C // self.T
        self.even = self.G == self.R
        self.Q = self.G if self.even else 1
        self.places = [(g, d, r) for g in range(self.G) for d in range(self.D) for r in range(self.R)]


def rows_cols(first, count, cols):
    position = (first + lax.broadcasted_iota(jnp.int32, (count, 1), 0)).astype(F32)
    row = jnp.floor((position + 0.5) / cols)
    return row, position - row * cols


def float_cols(bucket):
    return jnp.where(bucket == 0, 9.0 * UNIT / 2, jnp.where(bucket == 1, 3.0 * UNIT, 9.0 * UNIT / 4))


WIDTHS = (9 * UNIT // 2, 3 * UNIT, 9 * UNIT // 4)
SMALL = 16
VEC = 16
FACTS = 96


def cut_kernel(m, arrays):
    def kernel(h_ref, w_ref, b_ref, in_ref, qkv_ref, map_ref, clip_ref, lat_ref, cot_ref, cw_ref, *refs):
        vectors, refs = refs[:5], refs[5:]
        te_ref, tm_ref, f0, f1, f2 = refs[:5]
        in_out, qkv_out, map_out, clip_out, masked_out, gres_out, small_out, f_out, small, fv = refs[5:]
        for g in range(m.G):
            for t in range(m.T):
                start = m.FFS * (g * m.T + t)
                in_out[t, :, pl.ds(g * m.FFS, m.FFS)] = in_ref[:, pl.ds(start, m.FFS)]
        for d in range(m.D):
            for r in range(m.R):
                for j in range(3):
                    start = m.C * j + m.HW * (m.D * r + d)
                    qkv_out[d * m.R + r, :, pl.ds(j * m.HW, m.HW)] = qkv_ref[:, pl.ds(start, m.HW)]
        map_out[...] = jnp.zeros_like(map_out)
        for t in range(m.T):
            map_out[t, pl.ds(0, m.ms)] = map_ref[:, pl.ds(t * m.HW, m.HW)]
        clip_out[...] = jnp.zeros_like(clip_out)
        clip_out[pl.ds(0, m.slots)] = clip_ref[0]
        z = lax.axis_index("rows")
        row, col = rows_cols(z * m.N, m.N, float_cols(b_ref[0]))
        keep = (row < h_ref[0].astype(F32)) & (col < w_ref[0].astype(F32))
        masked_out[...] = jnp.where(keep, lat_ref[0].astype(F32), 0.0).astype(BF16)
        gres_out[...] = jnp.where(keep, cot_ref[0].astype(F32), 0.0).astype(BF16)
        small[...] = jnp.zeros_like(small)
        small[pl.ds(0, 9), pl.ds(0, m.cs)] = cw_ref[...].astype(F32)
        for number, ref in enumerate(vectors):
            small[pl.ds(9 + number, 1), pl.ds(0, ref.shape[0])] = ref[...].astype(F32).reshape(1, -1)
        small[pl.ds(14, 1), pl.ds(0, te_ref.shape[1])] = te_ref[...].astype(F32)
        lane = lax.broadcasted_iota(jnp.int32, (1, 128), 1)
        for number, ref in enumerate((h_ref, w_ref, b_ref)):
            fact = jnp.full((1, 128), ref[0]).astype(F32)
            row = small[pl.ds(14, 1)]
            small[pl.ds(14, 1)] = jnp.where(lane == FACTS + number, fact, row)
        small[pl.ds(15, 1), pl.ds(0, m.texts)] = tm_ref[...].astype(F32)
        small_out[...] = small[...].astype(BF16)
        fv[...] = jnp.zeros_like(fv)
        for number, ref in enumerate((f0, f1, f2)):
            fv[pl.ds(number, 1)] = ref[...].astype(F32).reshape(1, -1)
        f_out[...] = fv[...].astype(BF16)

    return local_kernel(
        "cut_weights",
        kernel,
        arrays,
        [
            ((m.T, m.cs, m.FL), BF16),
            ((m.T, m.cs, 3 * m.HW), BF16),
            ((m.T, m.mp, m.HW), BF16),
            ((m.sp, arrays[6].shape[2]), BF16),
            ((m.N, m.C), BF16),
            ((m.N, m.C), BF16),
            ((SMALL, 128), BF16),
            ((16, m.FFS), BF16),
        ],
        [pltpu.VMEM((SMALL, 128), F32), pltpu.VMEM((16, m.FFS), F32)],
        scalars=3,
    )


def fill_extended(m, extended, edges_ref, mid_ref):
    z = lax.axis_index("rows")
    extended[pl.ds(0, EDGE)] = jnp.where(z > 0, edges_ref[0].astype(F32), 0.0)
    extended[pl.ds(EDGE, m.N)] = mid_ref[...].astype(F32)
    extended[pl.ds(EDGE + m.N, EDGE)] = jnp.where(z < m.R - 1, edges_ref[1].astype(F32), 0.0)


def each_bucket(bucket, act):
    for number, width in enumerate(WIDTHS):
        pl.when(bucket == number)(functools.partial(act, width))


def each_column_block(m, act):
    @pl.loop(0, m.C // 128)
    def _(number):
        act(pl.ds(pl.multiple_of(number * 128, 128), 128))


def tap_steps():
    return [(index, index // 3 - 1, index % 3 - 1) for index in range(9)]


def conv_back_kernel(m, b_ref, grad_in, hat, inv, edges, masked, vec_grads, map_grad, qv_grads, modulate_grads):
    def kernel(b_ref, g_ref, hat_ref, inv_ref, edges_ref, mid_ref, vec_ref, map_ref, qv_ref, gm_ref, grad, low, tiny, extended, vec):
        values = layer_back(g_ref[...], hat_ref[...], inv_ref[...])
        grad[...] = values
        low[...] = values.astype(BF16)
        fill_extended(m, extended, edges_ref, mid_ref)
        vec[pl.ds(9, 1)] = jnp.sum(values, axis=0, keepdims=True)
        vec[pl.ds(10, 2)] = vec_ref[pl.ds(0, 2)]
        vec[pl.ds(12, 1)] = map_ref[pl.ds(0, 1)]
        vec[pl.ds(13, 3)] = jnp.zeros((3, m.C), F32)
        z = lax.axis_index("rows")

        def taps(width):
            _, col = rows_cols(z * m.N, m.N, float(width))

            def block(lanes):
                value = grad[:, lanes]
                for index, dy, dx in tap_steps():
                    piece = extended[pl.ds(EDGE + dy * width + dx, m.N), lanes]
                    ok = (col + dx >= 0) & (col + dx < width)
                    vec[pl.ds(index, 1), lanes] = jnp.sum(
                        jnp.where(ok, piece, 0.0) * value, axis=0, keepdims=True
                    )

            each_column_block(m, block)

        each_bucket(b_ref[0], taps)
        tiny[...] = jnp.zeros_like(tiny)
        half = m.S // 2
        pair = 2 * m.cs
        for s, (g, d, r) in enumerate(m.places):
            t = d * m.R + r
            tiny[t, g, pl.ds(0, 13), pl.ds(0, m.cs)] = vec[pl.ds(0, 13), pl.ds(s * m.cs, m.cs)]
            side, at = pl.ds(s // half, 1), pl.ds(pair * (s % half), pair)
            tiny[t, g, pl.ds(13, 1), pl.ds(0, pair)] = qv_ref[side, at]
            tiny[t, g, pl.ds(14, 1), pl.ds(0, pair)] = gm_ref[side, at]

    return local_kernel(
        "convolve_back",
        kernel,
        [b_ref, grad_in, hat, inv, edges, masked, vec_grads, map_grad, qv_grads, modulate_grads],
        [((m.N, m.C), F32), ((m.N, m.C), BF16), ((m.T, m.G, 16, 128), F32)],
        [pltpu.VMEM((m.N + 2 * EDGE, m.C), F32), pltpu.VMEM((VEC, m.C), F32)],
        scalars=1,
    )


def finish_kernel(m, b_ref, edges, low, after, pix, vec, in_team, qkv_team, map_team, proj_team, out_parts, tiny_all, f_parts, embed, rdim):
    def kernel(b_ref, edges_ref, low_ref, after_ref, pix_ref, vec_ref, in_ref, qkv_ref, map_ref, proj_ref, parts_ref, tiny_ref, f_ref, te_ref,
               lat_out, in_out, qkv_out, map_out, proj_out, out_out, cw_out, time_out, *refs):
        singles, (extended,) = refs[:10], refs[10:]
        total = jnp.zeros(tiny_ref.shape[2:], F32)
        times = jnp.zeros((128, 128), F32)
        turned = te_ref[...].T
        for g in range(m.G):
            for d in range(m.D):
                item = tiny_ref[g, d]
                total = total + item
                at = m.D * g + d
                times = times + turned[:, at : at + 1] * item[14:15]
        cw_out[...] = total[:9, : m.cs]
        time_out[...] = times[:rdim, : 2 * m.cs]
        for number, ref in enumerate(singles[:6]):
            ref[...] = total[9 + number, : ref.shape[0]]
        sums = f_ref[0]
        for g in range(1, m.G):
            sums = sums + f_ref[g]
        for number, ref in enumerate(singles[6:9]):
            ref[...] = sums[number, :]
        singles[9][...] = total[15, :]
        fill_extended(m, extended, edges_ref, low_ref)
        z = lax.axis_index("rows")
        keep = pix_ref[...] > 0

        def taps(width):
            _, col = rows_cols(z * m.N, m.N, float(width))

            def block(lanes):
                total = jnp.zeros((m.N, 128), F32)
                for index, dy, dx in tap_steps():
                    piece = extended[pl.ds(EDGE - dy * width - dx, m.N), lanes]
                    ok = (col - dx >= 0) & (col - dx < width)
                    total = total + jnp.where(ok, piece, 0.0) * vec_ref[pl.ds(index, 1), lanes]
                lat_out[0, :, lanes] = after_ref[:, lanes] + jnp.where(keep, total, 0.0)

            each_column_block(m, block)

        each_bucket(b_ref[0], taps)
        for g in range(m.G):
            for t in range(m.T):
                start = m.FFS * (g * m.T + t)
                in_out[:, pl.ds(start, m.FFS)] = in_ref[t, :, pl.ds(g * m.FFS, m.FFS)].astype(F32)
        for d in range(m.D):
            for r in range(m.R):
                for j in range(3):
                    start = m.C * j + m.HW * (m.D * r + d)
                    qkv_out[:, pl.ds(start, m.HW)] = qkv_ref[
                        d * m.R + r, :, pl.ds(j * m.HW, m.HW)
                    ].astype(F32)
        for t in range(m.T):
            map_out[:, pl.ds(t * m.HW, m.HW)] = map_ref[t].astype(F32)[: m.ms]
        total = parts_ref[0].astype(F32)
        for g in range(1, m.G):
            total = total + parts_ref[g].astype(F32)
        out_out[...] = total
        wide = m.C // m.Q
        for n in range(m.Q):
            proj_out[:, pl.ds(n * wide, wide)] = proj_ref[n].astype(F32)

    return local_kernel(
        "finish",
        kernel,
        [b_ref, edges, low, after, pix, vec, in_team, qkv_team, map_team, proj_team, out_parts]
        + [tiny_all, f_parts, embed],
        [
            ((1, m.N, m.C), F32),
            ((m.cs, m.FF), F32),
            ((m.cs, 3 * m.C), F32),
            ((m.ms, m.C), F32),
            ((m.cs, m.C), F32),
            ((m.FFS, m.C), F32),
            ((9, m.cs), F32),
            ((rdim, 2 * m.cs), F32),
        ]
        + [((m.cs,), F32)] * 4
        + [((2 * m.cs,), F32)] * 2
        + [((m.FFS,), F32)] * 3
        + [((128,), F32)],
        [pltpu.VMEM((m.N + 2 * EDGE, m.C), F32)],
        scalars=1,
    )


class Posted:
    def __init__(self, copy, lands):
        self.copy, self.lands, self.landed = copy, lands, False


def line_order(p, number):
    low = p.z < p.R // 2
    far, near = p.R - 1 - number // 2, number // 2
    if number % 2:
        far, near = near, far
    return jnp.where(low, far, near)


STRIPES = 3
AHEAD = 2


def chunks(count, act, step=16, first=0):
    @pl.loop(0, count // step)
    def _(number):
        act(pl.ds(pl.multiple_of(first + number * step, step), step))


def each_rows(count, step, act):
    if step % 16:
        for number in range(count):
            act(number, pl.ds(number * step, step))
    else:

        @pl.loop(0, count)
        def _(number):
            act(number, pl.ds(pl.multiple_of(number * step, 16), step))


def greet_all(p, targets):
    barrier = pltpu.get_barrier_semaphore()
    waits = 0
    for target, when in targets:
        if when is None:
            waits = waits + 1
        else:
            waits = waits + jnp.where(when, 1, 0).astype(jnp.int32)
        guarded(when, lambda target=target: signal_all(barrier, [target]))
    pl.semaphore_wait(barrier, waits)


def fused_kernel(
    ident, name, greet, act, near, loads, far, near_out, far_out, scratch, sems, local, numbers=0
):
    close = pl.BlockSpec(memory_space=pltpu.VMEM)
    spot = pl.BlockSpec(memory_space=pl.ANY)
    counts = [len(near), len(loads), len(far), len(near_out), len(far_out), len(scratch), len(loads)]

    def kernel(*refs):
        groups = []
        for count in counts:
            groups.append(refs[:count])
            refs = refs[count:]
        send_sem, recv_sem, local_sem, load_sem = refs
        near, sources, far, near_out, far_out, scratch, held = groups
        brought = []
        for number, (source, place) in enumerate(zip(sources, held)):
            copy = pltpu.make_async_copy(source, place, load_sem.at[number])
            copy.start()
            brought.append(Brought(copy, place))
        p = Place()
        flow = Flow(send_sem, recv_sem, local_sem)
        greet_all(p, greet(p))
        act(p, flow, near, brought, far, near_out, far_out, scratch)
        flow.finish()
        if flow.used > sems or flow.kept > local:
            raise ValueError(f"{name}: {flow.used} {flow.kept}")

    return pl.pallas_call(
        kernel,
        out_shape=spots(near_out + far_out),
        in_specs=[pl.BlockSpec(memory_space=pltpu.SMEM)] * numbers
        + [close] * (len(near) - numbers)
        + [spot] * (len(loads) + len(far)),
        out_specs=[close] * len(near_out) + [spot] * len(far_out),
        scratch_shapes=list(scratch)
        + [pltpu.VMEM(array.shape, array.dtype) for array in loads]
        + [
            pltpu.SemaphoreType.DMA((sems,)),
            pltpu.SemaphoreType.DMA((sems,)),
            pltpu.SemaphoreType.DMA((local,)),
            pltpu.SemaphoreType.DMA((max(len(loads), 1),)),
        ],
        compiler_params=pltpu.CompilerParams(
            collective_id=ident, has_side_effects=True, vmem_limit_bytes=63 * 2**20
        ),
        name=name,
    )(*near, *loads, *far)


class Brought:
    def __init__(self, copy, place):
        self.copy, self.place, self.here = copy, place, False

    def get(self):
        if not self.here:
            self.copy.wait()
            self.here = True
        return self.place


class Stripes:
    def __init__(self, flow, p, part, total, buffers, src, dst):
        count = part.shape[2]
        self.p, self.flow, self.src, self.dst = p, flow, src, dst
        step = count // STRIPES
        self.rows = [pl.ds(number * step, step) for number in range(STRIPES)]
        mate, passed, landed = buffers
        self.sums = [
            LineReduce(
                flow,
                p,
                part.at[:, :, rows],
                total.at[rows],
                mate.at[:, rows],
                passed.at[:, :, rows],
                landed.at[:, :, rows],
            )
            for rows in self.rows
        ]
        self.lines = [LineGather(flow, p, src.at[rows], dst.at[:, :, rows]) for rows in self.rows]

    def run(self, act, before=None, between=None):
        p = self.p
        for item in self.sums:
            for number in range(p.R):
                item.offer(line_order(p, number))
        for number, item in enumerate(self.sums[:AHEAD]):
            item.early()
            if before is not None and number == 0:
                before()
        size = self.rows[0].size
        hops = [0] * STRIPES

        def hop(number):
            if hops[number] < p.R - 1:
                hops[number] += 1
                self.lines[number].hop(hops[number])

        for number, item in enumerate(self.sums):
            for step in item.later():
                step()
            item.close()
            chunks(size, act, first=number * size)
            self.lines[number].start()
            rows = self.rows[number]
            self.flow.keep(self.src.at[rows], self.dst.at[p.c, p.z, rows])
            if number + AHEAD < STRIPES:
                self.sums[number + AHEAD].early()
            if between is not None:
                between(number)
        while min(hops) < p.R - 1:
            for number in range(STRIPES):
                hop(number)


def gather_sems(m):
    return 4 * m.R - 3


def reduce_sems(m):
    return 3 * m.R


def reduce_buffers(m, count, width, part=True):
    block = (m.R, count, width)
    mine = [pltpu.VMEM((m.D,) + block, BF16)] if part else []
    return mine + [
        pltpu.VMEM(block, BF16),
        pltpu.VMEM((2,) + block, BF16),
        pltpu.VMEM((2,) + block, BF16),
    ]


def spread_greet(m, p):
    greet = []
    for step in range(m.G):
        source = {"grp": p.z, "duo": p.c, "rows": lax.rem(p.q - step + m.G, m.G)}
        greet.append((source, None if step else p.q != p.z))
    return greet


def common_greet(p):
    return team_greet(p) + group_greet(p)


def front_kernel(m, time_weight, time_bias, masked, small, fvec, in_cut, out_weight, map_cut, qkv_cut, clip_pad, proj_weight):
    near = [time_weight, time_bias]
    loads = [masked]
    far = [masked, small, fvec, in_cut, out_weight, map_cut, qkv_cut, clip_pad]
    far += [proj_weight] if m.even else []
    N, C, FL, G, T = m.N, m.C, m.FL, m.G, m.T
    root = 0.5**0.5
    texts = m.D * m.texts
    cond = clip_pad.shape[1]
    wide = C // m.Q
    square = G == 4
    items = m.G * m.D
    mod_rows = -(-items // 8) * 8
    pair = 2 * m.cs

    def act(p, flow, near, loads, far, near_out, far_out, scratch):
        tw_ref, tb_ref = near
        norms, total, silu, mapped = near_out[:4]
        hat, inv, vec, fv, keep, pix, qkv_bias, embed, edges, normed = near_out[4:]
        x_out, in_out, active_out, slope_out, out_all, qkv_rows, mod_all, mod_line = far_out[:8]
        map_all, clip_all, squares, weight, text, small_all, f_all, extended, conv, te, mod = scratch[:11]
        x_all, in_all, active, slope = scratch[11:]
        mid, small_ref, fvec_ref, in_cut, out_own, map_cut, qkv_cut, clip = far[:8]
        mine = p.c * p.R + p.z
        own_in = in_all.at[p.q]
        small_posts = [
            flow.post(small_ref, small_all.at[mine, p.q], {"grp": to}) for to in p.groups()
        ]
        edge_posts = []
        for block, to, sends, lands in (
            (mid.at[pl.ds(N - EDGE, EDGE)], p.z + 1, p.z < p.R - 1, p.z > 0),
            (mid.at[pl.ds(0, EDGE)], p.z - 1, p.z > 0, p.z < p.R - 1),
        ):
            slot = jnp.where(to > p.z, 0, 1)
            edge_posts.append(
                flow.post(block, edges.at[slot], {"rows": to}, when=sends, lands=lands)
            )
        f_posts = [flow.post(fvec_ref, f_all.at[p.q], {"grp": to}) for to in p.groups()]
        flow.keep(small_ref, small_all.at[mine, p.q], now=True)
        for item in small_posts:
            flow.land(item)
        spread = [
            flow.post(small_all.at[mine], small_all.at[mine], {"duo": c, "rows": z})
            for c, z in p.team()
        ]
        in_team = [
            flow.post(in_cut.at[c * p.R + z], own_in.at[mine], {"duo": c, "rows": z})
            for c, z in p.team()
        ]
        if square:
            out_relay = flow.square(p, out_own, out_all)
            flow.keep(out_own, out_all.at[p.q])
        else:
            flow.gather_group(p, out_own, out_all)
        own_map = map_all.at[p.q]
        map_team = [
            flow.post(map_cut.at[c * p.R + z], own_map.at[mine], {"duo": c, "rows": z})
            for c, z in p.team()
        ]
        clip_line = LineGather(flow, p, clip, clip_all)
        clip_line.start()
        flow.keep(in_cut.at[mine], own_in.at[mine], now=True)
        flow.keep(map_cut.at[mine], own_map.at[mine], now=True)
        flow.keep(clip, clip_all.at[p.c, p.z], now=True)
        flow.keep(fvec_ref, f_all.at[p.q], now=True)
        for item in spread + edge_posts:
            flow.land(item)
        half = m.S // 2
        vec[...] = jnp.zeros_like(vec)
        for s, (g, d, r) in enumerate(m.places):
            piece = small_all[d * m.R + r, g].astype(F32)
            vec[pl.ds(0, 13), pl.ds(s * m.cs, m.cs)] = piece[:13, : m.cs]
            vec[pl.ds(13 + s // half, 1), pl.ds(pair * (s % half), pair)] = piece[13:14, :pair]
            if r == 0:
                embed[pl.ds(m.D * g + d, 1)] = piece[14:15]
        extended[pl.ds(0, EDGE)] = jnp.where(p.z > 0, edges[0].astype(F32), 0.0)
        extended[pl.ds(EDGE, N)] = loads[0].get()[...].astype(F32)
        extended[pl.ds(EDGE + N, EDGE)] = jnp.where(p.z < m.R - 1, edges[1].astype(F32), 0.0)
        kind = small_all[mine, p.q].astype(F32)[14:15, FACTS + 2 : FACTS + 3]
        real = float_cols(kind)
        _, col = rows_cols(p.z * N, N, real)

        def taps(lanes):
            sum_of = jnp.zeros((N, 128), F32) + vec[pl.ds(9, 1), lanes]
            for index, dy, dx in tap_steps():
                pieces = [
                    extended[pl.ds(EDGE + dy * width + dx, N), lanes]
                    for width in (WIDTHS if dy else WIDTHS[:1])
                ]
                piece = pieces[0]
                if dy:
                    piece = jnp.where(kind == 0, piece, jnp.where(kind == 1, pieces[1], pieces[2]))
                ok = (col + dx >= 0) & (col + dx < real)
                sum_of = sum_of + jnp.where(ok, piece, 0.0) * vec[pl.ds(index, 1), lanes]
            conv[:, lanes] = sum_of

        each_column_block(m, taps)
        values, inverse = layer_stats(conv[...])
        hat[...] = values
        normed[...] = values.astype(BF16)
        inv[...] = inverse
        line = LineGather(flow, p, normed, x_all)
        line.start()
        flow.keep(normed, x_all.at[p.c, p.z], now=True)
        te[...] = embed[...][:items, : te.shape[1]].astype(BF16)
        mod[...] = jnp.zeros_like(mod)
        mod[pl.ds(0, items), pl.ds(0, pair)] = mm(te[...], tw_ref[...]) + tb_ref[...].astype(F32)
        mod_posts = flow.gather_group(p, mod, mod_all)
        for item in in_team:
            flow.land(item)
        if square:
            in_relay = flow.square(p, own_in, in_all)
        else:
            in_posts = [flow.post(own_in, in_all.at[p.q], {"grp": q}) for q in p.groups()]
        for d in range(m.D):
            facts = small_all[d * m.R, p.q].astype(F32)
            row, col_all = rows_cols(0, m.pixels, float_cols(facts[14:15, FACTS + 2 : FACTS + 3]))
            inside = (row < facts[14:15, FACTS : FACTS + 1]) & (
                col_all < facts[14:15, FACTS + 1 : FACTS + 2]
            )
            keep[d, pl.ds(0, m.pixels)] = jnp.where(inside, 1.0, 0.0)
            shown = facts.T[: m.texts, 15:16]
            slot = lax.broadcasted_iota(jnp.int32, (m.texts, 1), 0)
            keep[d, pl.ds(m.pixels, m.texts)] = jnp.where(slot < TXT, shown, 0.0)
        pix[...] = keep[p.c, pl.ds(pl.multiple_of(p.z * N, 8), N)]
        for item in f_posts:
            flow.land(item)
        for g in range(G):
            fv[:, pl.ds(g * m.FFS, m.FFS)] = f_all[g].astype(F32)[:8]
        qkv_bias[...] = jnp.zeros_like(qkv_bias)
        for h in range(T):

            @pl.when(p.D * p.z + p.c == h)
            def _():
                at = pl.ds(h * m.HW, m.HW)
                qkv_bias[:, : m.HW] = vec[pl.ds(13, 1), at]
                qkv_bias[:, 2 * m.HW :] = vec[pl.ds(14, 1), at]

        for item in map_team:
            flow.land(item)
        map_posts = [flow.post(own_map, map_all.at[p.q], {"grp": q}) for q in p.groups()]
        for step in range(1, m.R):
            clip_line.hop(step)
        line.hop(1)
        if square:
            out_relay()
        clip_line.settle(m.R)
        for item in map_posts:
            flow.land(item)
        for d in range(m.D):
            for r in range(m.R):
                piece = clip_all[d, r].astype(F32)[: m.slots]
                text[pl.ds((d * m.R + r) * m.slots, m.slots)] = piece / (1.0 + jnp.exp(-piece))
        silu[...] = text[...].astype(BF16)
        for g in range(G):
            for t in range(T):
                piece = map_all[g, t].astype(F32)
                weight[pl.ds(m.ms * (g * T + t), m.ms)] = piece[: m.ms]
        product = mm(silu[...], weight[...].astype(BF16))
        for t in range(T):

            @pl.when(mine == t)
            def _():
                mapped[...] = (product + vec[pl.ds(11, 1), pl.ds(t * m.HW, m.HW)]).astype(BF16)

        line.hop(2)
        if square:
            in_posts = in_relay()
        for item in mod_posts:
            flow.land(item)
        flow.settle_kept()
        mods = LineGather(flow, p, mod_all, mod_line)
        mods.start()
        flow.keep(mod_all, mod_line.at[p.c, p.z])
        flow.swap_team(p, qkv_cut, qkv_rows)
        if m.even:
            for number in range(G):
                to = lax.rem(p.z + number, G)
                piece = far[8].at[:, pl.ds(pl.multiple_of(to * wide, 128), wide)]
                flow.post(
                    piece,
                    far_out[8].at[p.z],
                    {"grp": to, "duo": p.c, "rows": p.q},
                    when=None if number else p.q != p.z,
                )
            piece = far[8].at[:, pl.ds(pl.multiple_of(p.z * wide, 128), wide)]
            flow.keep(piece, far_out[8].at[p.z], p.q == p.z)
        squares[...] = jnp.zeros_like(squares)
        for item in in_posts:
            flow.land(item)
        flow.keep(in_all, in_out)

        def multiply(first, count):
            line.settle(first + count)

            @pl.loop(0, count * m.D)
            def _(number):
                d = number // count
                block = jnp.where(
                    number - d * count == 0, line.nth(first), line.nth(first + count - 1)
                )
                base = pl.multiple_of(block * N, 16)
                hidden = mm(x_all[d, block], in_all[...].reshape(C, FL)) + fv[pl.ds(0, 1)]
                gate = 0.5 * (1.0 + lax.erf(hidden * root))
                value = hidden * gate
                rows = pl.ds(pl.multiple_of(d * m.pixels + base, 16), N)
                active[rows] = value
                slope[rows] = gate + hidden * (
                    jnp.exp(-0.5 * hidden * hidden) * 0.3989422804014327
                )
                squares[pl.ds(d, 1)] += jnp.sum(
                    keep[d, pl.ds(base, N)] * value * value, axis=0, keepdims=True
                )

        first = m.R // 2
        multiply(0, first)
        for step in range(3, m.R):
            line.hop(step)
        mods.hop(1)
        multiply(first, m.R - first)
        flow.keep(x_all, x_out)
        flow.keep(active, active_out)
        flow.keep(slope, slope_out)
        norms[...] = jnp.sqrt(squares[...])
        total[...] = jnp.broadcast_to(jnp.sum(norms[...], axis=1, keepdims=True), total.shape)
        for step in range(2, m.R):
            mods.hop(step)

    near_out = [
        ((8, FL), F32),
        ((8, 128), F32),
        ((texts, cond), BF16),
        ((texts, m.HW), BF16),
        ((N, C), F32),
        ((N, 1), F32),
        ((VEC, C), F32),
        ((8, FL), F32),
        ((m.D, m.pixels + m.texts, 1), F32),
        ((N, 1), F32),
        ((1, 3 * m.HW), F32),
        ((mod_rows, 128), F32),
        ((2, EDGE, C), BF16),
        ((N, C), BF16),
    ]
    far_out = [
        ((m.D, m.R, N, C), BF16),
        ((G, T, m.cs, FL), BF16),
        ((m.D * m.pixels, FL), F32),
        ((m.D * m.pixels, FL), F32),
        ((G,) + out_weight.shape, BF16),
        (qkv_cut.shape, BF16),
        ((G, mod_rows, 128), F32),
        ((m.D, m.R, G, mod_rows, 128), F32),
    ]
    if m.even:
        far_out.append(((m.R, m.cs, wide), BF16))
    scratch = [
        pltpu.VMEM((G, T, m.mp, m.HW), BF16),
        pltpu.VMEM((m.D, m.R) + clip_pad.shape, BF16),
        pltpu.VMEM((8, FL), F32),
        pltpu.VMEM((cond, m.HW), F32),
        pltpu.VMEM((texts, cond), F32),
        pltpu.VMEM((T, G, SMALL, 128), BF16),
        pltpu.VMEM((G,) + fvec.shape, BF16),
        pltpu.VMEM((N + 2 * EDGE, C), F32),
        pltpu.VMEM((N, C), F32),
        pltpu.VMEM((items, time_weight.shape[0]), BF16),
        pltpu.VMEM((mod_rows, 128), F32),
        pltpu.VMEM((m.D, m.R, N, C), BF16),
        pltpu.VMEM((G, T, m.cs, FL), BF16),
        pltpu.VMEM((m.D * m.pixels, FL), F32),
        pltpu.VMEM((m.D * m.pixels, FL), F32),
    ]
    columns = 4 if square else G - 1
    return fused_kernel(
        1,
        "front",
        lambda p: common_greet(p) + (sources_greet(m, p) if m.even else []),
        act,
        near,
        loads,
        far,
        near_out,
        far_out,
        scratch,
        4 * (T - 1) + 2 + 2 * columns + 4 * (G - 1) + (G if m.even else 0) + 3 * gather_sems(m),
        16,
    )


def sources_greet(m, p):
    greet = []
    for step in range(m.G):
        source = {"grp": p.z, "duo": p.c, "rows": lax.rem(p.q - step + m.G, m.G)}
        greet.append((source, None if step else p.q != p.z))
    return greet


def team_sum(m, p, flow, own, everyone):
    mine = p.c * m.R + p.z
    posted = [
        flow.post(own, everyone.at[mine], {"duo": c, "rows": z}) for c, z in p.team()
    ]

    def total():
        for item in posted:
            flow.land(item)
        result = own[...]
        for step, (c, z) in enumerate(p.team()):
            result = result + everyone[c * m.R + z]
        return result

    return total


def branch_kernel(m, active, norms, total, out_full, fv, latents, keep, vec, mod_all, qkv_rows, mapped, proj_part):
    near = [norms, total, fv, keep, mod_all]
    loads = [active, out_full, latents, vec]
    far = [qkv_rows, mapped] + ([proj_part] if m.even else [])
    N, C = m.N, m.C
    rows_all = m.D * m.pixels

    def act(p, flow, near, loads, far, near_out, far_out, scratch):
        norms, total, fv, keep, mod_all = near
        gain, grn_bias = fv[pl.ds(1, 1)], fv[pl.ds(2, 1)]
        grn, after, hat, inv, two, ratio, means, mods = near_out
        two_all, mapped_all, qkv_all = far_out[:3]
        everyone, part, mate, passed, landed, branch, slopes = scratch
        add_up = team_sum(m, p, flow, total, everyone)
        flow.gather_group(p, far[0], qkv_all)
        if m.even:
            flow.gather_group(p, far[2], far_out[3])
        text_line = LineGather(flow, p, far[1], mapped_all)
        half = m.S // 2
        pair = 2 * m.cs
        for s, (g, d, r) in enumerate(m.places):
            item = pl.ds(m.D * p.q + p.c, 1)
            mods[pl.ds(s // half, 1), pl.ds(pair * (s % half), pair)] = mod_all[d, r, g, item, pl.ds(0, pair)]
        mean = add_up() / m.FF + grn_eps
        means[...] = mean
        ratio[...] = norms[...] / mean[:, :1]
        slopes[...] = gain * ratio[...] + 1.0
        active, out_w, lat, vec = (load.get() for load in loads)

        @pl.loop(0, m.D)
        def _(d):
            rows = pl.ds(pl.multiple_of(d * m.pixels, 16), m.pixels)
            low = (active[rows] * slopes[pl.ds(d, 1)] + grn_bias).astype(BF16)
            grn[rows] = low
            part[d] = mm(low, out_w[...]).astype(BF16).reshape(m.R, N, C)

        def tail(rows):
            value = lat[rows].astype(F32) + keep[rows] * (branch[rows] + vec[pl.ds(10, 1)])
            after[rows] = value
            second = value * (1.0 + mods[pl.ds(0, 1)]) + mods[pl.ds(1, 1)]
            normal, inverse = layer_stats(second)
            hat[rows] = normal
            inv[rows] = inverse
            two[rows] = normal.astype(BF16)

        stripes = Stripes(flow, p, part, branch, (mate, passed, landed), two, two_all)
        text_line.start()
        flow.keep(far[1], mapped_all.at[p.c, p.z])
        stripes.run(tail, None, lambda number: text_line.hop(number + 1))
        for step in range(STRIPES + 1, m.R):
            text_line.hop(step)

    near_out = [
        ((rows_all, m.FL), BF16),
        ((N, C), F32),
        ((N, C), F32),
        ((N, 1), F32),
        ((N, C), BF16),
        ((8, m.FL), F32),
        ((8, 128), F32),
        ((8, C), F32),
    ]
    far_out = [
        ((m.D, m.R, N, C), BF16),
        ((m.D, m.R) + mapped.shape, BF16),
        ((m.G,) + qkv_rows.shape, BF16),
    ]
    if m.even:
        far_out.append(((m.G,) + proj_part.shape, BF16))
    scratch = (
        [pltpu.VMEM((m.T, 8, 128), F32)]
        + reduce_buffers(m, N, C)
        + [pltpu.VMEM((N, C), F32), pltpu.VMEM((8, m.FL), F32)]
    )
    return fused_kernel(
        3,
        "branch",
        common_greet,
        act,
        near,
        loads,
        far,
        near_out,
        far_out,
        scratch,
        (m.T - 1) + 2 * (m.G - 1) + (1 + STRIPES) * gather_sems(m) + STRIPES * reduce_sems(m),
        4 + STRIPES,
    )


def attention_kernel(m, two_all, gres, mapped_all, weight, proj, bias, key_keep):
    near = [bias, key_keep]
    loads = [two_all, weight, proj, mapped_all]
    far = [gres]
    heads = m.HW // HEAD
    keys = m.pixels + m.texts
    scale = HEAD ** (-0.5)
    HW, C, N, D, R, G, pixels, texts = m.HW, m.C, m.N, m.D, m.R, m.G, m.pixels, m.texts
    wide = C // m.Q
    block_rows = 2 * HW

    def act(p, flow, near, loads, far, near_out, far_out, scratch):
        bias, keep = near
        result, map_out, gw_out, gp_out, qv_out = near_out
        (two_far,) = far_out
        (gres_all, part, mate, passed, landed, qkv, k_all, v_all, k_t, v_t, dk, dv, o_t, dq_t, o_low, att, g_all, probs, dqkv,
         dtext, piece, words, gb_out, two_out) = scratch
        line = LineGather(flow, p, far[0], gres_all)
        line.start()
        flow.keep(far[0], gres_all.at[p.c, p.z], now=True)
        two, w, proj, mapped = (load.get() for load in loads)
        red = LineReduce(flow, p, part, result, mate, passed, landed)

        @pl.loop(0, D)
        def _(d):
            qkv[d] = (mm(two[d], w[...]) + bias[...]).astype(BF16)
            words[...] = jnp.zeros((texts, 3 * HW), F32) + bias[...]

            @pl.loop(0, m.T)
            def _(t):
                words[...] += mm(mapped[t, d], w[pl.ds(pl.multiple_of(t * HW, 16), HW)])

            text = words[...].astype(BF16)
            k_all[d, pl.ds(0, pixels)] = qkv[d, :, HW : 2 * HW]
            k_all[d, pl.ds(pixels, texts)] = text[:, HW : 2 * HW]
            v_all[d, pl.ds(0, pixels)] = qkv[d, :, 2 * HW :]
            v_all[d, pl.ds(pixels, texts)] = text[:, 2 * HW :]
            k_t[d] = k_all[d].T
            v_t[d] = v_all[d].T
            dk[d] = jnp.zeros_like(dk[d])
            dv[d] = jnp.zeros_like(dv[d])
            o_t[d] = jnp.zeros_like(o_t[d])
            dq_t[d] = jnp.zeros_like(dq_t[d])

        lane = lax.broadcasted_iota(jnp.int32, (1, HW), 1)
        row = lax.broadcasted_iota(jnp.int32, (HW, 1), 0)

        def masks(number):
            d = number // heads
            low = (number - d * heads) * HEAD
            return d, (lane >= low) & (lane < low + HEAD), (row >= low) & (row < low + HEAD)

        def forward(number):
            d, in_head, in_row = masks(number)
            q_h = jnp.where(in_head, qkv[d, :, :HW], 0).astype(BF16)
            scores = mm_t(k_all[d], q_h) * scale
            scores = jnp.where(keep[d] > 0, scores, masked_score)
            weights = jnp.exp(scores - jnp.max(scores, axis=0, keepdims=True))
            low = (weights / jnp.sum(weights, axis=0, keepdims=True)).astype(BF16)
            probs[number] = low
            o_t[d] += mm(jnp.where(in_row, v_t[d], 0).astype(BF16), low)

        pl.loop(0, D * heads // 2)(forward)
        line.hop(1)
        pl.loop(D * heads // 2, D * heads)(forward)

        @pl.loop(0, D)
        def _(d):
            o_low[d] = o_t[d].astype(BF16)
            att[d] = o_t[d].T.astype(BF16)

        def lanes_of(n):
            return pl.ds(pl.multiple_of(n * wide, 128), wide)

        @pl.loop(0, D * R)
        def _(number):
            d = number // R
            block = number - d * R
            mine = att[d, pl.ds(pl.multiple_of(block * N, 16), N)]
            for n in range(m.Q):
                part[d, block, :, pl.ds(n * wide, wide)] = mm(mine, proj[n]).astype(BF16)

        red.start()
        line.hop(2)
        red.early()
        steps = list(red.later())
        for number in range(3, R):
            line.hop(number)
        line.settle(R)

        @pl.loop(0, D * R)
        def _(number):
            d = number // R
            block = number - d * R
            total = jnp.zeros((N, HW), F32)
            for n in range(m.Q):
                total = total + mm_t(gres_all[d, block, :, pl.ds(n * wide, wide)], proj[n])
            g_all[d, pl.ds(pl.multiple_of(block * N, 16), N)] = total.astype(BF16)

        def back(first, last):
            @pl.loop(first, last)
            def _(number):
                d, in_head, in_row = masks(number)
                q_h = jnp.where(in_head, qkv[d, :, :HW], 0).astype(BF16)
                g_h = jnp.where(in_head, g_all[d], 0).astype(BF16)
                low = probs[number]
                dv[d] += mm(low, g_h)
                grad_probs = mm_t(v_all[d], g_h)
                high = low.astype(F32)
                sums = jnp.sum(high * grad_probs, axis=0, keepdims=True)
                grad_scores = (high * (grad_probs - sums)).astype(BF16)
                dq_t[d] += mm(jnp.where(in_row, k_t[d], 0).astype(BF16), grad_scores)
                dk[d] += mm(grad_scores, q_h)

        cut = D * heads // 2
        steps[0]()
        back(0, cut)
        for step in steps[1:3]:
            step()
        back(cut, D * heads)
        for step in steps[3:]:
            step()
        gb_out[...] = jnp.zeros_like(gb_out)

        @pl.loop(0, D)
        def _(d):
            dqkv[d, :, :HW] = (dq_t[d].T * scale).astype(BF16)
            dqkv[d, :, HW : 2 * HW] = (dk[d, pl.ds(0, pixels)] * scale).astype(BF16)
            dqkv[d, :, 2 * HW :] = dv[d, pl.ds(0, pixels)].astype(BF16)
            dtext[d, :, :HW] = jnp.zeros((texts, HW), BF16)
            dtext[d, :, HW : 2 * HW] = (dk[d, pl.ds(pixels, texts)] * scale).astype(BF16)
            dtext[d, :, 2 * HW :] = dv[d, pl.ds(pixels, texts)].astype(BF16)
            gb_out[pl.ds(0, 1)] += jnp.sum(dqkv[d].astype(F32), axis=0, keepdims=True) + jnp.sum(
                dtext[d].astype(F32), axis=0, keepdims=True
            )
            two_out[d] = mm_t(dqkv[d], w[...]).astype(BF16)
            @pl.loop(0, m.T)
            def _(t):
                rows = pl.ds(pl.multiple_of(t * HW, 16), HW)
                map_out[t, d] = mm_t(dtext[d], w[rows]).astype(BF16)

        flow.keep(two_out, two_far)
        qv_out[...] = jnp.zeros_like(qv_out)
        for h in range(m.T):

            @pl.when(D * p.z + p.c == h)
            def _():
                qv_out[pl.ds(0, 1), pl.ds(h * HW, HW)] = gb_out[pl.ds(0, 1), pl.ds(0, HW)]
                qv_out[pl.ds(1, 1), pl.ds(h * HW, HW)] = gb_out[pl.ds(0, 1), pl.ds(2 * HW, HW)]

        @pl.loop(0, C // block_rows)
        def _(g):
            lanes = pl.ds(pl.multiple_of(g * block_rows, 128), block_rows)
            piece[...] = t_mm(two[0, :, lanes], dqkv[0])
            for d in range(1, D):
                piece[...] += t_mm(two[d, :, lanes], dqkv[d])
            for side in range(2):
                rows = pl.ds(side * HW, HW)
                for d in range(D):
                    piece[rows] += t_mm(mapped[2 * g + side, d], dtext[d])
            gw_out[pl.ds(pl.multiple_of(g * block_rows, 16), block_rows)] = piece[...].astype(BF16)

        @pl.loop(0, m.Q)
        def _(n):
            total = jnp.zeros((HW, wide), F32)
            for d in range(D):
                columns = gres_all[d, :, :, lanes_of(n)].reshape(pixels, wide)
                total = total + mm(o_low[d], columns)
            gp_out[n] = total.astype(BF16)
        red.close()

    near_out = [
        ((N, C), F32),
        ((m.T, D, texts, HW), BF16),
        ((C, 3 * HW), BF16),
        ((m.Q, HW, wide), BF16),
        ((8, C), F32),
    ]
    scratch = [pltpu.VMEM((D, R, N, C), BF16)] + reduce_buffers(m, N, C)
    scratch += [
        pltpu.VMEM((D, pixels, 3 * HW), BF16),
        pltpu.VMEM((D, keys, HW), BF16),
        pltpu.VMEM((D, keys, HW), BF16),
        pltpu.VMEM((D, HW, keys), BF16),
        pltpu.VMEM((D, HW, keys), BF16),
        pltpu.VMEM((D, keys, HW), F32),
        pltpu.VMEM((D, keys, HW), F32),
        pltpu.VMEM((D, HW, pixels), F32),
        pltpu.VMEM((D, HW, pixels), F32),
        pltpu.VMEM((D, HW, pixels), BF16),
        pltpu.VMEM((D, pixels, HW), BF16),
        pltpu.VMEM((D, pixels, HW), BF16),
        pltpu.VMEM((D * heads, keys, pixels), BF16),
        pltpu.VMEM((D, pixels, 3 * HW), BF16),
        pltpu.VMEM((D, texts, 3 * HW), BF16),
        pltpu.VMEM((block_rows, 3 * HW), F32),
        pltpu.VMEM((texts, 3 * HW), F32),
        pltpu.VMEM((8, 3 * HW), F32),
        pltpu.VMEM((D, pixels, C), BF16),
    ]
    return fused_kernel(
        4,
        "attention_block",
        team_greet,
        act,
        near,
        loads,
        far,
        near_out,
        [((D, pixels, C), BF16)],
        scratch,
        gather_sems(m) + reduce_sems(m),
        2,
    )


def attended_kernel(m, two_part, text_part, result, cot, gres, hat, inv, after, mods, keep, vec, grad_qkv, grad_proj):
    near = [inv, mods, keep]
    loads = [two_part, hat, after, cot, gres, text_part, result, vec]
    far = [grad_qkv] + ([grad_proj] if m.even else [])
    N, C = m.N, m.C
    texts = m.D * m.texts

    def act(p, flow, near, loads, far, near_out, far_out, scratch):
        inv, mods, keep = near
        two_part, hat, after, cot, gres, text_part, result, vec = (load.get() for load in loads)
        output, grad_after, branch, gm, vecg, text = near_out
        gb_all = far_out[0]
        two_sum, text_sum = scratch[:2]
        text_red = LineReduce(flow, p, text_part, text_sum, *scratch[5:8])
        stripes = Stripes(flow, p, two_part, two_sum, scratch[2:5], branch, gb_all)
        flow.swap_group(p, far[0], far_out[1])
        if m.even:
            flow.swap_group(p, far[1], far_out[2])
        gm[...] = jnp.zeros_like(gm)
        vecg[...] = jnp.zeros_like(vecg)

        def back(rows):
            grad = cot[rows].astype(F32) + layer_back(two_sum[rows], hat[rows], inv[rows])
            gm[pl.ds(0, 1)] += jnp.sum(grad * after[rows], axis=0, keepdims=True)
            gm[pl.ds(1, 1)] += jnp.sum(grad, axis=0, keepdims=True)
            scaled = grad * (1.0 + mods[pl.ds(0, 1)])
            grad_after[rows] = scaled
            low = (keep[rows] * scaled).astype(BF16)
            branch[rows] = low
            vecg[pl.ds(0, 1)] += jnp.sum(low.astype(F32), axis=0, keepdims=True)
            vecg[pl.ds(1, 1)] += jnp.sum(gres[rows].astype(F32), axis=0, keepdims=True)

        text_red.start()
        steps = list(text_red.later())

        def between(number):
            if number == 0:
                steps[0]()
            elif number == 1:
                for step in steps[1:]:
                    step()
                text_red.close()
                text[...] = text_sum[...].astype(BF16)

        stripes.run(back, text_red.early, between)

        def out(rows):
            second = after[rows] * (1.0 + mods[pl.ds(0, 1)]) + mods[pl.ds(1, 1)]
            value = keep[rows] * (result[rows] + vec[pl.ds(12, 1)])
            output[rows] = (second + value).astype(BF16)

        chunks(N, out)

    near_out = [
        ((N, C), BF16),
        ((N, C), F32),
        ((N, C), BF16),
        ((8, C), F32),
        ((8, C), F32),
        ((texts, m.HW), BF16),
    ]
    far_out = [((m.D, m.R, N, C), BF16), (grad_qkv.shape, BF16)]
    if m.even:
        far_out.append((grad_proj.shape, BF16))
    scratch = (
        [pltpu.VMEM((N, C), F32), pltpu.VMEM((texts, m.HW), F32)]
        + reduce_buffers(m, N, C, False)
        + reduce_buffers(m, texts, m.HW, False)
    )
    return fused_kernel(
        5,
        "attended",
        common_greet,
        act,
        near,
        loads,
        far,
        near_out,
        far_out,
        scratch,
        2 * (m.G - 1) + STRIPES * gather_sems(m) + (1 + STRIPES) * reduce_sems(m),
        3 + STRIPES,
    )


def text_back_kernel(m, silu, grad_mapped):
    def kernel(s_ref, g_ref, out, bias, weight):
        weight[...] = t_mm(s_ref[...], g_ref[...])
        out[...] = jnp.zeros_like(out)
        for g in range(m.G):
            for t in range(m.T):
                at = m.ms * (g * m.T + t)
                out[g, pl.ds(t * m.mp, m.ms)] = weight[pl.ds(at, m.ms)].astype(BF16)
        total = jnp.sum(g_ref[...].astype(F32), axis=0, keepdims=True)
        bias[...] = jnp.zeros_like(bias)
        for t in range(m.T):

            @pl.when(lax.axis_index("duo") * m.R + lax.axis_index("rows") == t)
            def _():
                bias[pl.ds(0, 1), pl.ds(t * m.HW, m.HW)] = total

    return local_kernel(
        "text_back",
        kernel,
        [silu, grad_mapped],
        [((m.G, m.T * m.mp, m.HW), BF16), ((8, m.C), F32)],
        [pltpu.VMEM((silu.shape[1], m.HW), F32)],
    )


def back_kernel(m, gb_all, out_full, active, slope, grn_out, normed_all, in_full, norms, ratio, means, fv, key_keep,
                qkv_parts, proj_parts, grad_map):
    near = [norms, ratio, means, fv, key_keep]
    loads = [gb_all, out_full, active, grn_out, slope, normed_all, in_full, qkv_parts]
    loads += [proj_parts] if m.even else []
    far = [grad_map]
    N, C, FL, G = m.N, m.C, m.FL, m.G
    rows_in = C // G
    wide = C // m.Q
    per = m.pixels // N

    def act(p, flow, near, loads, far, near_out, far_out, scratch):
        norms, ratio, means, fv, keep = near
        gain = fv[pl.ds(1, 1)]
        (back,) = near_out
        in_parts, f_parts, map_parts, qkv_team = far_out[:4]
        g_far = far_out[-1]
        everyone, mine, moments, slopes, shifts, grads, hidden, part, mate, passed, landed = scratch[:11]
        turned_g, turned_x, g_in, f_own, qkv_own = scratch[11:16]
        g_out = scratch[-1]
        flow.swap_group(p, far[0], map_parts)
        gb, out_w, active, grn = (load.get() for load in loads[:4])
        moments[...] = jnp.zeros_like(moments)

        @pl.loop(0, m.D * per)
        def _(number):
            rows = pl.ds(pl.multiple_of(number * N, 16), N)
            item = number // per
            grad = mm_t(gb[rows], out_w[...])
            grads[rows] = grad
            moments[pl.ds(item, 1)] += jnp.sum(grad * active[rows], axis=0, keepdims=True)
            moments[pl.ds(m.D, 1)] += jnp.sum(grad, axis=0, keepdims=True)

        scaled = moments[...] * gain
        cross = jnp.sum(scaled * norms[...], axis=1, keepdims=True)
        mine[...] = jnp.broadcast_to(cross, mine.shape)
        add_up = team_sum(m, p, flow, mine, everyone)
        turned_g[...] = grn[...].T

        def multiply_out(g, rows):
            g_out[g] = mm(turned_g[rows], gb[...]).astype(BF16)

        each_rows(G, m.FFS, multiply_out)
        flow.keep(g_out, g_far)

        slope, x, in_w, qkv_parts = (load.get() for load in loads[4:8])
        step = m.cs

        def add_parts(parts, own, count):
            for t in range(count):
                rows = pl.ds(t * step, step)
                total = parts[0, rows].astype(F32)
                for g in range(1, G):
                    total = total + parts[g, rows].astype(F32)
                own[t] = total.astype(BF16)

        add_parts(qkv_parts, qkv_own, m.T)
        if m.even:
            proj_own = scratch[16]
            add_parts(loads[8].get(), proj_own, m.R)
        mean = means[...][:, :1]
        cross = add_up()[:, :1]
        slopes[...] = gain * ratio[...] + 1.0
        shifts[...] = (scaled / mean - cross / (m.FF * mean * mean)) / norms[...]
        gains = jnp.sum(moments[pl.ds(0, m.D)] * ratio[pl.ds(0, m.D)], axis=0, keepdims=True)
        biases = moments[pl.ds(m.D, 1)]
        moments[pl.ds(m.D + 1, 1)] = jnp.zeros((1, FL), F32)
        flow.swap_team(p, qkv_own, qkv_team)
        if m.even:
            for number in range(G):
                to = lax.rem(p.q + number, G)
                flow.post(
                    proj_own.at[to],
                    far_out[4].at[p.q],
                    {"grp": p.z, "duo": p.c, "rows": to},
                    when=None if number else p.q != p.z,
                )
            flow.keep(proj_own.at[p.z], far_out[4].at[p.q], p.q == p.z)

        @pl.loop(0, m.D * per)
        def _(number):
            rows = pl.ds(pl.multiple_of(number * N, 16), N)
            item = number // per
            inside = pl.ds(pl.multiple_of((number - item * per) * N, 16), N)
            one = pl.ds(item, 1)
            grad = grads[rows] * slopes[one] + keep[item, inside] * (active[rows] * shifts[one])
            low = (grad * slope[rows]).astype(BF16)
            hidden[rows] = low
            moments[pl.ds(m.D + 1, 1)] += jnp.sum(low.astype(F32), axis=0, keepdims=True)

        inner = moments[pl.ds(m.D + 1, 1)]
        f_own[...] = jnp.zeros_like(f_own)
        for g in range(G):
            lanes = slice(g * m.FFS, (g + 1) * m.FFS)
            for row, values in enumerate((inner, gains, biases)):
                f_own[g, pl.ds(row, 1)] = values[:, lanes]
        flow.swap_group(p, f_own, f_parts)
        line = LineReduce(flow, p, part, back, mate, passed, landed)

        @pl.loop(0, m.D)
        def _(d):
            rows = pl.ds(pl.multiple_of(d * m.pixels, 16), m.pixels)
            part[d] = mm_t(hidden[rows], in_w[...]).astype(BF16).reshape(m.R, N, C)

        for number in range(m.R):
            line.offer(line_order(p, number))
        line.early()
        turned_x[...] = x[...].T
        first = flow.take(G - 1)

        def send_in(number):
            g = lax.rem(p.q + 1 + number, G)
            return flow.copy(g_in.at[g], in_parts.at[p.q], {"grp": g}, first + number)

        @pl.loop(0, G)
        def _(number):
            g = lax.rem(p.q + 1 + number, G)
            rows = pl.ds(pl.multiple_of(g * rows_in, 16), rows_in)
            g_in[g] = mm(turned_x[rows], hidden[...]).astype(BF16)
            pl.when(number < G - 1)(lambda: send_in(number).start())

        flow.keep(g_in.at[p.q], in_parts.at[p.q])
        for act_of in line.later():
            act_of()
        line.close()
        for number in range(G - 1):
            send_in(number).wait_recv()
            send_in(number).wait_send()

    near_out = [((N, C), F32)]
    far_out = [
        ((G, rows_in, FL), BF16),
        ((G, 8, m.FFS), F32),
        (grad_map.shape, BF16),
        ((m.T, m.cs, 3 * m.HW), BF16),
    ]
    scratch = [
        pltpu.VMEM((m.T, 8, 128), F32),
        pltpu.VMEM((8, 128), F32),
        pltpu.VMEM((8, FL), F32),
        pltpu.VMEM((8, FL), F32),
        pltpu.VMEM((8, FL), F32),
        pltpu.VMEM((m.D * m.pixels, FL), F32),
        pltpu.VMEM((m.D * m.pixels, FL), BF16),
    ]
    scratch += reduce_buffers(m, N, C)
    scratch += [
        pltpu.VMEM((FL, m.D * m.pixels), BF16),
        pltpu.VMEM((C, m.D * m.pixels), BF16),
        pltpu.VMEM((G, rows_in, FL), BF16),
        pltpu.VMEM((G, 8, m.FFS), F32),
        pltpu.VMEM((m.T, m.cs, 3 * m.HW), BF16),
    ]
    if m.even:
        far_out.append(((G, m.cs, wide), BF16))
        scratch.append(pltpu.VMEM((m.R, m.cs, wide), BF16))
    far_out.append(((G, m.FFS, C), BF16))
    scratch.append(pltpu.VMEM((G, m.FFS, C), BF16))
    return fused_kernel(
        9,
        "feed_forward_back",
        lambda p: common_greet(p) + (spread_greet(m, p) if m.even else []),
        act,
        near,
        loads,
        far,
        near_out,
        far_out,
        scratch,
        2 * (m.T - 1) + 4 * (G - 1) + reduce_sems(m) + (G if m.even else 0),
        7,
    )


def tail_kernel(m, grad_low, tiny, g_out, in_parts, map_parts):
    loads = [in_parts, map_parts]
    far = [grad_low, tiny, g_out]
    N, C, G, T = m.N, m.C, m.G, m.T

    def act(p, flow, near, loads, far, near_out, far_out, scratch):
        low, tiny, g_out = far
        edges, tiny_all, in_team, map_team, out_parts = far_out
        in_own, map_own, tiny_in, tiny_own = scratch
        for block, to, sends, lands in (
            (low.at[pl.ds(N - EDGE, EDGE)], p.z + 1, p.z < p.R - 1, p.z > 0),
            (low.at[pl.ds(0, EDGE)], p.z - 1, p.z > 0, p.z < p.R - 1),
        ):
            slot = jnp.where(to > p.z, 0, 1)
            flow.post(block, edges.at[slot], {"rows": to}, when=sends, lands=lands)
        posts = flow.swap_team(p, tiny, tiny_in)
        flow.swap_group(p, g_out, out_parts)
        for load, own, step in ((loads[0], in_own, m.cs), (loads[1], map_own, m.mp)):
            parts = load.get()

            def add(t, rows, parts=parts, own=own):
                total = parts[0, rows].astype(F32)
                for g in range(1, G):
                    total = total + parts[g, rows].astype(F32)
                own[t] = total.astype(BF16)

            each_rows(T, step, add)

        flow.swap_team(p, in_own, in_team)
        flow.swap_team(p, map_own, map_team)
        for item in posts:
            flow.land(item)
        flow.settle_kept()
        for d in range(m.D):
            for g in range(G):
                total = tiny_in[d * m.R, g]
                for r in range(1, m.R):
                    total = total + tiny_in[d * m.R + r, g]
                tiny_own[g, d] = total
        flow.swap_group(p, tiny_own, tiny_all)

    return fused_kernel(
        11,
        "tail",
        common_greet,
        act,
        [],
        loads,
        far,
        [],
        [
            ((2, EDGE, C), BF16),
            ((G, m.D) + tiny.shape[2:], F32),
            ((T, m.cs, m.FL), BF16),
            ((T, m.mp, m.HW), BF16),
            (g_out.shape, BF16),
        ],
        [
            pltpu.VMEM((T, m.cs, m.FL), BF16),
            pltpu.VMEM((T, m.mp, m.HW), BF16),
            pltpu.VMEM(tiny.shape, F32),
            pltpu.VMEM((G, m.D) + tiny.shape[2:], F32),
        ],
        2 + 3 * (T - 1) + 2 * (G - 1),
        5,
    )


def pad_rows(values, rows):
    return jnp.pad(values, ((0, rows - values.shape[0]),) + ((0, 0),) * (values.ndim - 1))


def body(
    latents,
    clip_tokens,
    time_embed,
    bucket_ids,
    heights,
    widths,
    text_mask,
    conv_weight,
    conv_bias,
    in_weight,
    in_bias,
    grn_gain,
    grn_bias,
    out_weight,
    out_bias,
    time_weight,
    time_bias,
    map_weight,
    map_bias,
    qkv_weight,
    qv_bias,
    proj_weight,
    proj_bias,
    cotangent,
):
    m = Sizes(latents, clip_tokens, in_weight, in_bias, conv_bias, map_weight)
    G, D, R, T, N, C = m.G, m.D, m.R, m.T, m.N, m.C
    pixels, texts, FFS, FL, FF, HW = m.pixels, m.texts, m.FFS, m.FL, m.FF, m.HW
    cs, ms, mp, sp, even, Q = m.cs, m.ms, m.mp, m.sp, m.even, m.Q
    q, c, z = (lax.axis_index(axis) for axis in AXES)
    head_slice = D * z + c

    vectors = [conv_bias, out_bias, map_bias, proj_bias, qv_bias]
    fvectors = [in_bias, grn_gain, grn_bias]
    in_cut, qkv_cut, map_cut, clip_pad, masked, grad_result, small, fvec = cut_kernel(
        m,
        [heights, widths, bucket_ids, in_weight, qkv_weight, map_weight, clip_tokens, latents]
        + [cotangent, conv_weight]
        + vectors
        + [time_embed, text_mask]
        + fvectors,
    )
    latents = latents[0]
    cotangent = cotangent[0]

    def swap_edges(plan, src, dst):
        p = plan.p
        for block, to, sends, lands in (
            (src.at[pl.ds(src.shape[0] - EDGE, EDGE)], p.z + 1, p.z < R - 1, p.z > 0),
            (src.at[pl.ds(0, EDGE)], p.z - 1, p.z > 0, p.z < R - 1),
        ):
            slot = jnp.where(to > p.z, 0, 1)
            plan.add(block, dst.at[slot], {"rows": to}, when=sends, lands=lands)

    outs = front_kernel(
        m,
        time_weight,
        time_bias[None],
        masked,
        small,
        fvec,
        in_cut,
        out_weight,
        map_cut,
        qkv_cut,
        clip_pad,
        proj_weight,
    )
    norms, total, silu, mapped_s = outs[:4]
    norm_hat, norm_inv, vec, fv, key_keep, keep, bias, embed, edges, _ = outs[4:14]
    normed_all, in_full, active, slope, out_full, qkv_rows, _, mod_all = outs[14:22]
    proj_part = outs[22].reshape(HW, C // G) if even else None
    normed_all = normed_all.reshape(D * pixels, C)
    in_full = in_full.reshape(C, FL)
    out_full = out_full.reshape(FL, C)
    outs = branch_kernel(
        m,
        active,
        norms,
        total,
        out_full,
        fv,
        latents,
        keep,
        vec,
        mod_all,
        qkv_rows.reshape(T * cs, 3 * HW),
        mapped_s,
        proj_part,
    )
    grn_out, after_res, two_hat, two_inv, _, ratio, means, mods, two_all, mapped = outs[:10]
    qkv_full = outs[10].reshape(C, 3 * HW)
    if even:
        proj_s = outs[11]
    else:
        proj_whole = lax.all_gather(proj_weight, AXES, axis=0, tiled=True)
        proj_s = lax.dynamic_slice_in_dim(proj_whole, head_slice * HW, HW, axis=0)[None]
    result, mapped_part, grad_qkv, grad_proj, qv_grads, two_part = attention_kernel(
        m,
        two_all.reshape(D, pixels, C),
        grad_result,
        mapped.reshape(T, D, texts, HW),
        qkv_full,
        proj_s,
        bias,
        key_keep,
    )
    outs = attended_kernel(
        m,
        two_part.reshape(D, R, N, C),
        mapped_part.reshape(D, R, D * texts, HW),
        result,
        cotangent,
        grad_result,
        two_hat,
        two_inv,
        after_res,
        mods,
        keep,
        vec,
        grad_qkv.reshape(G, T * cs, 3 * HW),
        grad_proj,
    )
    output, grad_after, _, grad_modulate, vec_sums, grad_mapped, gb_all, qkv_parts = outs[:8]
    if even:
        proj_parts = outs[8]
    else:
        proj_parts = None
        spread = jnp.zeros((C, C), F32)
        spread = lax.dynamic_update_slice_in_dim(
            spread, grad_proj[0].astype(F32), head_slice * HW, axis=0
        )
        proj_team = lax.psum_scatter(spread, AXES, scatter_dimension=0, tiled=True)[None]
    grad_map, map_bias_grad = text_back_kernel(m, silu, grad_mapped)
    outs = back_kernel(
        m,
        gb_all.reshape(D * pixels, C),
        out_full,
        active,
        slope,
        grn_out,
        normed_all,
        in_full,
        norms,
        ratio,
        means,
        fv,
        key_keep,
        qkv_parts,
        proj_parts,
        grad_map,
    )
    grad_conv_in, in_parts, f_sum, map_parts, qkv_team = outs[:5]
    grad_out = outs[-1]
    if even:
        proj_team = outs[5]

    grad_conv, conv_low, tiny = conv_back_kernel(
        m,
        bucket_ids,
        grad_conv_in,
        norm_hat,
        norm_inv,
        edges,
        masked,
        vec_sums,
        map_bias_grad,
        qv_grads,
        grad_modulate,
    )
    conv_edges, tiny_all, in_team, map_team, out_parts = tail_kernel(
        m, conv_low, tiny, grad_out, in_parts, map_parts
    )
    outs = finish_kernel(
        m,
        bucket_ids,
        conv_edges,
        conv_low,
        grad_after,
        keep,
        vec,
        in_team,
        qkv_team,
        map_team,
        proj_team,
        out_parts,
        tiny_all,
        f_sum,
        embed,
        time_embed.shape[1],
    )
    grad_latents, grad_in_shard, grad_qkv_shard, grad_map_shard, grad_proj_shard = outs[:5]
    grad_out_shard, grad_kernel, grad_time = outs[5:8]
    conv_b, out_b, proj_b, map_b, qv_b, time_b, in_b, gain_g, grn_b = outs[8:17]
    return (
        output[None],
        grad_latents,
        grad_kernel,
        conv_b,
        grad_in_shard,
        in_b,
        gain_g,
        grn_b,
        grad_out_shard,
        out_b,
        grad_time,
        time_b,
        grad_map_shard,
        map_b,
        grad_qkv_shard,
        qv_b,
        grad_proj_shard,
        proj_b,
    )


def solution(mesh):
    items, rows = mesh.devices.shape
    fine = Mesh(mesh.devices.reshape(items // 2, 2, rows), AXES)
    item = ("grp", "duo")
    full = AXES
    ins = (
        P(item, "rows", None),
        P(item, "rows", None),
        P(item, None),
        P(item),
        P(item),
        P(item),
        P(item, None),
        P(None, full),
        P(full),
        P(full, None),
        P(full),
        P(full),
        P(full),
        P(full, None),
        P(full),
        P(None, full),
        P(full),
        P(full, None),
        P(full),
        P(full, None),
        P(full),
        P(full, None),
        P(full),
        P(item, "rows", None),
    )
    outs = (
        P(item, "rows", None),
        P(item, "rows", None),
        P(None, full),
        P(full),
        P(full, None),
        P(full),
        P(full),
        P(full),
        P(full, None),
        P(full),
        P(None, full),
        P(full),
        P(full, None),
        P(full),
        P(full, None),
        P(full),
        P(full, None),
        P(full),
    )
    return jax.shard_map(body, mesh=fine, in_specs=ins, out_specs=outs, check_vma=False)
```

```python
import functools

import jax
import jax.numpy as jnp
from jax import lax
from jax.experimental import pallas as pl
from jax.experimental.pallas import tpu as pltpu
from jax.sharding import Mesh, PartitionSpec as P

HEAD = 64
TXT = 77
UNIT = 8
EDGE = 48

norm_eps = 1e-06
grn_eps = 1e-06
masked_score = -1000000000.0

AXES = ("grp", "duo", "rows")
MESH_ID = pl.DeviceIdType.MESH
F32 = jnp.float32
BF16 = jnp.bfloat16


class Place:
    def __init__(self):
        self.q, self.c, self.z = (lax.axis_index(axis) for axis in AXES)
        self.G, self.D, self.R = (lax.axis_size(axis) for axis in AXES)

    def team(self):
        for step in range(1, self.D * self.R):
            dc, dz = step // self.R, step % self.R
            yield lax.rem(self.c + dc, self.D), lax.rem(self.z + dz, self.R)

    def groups(self):
        for step in range(1, self.G):
            yield lax.rem(self.q + step, self.G)


def signal_all(barrier, targets):
    for target in targets:
        pl.semaphore_signal(barrier, inc=1, device_id=target, device_id_type=MESH_ID)


def guarded(when, act):
    if when is None:
        act()
    else:
        pl.when(when)(act)


class Flow:
    def __init__(self, send_sem, recv_sem, local_sem=None):
        self.send_sem, self.recv_sem, self.local_sem = send_sem, recv_sem, local_sem
        self.used = 0
        self.kept = 0
        self.open = []
        self.posted = []
        self.lines = []
        self.stays = []

    def take(self, count=1):
        at = self.used
        self.used += count
        return at

    def copy(self, src, dst, target, at):
        return pltpu.make_async_remote_copy(
            src_ref=src,
            dst_ref=dst,
            send_sem=self.send_sem.at[at],
            recv_sem=self.recv_sem.at[at],
            device_id=target,
            device_id_type=MESH_ID,
        )

    def post(self, src, dst, target, when=None, lands=None):
        copy = self.copy(src, dst, target, self.take())
        guarded(when, copy.start)
        item = Posted(copy, when if lands is None else lands)
        self.posted.append(item)
        self.open.append((copy.wait_send, when))
        return item

    def land(self, item):
        if not item.landed:
            item.landed = True
            guarded(item.lands, item.copy.wait_recv)

    def keep(self, src, dst, when=None, now=False):
        copy = pltpu.make_async_copy(src, dst, self.local_sem.at[self.kept])
        self.kept += 1
        guarded(when, copy.start)
        if now:
            guarded(when, copy.wait)
        else:
            self.stays.append((copy.wait, when))

    def square(self, p, src, dst):
        across = p.q + 1 - 2 * lax.rem(p.q, 2)
        along = lax.rem(p.q + 2, 4)
        one = self.post(src, dst.at[p.q], {"grp": across})
        two = self.post(src, dst.at[p.q], {"grp": along})
        half = dst.shape[1] // 2
        top, bottom = pl.ds(0, half), pl.ds(half, half)

        def relay():
            self.land(one)
            block = dst.at[across, top]
            first = self.post(block, block, {"grp": along})
            self.land(two)
            block = dst.at[along, bottom]
            second = self.post(block, block, {"grp": across})
            return first, second

        return relay

    def settle_kept(self):
        for act, when in self.stays:
            guarded(when, act)
        self.stays = []

    def gather_team(self, p, src, dst):
        mine = p.c * p.R + p.z
        self.keep(src, dst.at[mine])
        return [self.post(src, dst.at[mine], {"duo": c, "rows": z}) for c, z in p.team()]

    def gather_group(self, p, src, dst):
        self.keep(src, dst.at[p.q])
        return [self.post(src, dst.at[p.q], {"grp": q}) for q in p.groups()]

    def swap_group(self, p, src, dst):
        self.keep(src.at[p.q], dst.at[p.q])
        for q in p.groups():
            self.post(src.at[q], dst.at[p.q], {"grp": q})

    def swap_team(self, p, src, dst):
        mine = p.c * p.R + p.z
        self.keep(src.at[mine], dst.at[mine])
        return [
            self.post(src.at[c * p.R + z], dst.at[mine], {"duo": c, "rows": z}) for c, z in p.team()
        ]

    def finish(self):
        self.settle_kept()
        for line in self.lines:
            line.settle(line.p.R)
        for item in self.posted:
            self.land(item)
        for act, when in self.open:
            guarded(when, act)


class LineGather:
    def __init__(self, flow, place, src, dst):
        self.flow, self.p, self.src, self.dst = flow, place, src, dst
        self.up = flow.take(place.R - 1)
        self.down = flow.take(place.R - 1)
        self.side = flow.take(2 * place.R - 1)

    def send(self, block, hop, direction):
        p, dst = self.p, self.dst
        src = self.src if hop == 0 else dst.at[p.c, block]
        at = (self.up if direction > 0 else self.down) + hop
        return self.flow.copy(src, dst.at[p.c, block], {"rows": p.z + direction}, at)

    def across(self, block, number):
        p, dst = self.p, self.dst
        src = self.src if isinstance(number, int) and number == 0 else dst.at[p.c, block]
        other = {"duo": lax.rem(p.c + 1, p.D)}
        return self.flow.copy(src, dst.at[p.c, block], other, self.side + number)

    def start(self):
        p = self.p
        for direction, ok in ((1, p.z < p.R - 1), (-1, p.z > 0)):
            copy = self.send(p.z, 0, direction)
            guarded(ok, copy.start)
            self.flow.open.append((copy.wait_send, ok))
        copy = self.across(p.z, 0)
        copy.start()
        self.flow.open.append((copy.wait_send, None))
        self.flow.lines.append(self)
        self.settled = 0

    def hop(self, step):
        p = self.p
        for direction, number in ((1, step), (-1, p.R - 1 + step)):
            block = p.z - direction * step
            ok = (block >= 0) if direction > 0 else (block < p.R)
            last = (p.z < p.R - 1) if direction > 0 else (p.z > 0)
            arrived = self.send(block, step - 1, direction)
            side = self.across(block, number)

            def relay(arrived=arrived, side=side, block=block, direction=direction, last=last):
                arrived.wait_recv()
                if step < p.R - 1:
                    pl.when(last)(self.send(block, step, direction).start)
                side.start()

            pl.when(ok)(relay)
            if step < p.R - 1:
                self.flow.open.append((self.send(block, step, direction).wait_send, ok & last))
            self.flow.open.append((side.wait_send, ok))


    def nth(self, number):
        p = self.p
        reach = [p.z]
        for step in range(1, p.R):
            reach += [p.z - step, p.z + step]
        seen, found = 0, jnp.int32(0)
        for block in reach:
            ok = (block >= 0) & (block < p.R)
            found = jnp.where(ok & (seen == number), block, found)
            seen = seen + jnp.where(ok, 1, 0)
        return found

    def settle(self, upto):
        p = self.p
        while self.settled < upto:
            block = self.nth(self.settled)
            number = jnp.where(block <= p.z, p.z - block, p.R - 1 + block - p.z)
            self.across(block, number).wait_recv()
            self.settled += 1


class LineGatherOn(LineGather):
    def start_from(self, near):
        p, flow = self.p, self.flow
        flow.lines.append(self)
        self.settled = 0
        flow.keep(near.at[0], self.dst.at[p.c, jnp.maximum(p.z - 1, 0)], p.z > 0)
        flow.keep(near.at[1], self.dst.at[p.c, jnp.minimum(p.z + 1, p.R - 1)], p.z < p.R - 1)
        flow.keep(self.src, self.dst.at[p.c, p.z])
        flow.settle_kept()
        copy = self.across(p.z, 0)
        copy.start()
        flow.open.append((copy.wait_send, None))
        for direction, number in ((1, 1), (-1, p.R)):
            block = p.z - direction
            ok = (block >= 0) if direction > 0 else (block < p.R)
            last = (p.z < p.R - 1) if direction > 0 else (p.z > 0)
            side = self.across(block, number)

            def relay(side=side, block=block, direction=direction, last=last):
                pl.when(last)(self.send(block, 1, direction).start)
                side.start()

            pl.when(ok)(relay)
            flow.open.append((self.send(block, 1, direction).wait_send, ok & last))
            flow.open.append((side.wait_send, ok))


class LineReduce:
    def __init__(self, flow, place, part, total_ref, mate, passed, landed):
        self.flow, self.p, self.part, self.total = flow, place, part, total_ref
        self.mate, self.passed, self.landed = mate, passed, landed
        self.side = flow.take(place.R)
        self.line = flow.take(2 * place.R)

    def across(self, block):
        p = self.p
        other = lax.rem(p.c + 1, p.D)
        return self.flow.copy(
            self.part.at[other, block], self.mate.at[block], {"duo": other}, self.side + block
        )

    def along(self, upward, block):
        p = self.p
        way = jnp.where(upward, 1, 0)
        target = {"rows": jnp.where(upward, p.z + 1, p.z - 1)}
        return self.flow.copy(
            self.passed.at[way, block],
            self.landed.at[way, block],
            target,
            self.line + way * p.R + block,
        )

    def steps(self):
        p = self.p
        low = p.z < p.R // 2
        for k in range(p.R - 1):
            for first in (True, False):
                upward = low if first else jnp.logical_not(low)
                block = jnp.where(upward, p.R - 1 - k, k)
                yield upward, block, jnp.where(upward, block > p.z, block < p.z)

    def start(self):
        p = self.p
        for k in range(p.R):
            block = jnp.where(p.z < p.R // 2, p.R - 1 - k, k)
            copy = self.across(block)
            copy.start()
            self.flow.open.append((copy.wait_send, None))

    def rows_of(self, act):
        count = self.part.shape[2]
        step = 16

        @pl.loop(0, count // step)
        def _(number):
            act(pl.ds(pl.multiple_of(number * step, step), step))

    def offer(self, block):
        copy = self.across(block)
        copy.start()
        self.flow.open.append((copy.wait_send, None))

    def early(self):
        for upward, block, ok in self.steps():
            behind = jnp.where(upward, self.p.z > 0, self.p.z < self.p.R - 1)
            self.step(upward, block, ok & jnp.logical_not(behind), False)

    def later(self):
        for upward, block, ok in self.steps():
            behind = jnp.where(upward, self.p.z > 0, self.p.z < self.p.R - 1)
            yield functools.partial(self.step, upward, block, ok & behind, True)

    def step(self, upward, block, ok, relays=None):
        p = self.p
        way = jnp.where(upward, 1, 0)
        behind = jnp.where(upward, p.z > 0, p.z < p.R - 1)

        def act():
            self.across(block).wait_recv()
            if relays is False:

                def add(rows):
                    self.passed[way, block, rows] = (
                        self.part[p.c, block, rows].astype(F32) + self.mate[block, rows].astype(F32)
                    ).astype(BF16)

                self.rows_of(add)
                self.along(upward, block).start()
                return

            @pl.when(behind)
            def _():
                self.along(upward, block).wait_recv()

                def add(rows):
                    self.passed[way, block, rows] = (
                        self.part[p.c, block, rows].astype(F32)
                        + self.mate[block, rows].astype(F32)
                        + self.landed[way, block, rows].astype(F32)
                    ).astype(BF16)

                self.rows_of(add)

            if relays is None:

                @pl.when(jnp.logical_not(behind))
                def _():
                    def add(rows):
                        self.passed[way, block, rows] = (
                            self.part[p.c, block, rows].astype(F32)
                            + self.mate[block, rows].astype(F32)
                        ).astype(BF16)

                    self.rows_of(add)

            self.along(upward, block).start()

        pl.when(ok)(act)
        self.flow.open.append((self.along(upward, block).wait_send, ok))

    def close(self):
        p = self.p
        self.across(p.z).wait_recv()

        def base(rows):
            self.total[rows] = self.part[p.c, p.z, rows].astype(F32) + self.mate[
                p.z, rows
            ].astype(F32)

        self.rows_of(base)
        for way, ok in ((1, p.z > 0), (0, p.z < p.R - 1)):

            def more(way=way):
                self.along(way == 1, p.z).wait_recv()

                def add(rows):
                    self.total[rows] += self.landed[way, p.z, rows].astype(F32)

                self.rows_of(add)

            pl.when(ok)(more)

    def steps_all(self):
        self.early()
        for act in self.later():
            act()
        self.close()

    def run(self, produce=None, between=None):
        p = self.p
        if produce is None:
            self.steps_all()
            return
        ready = 0

        def more():
            block = line_order(p, ready)
            produce(block)
            copy = self.across(block)
            copy.start()
            self.flow.open.append((copy.wait_send, None))

        for number, (upward, block, ok) in enumerate(self.steps()):
            while ready < min(number + 2, p.R):
                more()
                ready += 1
            self.step(upward, block, ok)
            if between is not None:
                between(number)
        self.close()


def team_kernel(
    ident, name, plan, arrays, results, gathers=(), reduces=(), messages=0, local=1, late=None
):
    D, R = lax.axis_size("duo"), lax.axis_size("rows")
    count_a, count_g, count_r = len(arrays), len(gathers), len(reduces)
    extra = 0 if late is None else 1
    total_sems = messages + (count_g + extra) * (4 * R - 3) + count_r * 3 * R

    def kernel(*refs):
        refs = list(refs)
        ins = refs[:count_a]
        g_in = refs[count_a : count_a + count_g]
        r_in = refs[count_a + count_g : count_a + count_g + count_r]
        refs = refs[count_a + count_g + count_r :]
        outs = refs[: len(results)]
        refs = refs[len(results) :]
        late_out = refs[:extra]
        g_out = refs[extra : extra + count_g]
        r_out = refs[extra + count_g : extra + count_g + count_r]
        refs = refs[extra + count_g + count_r :]
        send_sem, recv_sem, local_sem = refs[:3]
        buffers = refs[3:]
        p = Place()
        flow = Flow(send_sem, recv_sem)
        greet, direct, stay = plan(p, ins, outs)
        barrier = pltpu.get_barrier_semaphore()
        waits = 0
        for target, when in greet:
            if when is None:
                waits = waits + 1
            else:
                waits = waits + jnp.where(when, 1, 0).astype(jnp.int32)
            guarded(when, lambda target=target: signal_all(barrier, [target]))
        pl.semaphore_wait(barrier, waits)
        lines = [LineGather(flow, p, src, dst) for src, dst in zip(g_in, g_out)]
        sums = [
            LineReduce(flow, p, src, dst, *buffers[3 * n : 3 * n + 3])
            for n, (src, dst) in enumerate(zip(r_in, r_out))
        ]
        base = flow.take(messages)
        copies = {}
        arrived = set()

        stays = []

        def landed(number):
            if number not in arrived:
                arrived.add(number)
                guarded(copies[number][2], copies[number][0].wait_recv)

        def run_stage(stage):
            for number, (src, dst, target, after, when, when_stage, lands) in enumerate(direct):
                if when_stage != stage:
                    continue
                for earlier in after:
                    landed(earlier)
                copy = flow.copy(src, dst, target, base + number)
                guarded(when, copy.start)
                copies[number] = (copy, when, lands)
            if late is not None and late[1] == stage:
                for number in range(late[2]):
                    landed(number)
                stays[0][0].wait()
                line = LineGather(flow, p, outs[late[0]], late_out[0])
                line.start()
                own = pltpu.make_async_copy(
                    outs[late[0]], late_out[0].at[p.c, p.z], local_sem.at[local + count_g]
                )
                own.start()
                stays[0] = (own, None)
                if stage:
                    for earlier in range(1, stage + 1):
                        line.hop(earlier)
                lines.append(line)

        for item in sums:
            item.start()
        for line in lines:
            line.start()
        for number, (src, dst, when) in enumerate(
            list(stay) + [(src, dst.at[p.c, p.z], None) for src, dst in zip(g_in, g_out)]
        ):
            copy = pltpu.make_async_copy(src, dst, local_sem.at[number])
            guarded(when, copy.start)
            stays.append((copy, when))
        run_stage(0)
        for step in range(1, R):
            for line in lines:
                line.hop(step)
            run_stage(step)
        for item in sums:
            item.run()
        for copy, when in stays:
            guarded(when, copy.wait)
        for number in copies:
            landed(number)
        for copy, when, _ in copies.values():
            guarded(when, copy.wait_send)
        flow.finish()

    spot = pl.BlockSpec(memory_space=pl.ANY)
    near = pl.BlockSpec(memory_space=pltpu.VMEM)
    out_shape = [jax.ShapeDtypeStruct(shape, kind) for shape, kind in results]
    if late is not None:
        shape, kind = results[late[0]]
        out_shape.append(jax.ShapeDtypeStruct((D, R) + shape, kind))
    out_shape += [jax.ShapeDtypeStruct((D, R) + g.shape, g.dtype) for g in gathers]
    out_shape += [jax.ShapeDtypeStruct(r.shape[2:], F32) for r in reduces]
    scratch = [
        pltpu.SemaphoreType.DMA((total_sems,)),
        pltpu.SemaphoreType.DMA((total_sems,)),
        pltpu.SemaphoreType.DMA((local + count_g + extra,)),
    ]
    for r in reduces:
        block = r.shape[1:]
        scratch += [
            pltpu.VMEM(block, BF16),
            pltpu.VMEM((2,) + block, BF16),
            pltpu.VMEM((2,) + block, BF16),
        ]
    return pl.pallas_call(
        kernel,
        out_shape=out_shape,
        in_specs=[spot] * (count_a + count_g) + [near] * count_r,
        out_specs=[spot] * (len(results) + extra + count_g) + [near] * count_r,
        scratch_shapes=scratch,
        compiler_params=pltpu.CompilerParams(
            collective_id=ident, has_side_effects=True, vmem_limit_bytes=56 * 2**20
        ),
        name=name,
    )(*arrays, *gathers, *reduces)


def team_greet(p):
    return [({"duo": c, "rows": z}, None) for c, z in p.team()]


def group_greet(p):
    return [({"grp": q}, None) for q in p.groups()]


class Plan:
    def __init__(self, p):
        self.p = p
        self.messages, self.local, self.greet = [], [], []

    def add(self, src, dst, target, after=(), when=None, stage=0, lands=None):
        self.messages.append((src, dst, target, after, when, stage, when if lands is None else lands))
        return len(self.messages) - 1

    def team_swap(self, src, dst, stage=0):
        p = self.p
        mine = p.c * p.R + p.z
        for c, z in p.team():
            self.add(src.at[c * p.R + z], dst.at[mine], {"duo": c, "rows": z}, stage=stage)
        self.local.append((src.at[mine], dst.at[mine], None))

    def team_gather(self, src, dst, stage=0):
        p = self.p
        mine = p.c * p.R + p.z
        for c, z in p.team():
            self.add(src, dst.at[mine], {"duo": c, "rows": z}, stage=stage)
        self.local.append((src, dst.at[mine], None))

    def group_gather(self, src, dst, late=None):
        p = self.p
        self.local.append((src, dst.at[p.q], None))
        if late is None or p.G != 4:
            for q in p.groups():
                self.add(src, dst.at[p.q], {"grp": q})
            return
        across = p.q + 1 - 2 * lax.rem(p.q, 2)
        along = lax.rem(p.q + 2, 4)
        one = self.add(src, dst.at[p.q], {"grp": across})
        two = self.add(src, dst.at[p.q], {"grp": along})
        half = src.shape[0] // 2
        top, bottom = pl.ds(0, half), pl.ds(half, half)
        self.add(
            dst.at[across, top], dst.at[across, top], {"grp": along}, after=(one,), stage=late
        )
        self.add(
            dst.at[along, bottom],
            dst.at[along, bottom],
            {"grp": across},
            after=(two,),
            stage=late,
        )

    def group_swap(self, src, dst, stage=0):
        p = self.p
        for q in p.groups():
            self.add(src.at[q], dst.at[p.q], {"grp": q}, stage=stage)
        self.local.append((src.at[p.q], dst.at[p.q], None))

    def done(self):
        p = self.p
        return team_greet(p) + group_greet(p) + self.greet, self.messages, self.local


def layer_stats(values):
    center = values - jnp.mean(values, axis=-1, keepdims=True)
    spread = jnp.mean(center * center, axis=-1, keepdims=True)
    inverse = lax.rsqrt(spread + norm_eps)
    return center * inverse, inverse


def layer_back(grad, hat, inverse):
    first = jnp.mean(grad, axis=-1, keepdims=True)
    second = jnp.mean(grad * hat, axis=-1, keepdims=True)
    return inverse * (grad - first - hat * second)


def mm(left, right):
    return jnp.dot(left, right, preferred_element_type=F32)


def mm_t(left, right):
    return lax.dot_general(left, right, (((1,), (1,)), ((), ())), preferred_element_type=F32)


def t_mm(left, right):
    return lax.dot_general(left, right, (((0,), (0,)), ((), ())), preferred_element_type=F32)


def columns_of(bucket_ids):
    return jnp.where(
        bucket_ids == 0, 9 * UNIT // 2, jnp.where(bucket_ids == 1, 3 * UNIT, 9 * UNIT // 4)
    )


def pixel_mask(positions, height, width, cols):
    row_at = positions // cols
    col_at = positions % cols
    return ((row_at < height) & (col_at < width)).astype(F32)


def spots(shapes):
    return [jax.ShapeDtypeStruct(shape, kind) for shape, kind in shapes]


def local_kernel(name, kernel, arrays, results, scratch=(), scalars=0):
    near = pl.BlockSpec(memory_space=pltpu.VMEM)
    numbers = pl.BlockSpec(memory_space=pltpu.SMEM)
    return pl.pallas_call(
        kernel,
        out_shape=spots(results),
        in_specs=[numbers] * scalars + [near] * (len(arrays) - scalars),
        out_specs=[near] * len(results),
        scratch_shapes=list(scratch),
        compiler_params=pltpu.CompilerParams(vmem_limit_bytes=56 * 2**20),
        name=name,
    )(*arrays)


class Sizes:
    def __init__(self, latents, clip_tokens, in_weight, in_bias, conv_bias, map_weight):
        self.G, self.D, self.R = (lax.axis_size(axis) for axis in AXES)
        self.T = self.D * self.R
        self.S = self.T * self.G
        self.N, self.C = latents.shape[1:]
        self.pixels = self.R * self.N
        self.FFS = in_bias.shape[0]
        self.FL = self.G * self.FFS
        self.FF = in_weight.shape[1]
        self.cs = conv_bias.shape[0]
        self.ms = map_weight.shape[0]
        self.mp = -(-self.ms // 16) * 16
        self.slots = clip_tokens.shape[1]
        self.sp = -(-self.slots // 16) * 16
        self.texts = self.R * self.slots
        self.HW = self.C // self.T
        self.even = self.G == self.R
        self.Q = self.G if self.even else 1
        self.places = [(g, d, r) for g in range(self.G) for d in range(self.D) for r in range(self.R)]


def rows_cols(first, count, cols):
    position = (first + lax.broadcasted_iota(jnp.int32, (count, 1), 0)).astype(F32)
    row = jnp.floor((position + 0.5) / cols)
    return row, position - row * cols


def float_cols(bucket):
    return jnp.where(bucket == 0, 9.0 * UNIT / 2, jnp.where(bucket == 1, 3.0 * UNIT, 9.0 * UNIT / 4))


WIDTHS = (9 * UNIT // 2, 3 * UNIT, 9 * UNIT // 4)
SMALL = 16
VEC = 16
FACTS = 96


def cut_kernel(m, arrays):
    def kernel(h_ref, w_ref, b_ref, in_ref, qkv_ref, map_ref, clip_ref, lat_ref, cot_ref, cw_ref, *refs):
        vectors, refs = refs[:5], refs[5:]
        te_ref, tm_ref, f0, f1, f2 = refs[:5]
        in_out, qkv_out, map_out, clip_out, masked_out, gres_out, small_out, f_out, small, fv = refs[5:]
        for g in range(m.G):
            for t in range(m.T):
                start = m.FFS * (g * m.T + t)
                in_out[t, :, pl.ds(g * m.FFS, m.FFS)] = in_ref[:, pl.ds(start, m.FFS)]
        for d in range(m.D):
            for r in range(m.R):
                for j in range(3):
                    start = m.C * j + m.HW * (m.D * r + d)
                    qkv_out[d * m.R + r, :, pl.ds(j * m.HW, m.HW)] = qkv_ref[:, pl.ds(start, m.HW)]
        map_out[...] = jnp.zeros_like(map_out)
        for t in range(m.T):
            map_out[t, pl.ds(0, m.ms)] = map_ref[:, pl.ds(t * m.HW, m.HW)]
        clip_out[...] = jnp.zeros_like(clip_out)
        clip_out[pl.ds(0, m.slots)] = clip_ref[0]
        z = lax.axis_index("rows")
        row, col = rows_cols(z * m.N, m.N, float_cols(b_ref[0]))
        keep = (row < h_ref[0].astype(F32)) & (col < w_ref[0].astype(F32))
        masked_out[...] = jnp.where(keep, lat_ref[0].astype(F32), 0.0).astype(BF16)
        gres_out[...] = jnp.where(keep, cot_ref[0].astype(F32), 0.0).astype(BF16)
        small[...] = jnp.zeros_like(small)
        small[pl.ds(0, 9), pl.ds(0, m.cs)] = cw_ref[...].astype(F32)
        for number, ref in enumerate(vectors):
            small[pl.ds(9 + number, 1), pl.ds(0, ref.shape[0])] = ref[...].astype(F32).reshape(1, -1)
        small[pl.ds(14, 1), pl.ds(0, te_ref.shape[1])] = te_ref[...].astype(F32)
        lane = lax.broadcasted_iota(jnp.int32, (1, 128), 1)
        for number, ref in enumerate((h_ref, w_ref, b_ref)):
            fact = jnp.full((1, 128), ref[0]).astype(F32)
            row = small[pl.ds(14, 1)]
            small[pl.ds(14, 1)] = jnp.where(lane == FACTS + number, fact, row)
        small[pl.ds(15, 1), pl.ds(0, m.texts)] = tm_ref[...].astype(F32)
        small_out[...] = small[...].astype(BF16)
        fv[...] = jnp.zeros_like(fv)
        for number, ref in enumerate((f0, f1, f2)):
            fv[pl.ds(number, 1)] = ref[...].astype(F32).reshape(1, -1)
        f_out[...] = fv[...].astype(BF16)

    return local_kernel(
        "cut_weights",
        kernel,
        arrays,
        [
            ((m.T, m.cs, m.FL), BF16),
            ((m.T, m.cs, 3 * m.HW), BF16),
            ((m.T, m.mp, m.HW), BF16),
            ((m.sp, arrays[6].shape[2]), BF16),
            ((m.N, m.C), BF16),
            ((m.N, m.C), BF16),
            ((SMALL, 128), BF16),
            ((16, m.FFS), BF16),
        ],
        [pltpu.VMEM((SMALL, 128), F32), pltpu.VMEM((16, m.FFS), F32)],
        scalars=3,
    )


def fill_extended(m, extended, edges_ref, mid_ref):
    z = lax.axis_index("rows")
    extended[pl.ds(0, EDGE)] = jnp.where(z > 0, edges_ref[0].astype(F32), 0.0)
    extended[pl.ds(EDGE, m.N)] = mid_ref[...].astype(F32)
    extended[pl.ds(EDGE + m.N, EDGE)] = jnp.where(z < m.R - 1, edges_ref[1].astype(F32), 0.0)


def each_bucket(bucket, act):
    for number, width in enumerate(WIDTHS):
        pl.when(bucket == number)(functools.partial(act, width))


def each_column_block(m, act):
    @pl.loop(0, m.C // 128)
    def _(number):
        act(pl.ds(pl.multiple_of(number * 128, 128), 128))


def tap_steps():
    return [(index, index // 3 - 1, index % 3 - 1) for index in range(9)]


def conv_back_kernel(m, b_ref, grad_in, hat, inv, edges, masked, vec_grads, map_grad, qv_grads, modulate_grads):
    def kernel(b_ref, g_ref, hat_ref, inv_ref, edges_ref, mid_ref, vec_ref, map_ref, qv_ref, gm_ref, grad, low, tiny, extended, vec):
        values = layer_back(g_ref[...], hat_ref[...], inv_ref[...])
        grad[...] = values
        low[...] = values.astype(BF16)
        fill_extended(m, extended, edges_ref, mid_ref)
        vec[pl.ds(9, 1)] = jnp.sum(values, axis=0, keepdims=True)
        vec[pl.ds(10, 2)] = vec_ref[pl.ds(0, 2)]
        vec[pl.ds(12, 1)] = map_ref[pl.ds(0, 1)]
        vec[pl.ds(13, 3)] = jnp.zeros((3, m.C), F32)
        z = lax.axis_index("rows")

        def taps(width):
            _, col = rows_cols(z * m.N, m.N, float(width))

            def block(lanes):
                value = grad[:, lanes]
                for index, dy, dx in tap_steps():
                    piece = extended[pl.ds(EDGE + dy * width + dx, m.N), lanes]
                    ok = (col + dx >= 0) & (col + dx < width)
                    vec[pl.ds(index, 1), lanes] = jnp.sum(
                        jnp.where(ok, piece, 0.0) * value, axis=0, keepdims=True
                    )

            each_column_block(m, block)

        each_bucket(b_ref[0], taps)
        tiny[...] = jnp.zeros_like(tiny)
        half = m.S // 2
        pair = 2 * m.cs
        for s, (g, d, r) in enumerate(m.places):
            t = d * m.R + r
            tiny[t, g, pl.ds(0, 13), pl.ds(0, m.cs)] = vec[pl.ds(0, 13), pl.ds(s * m.cs, m.cs)]
            side, at = pl.ds(s // half, 1), pl.ds(pair * (s % half), pair)
            tiny[t, g, pl.ds(13, 1), pl.ds(0, pair)] = qv_ref[side, at]
            tiny[t, g, pl.ds(14, 1), pl.ds(0, pair)] = gm_ref[side, at]

    return local_kernel(
        "convolve_back",
        kernel,
        [b_ref, grad_in, hat, inv, edges, masked, vec_grads, map_grad, qv_grads, modulate_grads],
        [((m.N, m.C), F32), ((m.N, m.C), BF16), ((m.T, m.G, 16, 128), F32)],
        [pltpu.VMEM((m.N + 2 * EDGE, m.C), F32), pltpu.VMEM((VEC, m.C), F32)],
        scalars=1,
    )


def finish_kernel(m, b_ref, edges, low, after, pix, vec, in_team, qkv_team, map_team, proj_team, out_parts, tiny_all, f_parts, embed, rdim):
    def kernel(b_ref, edges_ref, low_ref, after_ref, pix_ref, vec_ref, in_ref, qkv_ref, map_ref, proj_ref, parts_ref, tiny_ref, f_ref, te_ref,
               lat_out, in_out, qkv_out, map_out, proj_out, out_out, cw_out, time_out, *refs):
        singles, (extended,) = refs[:10], refs[10:]
        total = jnp.zeros(tiny_ref.shape[2:], F32)
        times = jnp.zeros((128, 128), F32)
        turned = te_ref[...].T
        for g in range(m.G):
            for d in range(m.D):
                item = tiny_ref[g, d]
                total = total + item
                at = m.D * g + d
                times = times + turned[:, at : at + 1] * item[14:15]
        cw_out[...] = total[:9, : m.cs]
        time_out[...] = times[:rdim, : 2 * m.cs]
        for number, ref in enumerate(singles[:6]):
            ref[...] = total[9 + number, : ref.shape[0]]
        sums = f_ref[0]
        for g in range(1, m.G):
            sums = sums + f_ref[g]
        for number, ref in enumerate(singles[6:9]):
            ref[...] = sums[number, :]
        singles[9][...] = total[15, :]
        fill_extended(m, extended, edges_ref, low_ref)
        z = lax.axis_index("rows")
        keep = pix_ref[...] > 0

        def taps(width):
            _, col = rows_cols(z * m.N, m.N, float(width))

            def block(lanes):
                total = jnp.zeros((m.N, 128), F32)
                for index, dy, dx in tap_steps():
                    piece = extended[pl.ds(EDGE - dy * width - dx, m.N), lanes]
                    ok = (col - dx >= 0) & (col - dx < width)
                    total = total + jnp.where(ok, piece, 0.0) * vec_ref[pl.ds(index, 1), lanes]
                lat_out[0, :, lanes] = after_ref[:, lanes] + jnp.where(keep, total, 0.0)

            each_column_block(m, block)

        each_bucket(b_ref[0], taps)
        for g in range(m.G):
            for t in range(m.T):
                start = m.FFS * (g * m.T + t)
                in_out[:, pl.ds(start, m.FFS)] = in_ref[t, :, pl.ds(g * m.FFS, m.FFS)].astype(F32)
        for d in range(m.D):
            for r in range(m.R):
                for j in range(3):
                    start = m.C * j + m.HW * (m.D * r + d)
                    qkv_out[:, pl.ds(start, m.HW)] = qkv_ref[
                        d * m.R + r, :, pl.ds(j * m.HW, m.HW)
                    ].astype(F32)
        for t in range(m.T):
            map_out[:, pl.ds(t * m.HW, m.HW)] = map_ref[t].astype(F32)[: m.ms]
        total = parts_ref[0].astype(F32)
        for g in range(1, m.G):
            total = total + parts_ref[g].astype(F32)
        out_out[...] = total
        wide = m.C // m.Q
        for n in range(m.Q):
            proj_out[:, pl.ds(n * wide, wide)] = proj_ref[n].astype(F32)

    return local_kernel(
        "finish",
        kernel,
        [b_ref, edges, low, after, pix, vec, in_team, qkv_team, map_team, proj_team, out_parts]
        + [tiny_all, f_parts, embed],
        [
            ((1, m.N, m.C), F32),
            ((m.cs, m.FF), F32),
            ((m.cs, 3 * m.C), F32),
            ((m.ms, m.C), F32),
            ((m.cs, m.C), F32),
            ((m.FFS, m.C), F32),
            ((9, m.cs), F32),
            ((rdim, 2 * m.cs), F32),
        ]
        + [((m.cs,), F32)] * 4
        + [((2 * m.cs,), F32)] * 2
        + [((m.FFS,), F32)] * 3
        + [((128,), F32)],
        [pltpu.VMEM((m.N + 2 * EDGE, m.C), F32)],
        scalars=1,
    )


class Posted:
    def __init__(self, copy, lands):
        self.copy, self.lands, self.landed = copy, lands, False


def line_order(p, number):
    low = p.z < p.R // 2
    far, near = p.R - 1 - number // 2, number // 2
    if number % 2:
        far, near = near, far
    return jnp.where(low, far, near)


STRIPES = 3
AHEAD = 2


def chunks(count, act, step=16, first=0):
    @pl.loop(0, count // step)
    def _(number):
        act(pl.ds(pl.multiple_of(first + number * step, step), step))


def each_rows(count, step, act):
    if step % 16:
        for number in range(count):
            act(number, pl.ds(number * step, step))
    else:

        @pl.loop(0, count)
        def _(number):
            act(number, pl.ds(pl.multiple_of(number * step, 16), step))


def greet_all(p, targets):
    barrier = pltpu.get_barrier_semaphore()
    waits = 0
    for target, when in targets:
        if when is None:
            waits = waits + 1
        else:
            waits = waits + jnp.where(when, 1, 0).astype(jnp.int32)
        guarded(when, lambda target=target: signal_all(barrier, [target]))
    pl.semaphore_wait(barrier, waits)


def fused_kernel(
    ident, name, greet, act, near, loads, far, near_out, far_out, scratch, sems, local, numbers=0
):
    close = pl.BlockSpec(memory_space=pltpu.VMEM)
    spot = pl.BlockSpec(memory_space=pl.ANY)
    counts = [len(near), len(loads), len(far), len(near_out), len(far_out), len(scratch), len(loads)]

    def kernel(*refs):
        groups = []
        for count in counts:
            groups.append(refs[:count])
            refs = refs[count:]
        send_sem, recv_sem, local_sem, load_sem = refs
        near, sources, far, near_out, far_out, scratch, held = groups
        brought = []
        for number, (source, place) in enumerate(zip(sources, held)):
            copy = pltpu.make_async_copy(source, place, load_sem.at[number])
            copy.start()
            brought.append(Brought(copy, place))
        p = Place()
        flow = Flow(send_sem, recv_sem, local_sem)
        greet_all(p, greet(p))
        act(p, flow, near, brought, far, near_out, far_out, scratch)
        flow.finish()
        if flow.used > sems or flow.kept > local:
            raise ValueError(f"{name}: {flow.used} {flow.kept}")

    return pl.pallas_call(
        kernel,
        out_shape=spots(near_out + far_out),
        in_specs=[pl.BlockSpec(memory_space=pltpu.SMEM)] * numbers
        + [close] * (len(near) - numbers)
        + [spot] * (len(loads) + len(far)),
        out_specs=[close] * len(near_out) + [spot] * len(far_out),
        scratch_shapes=list(scratch)
        + [pltpu.VMEM(array.shape, array.dtype) for array in loads]
        + [
            pltpu.SemaphoreType.DMA((sems,)),
            pltpu.SemaphoreType.DMA((sems,)),
            pltpu.SemaphoreType.DMA((local,)),
            pltpu.SemaphoreType.DMA((max(len(loads), 1),)),
        ],
        compiler_params=pltpu.CompilerParams(
            collective_id=ident, has_side_effects=True, vmem_limit_bytes=63 * 2**20
        ),
        name=name,
    )(*near, *loads, *far)


class Brought:
    def __init__(self, copy, place):
        self.copy, self.place, self.here = copy, place, False

    def get(self):
        if not self.here:
            self.copy.wait()
            self.here = True
        return self.place


class Stripes:
    def __init__(self, flow, p, part, total, buffers, src, dst):
        count = part.shape[2]
        self.p, self.flow, self.src, self.dst = p, flow, src, dst
        step = count // STRIPES
        self.rows = [pl.ds(number * step, step) for number in range(STRIPES)]
        mate, passed, landed = buffers
        self.sums = [
            LineReduce(
                flow,
                p,
                part.at[:, :, rows],
                total.at[rows],
                mate.at[:, rows],
                passed.at[:, :, rows],
                landed.at[:, :, rows],
            )
            for rows in self.rows
        ]
        self.lines = [LineGather(flow, p, src.at[rows], dst.at[:, :, rows]) for rows in self.rows]

    def run(self, act, before=None, between=None):
        p = self.p
        for item in self.sums:
            for number in range(p.R):
                item.offer(line_order(p, number))
        for number, item in enumerate(self.sums[:AHEAD]):
            item.early()
            if before is not None and number == 0:
                before()
        size = self.rows[0].size
        hops = [0] * STRIPES

        def hop(number):
            if hops[number] < p.R - 1:
                hops[number] += 1
                self.lines[number].hop(hops[number])

        for number, item in enumerate(self.sums):
            for step in item.later():
                step()
            item.close()
            chunks(size, act, first=number * size)
            self.lines[number].start()
            rows = self.rows[number]
            self.flow.keep(self.src.at[rows], self.dst.at[p.c, p.z, rows])
            if number + AHEAD < STRIPES:
                self.sums[number + AHEAD].early()
            if between is not None:
                between(number)
        while min(hops) < p.R - 1:
            for number in range(STRIPES):
                hop(number)


def gather_sems(m):
    return 4 * m.R - 3


def reduce_sems(m):
    return 3 * m.R


def reduce_buffers(m, count, width, part=True):
    block = (m.R, count, width)
    mine = [pltpu.VMEM((m.D,) + block, BF16)] if part else []
    return mine + [
        pltpu.VMEM(block, BF16),
        pltpu.VMEM((2,) + block, BF16),
        pltpu.VMEM((2,) + block, BF16),
    ]


def spread_greet(m, p):
    greet = []
    for step in range(m.G):
        source = {"grp": p.z, "duo": p.c, "rows": lax.rem(p.q - step + m.G, m.G)}
        greet.append((source, None if step else p.q != p.z))
    return greet


def common_greet(p):
    return team_greet(p) + group_greet(p)


def front_kernel(m, time_weight, time_bias, masked, small, fvec, in_cut, out_weight, map_cut, qkv_cut, clip_pad, proj_weight):
    near = [time_weight, time_bias]
    loads = [masked]
    far = [masked, small, fvec, in_cut, out_weight, map_cut, qkv_cut, clip_pad]
    far += [proj_weight] if m.even else []
    N, C, FL, G, T = m.N, m.C, m.FL, m.G, m.T
    root = 0.5**0.5
    texts = m.D * m.texts
    cond = clip_pad.shape[1]
    wide = C // m.Q
    square = G == 4
    items = m.G * m.D
    mod_rows = -(-items // 8) * 8
    pair = 2 * m.cs

    def act(p, flow, near, loads, far, near_out, far_out, scratch):
        tw_ref, tb_ref = near
        norms, total, silu, mapped = near_out[:4]
        hat, inv, vec, fv, keep, pix, qkv_bias, embed, edges, normed = near_out[4:]
        x_out, in_out, active_out, slope_out, out_all, qkv_rows, mod_all, mod_line = far_out[:8]
        map_all, clip_all, squares, weight, text, small_all, f_all, extended, conv, te, mod = scratch[:11]
        x_all, in_all, active, slope = scratch[11:]
        mid, small_ref, fvec_ref, in_cut, out_own, map_cut, qkv_cut, clip = far[:8]
        mine = p.c * p.R + p.z
        own_in = in_all.at[p.q]
        small_posts = [
            flow.post(small_ref, small_all.at[mine, p.q], {"grp": to}) for to in p.groups()
        ]
        edge_posts = []
        for block, to, sends, lands in (
            (mid.at[pl.ds(N - EDGE, EDGE)], p.z + 1, p.z < p.R - 1, p.z > 0),
            (mid.at[pl.ds(0, EDGE)], p.z - 1, p.z > 0, p.z < p.R - 1),
        ):
            slot = jnp.where(to > p.z, 0, 1)
            edge_posts.append(
                flow.post(block, edges.at[slot], {"rows": to}, when=sends, lands=lands)
            )
        f_posts = [flow.post(fvec_ref, f_all.at[p.q], {"grp": to}) for to in p.groups()]
        flow.keep(small_ref, small_all.at[mine, p.q], now=True)
        for item in small_posts:
            flow.land(item)
        spread = [
            flow.post(small_all.at[mine], small_all.at[mine], {"duo": c, "rows": z})
            for c, z in p.team()
        ]
        in_team = [
            flow.post(in_cut.at[c * p.R + z], own_in.at[mine], {"duo": c, "rows": z})
            for c, z in p.team()
        ]
        if square:
            out_relay = flow.square(p, out_own, out_all)
            flow.keep(out_own, out_all.at[p.q])
        else:
            flow.gather_group(p, out_own, out_all)
        own_map = map_all.at[p.q]
        map_team = [
            flow.post(map_cut.at[c * p.R + z], own_map.at[mine], {"duo": c, "rows": z})
            for c, z in p.team()
        ]
        clip_line = LineGather(flow, p, clip, clip_all)
        clip_line.start()
        flow.keep(in_cut.at[mine], own_in.at[mine], now=True)
        flow.keep(map_cut.at[mine], own_map.at[mine], now=True)
        flow.keep(clip, clip_all.at[p.c, p.z], now=True)
        flow.keep(fvec_ref, f_all.at[p.q], now=True)
        for item in spread + edge_posts:
            flow.land(item)
        half = m.S // 2
        vec[...] = jnp.zeros_like(vec)
        for s, (g, d, r) in enumerate(m.places):
            piece = small_all[d * m.R + r, g].astype(F32)
            vec[pl.ds(0, 13), pl.ds(s * m.cs, m.cs)] = piece[:13, : m.cs]
            vec[pl.ds(13 + s // half, 1), pl.ds(pair * (s % half), pair)] = piece[13:14, :pair]
            if r == 0:
                embed[pl.ds(m.D * g + d, 1)] = piece[14:15]
        extended[pl.ds(0, EDGE)] = jnp.where(p.z > 0, edges[0].astype(F32), 0.0)
        extended[pl.ds(EDGE, N)] = loads[0].get()[...].astype(F32)
        extended[pl.ds(EDGE + N, EDGE)] = jnp.where(p.z < m.R - 1, edges[1].astype(F32), 0.0)
        kind = small_all[mine, p.q].astype(F32)[14:15, FACTS + 2 : FACTS + 3]
        real = float_cols(kind)
        _, col = rows_cols(p.z * N, N, real)

        def taps(lanes):
            sum_of = jnp.zeros((N, 128), F32) + vec[pl.ds(9, 1), lanes]
            for index, dy, dx in tap_steps():
                pieces = [
                    extended[pl.ds(EDGE + dy * width + dx, N), lanes]
                    for width in (WIDTHS if dy else WIDTHS[:1])
                ]
                piece = pieces[0]
                if dy:
                    piece = jnp.where(kind == 0, piece, jnp.where(kind == 1, pieces[1], pieces[2]))
                ok = (col + dx >= 0) & (col + dx < real)
                sum_of = sum_of + jnp.where(ok, piece, 0.0) * vec[pl.ds(index, 1), lanes]
            conv[:, lanes] = sum_of

        each_column_block(m, taps)
        values, inverse = layer_stats(conv[...])
        hat[...] = values
        normed[...] = values.astype(BF16)
        inv[...] = inverse
        line = LineGather(flow, p, normed, x_all)
        line.start()
        flow.keep(normed, x_all.at[p.c, p.z], now=True)
        te[...] = embed[...][:items, : te.shape[1]].astype(BF16)
        mod[...] = jnp.zeros_like(mod)
        mod[pl.ds(0, items), pl.ds(0, pair)] = mm(te[...], tw_ref[...]) + tb_ref[...].astype(F32)
        mod_posts = flow.gather_group(p, mod, mod_all)
        for item in in_team:
            flow.land(item)
        if square:
            in_relay = flow.square(p, own_in, in_all)
        else:
            in_posts = [flow.post(own_in, in_all.at[p.q], {"grp": q}) for q in p.groups()]
        for d in range(m.D):
            facts = small_all[d * m.R, p.q].astype(F32)
            row, col_all = rows_cols(0, m.pixels, float_cols(facts[14:15, FACTS + 2 : FACTS + 3]))
            inside = (row < facts[14:15, FACTS : FACTS + 1]) & (
                col_all < facts[14:15, FACTS + 1 : FACTS + 2]
            )
            keep[d, pl.ds(0, m.pixels)] = jnp.where(inside, 1.0, 0.0)
            shown = facts.T[: m.texts, 15:16]
            slot = lax.broadcasted_iota(jnp.int32, (m.texts, 1), 0)
            keep[d, pl.ds(m.pixels, m.texts)] = jnp.where(slot < TXT, shown, 0.0)
        pix[...] = keep[p.c, pl.ds(pl.multiple_of(p.z * N, 8), N)]
        for item in f_posts:
            flow.land(item)
        for g in range(G):
            fv[:, pl.ds(g * m.FFS, m.FFS)] = f_all[g].astype(F32)[:8]
        qkv_bias[...] = jnp.zeros_like(qkv_bias)
        for h in range(T):

            @pl.when(p.D * p.z + p.c == h)
            def _():
                at = pl.ds(h * m.HW, m.HW)
                qkv_bias[:, : m.HW] = vec[pl.ds(13, 1), at]
                qkv_bias[:, 2 * m.HW :] = vec[pl.ds(14, 1), at]

        for item in map_team:
            flow.land(item)
        map_posts = [flow.post(own_map, map_all.at[p.q], {"grp": q}) for q in p.groups()]
        for step in range(1, m.R):
            clip_line.hop(step)
        line.hop(1)
        if square:
            out_relay()
        clip_line.settle(m.R)
        for item in map_posts:
            flow.land(item)
        for d in range(m.D):
            for r in range(m.R):
                piece = clip_all[d, r].astype(F32)[: m.slots]
                text[pl.ds((d * m.R + r) * m.slots, m.slots)] = piece / (1.0 + jnp.exp(-piece))
        silu[...] = text[...].astype(BF16)
        for g in range(G):
            for t in range(T):
                piece = map_all[g, t].astype(F32)
                weight[pl.ds(m.ms * (g * T + t), m.ms)] = piece[: m.ms]
        product = mm(silu[...], weight[...].astype(BF16))
        for t in range(T):

            @pl.when(mine == t)
            def _():
                mapped[...] = (product + vec[pl.ds(11, 1), pl.ds(t * m.HW, m.HW)]).astype(BF16)

        line.hop(2)
        if square:
            in_posts = in_relay()
        for item in mod_posts:
            flow.land(item)
        flow.settle_kept()
        mods = LineGather(flow, p, mod_all, mod_line)
        mods.start()
        flow.keep(mod_all, mod_line.at[p.c, p.z])
        flow.swap_team(p, qkv_cut, qkv_rows)
        if m.even:
            for number in range(G):
                to = lax.rem(p.z + number, G)
                piece = far[8].at[:, pl.ds(pl.multiple_of(to * wide, 128), wide)]
                flow.post(
                    piece,
                    far_out[8].at[p.z],
                    {"grp": to, "duo": p.c, "rows": p.q},
                    when=None if number else p.q != p.z,
                )
            piece = far[8].at[:, pl.ds(pl.multiple_of(p.z * wide, 128), wide)]
            flow.keep(piece, far_out[8].at[p.z], p.q == p.z)
        squares[...] = jnp.zeros_like(squares)
        for item in in_posts:
            flow.land(item)
        flow.keep(in_all, in_out)

        def multiply(first, count):
            line.settle(first + count)

            @pl.loop(0, count * m.D)
            def _(number):
                d = number // count
                block = jnp.where(
                    number - d * count == 0, line.nth(first), line.nth(first + count - 1)
                )
                base = pl.multiple_of(block * N, 16)
                hidden = mm(x_all[d, block], in_all[...].reshape(C, FL)) + fv[pl.ds(0, 1)]
                gate = 0.5 * (1.0 + lax.erf(hidden * root))
                value = hidden * gate
                rows = pl.ds(pl.multiple_of(d * m.pixels + base, 16), N)
                active[rows] = value
                slope[rows] = gate + hidden * (
                    jnp.exp(-0.5 * hidden * hidden) * 0.3989422804014327
                )
                squares[pl.ds(d, 1)] += jnp.sum(
                    keep[d, pl.ds(base, N)] * value * value, axis=0, keepdims=True
                )

        first = m.R // 2
        multiply(0, first)
        for step in range(3, m.R):
            line.hop(step)
        mods.hop(1)
        multiply(first, m.R - first)
        flow.keep(x_all, x_out)
        flow.keep(active, active_out)
        flow.keep(slope, slope_out)
        norms[...] = jnp.sqrt(squares[...])
        total[...] = jnp.broadcast_to(jnp.sum(norms[...], axis=1, keepdims=True), total.shape)
        for step in range(2, m.R):
            mods.hop(step)

    near_out = [
        ((8, FL), F32),
        ((8, 128), F32),
        ((texts, cond), BF16),
        ((texts, m.HW), BF16),
        ((N, C), F32),
        ((N, 1), F32),
        ((VEC, C), F32),
        ((8, FL), F32),
        ((m.D, m.pixels + m.texts, 1), F32),
        ((N, 1), F32),
        ((1, 3 * m.HW), F32),
        ((mod_rows, 128), F32),
        ((2, EDGE, C), BF16),
        ((N, C), BF16),
    ]
    far_out = [
        ((m.D, m.R, N, C), BF16),
        ((G, T, m.cs, FL), BF16),
        ((m.D * m.pixels, FL), F32),
        ((m.D * m.pixels, FL), F32),
        ((G,) + out_weight.shape, BF16),
        (qkv_cut.shape, BF16),
        ((G, mod_rows, 128), F32),
        ((m.D, m.R, G, mod_rows, 128), F32),
    ]
    if m.even:
        far_out.append(((m.R, m.cs, wide), BF16))
    scratch = [
        pltpu.VMEM((G, T, m.mp, m.HW), BF16),
        pltpu.VMEM((m.D, m.R) + clip_pad.shape, BF16),
        pltpu.VMEM((8, FL), F32),
        pltpu.VMEM((cond, m.HW), F32),
        pltpu.VMEM((texts, cond), F32),
        pltpu.VMEM((T, G, SMALL, 128), BF16),
        pltpu.VMEM((G,) + fvec.shape, BF16),
        pltpu.VMEM((N + 2 * EDGE, C), F32),
        pltpu.VMEM((N, C), F32),
        pltpu.VMEM((items, time_weight.shape[0]), BF16),
        pltpu.VMEM((mod_rows, 128), F32),
        pltpu.VMEM((m.D, m.R, N, C), BF16),
        pltpu.VMEM((G, T, m.cs, FL), BF16),
        pltpu.VMEM((m.D * m.pixels, FL), F32),
        pltpu.VMEM((m.D * m.pixels, FL), F32),
    ]
    columns = 4 if square else G - 1
    return fused_kernel(
        1,
        "front",
        lambda p: common_greet(p) + (sources_greet(m, p) if m.even else []),
        act,
        near,
        loads,
        far,
        near_out,
        far_out,
        scratch,
        4 * (T - 1) + 2 + 2 * columns + 4 * (G - 1) + (G if m.even else 0) + 3 * gather_sems(m),
        16,
    )


def sources_greet(m, p):
    greet = []
    for step in range(m.G):
        source = {"grp": p.z, "duo": p.c, "rows": lax.rem(p.q - step + m.G, m.G)}
        greet.append((source, None if step else p.q != p.z))
    return greet


def team_sum(m, p, flow, own, everyone):
    mine = p.c * m.R + p.z
    posted = [
        flow.post(own, everyone.at[mine], {"duo": c, "rows": z}) for c, z in p.team()
    ]

    def total():
        for item in posted:
            flow.land(item)
        result = own[...]
        for step, (c, z) in enumerate(p.team()):
            result = result + everyone[c * m.R + z]
        return result

    return total


def branch_kernel(m, active, norms, total, out_full, fv, latents, keep, vec, mod_all, qkv_rows, mapped, gres, proj_part):
    near = [norms, total, fv, keep, mod_all]
    loads = [active, out_full, latents, vec]
    far = [qkv_rows, mapped, gres] + ([proj_part] if m.even else [])
    N, C = m.N, m.C
    rows_all = m.D * m.pixels

    def act(p, flow, near, loads, far, near_out, far_out, scratch):
        norms, total, fv, keep, mod_all = near
        gain, grn_bias = fv[pl.ds(1, 1)], fv[pl.ds(2, 1)]
        grn, after, hat, inv, two, ratio, means, mods = near_out
        two_all, mapped_all, qkv_all, gres_near = far_out[:4]
        everyone, part, mate, passed, landed, branch, slopes = scratch
        add_up = team_sum(m, p, flow, total, everyone)
        for slot, to, sends, lands in (
            (0, p.z + 1, p.z < p.R - 1, p.z > 0),
            (1, p.z - 1, p.z > 0, p.z < p.R - 1),
        ):
            flow.post(far[2], gres_near.at[slot], {"rows": to}, when=sends, lands=lands)
        flow.gather_group(p, far[0], qkv_all)
        if m.even:
            flow.gather_group(p, far[3], far_out[4])
        text_line = LineGather(flow, p, far[1], mapped_all)
        half = m.S // 2
        pair = 2 * m.cs
        for s, (g, d, r) in enumerate(m.places):
            item = pl.ds(m.D * p.q + p.c, 1)
            mods[pl.ds(s // half, 1), pl.ds(pair * (s % half), pair)] = mod_all[d, r, g, item, pl.ds(0, pair)]
        mean = add_up() / m.FF + grn_eps
        means[...] = mean
        ratio[...] = norms[...] / mean[:, :1]
        slopes[...] = gain * ratio[...] + 1.0
        active, out_w, lat, vec = (load.get() for load in loads)

        @pl.loop(0, m.D)
        def _(d):
            rows = pl.ds(pl.multiple_of(d * m.pixels, 16), m.pixels)
            low = (active[rows] * slopes[pl.ds(d, 1)] + grn_bias).astype(BF16)
            grn[rows] = low
            part[d] = mm(low, out_w[...]).astype(BF16).reshape(m.R, N, C)

        def tail(rows):
            value = lat[rows].astype(F32) + keep[rows] * (branch[rows] + vec[pl.ds(10, 1)])
            after[rows] = value
            second = value * (1.0 + mods[pl.ds(0, 1)]) + mods[pl.ds(1, 1)]
            normal, inverse = layer_stats(second)
            hat[rows] = normal
            inv[rows] = inverse
            two[rows] = normal.astype(BF16)

        stripes = Stripes(flow, p, part, branch, (mate, passed, landed), two, two_all)
        text_line.start()
        flow.keep(far[1], mapped_all.at[p.c, p.z])
        stripes.run(tail, None, lambda number: text_line.hop(number + 1))
        for step in range(STRIPES + 1, m.R):
            text_line.hop(step)

    near_out = [
        ((rows_all, m.FL), BF16),
        ((N, C), F32),
        ((N, C), F32),
        ((N, 1), F32),
        ((N, C), BF16),
        ((8, m.FL), F32),
        ((8, 128), F32),
        ((8, C), F32),
    ]
    far_out = [
        ((m.D, m.R, N, C), BF16),
        ((m.D, m.R) + mapped.shape, BF16),
        ((m.G,) + qkv_rows.shape, BF16),
        ((2, N, C), BF16),
    ]
    if m.even:
        far_out.append(((m.G,) + proj_part.shape, BF16))
    scratch = (
        [pltpu.VMEM((m.T, 8, 128), F32)]
        + reduce_buffers(m, N, C)
        + [pltpu.VMEM((N, C), F32), pltpu.VMEM((8, m.FL), F32)]
    )
    return fused_kernel(
        3,
        "branch",
        common_greet,
        act,
        near,
        loads,
        far,
        near_out,
        far_out,
        scratch,
        (m.T + 1) + 2 * (m.G - 1) + (1 + STRIPES) * gather_sems(m) + STRIPES * reduce_sems(m),
        4 + STRIPES,
    )


def attention_kernel(m, two_all, gres, gres_near, mapped_all, weight, proj, bias, key_keep):
    near = [bias, key_keep]
    loads = [two_all, weight, proj, mapped_all]
    far = [gres, gres_near]
    heads = m.HW // HEAD
    keys = m.pixels + m.texts
    scale = HEAD ** (-0.5)
    HW, C, N, D, R, G, pixels, texts = m.HW, m.C, m.N, m.D, m.R, m.G, m.pixels, m.texts
    wide = C // m.Q
    block_rows = 2 * HW

    def act(p, flow, near, loads, far, near_out, far_out, scratch):
        bias, keep = near
        result, map_out, gw_out, gp_out, qv_out = near_out
        (two_far,) = far_out
        (gres_all, part, mate, passed, landed, qkv, k_all, v_all, k_t, v_t, dk, dv, o_t, dq_t, o_low, att, g_all, probs, dqkv,
         dtext, piece, words, gb_out, two_out) = scratch
        line = LineGatherOn(flow, p, far[0], gres_all)
        line.start_from(far[1])
        two, w, proj, mapped = (load.get() for load in loads)
        red = LineReduce(flow, p, part, result, mate, passed, landed)

        @pl.loop(0, D)
        def _(d):
            qkv[d] = (mm(two[d], w[...]) + bias[...]).astype(BF16)
            words[...] = jnp.zeros((texts, 3 * HW), F32) + bias[...]

            @pl.loop(0, m.T)
            def _(t):
                words[...] += mm(mapped[t, d], w[pl.ds(pl.multiple_of(t * HW, 16), HW)])

            text = words[...].astype(BF16)
            k_all[d, pl.ds(0, pixels)] = qkv[d, :, HW : 2 * HW]
            k_all[d, pl.ds(pixels, texts)] = text[:, HW : 2 * HW]
            v_all[d, pl.ds(0, pixels)] = qkv[d, :, 2 * HW :]
            v_all[d, pl.ds(pixels, texts)] = text[:, 2 * HW :]
            k_t[d] = k_all[d].T
            v_t[d] = v_all[d].T
            dk[d] = jnp.zeros_like(dk[d])
            dv[d] = jnp.zeros_like(dv[d])
            o_t[d] = jnp.zeros_like(o_t[d])
            dq_t[d] = jnp.zeros_like(dq_t[d])

        lane = lax.broadcasted_iota(jnp.int32, (1, HW), 1)
        row = lax.broadcasted_iota(jnp.int32, (HW, 1), 0)

        def masks(number):
            d = number // heads
            low = (number - d * heads) * HEAD
            return d, (lane >= low) & (lane < low + HEAD), (row >= low) & (row < low + HEAD)

        def forward(number):
            d, in_head, in_row = masks(number)
            q_h = jnp.where(in_head, qkv[d, :, :HW], 0).astype(BF16)
            scores = mm_t(k_all[d], q_h) * scale
            scores = jnp.where(keep[d] > 0, scores, masked_score)
            weights = jnp.exp(scores - jnp.max(scores, axis=0, keepdims=True))
            low = (weights / jnp.sum(weights, axis=0, keepdims=True)).astype(BF16)
            probs[number] = low
            o_t[d] += mm(jnp.where(in_row, v_t[d], 0).astype(BF16), low)

        pl.loop(0, D * heads // 2)(forward)
        line.hop(2)
        pl.loop(D * heads // 2, D * heads)(forward)

        @pl.loop(0, D)
        def _(d):
            o_low[d] = o_t[d].astype(BF16)
            att[d] = o_t[d].T.astype(BF16)

        def lanes_of(n):
            return pl.ds(pl.multiple_of(n * wide, 128), wide)

        @pl.loop(0, D * R)
        def _(number):
            d = number // R
            block = number - d * R
            mine = att[d, pl.ds(pl.multiple_of(block * N, 16), N)]
            for n in range(m.Q):
                part[d, block, :, pl.ds(n * wide, wide)] = mm(mine, proj[n]).astype(BF16)

        red.start()
        red.early()
        steps = list(red.later())
        for number in range(3, R):
            line.hop(number)
        line.settle(R)

        @pl.loop(0, D * R)
        def _(number):
            d = number // R
            block = number - d * R
            total = jnp.zeros((N, HW), F32)
            for n in range(m.Q):
                total = total + mm_t(gres_all[d, block, :, pl.ds(n * wide, wide)], proj[n])
            g_all[d, pl.ds(pl.multiple_of(block * N, 16), N)] = total.astype(BF16)

        def back(first, last):
            @pl.loop(first, last)
            def _(number):
                d, in_head, in_row = masks(number)
                q_h = jnp.where(in_head, qkv[d, :, :HW], 0).astype(BF16)
                g_h = jnp.where(in_head, g_all[d], 0).astype(BF16)
                low = probs[number]
                dv[d] += mm(low, g_h)
                grad_probs = mm_t(v_all[d], g_h)
                high = low.astype(F32)
                sums = jnp.sum(high * grad_probs, axis=0, keepdims=True)
                grad_scores = (high * (grad_probs - sums)).astype(BF16)
                dq_t[d] += mm(jnp.where(in_row, k_t[d], 0).astype(BF16), grad_scores)
                dk[d] += mm(grad_scores, q_h)

        cut = D * heads // 3
        back(0, cut)
        steps[0]()
        back(cut, D * heads)
        for step in steps[1:]:
            step()
        gb_out[...] = jnp.zeros_like(gb_out)

        @pl.loop(0, D)
        def _(d):
            dqkv[d, :, :HW] = (dq_t[d].T * scale).astype(BF16)
            dqkv[d, :, HW : 2 * HW] = (dk[d, pl.ds(0, pixels)] * scale).astype(BF16)
            dqkv[d, :, 2 * HW :] = dv[d, pl.ds(0, pixels)].astype(BF16)
            dtext[d, :, :HW] = jnp.zeros((texts, HW), BF16)
            dtext[d, :, HW : 2 * HW] = (dk[d, pl.ds(pixels, texts)] * scale).astype(BF16)
            dtext[d, :, 2 * HW :] = dv[d, pl.ds(pixels, texts)].astype(BF16)
            gb_out[pl.ds(0, 1)] += jnp.sum(dqkv[d].astype(F32), axis=0, keepdims=True) + jnp.sum(
                dtext[d].astype(F32), axis=0, keepdims=True
            )
            two_out[d] = mm_t(dqkv[d], w[...]).astype(BF16)
            @pl.loop(0, m.T)
            def _(t):
                rows = pl.ds(pl.multiple_of(t * HW, 16), HW)
                map_out[t, d] = mm_t(dtext[d], w[rows]).astype(BF16)

        flow.keep(two_out, two_far)
        qv_out[...] = jnp.zeros_like(qv_out)
        for h in range(m.T):

            @pl.when(D * p.z + p.c == h)
            def _():
                qv_out[pl.ds(0, 1), pl.ds(h * HW, HW)] = gb_out[pl.ds(0, 1), pl.ds(0, HW)]
                qv_out[pl.ds(1, 1), pl.ds(h * HW, HW)] = gb_out[pl.ds(0, 1), pl.ds(2 * HW, HW)]

        @pl.loop(0, C // block_rows)
        def _(g):
            lanes = pl.ds(pl.multiple_of(g * block_rows, 128), block_rows)
            piece[...] = t_mm(two[0, :, lanes], dqkv[0])
            for d in range(1, D):
                piece[...] += t_mm(two[d, :, lanes], dqkv[d])
            for side in range(2):
                rows = pl.ds(side * HW, HW)
                for d in range(D):
                    piece[rows] += t_mm(mapped[2 * g + side, d], dtext[d])
            gw_out[pl.ds(pl.multiple_of(g * block_rows, 16), block_rows)] = piece[...].astype(BF16)

        @pl.loop(0, m.Q)
        def _(n):
            total = jnp.zeros((HW, wide), F32)
            for d in range(D):
                columns = gres_all[d, :, :, lanes_of(n)].reshape(pixels, wide)
                total = total + mm(o_low[d], columns)
            gp_out[n] = total.astype(BF16)
        red.close()

    near_out = [
        ((N, C), F32),
        ((m.T, D, texts, HW), BF16),
        ((C, 3 * HW), BF16),
        ((m.Q, HW, wide), BF16),
        ((8, C), F32),
    ]
    scratch = [pltpu.VMEM((D, R, N, C), BF16)] + reduce_buffers(m, N, C)
    scratch += [
        pltpu.VMEM((D, pixels, 3 * HW), BF16),
        pltpu.VMEM((D, keys, HW), BF16),
        pltpu.VMEM((D, keys, HW), BF16),
        pltpu.VMEM((D, HW, keys), BF16),
        pltpu.VMEM((D, HW, keys), BF16),
        pltpu.VMEM((D, keys, HW), F32),
        pltpu.VMEM((D, keys, HW), F32),
        pltpu.VMEM((D, HW, pixels), F32),
        pltpu.VMEM((D, HW, pixels), F32),
        pltpu.VMEM((D, HW, pixels), BF16),
        pltpu.VMEM((D, pixels, HW), BF16),
        pltpu.VMEM((D, pixels, HW), BF16),
        pltpu.VMEM((D * heads, keys, pixels), BF16),
        pltpu.VMEM((D, pixels, 3 * HW), BF16),
        pltpu.VMEM((D, texts, 3 * HW), BF16),
        pltpu.VMEM((block_rows, 3 * HW), F32),
        pltpu.VMEM((texts, 3 * HW), F32),
        pltpu.VMEM((8, 3 * HW), F32),
        pltpu.VMEM((D, pixels, C), BF16),
    ]
    return fused_kernel(
        4,
        "attention_block",
        team_greet,
        act,
        near,
        loads,
        far,
        near_out,
        [((D, pixels, C), BF16)],
        scratch,
        gather_sems(m) + reduce_sems(m),
        4,
    )


def attended_kernel(m, two_part, text_part, result, cot, gres, hat, inv, after, mods, keep, vec, grad_qkv, grad_proj):
    near = [inv, mods, keep]
    loads = [two_part, hat, after, cot, gres, text_part, result, vec]
    far = [grad_qkv] + ([grad_proj] if m.even else [])
    N, C = m.N, m.C
    texts = m.D * m.texts

    def act(p, flow, near, loads, far, near_out, far_out, scratch):
        inv, mods, keep = near
        two_part, hat, after, cot, gres, text_part, result, vec = (load.get() for load in loads)
        output, grad_after, branch, gm, vecg, text = near_out
        gb_all = far_out[0]
        two_sum, text_sum = scratch[:2]
        text_red = LineReduce(flow, p, text_part, text_sum, *scratch[5:8])
        stripes = Stripes(flow, p, two_part, two_sum, scratch[2:5], branch, gb_all)
        flow.swap_group(p, far[0], far_out[1])
        if m.even:
            flow.swap_group(p, far[1], far_out[2])
        gm[...] = jnp.zeros_like(gm)
        vecg[...] = jnp.zeros_like(vecg)

        def back(rows):
            grad = cot[rows].astype(F32) + layer_back(two_sum[rows], hat[rows], inv[rows])
            gm[pl.ds(0, 1)] += jnp.sum(grad * after[rows], axis=0, keepdims=True)
            gm[pl.ds(1, 1)] += jnp.sum(grad, axis=0, keepdims=True)
            scaled = grad * (1.0 + mods[pl.ds(0, 1)])
            grad_after[rows] = scaled
            low = (keep[rows] * scaled).astype(BF16)
            branch[rows] = low
            vecg[pl.ds(0, 1)] += jnp.sum(low.astype(F32), axis=0, keepdims=True)
            vecg[pl.ds(1, 1)] += jnp.sum(gres[rows].astype(F32), axis=0, keepdims=True)

        text_red.start()
        steps = list(text_red.later())

        def between(number):
            if number == 0:
                steps[0]()
            elif number == 1:
                for step in steps[1:]:
                    step()
                text_red.close()
                text[...] = text_sum[...].astype(BF16)

        stripes.run(back, text_red.early, between)

        def out(rows):
            second = after[rows] * (1.0 + mods[pl.ds(0, 1)]) + mods[pl.ds(1, 1)]
            value = keep[rows] * (result[rows] + vec[pl.ds(12, 1)])
            output[rows] = (second + value).astype(BF16)

        chunks(N, out)

    near_out = [
        ((N, C), BF16),
        ((N, C), F32),
        ((N, C), BF16),
        ((8, C), F32),
        ((8, C), F32),
        ((texts, m.HW), BF16),
    ]
    far_out = [((m.D, m.R, N, C), BF16), (grad_qkv.shape, BF16)]
    if m.even:
        far_out.append((grad_proj.shape, BF16))
    scratch = (
        [pltpu.VMEM((N, C), F32), pltpu.VMEM((texts, m.HW), F32)]
        + reduce_buffers(m, N, C, False)
        + reduce_buffers(m, texts, m.HW, False)
    )
    return fused_kernel(
        5,
        "attended",
        common_greet,
        act,
        near,
        loads,
        far,
        near_out,
        far_out,
        scratch,
        2 * (m.G - 1) + STRIPES * gather_sems(m) + (1 + STRIPES) * reduce_sems(m),
        3 + STRIPES,
    )


def text_back_kernel(m, silu, grad_mapped):
    def kernel(s_ref, g_ref, out, bias, weight):
        weight[...] = t_mm(s_ref[...], g_ref[...])
        out[...] = jnp.zeros_like(out)
        for g in range(m.G):
            for t in range(m.T):
                at = m.ms * (g * m.T + t)
                out[g, pl.ds(t * m.mp, m.ms)] = weight[pl.ds(at, m.ms)].astype(BF16)
        total = jnp.sum(g_ref[...].astype(F32), axis=0, keepdims=True)
        bias[...] = jnp.zeros_like(bias)
        for t in range(m.T):

            @pl.when(lax.axis_index("duo") * m.R + lax.axis_index("rows") == t)
            def _():
                bias[pl.ds(0, 1), pl.ds(t * m.HW, m.HW)] = total

    return local_kernel(
        "text_back",
        kernel,
        [silu, grad_mapped],
        [((m.G, m.T * m.mp, m.HW), BF16), ((8, m.C), F32)],
        [pltpu.VMEM((silu.shape[1], m.HW), F32)],
    )


def back_kernel(m, gb_all, out_full, active, slope, grn_out, normed_all, in_full, norms, ratio, means, fv, key_keep,
                qkv_parts, proj_parts, grad_map):
    near = [norms, ratio, means, fv, key_keep]
    loads = [gb_all, out_full, active, grn_out, slope, normed_all, in_full, qkv_parts]
    loads += [proj_parts] if m.even else []
    far = [grad_map]
    N, C, FL, G = m.N, m.C, m.FL, m.G
    rows_in = C // G
    wide = C // m.Q
    per = m.pixels // N

    def act(p, flow, near, loads, far, near_out, far_out, scratch):
        norms, ratio, means, fv, keep = near
        gain = fv[pl.ds(1, 1)]
        (back,) = near_out
        in_parts, f_parts, map_parts, qkv_team = far_out[:4]
        g_far = far_out[-1]
        everyone, mine, moments, slopes, shifts, grads, hidden, part, mate, passed, landed = scratch[:11]
        turned_g, turned_x, g_in, f_own, qkv_own = scratch[11:16]
        g_out = scratch[-1]
        flow.swap_group(p, far[0], map_parts)
        gb, out_w, active, grn = (load.get() for load in loads[:4])
        moments[...] = jnp.zeros_like(moments)

        @pl.loop(0, m.D * per)
        def _(number):
            rows = pl.ds(pl.multiple_of(number * N, 16), N)
            item = number // per
            grad = mm_t(gb[rows], out_w[...])
            grads[rows] = grad
            moments[pl.ds(item, 1)] += jnp.sum(grad * active[rows], axis=0, keepdims=True)
            moments[pl.ds(m.D, 1)] += jnp.sum(grad, axis=0, keepdims=True)

        scaled = moments[...] * gain
        cross = jnp.sum(scaled * norms[...], axis=1, keepdims=True)
        mine[...] = jnp.broadcast_to(cross, mine.shape)
        add_up = team_sum(m, p, flow, mine, everyone)
        slope, x, in_w, qkv_parts = (load.get() for load in loads[4:8])
        step = m.cs

        def add_parts(parts, own, count):
            for t in range(count):
                rows = pl.ds(t * step, step)
                total = parts[0, rows].astype(F32)
                for g in range(1, G):
                    total = total + parts[g, rows].astype(F32)
                own[t] = total.astype(BF16)

        add_parts(qkv_parts, qkv_own, m.T)
        if m.even:
            proj_own = scratch[16]
            add_parts(loads[8].get(), proj_own, m.R)
        mean = means[...][:, :1]
        cross = add_up()[:, :1]
        slopes[...] = gain * ratio[...] + 1.0
        shifts[...] = (scaled / mean - cross / (m.FF * mean * mean)) / norms[...]
        gains = jnp.sum(moments[pl.ds(0, m.D)] * ratio[pl.ds(0, m.D)], axis=0, keepdims=True)
        biases = moments[pl.ds(m.D, 1)]
        moments[pl.ds(m.D + 1, 1)] = jnp.zeros((1, FL), F32)
        flow.swap_team(p, qkv_own, qkv_team)
        if m.even:
            for number in range(G):
                to = lax.rem(p.q + number, G)
                flow.post(
                    proj_own.at[to],
                    far_out[4].at[p.q],
                    {"grp": p.z, "duo": p.c, "rows": to},
                    when=None if number else p.q != p.z,
                )
            flow.keep(proj_own.at[p.z], far_out[4].at[p.q], p.q == p.z)

        @pl.loop(0, m.D * per)
        def _(number):
            rows = pl.ds(pl.multiple_of(number * N, 16), N)
            item = number // per
            inside = pl.ds(pl.multiple_of((number - item * per) * N, 16), N)
            one = pl.ds(item, 1)
            grad = grads[rows] * slopes[one] + keep[item, inside] * (active[rows] * shifts[one])
            low = (grad * slope[rows]).astype(BF16)
            hidden[rows] = low
            moments[pl.ds(m.D + 1, 1)] += jnp.sum(low.astype(F32), axis=0, keepdims=True)

        inner = moments[pl.ds(m.D + 1, 1)]
        f_own[...] = jnp.zeros_like(f_own)
        for g in range(G):
            lanes = slice(g * m.FFS, (g + 1) * m.FFS)
            for row, values in enumerate((inner, gains, biases)):
                f_own[g, pl.ds(row, 1)] = values[:, lanes]
        flow.swap_group(p, f_own, f_parts)
        line = LineReduce(flow, p, part, back, mate, passed, landed)

        @pl.loop(0, m.D)
        def _(d):
            rows = pl.ds(pl.multiple_of(d * m.pixels, 16), m.pixels)
            part[d] = mm_t(hidden[rows], in_w[...]).astype(BF16).reshape(m.R, N, C)

        for number in range(m.R):
            line.offer(line_order(p, number))
        line.early()
        turned_x[...] = x[...].T
        first = flow.take(G - 1)

        def send_in(number):
            g = lax.rem(p.q + 1 + number, G)
            return flow.copy(g_in.at[g], in_parts.at[p.q], {"grp": g}, first + number)

        @pl.loop(0, G)
        def _(number):
            g = lax.rem(p.q + 1 + number, G)
            rows = pl.ds(pl.multiple_of(g * rows_in, 16), rows_in)
            g_in[g] = mm(turned_x[rows], hidden[...]).astype(BF16)
            pl.when(number < G - 1)(lambda: send_in(number).start())

        flow.keep(g_in.at[p.q], in_parts.at[p.q])
        acts = list(line.later())
        acts[0]()
        turned_g[...] = grn[...].T

        def multiply_out(g, rows):
            g_out[g] = mm(turned_g[rows], gb[...]).astype(BF16)

        each_rows(G, m.FFS, multiply_out)
        flow.keep(g_out, g_far)

        for act_of in acts[1:]:
            act_of()
        line.close()
        for number in range(G - 1):
            send_in(number).wait_recv()
            send_in(number).wait_send()

    near_out = [((N, C), F32)]
    far_out = [
        ((G, rows_in, FL), BF16),
        ((G, 8, m.FFS), F32),
        (grad_map.shape, BF16),
        ((m.T, m.cs, 3 * m.HW), BF16),
    ]
    scratch = [
        pltpu.VMEM((m.T, 8, 128), F32),
        pltpu.VMEM((8, 128), F32),
        pltpu.VMEM((8, FL), F32),
        pltpu.VMEM((8, FL), F32),
        pltpu.VMEM((8, FL), F32),
        pltpu.VMEM((m.D * m.pixels, FL), F32),
        pltpu.VMEM((m.D * m.pixels, FL), BF16),
    ]
    scratch += reduce_buffers(m, N, C)
    scratch += [
        pltpu.VMEM((FL, m.D * m.pixels), BF16),
        pltpu.VMEM((C, m.D * m.pixels), BF16),
        pltpu.VMEM((G, rows_in, FL), BF16),
        pltpu.VMEM((G, 8, m.FFS), F32),
        pltpu.VMEM((m.T, m.cs, 3 * m.HW), BF16),
    ]
    if m.even:
        far_out.append(((G, m.cs, wide), BF16))
        scratch.append(pltpu.VMEM((m.R, m.cs, wide), BF16))
    far_out.append(((G, m.FFS, C), BF16))
    scratch.append(pltpu.VMEM((G, m.FFS, C), BF16))
    return fused_kernel(
        9,
        "feed_forward_back",
        lambda p: common_greet(p) + (spread_greet(m, p) if m.even else []),
        act,
        near,
        loads,
        far,
        near_out,
        far_out,
        scratch,
        2 * (m.T - 1) + 4 * (G - 1) + reduce_sems(m) + (G if m.even else 0),
        7,
    )


def tail_kernel(m, grad_low, tiny, g_out, in_parts, map_parts):
    loads = [in_parts, map_parts]
    far = [grad_low, tiny, g_out]
    N, C, G, T = m.N, m.C, m.G, m.T

    def act(p, flow, near, loads, far, near_out, far_out, scratch):
        low, tiny, g_out = far
        edges, tiny_all, in_team, map_team, out_parts = far_out
        in_own, map_own, tiny_in, tiny_own = scratch
        for block, to, sends, lands in (
            (low.at[pl.ds(N - EDGE, EDGE)], p.z + 1, p.z < p.R - 1, p.z > 0),
            (low.at[pl.ds(0, EDGE)], p.z - 1, p.z > 0, p.z < p.R - 1),
        ):
            slot = jnp.where(to > p.z, 0, 1)
            flow.post(block, edges.at[slot], {"rows": to}, when=sends, lands=lands)
        posts = flow.swap_team(p, tiny, tiny_in)
        flow.swap_group(p, g_out, out_parts)
        for load, own, step in ((loads[0], in_own, m.cs), (loads[1], map_own, m.mp)):
            parts = load.get()

            def add(t, rows, parts=parts, own=own):
                total = parts[0, rows].astype(F32)
                for g in range(1, G):
                    total = total + parts[g, rows].astype(F32)
                own[t] = total.astype(BF16)

            each_rows(T, step, add)

        flow.swap_team(p, in_own, in_team)
        flow.swap_team(p, map_own, map_team)
        for item in posts:
            flow.land(item)
        flow.settle_kept()
        for d in range(m.D):
            for g in range(G):
                total = tiny_in[d * m.R, g]
                for r in range(1, m.R):
                    total = total + tiny_in[d * m.R + r, g]
                tiny_own[g, d] = total
        flow.swap_group(p, tiny_own, tiny_all)

    return fused_kernel(
        11,
        "tail",
        common_greet,
        act,
        [],
        loads,
        far,
        [],
        [
            ((2, EDGE, C), BF16),
            ((G, m.D) + tiny.shape[2:], F32),
            ((T, m.cs, m.FL), BF16),
            ((T, m.mp, m.HW), BF16),
            (g_out.shape, BF16),
        ],
        [
            pltpu.VMEM((T, m.cs, m.FL), BF16),
            pltpu.VMEM((T, m.mp, m.HW), BF16),
            pltpu.VMEM(tiny.shape, F32),
            pltpu.VMEM((G, m.D) + tiny.shape[2:], F32),
        ],
        2 + 3 * (T - 1) + 2 * (G - 1),
        5,
    )


def pad_rows(values, rows):
    return jnp.pad(values, ((0, rows - values.shape[0]),) + ((0, 0),) * (values.ndim - 1))


def body(
    latents,
    clip_tokens,
    time_embed,
    bucket_ids,
    heights,
    widths,
    text_mask,
    conv_weight,
    conv_bias,
    in_weight,
    in_bias,
    grn_gain,
    grn_bias,
    out_weight,
    out_bias,
    time_weight,
    time_bias,
    map_weight,
    map_bias,
    qkv_weight,
    qv_bias,
    proj_weight,
    proj_bias,
    cotangent,
):
    m = Sizes(latents, clip_tokens, in_weight, in_bias, conv_bias, map_weight)
    G, D, R, T, N, C = m.G, m.D, m.R, m.T, m.N, m.C
    pixels, texts, FFS, FL, FF, HW = m.pixels, m.texts, m.FFS, m.FL, m.FF, m.HW
    cs, ms, mp, sp, even, Q = m.cs, m.ms, m.mp, m.sp, m.even, m.Q
    q, c, z = (lax.axis_index(axis) for axis in AXES)
    head_slice = D * z + c

    vectors = [conv_bias, out_bias, map_bias, proj_bias, qv_bias]
    fvectors = [in_bias, grn_gain, grn_bias]
    in_cut, qkv_cut, map_cut, clip_pad, masked, grad_result, small, fvec = cut_kernel(
        m,
        [heights, widths, bucket_ids, in_weight, qkv_weight, map_weight, clip_tokens, latents]
        + [cotangent, conv_weight]
        + vectors
        + [time_embed, text_mask]
        + fvectors,
    )
    latents = latents[0]
    cotangent = cotangent[0]

    def swap_edges(plan, src, dst):
        p = plan.p
        for block, to, sends, lands in (
            (src.at[pl.ds(src.shape[0] - EDGE, EDGE)], p.z + 1, p.z < R - 1, p.z > 0),
            (src.at[pl.ds(0, EDGE)], p.z - 1, p.z > 0, p.z < R - 1),
        ):
            slot = jnp.where(to > p.z, 0, 1)
            plan.add(block, dst.at[slot], {"rows": to}, when=sends, lands=lands)

    outs = front_kernel(
        m,
        time_weight,
        time_bias[None],
        masked,
        small,
        fvec,
        in_cut,
        out_weight,
        map_cut,
        qkv_cut,
        clip_pad,
        proj_weight,
    )
    norms, total, silu, mapped_s = outs[:4]
    norm_hat, norm_inv, vec, fv, key_keep, keep, bias, embed, edges, _ = outs[4:14]
    normed_all, in_full, active, slope, out_full, qkv_rows, _, mod_all = outs[14:22]
    proj_part = outs[22].reshape(HW, C // G) if even else None
    normed_all = normed_all.reshape(D * pixels, C)
    in_full = in_full.reshape(C, FL)
    out_full = out_full.reshape(FL, C)
    outs = branch_kernel(
        m,
        active,
        norms,
        total,
        out_full,
        fv,
        latents,
        keep,
        vec,
        mod_all,
        qkv_rows.reshape(T * cs, 3 * HW),
        mapped_s,
        grad_result,
        proj_part,
    )
    grn_out, after_res, two_hat, two_inv, _, ratio, means, mods, two_all, mapped = outs[:10]
    qkv_full, gres_near = outs[10].reshape(C, 3 * HW), outs[11]
    if even:
        proj_s = outs[12]
    else:
        proj_whole = lax.all_gather(proj_weight, AXES, axis=0, tiled=True)
        proj_s = lax.dynamic_slice_in_dim(proj_whole, head_slice * HW, HW, axis=0)[None]
    result, mapped_part, grad_qkv, grad_proj, qv_grads, two_part = attention_kernel(
        m,
        two_all.reshape(D, pixels, C),
        grad_result,
        gres_near,
        mapped.reshape(T, D, texts, HW),
        qkv_full,
        proj_s,
        bias,
        key_keep,
    )
    outs = attended_kernel(
        m,
        two_part.reshape(D, R, N, C),
        mapped_part.reshape(D, R, D * texts, HW),
        result,
        cotangent,
        grad_result,
        two_hat,
        two_inv,
        after_res,
        mods,
        keep,
        vec,
        grad_qkv.reshape(G, T * cs, 3 * HW),
        grad_proj,
    )
    output, grad_after, _, grad_modulate, vec_sums, grad_mapped, gb_all, qkv_parts = outs[:8]
    if even:
        proj_parts = outs[8]
    else:
        proj_parts = None
        spread = jnp.zeros((C, C), F32)
        spread = lax.dynamic_update_slice_in_dim(
            spread, grad_proj[0].astype(F32), head_slice * HW, axis=0
        )
        proj_team = lax.psum_scatter(spread, AXES, scatter_dimension=0, tiled=True)[None]
    grad_map, map_bias_grad = text_back_kernel(m, silu, grad_mapped)
    outs = back_kernel(
        m,
        gb_all.reshape(D * pixels, C),
        out_full,
        active,
        slope,
        grn_out,
        normed_all,
        in_full,
        norms,
        ratio,
        means,
        fv,
        key_keep,
        qkv_parts,
        proj_parts,
        grad_map,
    )
    grad_conv_in, in_parts, f_sum, map_parts, qkv_team = outs[:5]
    grad_out = outs[-1]
    if even:
        proj_team = outs[5]

    grad_conv, conv_low, tiny = conv_back_kernel(
        m,
        bucket_ids,
        grad_conv_in,
        norm_hat,
        norm_inv,
        edges,
        masked,
        vec_sums,
        map_bias_grad,
        qv_grads,
        grad_modulate,
    )
    conv_edges, tiny_all, in_team, map_team, out_parts = tail_kernel(
        m, conv_low, tiny, grad_out, in_parts, map_parts
    )
    outs = finish_kernel(
        m,
        bucket_ids,
        conv_edges,
        conv_low,
        grad_after,
        keep,
        vec,
        in_team,
        qkv_team,
        map_team,
        proj_team,
        out_parts,
        tiny_all,
        f_sum,
        embed,
        time_embed.shape[1],
    )
    grad_latents, grad_in_shard, grad_qkv_shard, grad_map_shard, grad_proj_shard = outs[:5]
    grad_out_shard, grad_kernel, grad_time = outs[5:8]
    conv_b, out_b, proj_b, map_b, qv_b, time_b, in_b, gain_g, grn_b = outs[8:17]
    return (
        output[None],
        grad_latents,
        grad_kernel,
        conv_b,
        grad_in_shard,
        in_b,
        gain_g,
        grn_b,
        grad_out_shard,
        out_b,
        grad_time,
        time_b,
        grad_map_shard,
        map_b,
        grad_qkv_shard,
        qv_b,
        grad_proj_shard,
        proj_b,
    )


def solution(mesh):
    items, rows = mesh.devices.shape
    fine = Mesh(mesh.devices.reshape(items // 2, 2, rows), AXES)
    item = ("grp", "duo")
    full = AXES
    ins = (
        P(item, "rows", None),
        P(item, "rows", None),
        P(item, None),
        P(item),
        P(item),
        P(item),
        P(item, None),
        P(None, full),
        P(full),
        P(full, None),
        P(full),
        P(full),
        P(full),
        P(full, None),
        P(full),
        P(None, full),
        P(full),
        P(full, None),
        P(full),
        P(full, None),
        P(full),
        P(full, None),
        P(full),
        P(item, "rows", None),
    )
    outs = (
        P(item, "rows", None),
        P(item, "rows", None),
        P(None, full),
        P(full),
        P(full, None),
        P(full),
        P(full),
        P(full),
        P(full, None),
        P(full),
        P(None, full),
        P(full),
        P(full, None),
        P(full),
        P(full, None),
        P(full),
        P(full, None),
        P(full),
    )
    return jax.shard_map(body, mesh=fine, in_specs=ins, out_specs=outs, check_vma=False)
```

```python
import functools

import jax
import jax.numpy as jnp
from jax import lax
from jax.experimental import pallas as pl
from jax.experimental.pallas import tpu as pltpu
from jax.sharding import Mesh, PartitionSpec as P

HEAD = 64
TXT = 77
UNIT = 8
EDGE = 48

norm_eps = 1e-06
grn_eps = 1e-06
masked_score = -1000000000.0

AXES = ("grp", "duo", "rows")
MESH_ID = pl.DeviceIdType.MESH
F32 = jnp.float32
BF16 = jnp.bfloat16


class Place:
    def __init__(self):
        self.q, self.c, self.z = (lax.axis_index(axis) for axis in AXES)
        self.G, self.D, self.R = (lax.axis_size(axis) for axis in AXES)

    def team(self):
        for step in range(1, self.D * self.R):
            dc, dz = step // self.R, step % self.R
            yield lax.rem(self.c + dc, self.D), lax.rem(self.z + dz, self.R)

    def groups(self):
        for step in range(1, self.G):
            yield lax.rem(self.q + step, self.G)


def signal_all(barrier, targets):
    for target in targets:
        pl.semaphore_signal(barrier, inc=1, device_id=target, device_id_type=MESH_ID)


def guarded(when, act):
    if when is None:
        act()
    else:
        pl.when(when)(act)


class Flow:
    def __init__(self, send_sem, recv_sem, local_sem=None):
        self.send_sem, self.recv_sem, self.local_sem = send_sem, recv_sem, local_sem
        self.used = 0
        self.kept = 0
        self.open = []
        self.posted = []
        self.lines = []
        self.stays = []

    def take(self, count=1):
        at = self.used
        self.used += count
        return at

    def copy(self, src, dst, target, at):
        return pltpu.make_async_remote_copy(
            src_ref=src,
            dst_ref=dst,
            send_sem=self.send_sem.at[at],
            recv_sem=self.recv_sem.at[at],
            device_id=target,
            device_id_type=MESH_ID,
        )

    def post(self, src, dst, target, when=None, lands=None):
        copy = self.copy(src, dst, target, self.take())
        guarded(when, copy.start)
        item = Posted(copy, when if lands is None else lands)
        self.posted.append(item)
        self.open.append((copy.wait_send, when))
        return item

    def land(self, item):
        if not item.landed:
            item.landed = True
            guarded(item.lands, item.copy.wait_recv)

    def keep(self, src, dst, when=None, now=False):
        copy = pltpu.make_async_copy(src, dst, self.local_sem.at[self.kept])
        self.kept += 1
        guarded(when, copy.start)
        if now:
            guarded(when, copy.wait)
        else:
            self.stays.append((copy.wait, when))

    def square(self, p, src, dst):
        across = p.q + 1 - 2 * lax.rem(p.q, 2)
        along = lax.rem(p.q + 2, 4)
        one = self.post(src, dst.at[p.q], {"grp": across})
        two = self.post(src, dst.at[p.q], {"grp": along})
        half = dst.shape[1] // 2
        top, bottom = pl.ds(0, half), pl.ds(half, half)

        def relay():
            self.land(one)
            block = dst.at[across, top]
            first = self.post(block, block, {"grp": along})
            self.land(two)
            block = dst.at[along, bottom]
            second = self.post(block, block, {"grp": across})
            return first, second

        return relay

    def settle_kept(self):
        for act, when in self.stays:
            guarded(when, act)
        self.stays = []

    def gather_team(self, p, src, dst):
        mine = p.c * p.R + p.z
        self.keep(src, dst.at[mine])
        return [self.post(src, dst.at[mine], {"duo": c, "rows": z}) for c, z in p.team()]

    def gather_group(self, p, src, dst):
        self.keep(src, dst.at[p.q])
        return [self.post(src, dst.at[p.q], {"grp": q}) for q in p.groups()]

    def swap_group(self, p, src, dst):
        self.keep(src.at[p.q], dst.at[p.q])
        for q in p.groups():
            self.post(src.at[q], dst.at[p.q], {"grp": q})

    def swap_team(self, p, src, dst):
        mine = p.c * p.R + p.z
        self.keep(src.at[mine], dst.at[mine])
        return [
            self.post(src.at[c * p.R + z], dst.at[mine], {"duo": c, "rows": z}) for c, z in p.team()
        ]

    def finish(self):
        self.settle_kept()
        for line in self.lines:
            line.settle(line.p.R)
        for item in self.posted:
            self.land(item)
        for act, when in self.open:
            guarded(when, act)


class LineGather:
    def __init__(self, flow, place, src, dst):
        self.flow, self.p, self.src, self.dst = flow, place, src, dst
        self.up = flow.take(place.R - 1)
        self.down = flow.take(place.R - 1)
        self.side = flow.take(2 * place.R - 1)

    def send(self, block, hop, direction):
        p, dst = self.p, self.dst
        src = self.src if hop == 0 else dst.at[p.c, block]
        at = (self.up if direction > 0 else self.down) + hop
        return self.flow.copy(src, dst.at[p.c, block], {"rows": p.z + direction}, at)

    def across(self, block, number):
        p, dst = self.p, self.dst
        src = self.src if isinstance(number, int) and number == 0 else dst.at[p.c, block]
        other = {"duo": lax.rem(p.c + 1, p.D)}
        return self.flow.copy(src, dst.at[p.c, block], other, self.side + number)

    def start(self):
        p = self.p
        for direction, ok in ((1, p.z < p.R - 1), (-1, p.z > 0)):
            copy = self.send(p.z, 0, direction)
            guarded(ok, copy.start)
            self.flow.open.append((copy.wait_send, ok))
        copy = self.across(p.z, 0)
        copy.start()
        self.flow.open.append((copy.wait_send, None))
        self.flow.lines.append(self)
        self.settled = 0

    def hop(self, step):
        p = self.p
        for direction, number in ((1, step), (-1, p.R - 1 + step)):
            block = p.z - direction * step
            ok = (block >= 0) if direction > 0 else (block < p.R)
            last = (p.z < p.R - 1) if direction > 0 else (p.z > 0)
            arrived = self.send(block, step - 1, direction)
            side = self.across(block, number)

            def relay(arrived=arrived, side=side, block=block, direction=direction, last=last):
                arrived.wait_recv()
                if step < p.R - 1:
                    pl.when(last)(self.send(block, step, direction).start)
                side.start()

            pl.when(ok)(relay)
            if step < p.R - 1:
                self.flow.open.append((self.send(block, step, direction).wait_send, ok & last))
            self.flow.open.append((side.wait_send, ok))


    def nth(self, number):
        p = self.p
        reach = [p.z]
        for step in range(1, p.R):
            reach += [p.z - step, p.z + step]
        seen, found = 0, jnp.int32(0)
        for block in reach:
            ok = (block >= 0) & (block < p.R)
            found = jnp.where(ok & (seen == number), block, found)
            seen = seen + jnp.where(ok, 1, 0)
        return found

    def settle(self, upto):
        p = self.p
        while self.settled < upto:
            block = self.nth(self.settled)
            number = jnp.where(block <= p.z, p.z - block, p.R - 1 + block - p.z)
            self.across(block, number).wait_recv()
            self.settled += 1


class LineGatherOn(LineGather):
    def start_from(self, near):
        p, flow = self.p, self.flow
        flow.lines.append(self)
        self.settled = 0
        flow.keep(near.at[0], self.dst.at[p.c, jnp.maximum(p.z - 1, 0)], p.z > 0)
        flow.keep(near.at[1], self.dst.at[p.c, jnp.minimum(p.z + 1, p.R - 1)], p.z < p.R - 1)
        flow.keep(self.src, self.dst.at[p.c, p.z])
        flow.settle_kept()
        copy = self.across(p.z, 0)
        copy.start()
        flow.open.append((copy.wait_send, None))
        for direction, number in ((1, 1), (-1, p.R)):
            block = p.z - direction
            ok = (block >= 0) if direction > 0 else (block < p.R)
            last = (p.z < p.R - 1) if direction > 0 else (p.z > 0)
            side = self.across(block, number)

            def relay(side=side, block=block, direction=direction, last=last):
                pl.when(last)(self.send(block, 1, direction).start)
                side.start()

            pl.when(ok)(relay)
            flow.open.append((self.send(block, 1, direction).wait_send, ok & last))
            flow.open.append((side.wait_send, ok))


class LineReduce:
    def __init__(self, flow, place, part, total_ref, mate, passed, landed):
        self.flow, self.p, self.part, self.total = flow, place, part, total_ref
        self.mate, self.passed, self.landed = mate, passed, landed
        self.side = flow.take(place.R)
        self.line = flow.take(2 * place.R)

    def across(self, block):
        p = self.p
        other = lax.rem(p.c + 1, p.D)
        return self.flow.copy(
            self.part.at[other, block], self.mate.at[block], {"duo": other}, self.side + block
        )

    def along(self, upward, block):
        p = self.p
        way = jnp.where(upward, 1, 0)
        target = {"rows": jnp.where(upward, p.z + 1, p.z - 1)}
        return self.flow.copy(
            self.passed.at[way, block],
            self.landed.at[way, block],
            target,
            self.line + way * p.R + block,
        )

    def steps(self):
        p = self.p
        low = p.z < p.R // 2
        for k in range(p.R - 1):
            for first in (True, False):
                upward = low if first else jnp.logical_not(low)
                block = jnp.where(upward, p.R - 1 - k, k)
                yield upward, block, jnp.where(upward, block > p.z, block < p.z)

    def start(self):
        p = self.p
        for k in range(p.R):
            block = jnp.where(p.z < p.R // 2, p.R - 1 - k, k)
            copy = self.across(block)
            copy.start()
            self.flow.open.append((copy.wait_send, None))

    def rows_of(self, act):
        count = self.part.shape[2]
        step = 16

        @pl.loop(0, count // step)
        def _(number):
            act(pl.ds(pl.multiple_of(number * step, step), step))

    def offer(self, block):
        copy = self.across(block)
        copy.start()
        self.flow.open.append((copy.wait_send, None))

    def early(self):
        for upward, block, ok in self.steps():
            behind = jnp.where(upward, self.p.z > 0, self.p.z < self.p.R - 1)
            self.step(upward, block, ok & jnp.logical_not(behind), False)

    def later(self):
        for upward, block, ok in self.steps():
            behind = jnp.where(upward, self.p.z > 0, self.p.z < self.p.R - 1)
            yield functools.partial(self.step, upward, block, ok & behind, True)

    def step(self, upward, block, ok, relays=None):
        p = self.p
        way = jnp.where(upward, 1, 0)
        behind = jnp.where(upward, p.z > 0, p.z < p.R - 1)

        def act():
            self.across(block).wait_recv()
            if relays is False:

                def add(rows):
                    self.passed[way, block, rows] = (
                        self.part[p.c, block, rows].astype(F32) + self.mate[block, rows].astype(F32)
                    ).astype(BF16)

                self.rows_of(add)
                self.along(upward, block).start()
                return

            @pl.when(behind)
            def _():
                self.along(upward, block).wait_recv()

                def add(rows):
                    self.passed[way, block, rows] = (
                        self.part[p.c, block, rows].astype(F32)
                        + self.mate[block, rows].astype(F32)
                        + self.landed[way, block, rows].astype(F32)
                    ).astype(BF16)

                self.rows_of(add)

            if relays is None:

                @pl.when(jnp.logical_not(behind))
                def _():
                    def add(rows):
                        self.passed[way, block, rows] = (
                            self.part[p.c, block, rows].astype(F32)
                            + self.mate[block, rows].astype(F32)
                        ).astype(BF16)

                    self.rows_of(add)

            self.along(upward, block).start()

        pl.when(ok)(act)
        self.flow.open.append((self.along(upward, block).wait_send, ok))

    def close(self):
        p = self.p
        self.across(p.z).wait_recv()

        def base(rows):
            self.total[rows] = self.part[p.c, p.z, rows].astype(F32) + self.mate[
                p.z, rows
            ].astype(F32)

        self.rows_of(base)
        for way, ok in ((1, p.z > 0), (0, p.z < p.R - 1)):

            def more(way=way):
                self.along(way == 1, p.z).wait_recv()

                def add(rows):
                    self.total[rows] += self.landed[way, p.z, rows].astype(F32)

                self.rows_of(add)

            pl.when(ok)(more)

    def steps_all(self):
        self.early()
        for act in self.later():
            act()
        self.close()

    def run(self, produce=None, between=None):
        p = self.p
        if produce is None:
            self.steps_all()
            return
        ready = 0

        def more():
            block = line_order(p, ready)
            produce(block)
            copy = self.across(block)
            copy.start()
            self.flow.open.append((copy.wait_send, None))

        for number, (upward, block, ok) in enumerate(self.steps()):
            while ready < min(number + 2, p.R):
                more()
                ready += 1
            self.step(upward, block, ok)
            if between is not None:
                between(number)
        self.close()


def team_kernel(
    ident, name, plan, arrays, results, gathers=(), reduces=(), messages=0, local=1, late=None
):
    D, R = lax.axis_size("duo"), lax.axis_size("rows")
    count_a, count_g, count_r = len(arrays), len(gathers), len(reduces)
    extra = 0 if late is None else 1
    total_sems = messages + (count_g + extra) * (4 * R - 3) + count_r * 3 * R

    def kernel(*refs):
        refs = list(refs)
        ins = refs[:count_a]
        g_in = refs[count_a : count_a + count_g]
        r_in = refs[count_a + count_g : count_a + count_g + count_r]
        refs = refs[count_a + count_g + count_r :]
        outs = refs[: len(results)]
        refs = refs[len(results) :]
        late_out = refs[:extra]
        g_out = refs[extra : extra + count_g]
        r_out = refs[extra + count_g : extra + count_g + count_r]
        refs = refs[extra + count_g + count_r :]
        send_sem, recv_sem, local_sem = refs[:3]
        buffers = refs[3:]
        p = Place()
        flow = Flow(send_sem, recv_sem)
        greet, direct, stay = plan(p, ins, outs)
        barrier = pltpu.get_barrier_semaphore()
        waits = 0
        for target, when in greet:
            if when is None:
                waits = waits + 1
            else:
                waits = waits + jnp.where(when, 1, 0).astype(jnp.int32)
            guarded(when, lambda target=target: signal_all(barrier, [target]))
        pl.semaphore_wait(barrier, waits)
        lines = [LineGather(flow, p, src, dst) for src, dst in zip(g_in, g_out)]
        sums = [
            LineReduce(flow, p, src, dst, *buffers[3 * n : 3 * n + 3])
            for n, (src, dst) in enumerate(zip(r_in, r_out))
        ]
        base = flow.take(messages)
        copies = {}
        arrived = set()

        stays = []

        def landed(number):
            if number not in arrived:
                arrived.add(number)
                guarded(copies[number][2], copies[number][0].wait_recv)

        def run_stage(stage):
            for number, (src, dst, target, after, when, when_stage, lands) in enumerate(direct):
                if when_stage != stage:
                    continue
                for earlier in after:
                    landed(earlier)
                copy = flow.copy(src, dst, target, base + number)
                guarded(when, copy.start)
                copies[number] = (copy, when, lands)
            if late is not None and late[1] == stage:
                for number in range(late[2]):
                    landed(number)
                stays[0][0].wait()
                line = LineGather(flow, p, outs[late[0]], late_out[0])
                line.start()
                own = pltpu.make_async_copy(
                    outs[late[0]], late_out[0].at[p.c, p.z], local_sem.at[local + count_g]
                )
                own.start()
                stays[0] = (own, None)
                if stage:
                    for earlier in range(1, stage + 1):
                        line.hop(earlier)
                lines.append(line)

        for item in sums:
            item.start()
        for line in lines:
            line.start()
        for number, (src, dst, when) in enumerate(
            list(stay) + [(src, dst.at[p.c, p.z], None) for src, dst in zip(g_in, g_out)]
        ):
            copy = pltpu.make_async_copy(src, dst, local_sem.at[number])
            guarded(when, copy.start)
            stays.append((copy, when))
        run_stage(0)
        for step in range(1, R):
            for line in lines:
                line.hop(step)
            run_stage(step)
        for item in sums:
            item.run()
        for copy, when in stays:
            guarded(when, copy.wait)
        for number in copies:
            landed(number)
        for copy, when, _ in copies.values():
            guarded(when, copy.wait_send)
        flow.finish()

    spot = pl.BlockSpec(memory_space=pl.ANY)
    near = pl.BlockSpec(memory_space=pltpu.VMEM)
    out_shape = [jax.ShapeDtypeStruct(shape, kind) for shape, kind in results]
    if late is not None:
        shape, kind = results[late[0]]
        out_shape.append(jax.ShapeDtypeStruct((D, R) + shape, kind))
    out_shape += [jax.ShapeDtypeStruct((D, R) + g.shape, g.dtype) for g in gathers]
    out_shape += [jax.ShapeDtypeStruct(r.shape[2:], F32) for r in reduces]
    scratch = [
        pltpu.SemaphoreType.DMA((total_sems,)),
        pltpu.SemaphoreType.DMA((total_sems,)),
        pltpu.SemaphoreType.DMA((local + count_g + extra,)),
    ]
    for r in reduces:
        block = r.shape[1:]
        scratch += [
            pltpu.VMEM(block, BF16),
            pltpu.VMEM((2,) + block, BF16),
            pltpu.VMEM((2,) + block, BF16),
        ]
    return pl.pallas_call(
        kernel,
        out_shape=out_shape,
        in_specs=[spot] * (count_a + count_g) + [near] * count_r,
        out_specs=[spot] * (len(results) + extra + count_g) + [near] * count_r,
        scratch_shapes=scratch,
        compiler_params=pltpu.CompilerParams(
            collective_id=ident, has_side_effects=True, vmem_limit_bytes=56 * 2**20
        ),
        name=name,
    )(*arrays, *gathers, *reduces)


def team_greet(p):
    return [({"duo": c, "rows": z}, None) for c, z in p.team()]


def group_greet(p):
    return [({"grp": q}, None) for q in p.groups()]


class Plan:
    def __init__(self, p):
        self.p = p
        self.messages, self.local, self.greet = [], [], []

    def add(self, src, dst, target, after=(), when=None, stage=0, lands=None):
        self.messages.append((src, dst, target, after, when, stage, when if lands is None else lands))
        return len(self.messages) - 1

    def team_swap(self, src, dst, stage=0):
        p = self.p
        mine = p.c * p.R + p.z
        for c, z in p.team():
            self.add(src.at[c * p.R + z], dst.at[mine], {"duo": c, "rows": z}, stage=stage)
        self.local.append((src.at[mine], dst.at[mine], None))

    def team_gather(self, src, dst, stage=0):
        p = self.p
        mine = p.c * p.R + p.z
        for c, z in p.team():
            self.add(src, dst.at[mine], {"duo": c, "rows": z}, stage=stage)
        self.local.append((src, dst.at[mine], None))

    def group_gather(self, src, dst, late=None):
        p = self.p
        self.local.append((src, dst.at[p.q], None))
        if late is None or p.G != 4:
            for q in p.groups():
                self.add(src, dst.at[p.q], {"grp": q})
            return
        across = p.q + 1 - 2 * lax.rem(p.q, 2)
        along = lax.rem(p.q + 2, 4)
        one = self.add(src, dst.at[p.q], {"grp": across})
        two = self.add(src, dst.at[p.q], {"grp": along})
        half = src.shape[0] // 2
        top, bottom = pl.ds(0, half), pl.ds(half, half)
        self.add(
            dst.at[across, top], dst.at[across, top], {"grp": along}, after=(one,), stage=late
        )
        self.add(
            dst.at[along, bottom],
            dst.at[along, bottom],
            {"grp": across},
            after=(two,),
            stage=late,
        )

    def group_swap(self, src, dst, stage=0):
        p = self.p
        for q in p.groups():
            self.add(src.at[q], dst.at[p.q], {"grp": q}, stage=stage)
        self.local.append((src.at[p.q], dst.at[p.q], None))

    def done(self):
        p = self.p
        return team_greet(p) + group_greet(p) + self.greet, self.messages, self.local


def layer_stats(values):
    center = values - jnp.mean(values, axis=-1, keepdims=True)
    spread = jnp.mean(center * center, axis=-1, keepdims=True)
    inverse = lax.rsqrt(spread + norm_eps)
    return center * inverse, inverse


def layer_back(grad, hat, inverse):
    first = jnp.mean(grad, axis=-1, keepdims=True)
    second = jnp.mean(grad * hat, axis=-1, keepdims=True)
    return inverse * (grad - first - hat * second)


def mm(left, right):
    return jnp.dot(left, right, preferred_element_type=F32)


def mm_t(left, right):
    return lax.dot_general(left, right, (((1,), (1,)), ((), ())), preferred_element_type=F32)


def t_mm(left, right):
    return lax.dot_general(left, right, (((0,), (0,)), ((), ())), preferred_element_type=F32)


def columns_of(bucket_ids):
    return jnp.where(
        bucket_ids == 0, 9 * UNIT // 2, jnp.where(bucket_ids == 1, 3 * UNIT, 9 * UNIT // 4)
    )


def pixel_mask(positions, height, width, cols):
    row_at = positions // cols
    col_at = positions % cols
    return ((row_at < height) & (col_at < width)).astype(F32)


def spots(shapes):
    return [jax.ShapeDtypeStruct(shape, kind) for shape, kind in shapes]


def local_kernel(name, kernel, arrays, results, scratch=(), scalars=0):
    near = pl.BlockSpec(memory_space=pltpu.VMEM)
    numbers = pl.BlockSpec(memory_space=pltpu.SMEM)
    return pl.pallas_call(
        kernel,
        out_shape=spots(results),
        in_specs=[numbers] * scalars + [near] * (len(arrays) - scalars),
        out_specs=[near] * len(results),
        scratch_shapes=list(scratch),
        compiler_params=pltpu.CompilerParams(vmem_limit_bytes=56 * 2**20),
        name=name,
    )(*arrays)


class Sizes:
    def __init__(self, latents, clip_tokens, in_weight, in_bias, conv_bias, map_weight):
        self.G, self.D, self.R = (lax.axis_size(axis) for axis in AXES)
        self.T = self.D * self.R
        self.S = self.T * self.G
        self.N, self.C = latents.shape[1:]
        self.pixels = self.R * self.N
        self.FFS = in_bias.shape[0]
        self.FL = self.G * self.FFS
        self.FF = in_weight.shape[1]
        self.cs = conv_bias.shape[0]
        self.ms = map_weight.shape[0]
        self.mp = -(-self.ms // 8) * 8
        self.slots = clip_tokens.shape[1]
        self.sp = -(-self.slots // 8) * 8
        self.texts = self.R * self.slots
        self.HW = self.C // self.T
        self.even = self.G == self.R
        self.Q = self.G if self.even else 1
        self.places = [(g, d, r) for g in range(self.G) for d in range(self.D) for r in range(self.R)]


def rows_cols(first, count, cols):
    position = (first + lax.broadcasted_iota(jnp.int32, (count, 1), 0)).astype(F32)
    row = jnp.floor((position + 0.5) / cols)
    return row, position - row * cols


def float_cols(bucket):
    return jnp.where(bucket == 0, 9.0 * UNIT / 2, jnp.where(bucket == 1, 3.0 * UNIT, 9.0 * UNIT / 4))


WIDTHS = (9 * UNIT // 2, 3 * UNIT, 9 * UNIT // 4)
SMALL = 16
VEC = 16
FACTS = 96


def cut_kernel(m, arrays):
    def kernel(h_ref, w_ref, b_ref, in_ref, qkv_ref, map_ref, clip_ref, lat_ref, cot_ref, cw_ref, *refs):
        vectors, refs = refs[:5], refs[5:]
        te_ref, tm_ref, f0, f1, f2 = refs[:5]
        in_out, qkv_out, map_out, clip_out, masked_out, gres_out, small_out, f_out, small, fv = refs[5:]
        for g in range(m.G):
            for t in range(m.T):
                start = m.FFS * (g * m.T + t)
                in_out[t, :, pl.ds(g * m.FFS, m.FFS)] = in_ref[:, pl.ds(start, m.FFS)]
        for d in range(m.D):
            for r in range(m.R):
                for j in range(3):
                    start = m.C * j + m.HW * (m.D * r + d)
                    qkv_out[d * m.R + r, :, pl.ds(j * m.HW, m.HW)] = qkv_ref[:, pl.ds(start, m.HW)]
        map_out[...] = jnp.zeros_like(map_out)
        for t in range(m.T):
            map_out[t, pl.ds(0, m.ms)] = map_ref[:, pl.ds(t * m.HW, m.HW)]
        clip_out[...] = jnp.zeros_like(clip_out)
        clip_out[pl.ds(0, m.slots)] = clip_ref[0]
        z = lax.axis_index("rows")
        row, col = rows_cols(z * m.N, m.N, float_cols(b_ref[0]))
        keep = (row < h_ref[0].astype(F32)) & (col < w_ref[0].astype(F32))
        masked_out[...] = jnp.where(keep, lat_ref[0].astype(F32), 0.0).astype(BF16)
        gres_out[...] = jnp.where(keep, cot_ref[0].astype(F32), 0.0).astype(BF16)
        small[...] = jnp.zeros_like(small)
        small[pl.ds(0, 9), pl.ds(0, m.cs)] = cw_ref[...].astype(F32)
        for number, ref in enumerate(vectors):
            small[pl.ds(9 + number, 1), pl.ds(0, ref.shape[0])] = ref[...].astype(F32).reshape(1, -1)
        small[pl.ds(14, 1), pl.ds(0, te_ref.shape[1])] = te_ref[...].astype(F32)
        lane = lax.broadcasted_iota(jnp.int32, (1, 128), 1)
        for number, ref in enumerate((h_ref, w_ref, b_ref)):
            fact = jnp.full((1, 128), ref[0]).astype(F32)
            row = small[pl.ds(14, 1)]
            small[pl.ds(14, 1)] = jnp.where(lane == FACTS + number, fact, row)
        small[pl.ds(15, 1), pl.ds(0, m.texts)] = tm_ref[...].astype(F32)
        small_out[...] = small[...].astype(BF16)
        fv[...] = jnp.zeros_like(fv)
        for number, ref in enumerate((f0, f1, f2)):
            fv[pl.ds(number, 1)] = ref[...].astype(F32).reshape(1, -1)
        f_out[...] = fv[...].astype(BF16)

    return local_kernel(
        "cut_weights",
        kernel,
        arrays,
        [
            ((m.T, m.cs, m.FL), BF16),
            ((m.T, m.cs, 3 * m.HW), BF16),
            ((m.T, m.mp, m.HW), BF16),
            ((m.sp, arrays[6].shape[2]), BF16),
            ((m.N, m.C), BF16),
            ((m.N, m.C), BF16),
            ((SMALL, 128), BF16),
            ((16, m.FFS), BF16),
        ],
        [pltpu.VMEM((SMALL, 128), F32), pltpu.VMEM((16, m.FFS), F32)],
        scalars=3,
    )


def fill_extended(m, extended, edges_ref, mid_ref):
    z = lax.axis_index("rows")
    extended[pl.ds(0, EDGE)] = jnp.where(z > 0, edges_ref[0].astype(F32), 0.0)
    extended[pl.ds(EDGE, m.N)] = mid_ref[...].astype(F32)
    extended[pl.ds(EDGE + m.N, EDGE)] = jnp.where(z < m.R - 1, edges_ref[1].astype(F32), 0.0)


def each_bucket(bucket, act):
    for number, width in enumerate(WIDTHS):
        pl.when(bucket == number)(functools.partial(act, width))


def each_column_block(m, act):
    @pl.loop(0, m.C // 128)
    def _(number):
        act(pl.ds(pl.multiple_of(number * 128, 128), 128))


def tap_steps():
    return [(index, index // 3 - 1, index % 3 - 1) for index in range(9)]


def conv_back_kernel(m, b_ref, grad_in, hat, inv, edges, masked, vec_grads, map_grad, qv_grads, modulate_grads):
    def kernel(b_ref, g_ref, hat_ref, inv_ref, edges_ref, mid_ref, vec_ref, map_ref, qv_ref, gm_ref, grad, low, tiny_low, extended, vec, tiny):
        values = layer_back(g_ref[...], hat_ref[...], inv_ref[...])
        grad[...] = values
        low[...] = values.astype(BF16)
        fill_extended(m, extended, edges_ref, mid_ref)
        vec[pl.ds(9, 1)] = jnp.sum(values, axis=0, keepdims=True)
        vec[pl.ds(10, 2)] = vec_ref[pl.ds(0, 2)]
        vec[pl.ds(12, 1)] = map_ref[pl.ds(0, 1)]
        vec[pl.ds(13, 3)] = jnp.zeros((3, m.C), F32)
        z = lax.axis_index("rows")

        def taps(width):
            _, col = rows_cols(z * m.N, m.N, float(width))

            def block(lanes):
                value = grad[:, lanes]
                for index, dy, dx in tap_steps():
                    piece = extended[pl.ds(EDGE + dy * width + dx, m.N), lanes]
                    ok = (col + dx >= 0) & (col + dx < width)
                    vec[pl.ds(index, 1), lanes] = jnp.sum(
                        jnp.where(ok, piece, 0.0) * value, axis=0, keepdims=True
                    )

            each_column_block(m, block)

        each_bucket(b_ref[0], taps)
        tiny[...] = jnp.zeros_like(tiny)
        half = m.S // 2
        pair = 2 * m.cs
        for s, (g, d, r) in enumerate(m.places):
            t = d * m.R + r
            tiny[t, g, pl.ds(0, 13), pl.ds(0, m.cs)] = vec[pl.ds(0, 13), pl.ds(s * m.cs, m.cs)]
            side, at = pl.ds(s // half, 1), pl.ds(pair * (s % half), pair)
            tiny[t, g, pl.ds(13, 1), pl.ds(0, pair)] = qv_ref[side, at]
            tiny[t, g, pl.ds(14, 1), pl.ds(0, pair)] = gm_ref[side, at]
        tiny_low[...] = tiny[...].astype(BF16)

    return local_kernel(
        "convolve_back",
        kernel,
        [b_ref, grad_in, hat, inv, edges, masked, vec_grads, map_grad, qv_grads, modulate_grads],
        [((m.N, m.C), F32), ((m.N, m.C), BF16), ((m.T, m.G, 16, 128), BF16)],
        [
            pltpu.VMEM((m.N + 2 * EDGE, m.C), F32),
            pltpu.VMEM((VEC, m.C), F32),
            pltpu.VMEM((m.T, m.G, 16, 128), F32),
        ],
        scalars=1,
    )


def finish_kernel(m, b_ref, edges, low, after, pix, vec, in_team, qkv_team, map_team, proj_team, out_parts, tiny_all, f_parts, embed, rdim):
    def kernel(b_ref, edges_ref, low_ref, after_ref, pix_ref, vec_ref, in_ref, qkv_ref, map_ref, proj_ref, parts_ref, tiny_ref, f_ref, te_ref,
               lat_out, in_out, qkv_out, map_out, proj_out, out_out, cw_out, time_out, *refs):
        singles, (extended,) = refs[:10], refs[10:]
        total = jnp.zeros(tiny_ref.shape[2:], F32)
        times = jnp.zeros((128, 128), F32)
        turned = te_ref[...].T
        for g in range(m.G):
            for d in range(m.D):
                item = tiny_ref[g, d]
                total = total + item
                at = m.D * g + d
                times = times + turned[:, at : at + 1] * item[14:15]
        cw_out[...] = total[:9, : m.cs]
        time_out[...] = times[:rdim, : 2 * m.cs]
        for number, ref in enumerate(singles[:6]):
            ref[...] = total[9 + number, : ref.shape[0]]
        sums = f_ref[0]
        for g in range(1, m.G):
            sums = sums + f_ref[g]
        for number, ref in enumerate(singles[6:9]):
            ref[...] = sums[number, :]
        singles[9][...] = total[15, :]
        fill_extended(m, extended, edges_ref, low_ref)
        z = lax.axis_index("rows")
        keep = pix_ref[...] > 0

        def taps(width):
            _, col = rows_cols(z * m.N, m.N, float(width))

            def block(lanes):
                total = jnp.zeros((m.N, 128), F32)
                for index, dy, dx in tap_steps():
                    piece = extended[pl.ds(EDGE - dy * width - dx, m.N), lanes]
                    ok = (col - dx >= 0) & (col - dx < width)
                    total = total + jnp.where(ok, piece, 0.0) * vec_ref[pl.ds(index, 1), lanes]
                lat_out[0, :, lanes] = after_ref[:, lanes] + jnp.where(keep, total, 0.0)

            each_column_block(m, block)

        each_bucket(b_ref[0], taps)
        for g in range(m.G):
            for t in range(m.T):
                start = m.FFS * (g * m.T + t)
                in_out[:, pl.ds(start, m.FFS)] = in_ref[t, :, pl.ds(g * m.FFS, m.FFS)].astype(F32)
        for d in range(m.D):
            for r in range(m.R):
                for j in range(3):
                    start = m.C * j + m.HW * (m.D * r + d)
                    qkv_out[:, pl.ds(start, m.HW)] = qkv_ref[
                        d * m.R + r, :, pl.ds(j * m.HW, m.HW)
                    ].astype(F32)
        for t in range(m.T):
            map_out[:, pl.ds(t * m.HW, m.HW)] = map_ref[t].astype(F32)[: m.ms]
        total = parts_ref[0].astype(F32)
        for g in range(1, m.G):
            total = total + parts_ref[g].astype(F32)
        out_out[...] = total
        wide = m.C // m.Q
        for n in range(m.Q):
            proj_out[:, pl.ds(n * wide, wide)] = proj_ref[n].astype(F32)

    return local_kernel(
        "finish",
        kernel,
        [b_ref, edges, low, after, pix, vec, in_team, qkv_team, map_team, proj_team, out_parts]
        + [tiny_all, f_parts, embed],
        [
            ((1, m.N, m.C), F32),
            ((m.cs, m.FF), F32),
            ((m.cs, 3 * m.C), F32),
            ((m.ms, m.C), F32),
            ((m.cs, m.C), F32),
            ((m.FFS, m.C), F32),
            ((9, m.cs), F32),
            ((rdim, 2 * m.cs), F32),
        ]
        + [((m.cs,), F32)] * 4
        + [((2 * m.cs,), F32)] * 2
        + [((m.FFS,), F32)] * 3
        + [((128,), F32)],
        [pltpu.VMEM((m.N + 2 * EDGE, m.C), F32)],
        scalars=1,
    )


class Posted:
    def __init__(self, copy, lands):
        self.copy, self.lands, self.landed = copy, lands, False


def line_order(p, number):
    low = p.z < p.R // 2
    far, near = p.R - 1 - number // 2, number // 2
    if number % 2:
        far, near = near, far
    return jnp.where(low, far, near)


STRIPES = 3
AHEAD = 2


def chunks(count, act, step=16, first=0):
    @pl.loop(0, count // step)
    def _(number):
        act(pl.ds(pl.multiple_of(first + number * step, step), step))


def each_rows(count, step, act):
    if step % 16:
        for number in range(count):
            act(number, pl.ds(number * step, step))
    else:

        @pl.loop(0, count)
        def _(number):
            act(number, pl.ds(pl.multiple_of(number * step, 16), step))


def greet_all(p, targets):
    barrier = pltpu.get_barrier_semaphore()
    waits = 0
    for target, when in targets:
        if when is None:
            waits = waits + 1
        else:
            waits = waits + jnp.where(when, 1, 0).astype(jnp.int32)
        guarded(when, lambda target=target: signal_all(barrier, [target]))
    pl.semaphore_wait(barrier, waits)


def fused_kernel(
    ident, name, greet, act, near, loads, far, near_out, far_out, scratch, sems, local, numbers=0
):
    close = pl.BlockSpec(memory_space=pltpu.VMEM)
    spot = pl.BlockSpec(memory_space=pl.ANY)
    counts = [len(near), len(loads), len(far), len(near_out), len(far_out), len(scratch), len(loads)]

    def kernel(*refs):
        groups = []
        for count in counts:
            groups.append(refs[:count])
            refs = refs[count:]
        send_sem, recv_sem, local_sem, load_sem = refs
        near, sources, far, near_out, far_out, scratch, held = groups
        brought = []
        for number, (source, place) in enumerate(zip(sources, held)):
            copy = pltpu.make_async_copy(source, place, load_sem.at[number])
            copy.start()
            brought.append(Brought(copy, place))
        p = Place()
        flow = Flow(send_sem, recv_sem, local_sem)
        greet_all(p, greet(p))
        act(p, flow, near, brought, far, near_out, far_out, scratch)
        flow.finish()
        if flow.used > sems or flow.kept > local:
            raise ValueError(f"{name}: {flow.used} {flow.kept}")

    return pl.pallas_call(
        kernel,
        out_shape=spots(near_out + far_out),
        in_specs=[pl.BlockSpec(memory_space=pltpu.SMEM)] * numbers
        + [close] * (len(near) - numbers)
        + [spot] * (len(loads) + len(far)),
        out_specs=[close] * len(near_out) + [spot] * len(far_out),
        scratch_shapes=list(scratch)
        + [pltpu.VMEM(array.shape, array.dtype) for array in loads]
        + [
            pltpu.SemaphoreType.DMA((sems,)),
            pltpu.SemaphoreType.DMA((sems,)),
            pltpu.SemaphoreType.DMA((local,)),
            pltpu.SemaphoreType.DMA((max(len(loads), 1),)),
        ],
        compiler_params=pltpu.CompilerParams(
            collective_id=ident, has_side_effects=True, vmem_limit_bytes=63 * 2**20
        ),
        name=name,
    )(*near, *loads, *far)


class Brought:
    def __init__(self, copy, place):
        self.copy, self.place, self.here = copy, place, False

    def get(self):
        if not self.here:
            self.copy.wait()
            self.here = True
        return self.place


class Stripes:
    def __init__(self, flow, p, part, total, buffers, src, dst):
        count = part.shape[2]
        self.p, self.flow, self.src, self.dst = p, flow, src, dst
        step = count // STRIPES
        self.rows = [pl.ds(number * step, step) for number in range(STRIPES)]
        mate, passed, landed = buffers
        self.sums = [
            LineReduce(
                flow,
                p,
                part.at[:, :, rows],
                total.at[rows],
                mate.at[:, rows],
                passed.at[:, :, rows],
                landed.at[:, :, rows],
            )
            for rows in self.rows
        ]
        self.lines = [LineGather(flow, p, src.at[rows], dst.at[:, :, rows]) for rows in self.rows]

    def run(self, act, before=None, between=None):
        p = self.p
        for item in self.sums:
            for number in range(p.R):
                item.offer(line_order(p, number))
        for number, item in enumerate(self.sums[:AHEAD]):
            item.early()
            if before is not None and number == 0:
                before()
        size = self.rows[0].size
        hops = [0] * STRIPES

        def hop(number):
            if hops[number] < p.R - 1:
                hops[number] += 1
                self.lines[number].hop(hops[number])

        for number, item in enumerate(self.sums):
            for step in item.later():
                step()
            item.close()
            chunks(size, act, first=number * size)
            self.lines[number].start()
            rows = self.rows[number]
            self.flow.keep(self.src.at[rows], self.dst.at[p.c, p.z, rows])
            if number + AHEAD < STRIPES:
                self.sums[number + AHEAD].early()
            if between is not None:
                between(number)
        while min(hops) < p.R - 1:
            for number in range(STRIPES):
                hop(number)


def gather_sems(m):
    return 4 * m.R - 3


def reduce_sems(m):
    return 3 * m.R


def reduce_buffers(m, count, width, part=True):
    block = (m.R, count, width)
    mine = [pltpu.VMEM((m.D,) + block, BF16)] if part else []
    return mine + [
        pltpu.VMEM(block, BF16),
        pltpu.VMEM((2,) + block, BF16),
        pltpu.VMEM((2,) + block, BF16),
    ]


def spread_greet(m, p):
    greet = []
    for step in range(m.G):
        source = {"grp": p.z, "duo": p.c, "rows": lax.rem(p.q - step + m.G, m.G)}
        greet.append((source, None if step else p.q != p.z))
    return greet


def common_greet(p):
    return team_greet(p) + group_greet(p)


def front_kernel(m, time_weight, time_bias, masked, small, fvec, in_cut, out_weight, map_cut, qkv_cut, clip_pad, proj_weight):
    near = [time_weight, time_bias]
    loads = [masked]
    far = [masked, small, fvec, in_cut, out_weight, map_cut, qkv_cut, clip_pad]
    far += [proj_weight] if m.even else []
    N, C, FL, G, T = m.N, m.C, m.FL, m.G, m.T
    root = 0.5**0.5
    texts = m.D * m.texts
    cond = clip_pad.shape[1]
    wide = C // m.Q
    square = G == 4
    items = m.G * m.D
    mod_rows = -(-items // 8) * 8
    pair = 2 * m.cs

    def act(p, flow, near, loads, far, near_out, far_out, scratch):
        tw_ref, tb_ref = near
        norms, total, silu, mapped = near_out[:4]
        hat, inv, vec, fv, keep, pix, qkv_bias, embed, edges, normed = near_out[4:]
        x_out, in_out, active_out, slope_out, out_all, qkv_rows, mod_all, mod_line = far_out[:8]
        map_all, clip_all, squares, weight, text, small_all, f_all, extended, conv, te, mod = scratch[:11]
        x_all, in_all, active, slope = scratch[11:]
        mid, small_ref, fvec_ref, in_cut, out_own, map_cut, qkv_cut, clip = far[:8]
        mine = p.c * p.R + p.z
        own_in = in_all.at[p.q]
        small_posts = [
            flow.post(small_ref, small_all.at[mine, p.q], {"grp": to}) for to in p.groups()
        ]
        edge_posts = []
        for block, to, sends, lands in (
            (mid.at[pl.ds(N - EDGE, EDGE)], p.z + 1, p.z < p.R - 1, p.z > 0),
            (mid.at[pl.ds(0, EDGE)], p.z - 1, p.z > 0, p.z < p.R - 1),
        ):
            slot = jnp.where(to > p.z, 0, 1)
            edge_posts.append(
                flow.post(block, edges.at[slot], {"rows": to}, when=sends, lands=lands)
            )
        f_posts = [flow.post(fvec_ref, f_all.at[p.q], {"grp": to}) for to in p.groups()]
        flow.keep(small_ref, small_all.at[mine, p.q], now=True)
        for item in small_posts:
            flow.land(item)
        spread = [
            flow.post(small_all.at[mine], small_all.at[mine], {"duo": c, "rows": z})
            for c, z in p.team()
        ]
        in_team = [
            flow.post(in_cut.at[c * p.R + z], own_in.at[mine], {"duo": c, "rows": z})
            for c, z in p.team()
        ]
        if square:
            out_relay = flow.square(p, out_own, out_all)
            flow.keep(out_own, out_all.at[p.q])
        else:
            flow.gather_group(p, out_own, out_all)
        own_map = map_all.at[p.q]
        map_team = [
            flow.post(map_cut.at[c * p.R + z], own_map.at[mine], {"duo": c, "rows": z})
            for c, z in p.team()
        ]
        clip_line = LineGather(flow, p, clip, clip_all)
        clip_line.start()
        flow.keep(in_cut.at[mine], own_in.at[mine], now=True)
        flow.keep(map_cut.at[mine], own_map.at[mine], now=True)
        flow.keep(clip, clip_all.at[p.c, p.z], now=True)
        flow.keep(fvec_ref, f_all.at[p.q], now=True)
        for item in spread + edge_posts:
            flow.land(item)
        half = m.S // 2
        vec[...] = jnp.zeros_like(vec)
        for s, (g, d, r) in enumerate(m.places):
            piece = small_all[d * m.R + r, g].astype(F32)
            vec[pl.ds(0, 13), pl.ds(s * m.cs, m.cs)] = piece[:13, : m.cs]
            vec[pl.ds(13 + s // half, 1), pl.ds(pair * (s % half), pair)] = piece[13:14, :pair]
            if r == 0:
                embed[pl.ds(m.D * g + d, 1)] = piece[14:15]
        extended[pl.ds(0, EDGE)] = jnp.where(p.z > 0, edges[0].astype(F32), 0.0)
        extended[pl.ds(EDGE, N)] = loads[0].get()[...].astype(F32)
        extended[pl.ds(EDGE + N, EDGE)] = jnp.where(p.z < m.R - 1, edges[1].astype(F32), 0.0)
        kind = small_all[mine, p.q].astype(F32)[14:15, FACTS + 2 : FACTS + 3]
        real = float_cols(kind)
        _, col = rows_cols(p.z * N, N, real)

        def taps(lanes):
            sum_of = jnp.zeros((N, 128), F32) + vec[pl.ds(9, 1), lanes]
            for index, dy, dx in tap_steps():
                pieces = [
                    extended[pl.ds(EDGE + dy * width + dx, N), lanes]
                    for width in (WIDTHS if dy else WIDTHS[:1])
                ]
                piece = pieces[0]
                if dy:
                    piece = jnp.where(kind == 0, piece, jnp.where(kind == 1, pieces[1], pieces[2]))
                ok = (col + dx >= 0) & (col + dx < real)
                sum_of = sum_of + jnp.where(ok, piece, 0.0) * vec[pl.ds(index, 1), lanes]
            conv[:, lanes] = sum_of

        each_column_block(m, taps)
        values, inverse = layer_stats(conv[...])
        hat[...] = values
        normed[...] = values.astype(BF16)
        inv[...] = inverse
        line = LineGather(flow, p, normed, x_all)
        line.start()
        flow.keep(normed, x_all.at[p.c, p.z], now=True)
        te[...] = embed[...][:items, : te.shape[1]].astype(BF16)
        mod[...] = jnp.zeros_like(mod)
        mod[pl.ds(0, items), pl.ds(0, pair)] = mm(te[...], tw_ref[...]) + tb_ref[...].astype(F32)
        mod_posts = flow.gather_group(p, mod, mod_all)
        for item in in_team:
            flow.land(item)
        if square:
            in_relay = flow.square(p, own_in, in_all)
        else:
            in_posts = [flow.post(own_in, in_all.at[p.q], {"grp": q}) for q in p.groups()]
        for d in range(m.D):
            facts = small_all[d * m.R, p.q].astype(F32)
            row, col_all = rows_cols(0, m.pixels, float_cols(facts[14:15, FACTS + 2 : FACTS + 3]))
            inside = (row < facts[14:15, FACTS : FACTS + 1]) & (
                col_all < facts[14:15, FACTS + 1 : FACTS + 2]
            )
            keep[d, pl.ds(0, m.pixels)] = jnp.where(inside, 1.0, 0.0)
            shown = facts.T[: m.texts, 15:16]
            slot = lax.broadcasted_iota(jnp.int32, (m.texts, 1), 0)
            keep[d, pl.ds(m.pixels, m.texts)] = jnp.where(slot < TXT, shown, 0.0)
        pix[...] = keep[p.c, pl.ds(pl.multiple_of(p.z * N, 8), N)]
        for item in f_posts:
            flow.land(item)
        for g in range(G):
            fv[:, pl.ds(g * m.FFS, m.FFS)] = f_all[g].astype(F32)[:8]
        qkv_bias[...] = jnp.zeros_like(qkv_bias)
        for h in range(T):

            @pl.when(p.D * p.z + p.c == h)
            def _():
                at = pl.ds(h * m.HW, m.HW)
                qkv_bias[:, : m.HW] = vec[pl.ds(13, 1), at]
                qkv_bias[:, 2 * m.HW :] = vec[pl.ds(14, 1), at]

        for item in map_team:
            flow.land(item)
        map_posts = [flow.post(own_map, map_all.at[p.q], {"grp": q}) for q in p.groups()]
        for step in range(1, m.R):
            clip_line.hop(step)
        line.hop(1)
        if square:
            out_relay()
        clip_line.settle(m.R)
        for item in map_posts:
            flow.land(item)
        for d in range(m.D):
            for r in range(m.R):
                piece = clip_all[d, r].astype(F32)[: m.slots]
                text[pl.ds((d * m.R + r) * m.slots, m.slots)] = piece / (1.0 + jnp.exp(-piece))
        silu[...] = text[...].astype(BF16)
        for g in range(G):
            for t in range(T):
                piece = map_all[g, t].astype(F32)
                weight[pl.ds(m.ms * (g * T + t), m.ms)] = piece[: m.ms]
        product = mm(silu[...], weight[...].astype(BF16))
        for t in range(T):

            @pl.when(mine == t)
            def _():
                mapped[...] = (product + vec[pl.ds(11, 1), pl.ds(t * m.HW, m.HW)]).astype(BF16)

        line.hop(2)
        if square:
            in_posts = in_relay()
        for item in mod_posts:
            flow.land(item)
        flow.settle_kept()
        mods = LineGather(flow, p, mod_all, mod_line)
        mods.start()
        flow.keep(mod_all, mod_line.at[p.c, p.z])
        flow.swap_team(p, qkv_cut, qkv_rows)
        if m.even:
            for number in range(G):
                to = lax.rem(p.z + number, G)
                piece = far[8].at[:, pl.ds(pl.multiple_of(to * wide, 128), wide)]
                flow.post(
                    piece,
                    far_out[8].at[p.z],
                    {"grp": to, "duo": p.c, "rows": p.q},
                    when=None if number else p.q != p.z,
                )
            piece = far[8].at[:, pl.ds(pl.multiple_of(p.z * wide, 128), wide)]
            flow.keep(piece, far_out[8].at[p.z], p.q == p.z)
        squares[...] = jnp.zeros_like(squares)
        for item in in_posts:
            flow.land(item)
        flow.keep(in_all, in_out)

        def multiply(first, count):
            line.settle(first + count)

            @pl.loop(0, count * m.D)
            def _(number):
                d = number // count
                block = jnp.where(
                    number - d * count == 0, line.nth(first), line.nth(first + count - 1)
                )
                base = pl.multiple_of(block * N, 16)
                hidden = mm(x_all[d, block], in_all[...].reshape(C, FL)) + fv[pl.ds(0, 1)]
                gate = 0.5 * (1.0 + lax.erf(hidden * root))
                value = hidden * gate
                rows = pl.ds(pl.multiple_of(d * m.pixels + base, 16), N)
                active[rows] = value
                slope[rows] = gate + hidden * (
                    jnp.exp(-0.5 * hidden * hidden) * 0.3989422804014327
                )
                squares[pl.ds(d, 1)] += jnp.sum(
                    keep[d, pl.ds(base, N)] * value * value, axis=0, keepdims=True
                )

        first = m.R // 2
        multiply(0, first)
        for step in range(3, m.R):
            line.hop(step)
        mods.hop(1)
        multiply(first, m.R - first)
        flow.keep(x_all, x_out)
        flow.keep(active, active_out)
        flow.keep(slope, slope_out)
        norms[...] = jnp.sqrt(squares[...])
        total[...] = jnp.broadcast_to(jnp.sum(norms[...], axis=1, keepdims=True), total.shape)
        for step in range(2, m.R):
            mods.hop(step)

    near_out = [
        ((8, FL), F32),
        ((8, 128), F32),
        ((texts, cond), BF16),
        ((texts, m.HW), BF16),
        ((N, C), F32),
        ((N, 1), F32),
        ((VEC, C), F32),
        ((8, FL), F32),
        ((m.D, m.pixels + m.texts, 1), F32),
        ((N, 1), F32),
        ((1, 3 * m.HW), F32),
        ((mod_rows, 128), F32),
        ((2, EDGE, C), BF16),
        ((N, C), BF16),
    ]
    far_out = [
        ((m.D, m.R, N, C), BF16),
        ((G, T, m.cs, FL), BF16),
        ((m.D * m.pixels, FL), F32),
        ((m.D * m.pixels, FL), F32),
        ((G,) + out_weight.shape, BF16),
        (qkv_cut.shape, BF16),
        ((G, mod_rows, 128), F32),
        ((m.D, m.R, G, mod_rows, 128), F32),
    ]
    if m.even:
        far_out.append(((m.R, m.cs, wide), BF16))
    scratch = [
        pltpu.VMEM((G, T, m.mp, m.HW), BF16),
        pltpu.VMEM((m.D, m.R) + clip_pad.shape, BF16),
        pltpu.VMEM((8, FL), F32),
        pltpu.VMEM((cond, m.HW), F32),
        pltpu.VMEM((texts, cond), F32),
        pltpu.VMEM((T, G, SMALL, 128), BF16),
        pltpu.VMEM((G,) + fvec.shape, BF16),
        pltpu.VMEM((N + 2 * EDGE, C), F32),
        pltpu.VMEM((N, C), F32),
        pltpu.VMEM((items, time_weight.shape[0]), BF16),
        pltpu.VMEM((mod_rows, 128), F32),
        pltpu.VMEM((m.D, m.R, N, C), BF16),
        pltpu.VMEM((G, T, m.cs, FL), BF16),
        pltpu.VMEM((m.D * m.pixels, FL), F32),
        pltpu.VMEM((m.D * m.pixels, FL), F32),
    ]
    columns = 4 if square else G - 1
    return fused_kernel(
        1,
        "front",
        lambda p: common_greet(p) + (sources_greet(m, p) if m.even else []),
        act,
        near,
        loads,
        far,
        near_out,
        far_out,
        scratch,
        4 * (T - 1) + 2 + 2 * columns + 4 * (G - 1) + (G if m.even else 0) + 3 * gather_sems(m),
        16,
    )


def sources_greet(m, p):
    greet = []
    for step in range(m.G):
        source = {"grp": p.z, "duo": p.c, "rows": lax.rem(p.q - step + m.G, m.G)}
        greet.append((source, None if step else p.q != p.z))
    return greet


def team_sum(m, p, flow, own, everyone):
    mine = p.c * m.R + p.z
    posted = [
        flow.post(own, everyone.at[mine], {"duo": c, "rows": z}) for c, z in p.team()
    ]

    def total():
        for item in posted:
            flow.land(item)
        result = own[...]
        for step, (c, z) in enumerate(p.team()):
            result = result + everyone[c * m.R + z]
        return result

    return total


def branch_kernel(m, active, norms, total, out_full, fv, latents, keep, vec, mod_all, qkv_rows, mapped, gres, proj_part):
    near = [norms, total, fv, keep, mod_all]
    loads = [active, out_full, latents, vec]
    far = [qkv_rows, mapped, gres] + ([proj_part] if m.even else [])
    N, C = m.N, m.C
    rows_all = m.D * m.pixels

    def act(p, flow, near, loads, far, near_out, far_out, scratch):
        norms, total, fv, keep, mod_all = near
        gain, grn_bias = fv[pl.ds(1, 1)], fv[pl.ds(2, 1)]
        grn, after, hat, inv, two, ratio, means, mods = near_out
        two_all, mapped_all, qkv_all, gres_near = far_out[:4]
        everyone, part, mate, passed, landed, branch, slopes = scratch
        add_up = team_sum(m, p, flow, total, everyone)
        for slot, to, sends, lands in (
            (0, p.z + 1, p.z < p.R - 1, p.z > 0),
            (1, p.z - 1, p.z > 0, p.z < p.R - 1),
        ):
            flow.post(far[2], gres_near.at[slot], {"rows": to}, when=sends, lands=lands)
        flow.gather_group(p, far[0], qkv_all)
        if m.even:
            flow.gather_group(p, far[3], far_out[4])
        text_line = LineGather(flow, p, far[1], mapped_all)
        half = m.S // 2
        pair = 2 * m.cs
        for s, (g, d, r) in enumerate(m.places):
            item = pl.ds(m.D * p.q + p.c, 1)
            mods[pl.ds(s // half, 1), pl.ds(pair * (s % half), pair)] = mod_all[d, r, g, item, pl.ds(0, pair)]
        mean = add_up() / m.FF + grn_eps
        means[...] = mean
        ratio[...] = norms[...] / mean[:, :1]
        slopes[...] = gain * ratio[...] + 1.0
        active, out_w, lat, vec = (load.get() for load in loads)

        @pl.loop(0, m.D)
        def _(d):
            rows = pl.ds(pl.multiple_of(d * m.pixels, 16), m.pixels)
            low = (active[rows] * slopes[pl.ds(d, 1)] + grn_bias).astype(BF16)
            grn[rows] = low
            part[d] = mm(low, out_w[...]).astype(BF16).reshape(m.R, N, C)

        def tail(rows):
            value = lat[rows].astype(F32) + keep[rows] * (branch[rows] + vec[pl.ds(10, 1)])
            after[rows] = value
            second = value * (1.0 + mods[pl.ds(0, 1)]) + mods[pl.ds(1, 1)]
            normal, inverse = layer_stats(second)
            hat[rows] = normal
            inv[rows] = inverse
            two[rows] = normal.astype(BF16)

        stripes = Stripes(flow, p, part, branch, (mate, passed, landed), two, two_all)
        text_line.start()
        flow.keep(far[1], mapped_all.at[p.c, p.z])
        stripes.run(tail, None, lambda number: text_line.hop(number + 1))
        for step in range(STRIPES + 1, m.R):
            text_line.hop(step)

    near_out = [
        ((rows_all, m.FL), BF16),
        ((N, C), F32),
        ((N, C), F32),
        ((N, 1), F32),
        ((N, C), BF16),
        ((8, m.FL), F32),
        ((8, 128), F32),
        ((8, C), F32),
    ]
    far_out = [
        ((m.D, m.R, N, C), BF16),
        ((m.D, m.R) + mapped.shape, BF16),
        ((m.G,) + qkv_rows.shape, BF16),
        ((2, N, C), BF16),
    ]
    if m.even:
        far_out.append(((m.G,) + proj_part.shape, BF16))
    scratch = (
        [pltpu.VMEM((m.T, 8, 128), F32)]
        + reduce_buffers(m, N, C)
        + [pltpu.VMEM((N, C), F32), pltpu.VMEM((8, m.FL), F32)]
    )
    return fused_kernel(
        3,
        "branch",
        common_greet,
        act,
        near,
        loads,
        far,
        near_out,
        far_out,
        scratch,
        (m.T + 1) + 2 * (m.G - 1) + (1 + STRIPES) * gather_sems(m) + STRIPES * reduce_sems(m),
        4 + STRIPES,
    )


def attention_kernel(m, two_all, gres, gres_near, mapped_all, weight, proj, bias, key_keep):
    near = [bias, key_keep]
    loads = [two_all, weight, proj, mapped_all]
    far = [gres, gres_near]
    heads = m.HW // HEAD
    keys = m.pixels + m.texts
    scale = HEAD ** (-0.5)
    HW, C, N, D, R, G, pixels, texts = m.HW, m.C, m.N, m.D, m.R, m.G, m.pixels, m.texts
    wide = C // m.Q
    block_rows = 2 * HW

    def act(p, flow, near, loads, far, near_out, far_out, scratch):
        bias, keep = near
        result, map_out, gw_out, gp_out, qv_out = near_out
        (two_far,) = far_out
        (gres_all, part, mate, passed, landed, qkv, k_all, v_all, k_t, v_t, dk, dv, o_t, dq_t, o_low, att, g_all, probs, dqkv,
         dtext, piece, words, gb_out, two_out) = scratch
        line = LineGatherOn(flow, p, far[0], gres_all)
        line.start_from(far[1])
        two, w, proj, mapped = (load.get() for load in loads)
        red = LineReduce(flow, p, part, result, mate, passed, landed)

        @pl.loop(0, D)
        def _(d):
            qkv[d] = (mm(two[d], w[...]) + bias[...]).astype(BF16)
            words[...] = jnp.zeros((texts, 3 * HW), F32) + bias[...]

            @pl.loop(0, m.T)
            def _(t):
                words[...] += mm(mapped[t, d], w[pl.ds(pl.multiple_of(t * HW, 16), HW)])

            text = words[...].astype(BF16)
            k_all[d, pl.ds(0, pixels)] = qkv[d, :, HW : 2 * HW]
            k_all[d, pl.ds(pixels, texts)] = text[:, HW : 2 * HW]
            v_all[d, pl.ds(0, pixels)] = qkv[d, :, 2 * HW :]
            v_all[d, pl.ds(pixels, texts)] = text[:, 2 * HW :]
            k_t[d] = k_all[d].T
            v_t[d] = v_all[d].T
            dk[d] = jnp.zeros_like(dk[d])
            dv[d] = jnp.zeros_like(dv[d])
            o_t[d] = jnp.zeros_like(o_t[d])
            dq_t[d] = jnp.zeros_like(dq_t[d])

        lane = lax.broadcasted_iota(jnp.int32, (1, HW), 1)
        row = lax.broadcasted_iota(jnp.int32, (HW, 1), 0)

        def masks(number):
            d = number // heads
            low = (number - d * heads) * HEAD
            return d, (lane >= low) & (lane < low + HEAD), (row >= low) & (row < low + HEAD)

        def forward(number):
            d, in_head, in_row = masks(number)
            q_h = jnp.where(in_head, qkv[d, :, :HW], 0).astype(BF16)
            scores = mm_t(k_all[d], q_h) * scale
            scores = jnp.where(keep[d] > 0, scores, masked_score)
            weights = jnp.exp(scores - jnp.max(scores, axis=0, keepdims=True))
            low = (weights / jnp.sum(weights, axis=0, keepdims=True)).astype(BF16)
            probs[number] = low
            o_t[d] += mm(jnp.where(in_row, v_t[d], 0).astype(BF16), low)

        pl.loop(0, D * heads // 2)(forward)
        line.hop(2)
        pl.loop(D * heads // 2, D * heads)(forward)

        @pl.loop(0, D)
        def _(d):
            o_low[d] = o_t[d].astype(BF16)
            att[d] = o_t[d].T.astype(BF16)

        def lanes_of(n):
            return pl.ds(pl.multiple_of(n * wide, 128), wide)

        @pl.loop(0, D * R)
        def _(number):
            d = number // R
            block = number - d * R
            mine = att[d, pl.ds(pl.multiple_of(block * N, 16), N)]
            for n in range(m.Q):
                part[d, block, :, pl.ds(n * wide, wide)] = mm(mine, proj[n]).astype(BF16)

        red.start()
        red.early()
        steps = list(red.later())
        for number in range(3, R):
            line.hop(number)
        line.settle(R)

        @pl.loop(0, D * R)
        def _(number):
            d = number // R
            block = number - d * R
            total = jnp.zeros((N, HW), F32)
            for n in range(m.Q):
                total = total + mm_t(gres_all[d, block, :, pl.ds(n * wide, wide)], proj[n])
            g_all[d, pl.ds(pl.multiple_of(block * N, 16), N)] = total.astype(BF16)

        def back(first, last):
            @pl.loop(first, last)
            def _(number):
                d, in_head, in_row = masks(number)
                q_h = jnp.where(in_head, qkv[d, :, :HW], 0).astype(BF16)
                g_h = jnp.where(in_head, g_all[d], 0).astype(BF16)
                low = probs[number]
                dv[d] += mm(low, g_h)
                grad_probs = mm_t(v_all[d], g_h)
                high = low.astype(F32)
                sums = jnp.sum(high * grad_probs, axis=0, keepdims=True)
                grad_scores = (high * (grad_probs - sums)).astype(BF16)
                dq_t[d] += mm(jnp.where(in_row, k_t[d], 0).astype(BF16), grad_scores)
                dk[d] += mm(grad_scores, q_h)

        cut = D * heads // 3
        back(0, cut)
        steps[0]()
        back(cut, D * heads)
        for step in steps[1:]:
            step()
        gb_out[...] = jnp.zeros_like(gb_out)

        @pl.loop(0, D)
        def _(d):
            dqkv[d, :, :HW] = (dq_t[d].T * scale).astype(BF16)
            dqkv[d, :, HW : 2 * HW] = (dk[d, pl.ds(0, pixels)] * scale).astype(BF16)
            dqkv[d, :, 2 * HW :] = dv[d, pl.ds(0, pixels)].astype(BF16)
            dtext[d, :, :HW] = jnp.zeros((texts, HW), BF16)
            dtext[d, :, HW : 2 * HW] = (dk[d, pl.ds(pixels, texts)] * scale).astype(BF16)
            dtext[d, :, 2 * HW :] = dv[d, pl.ds(pixels, texts)].astype(BF16)
            gb_out[pl.ds(0, 1)] += jnp.sum(dqkv[d].astype(F32), axis=0, keepdims=True) + jnp.sum(
                dtext[d].astype(F32), axis=0, keepdims=True
            )
            two_out[d] = mm_t(dqkv[d], w[...]).astype(BF16)
            @pl.loop(0, m.T)
            def _(t):
                rows = pl.ds(pl.multiple_of(t * HW, 16), HW)
                map_out[t, d] = mm_t(dtext[d], w[rows]).astype(BF16)

        flow.keep(two_out, two_far)
        qv_out[...] = jnp.zeros_like(qv_out)
        for h in range(m.T):

            @pl.when(D * p.z + p.c == h)
            def _():
                qv_out[pl.ds(0, 1), pl.ds(h * HW, HW)] = gb_out[pl.ds(0, 1), pl.ds(0, HW)]
                qv_out[pl.ds(1, 1), pl.ds(h * HW, HW)] = gb_out[pl.ds(0, 1), pl.ds(2 * HW, HW)]

        @pl.loop(0, C // block_rows)
        def _(g):
            lanes = pl.ds(pl.multiple_of(g * block_rows, 128), block_rows)
            piece[...] = t_mm(two[0, :, lanes], dqkv[0])
            for d in range(1, D):
                piece[...] += t_mm(two[d, :, lanes], dqkv[d])
            for side in range(2):
                rows = pl.ds(side * HW, HW)
                for d in range(D):
                    piece[rows] += t_mm(mapped[2 * g + side, d], dtext[d])
            gw_out[pl.ds(pl.multiple_of(g * block_rows, 16), block_rows)] = piece[...].astype(BF16)

        @pl.loop(0, m.Q)
        def _(n):
            total = jnp.zeros((HW, wide), F32)
            for d in range(D):
                columns = gres_all[d, :, :, lanes_of(n)].reshape(pixels, wide)
                total = total + mm(o_low[d], columns)
            gp_out[n] = total.astype(BF16)
        red.close()

    near_out = [
        ((N, C), F32),
        ((m.T, D, texts, HW), BF16),
        ((C, 3 * HW), BF16),
        ((m.Q, HW, wide), BF16),
        ((8, C), F32),
    ]
    scratch = [pltpu.VMEM((D, R, N, C), BF16)] + reduce_buffers(m, N, C)
    scratch += [
        pltpu.VMEM((D, pixels, 3 * HW), BF16),
        pltpu.VMEM((D, keys, HW), BF16),
        pltpu.VMEM((D, keys, HW), BF16),
        pltpu.VMEM((D, HW, keys), BF16),
        pltpu.VMEM((D, HW, keys), BF16),
        pltpu.VMEM((D, keys, HW), F32),
        pltpu.VMEM((D, keys, HW), F32),
        pltpu.VMEM((D, HW, pixels), F32),
        pltpu.VMEM((D, HW, pixels), F32),
        pltpu.VMEM((D, HW, pixels), BF16),
        pltpu.VMEM((D, pixels, HW), BF16),
        pltpu.VMEM((D, pixels, HW), BF16),
        pltpu.VMEM((D * heads, keys, pixels), BF16),
        pltpu.VMEM((D, pixels, 3 * HW), BF16),
        pltpu.VMEM((D, texts, 3 * HW), BF16),
        pltpu.VMEM((block_rows, 3 * HW), F32),
        pltpu.VMEM((texts, 3 * HW), F32),
        pltpu.VMEM((8, 3 * HW), F32),
        pltpu.VMEM((D, pixels, C), BF16),
    ]
    return fused_kernel(
        4,
        "attention_block",
        team_greet,
        act,
        near,
        loads,
        far,
        near_out,
        [((D, pixels, C), BF16)],
        scratch,
        gather_sems(m) + reduce_sems(m),
        4,
    )


def attended_kernel(m, two_part, text_part, result, cot, gres, hat, inv, after, mods, keep, vec, grad_qkv, grad_proj):
    near = [inv, mods, keep]
    loads = [two_part, hat, after, cot, gres, text_part, result, vec]
    far = [grad_qkv] + ([grad_proj] if m.even else [])
    N, C = m.N, m.C
    texts = m.D * m.texts

    def act(p, flow, near, loads, far, near_out, far_out, scratch):
        inv, mods, keep = near
        two_part, hat, after, cot, gres, text_part, result, vec = (load.get() for load in loads)
        output, grad_after, branch, gm, vecg, text = near_out
        gb_all = far_out[0]
        two_sum, text_sum = scratch[:2]
        text_red = LineReduce(flow, p, text_part, text_sum, *scratch[5:8])
        stripes = Stripes(flow, p, two_part, two_sum, scratch[2:5], branch, gb_all)
        flow.swap_group(p, far[0], far_out[1])
        if m.even:
            flow.swap_group(p, far[1], far_out[2])
        gm[...] = jnp.zeros_like(gm)
        vecg[...] = jnp.zeros_like(vecg)

        def back(rows):
            grad = cot[rows].astype(F32) + layer_back(two_sum[rows], hat[rows], inv[rows])
            gm[pl.ds(0, 1)] += jnp.sum(grad * after[rows], axis=0, keepdims=True)
            gm[pl.ds(1, 1)] += jnp.sum(grad, axis=0, keepdims=True)
            scaled = grad * (1.0 + mods[pl.ds(0, 1)])
            grad_after[rows] = scaled
            low = (keep[rows] * scaled).astype(BF16)
            branch[rows] = low
            vecg[pl.ds(0, 1)] += jnp.sum(low.astype(F32), axis=0, keepdims=True)
            vecg[pl.ds(1, 1)] += jnp.sum(gres[rows].astype(F32), axis=0, keepdims=True)

        text_red.start()
        steps = list(text_red.later())

        def between(number):
            if number == 0:
                steps[0]()
            elif number == 1:
                for step in steps[1:]:
                    step()
                text_red.close()
                text[...] = text_sum[...].astype(BF16)

        stripes.run(back, text_red.early, between)

        def out(rows):
            second = after[rows] * (1.0 + mods[pl.ds(0, 1)]) + mods[pl.ds(1, 1)]
            value = keep[rows] * (result[rows] + vec[pl.ds(12, 1)])
            output[rows] = (second + value).astype(BF16)

        chunks(N, out)

    near_out = [
        ((N, C), BF16),
        ((N, C), F32),
        ((N, C), BF16),
        ((8, C), F32),
        ((8, C), F32),
        ((texts, m.HW), BF16),
    ]
    far_out = [((m.D, m.R, N, C), BF16), (grad_qkv.shape, BF16)]
    if m.even:
        far_out.append((grad_proj.shape, BF16))
    scratch = (
        [pltpu.VMEM((N, C), F32), pltpu.VMEM((texts, m.HW), F32)]
        + reduce_buffers(m, N, C, False)
        + reduce_buffers(m, texts, m.HW, False)
    )
    return fused_kernel(
        5,
        "attended",
        common_greet,
        act,
        near,
        loads,
        far,
        near_out,
        far_out,
        scratch,
        2 * (m.G - 1) + STRIPES * gather_sems(m) + (1 + STRIPES) * reduce_sems(m),
        3 + STRIPES,
    )


def text_back_kernel(m, silu, grad_mapped):
    def kernel(s_ref, g_ref, out, bias, weight):
        weight[...] = t_mm(s_ref[...], g_ref[...])
        out[...] = jnp.zeros_like(out)
        for g in range(m.G):
            for t in range(m.T):
                at = m.ms * (g * m.T + t)
                out[g, pl.ds(t * m.mp, m.ms)] = weight[pl.ds(at, m.ms)].astype(BF16)
        total = jnp.sum(g_ref[...].astype(F32), axis=0, keepdims=True)
        bias[...] = jnp.zeros_like(bias)
        for t in range(m.T):

            @pl.when(lax.axis_index("duo") * m.R + lax.axis_index("rows") == t)
            def _():
                bias[pl.ds(0, 1), pl.ds(t * m.HW, m.HW)] = total

    return local_kernel(
        "text_back",
        kernel,
        [silu, grad_mapped],
        [((m.G, m.T * m.mp, m.HW), BF16), ((8, m.C), F32)],
        [pltpu.VMEM((silu.shape[1], m.HW), F32)],
    )


def back_kernel(m, gb_all, out_full, active, slope, grn_out, normed_all, in_full, norms, ratio, means, fv, key_keep,
                qkv_parts, proj_parts, grad_map):
    near = [norms, ratio, means, fv, key_keep]
    loads = [gb_all, out_full, active, grn_out, slope, normed_all, in_full, qkv_parts]
    loads += [proj_parts] if m.even else []
    far = [grad_map]
    N, C, FL, G = m.N, m.C, m.FL, m.G
    rows_in = C // G
    wide = C // m.Q
    per = m.pixels // N

    def act(p, flow, near, loads, far, near_out, far_out, scratch):
        norms, ratio, means, fv, keep = near
        gain = fv[pl.ds(1, 1)]
        (back,) = near_out
        in_parts, f_parts, map_parts, qkv_team = far_out[:4]
        g_far = far_out[-1]
        everyone, mine, moments, slopes, shifts, grads, hidden, part, mate, passed, landed = scratch[:11]
        turned_g, turned_x, g_in, f_own, qkv_own = scratch[11:16]
        g_out = scratch[-1]
        flow.swap_group(p, far[0], map_parts)
        gb, out_w, active, grn = (load.get() for load in loads[:4])
        moments[...] = jnp.zeros_like(moments)

        @pl.loop(0, m.D * per)
        def _(number):
            rows = pl.ds(pl.multiple_of(number * N, 16), N)
            item = number // per
            grad = mm_t(gb[rows], out_w[...])
            grads[rows] = grad
            moments[pl.ds(item, 1)] += jnp.sum(grad * active[rows], axis=0, keepdims=True)
            moments[pl.ds(m.D, 1)] += jnp.sum(grad, axis=0, keepdims=True)

        scaled = moments[...] * gain
        cross = jnp.sum(scaled * norms[...], axis=1, keepdims=True)
        mine[...] = jnp.broadcast_to(cross, mine.shape)
        add_up = team_sum(m, p, flow, mine, everyone)
        slope, x, in_w, qkv_parts = (load.get() for load in loads[4:8])
        step = m.cs

        def add_parts(parts, own, count):
            for t in range(count):
                rows = pl.ds(t * step, step)
                total = parts[0, rows].astype(F32)
                for g in range(1, G):
                    total = total + parts[g, rows].astype(F32)
                own[t] = total.astype(BF16)

        add_parts(qkv_parts, qkv_own, m.T)
        if m.even:
            proj_own = scratch[16]
            add_parts(loads[8].get(), proj_own, m.R)
        mean = means[...][:, :1]
        cross = add_up()[:, :1]
        slopes[...] = gain * ratio[...] + 1.0
        shifts[...] = (scaled / mean - cross / (m.FF * mean * mean)) / norms[...]
        gains = jnp.sum(moments[pl.ds(0, m.D)] * ratio[pl.ds(0, m.D)], axis=0, keepdims=True)
        biases = moments[pl.ds(m.D, 1)]
        moments[pl.ds(m.D + 1, 1)] = jnp.zeros((1, FL), F32)
        flow.swap_team(p, qkv_own, qkv_team)
        if m.even:
            for number in range(G):
                to = lax.rem(p.q + number, G)
                flow.post(
                    proj_own.at[to],
                    far_out[4].at[p.q],
                    {"grp": p.z, "duo": p.c, "rows": to},
                    when=None if number else p.q != p.z,
                )
            flow.keep(proj_own.at[p.z], far_out[4].at[p.q], p.q == p.z)

        @pl.loop(0, m.D * per)
        def _(number):
            rows = pl.ds(pl.multiple_of(number * N, 16), N)
            item = number // per
            inside = pl.ds(pl.multiple_of((number - item * per) * N, 16), N)
            one = pl.ds(item, 1)
            grad = grads[rows] * slopes[one] + keep[item, inside] * (active[rows] * shifts[one])
            low = (grad * slope[rows]).astype(BF16)
            hidden[rows] = low
            moments[pl.ds(m.D + 1, 1)] += jnp.sum(low.astype(F32), axis=0, keepdims=True)

        inner = moments[pl.ds(m.D + 1, 1)]
        f_own[...] = jnp.zeros_like(f_own)
        for g in range(G):
            lanes = slice(g * m.FFS, (g + 1) * m.FFS)
            for row, values in enumerate((inner, gains, biases)):
                f_own[g, pl.ds(row, 1)] = values[:, lanes]
        flow.swap_group(p, f_own, f_parts)
        line = LineReduce(flow, p, part, back, mate, passed, landed)

        @pl.loop(0, m.D)
        def _(d):
            rows = pl.ds(pl.multiple_of(d * m.pixels, 16), m.pixels)
            part[d] = mm_t(hidden[rows], in_w[...]).astype(BF16).reshape(m.R, N, C)

        for number in range(m.R):
            line.offer(line_order(p, number))
        line.early()
        turned_x[...] = x[...].T
        first = flow.take(G - 1)

        def send_in(number):
            g = lax.rem(p.q + 1 + number, G)
            return flow.copy(g_in.at[g], in_parts.at[p.q], {"grp": g}, first + number)

        @pl.loop(0, G)
        def _(number):
            g = lax.rem(p.q + 1 + number, G)
            rows = pl.ds(pl.multiple_of(g * rows_in, 16), rows_in)
            g_in[g] = mm(turned_x[rows], hidden[...]).astype(BF16)
            pl.when(number < G - 1)(lambda: send_in(number).start())

        flow.keep(g_in.at[p.q], in_parts.at[p.q])
        acts = list(line.later())
        acts[0]()
        turned_g[...] = grn[...].T

        def multiply_out(g, rows):
            g_out[g] = mm(turned_g[rows], gb[...]).astype(BF16)

        each_rows(G, m.FFS, multiply_out)
        flow.keep(g_out, g_far)

        for act_of in acts[1:]:
            act_of()
        line.close()
        for number in range(G - 1):
            send_in(number).wait_recv()
            send_in(number).wait_send()

    near_out = [((N, C), F32)]
    far_out = [
        ((G, rows_in, FL), BF16),
        ((G, 8, m.FFS), F32),
        (grad_map.shape, BF16),
        ((m.T, m.cs, 3 * m.HW), BF16),
    ]
    scratch = [
        pltpu.VMEM((m.T, 8, 128), F32),
        pltpu.VMEM((8, 128), F32),
        pltpu.VMEM((8, FL), F32),
        pltpu.VMEM((8, FL), F32),
        pltpu.VMEM((8, FL), F32),
        pltpu.VMEM((m.D * m.pixels, FL), F32),
        pltpu.VMEM((m.D * m.pixels, FL), BF16),
    ]
    scratch += reduce_buffers(m, N, C)
    scratch += [
        pltpu.VMEM((FL, m.D * m.pixels), BF16),
        pltpu.VMEM((C, m.D * m.pixels), BF16),
        pltpu.VMEM((G, rows_in, FL), BF16),
        pltpu.VMEM((G, 8, m.FFS), F32),
        pltpu.VMEM((m.T, m.cs, 3 * m.HW), BF16),
    ]
    if m.even:
        far_out.append(((G, m.cs, wide), BF16))
        scratch.append(pltpu.VMEM((m.R, m.cs, wide), BF16))
    far_out.append(((G, m.FFS, C), BF16))
    scratch.append(pltpu.VMEM((G, m.FFS, C), BF16))
    return fused_kernel(
        9,
        "feed_forward_back",
        lambda p: common_greet(p) + (spread_greet(m, p) if m.even else []),
        act,
        near,
        loads,
        far,
        near_out,
        far_out,
        scratch,
        2 * (m.T - 1) + 4 * (G - 1) + reduce_sems(m) + (G if m.even else 0),
        7,
    )


def tail_kernel(m, grad_low, tiny, g_out, in_parts, map_parts):
    loads = [in_parts, map_parts]
    far = [grad_low, tiny, g_out]
    N, C, G, T = m.N, m.C, m.G, m.T

    def act(p, flow, near, loads, far, near_out, far_out, scratch):
        low, tiny, g_out = far
        edges, tiny_all, in_team, map_team, out_parts = far_out
        in_own, map_own, tiny_in, tiny_own = scratch
        for block, to, sends, lands in (
            (low.at[pl.ds(N - EDGE, EDGE)], p.z + 1, p.z < p.R - 1, p.z > 0),
            (low.at[pl.ds(0, EDGE)], p.z - 1, p.z > 0, p.z < p.R - 1),
        ):
            slot = jnp.where(to > p.z, 0, 1)
            flow.post(block, edges.at[slot], {"rows": to}, when=sends, lands=lands)
        posts = flow.swap_team(p, tiny, tiny_in)
        flow.swap_group(p, g_out, out_parts)
        for load, own, step in ((loads[0], in_own, m.cs), (loads[1], map_own, m.mp)):
            parts = load.get()

            def add(t, rows, parts=parts, own=own):
                total = parts[0, rows].astype(F32)
                for g in range(1, G):
                    total = total + parts[g, rows].astype(F32)
                own[t] = total.astype(BF16)

            each_rows(T, step, add)

        flow.swap_team(p, in_own, in_team)
        flow.swap_team(p, map_own, map_team)
        for item in posts:
            flow.land(item)
        flow.settle_kept()
        for d in range(m.D):
            for g in range(G):
                total = tiny_in[d * m.R, g].astype(F32)
                for r in range(1, m.R):
                    total = total + tiny_in[d * m.R + r, g].astype(F32)
                tiny_own[g, d] = total
        flow.swap_group(p, tiny_own, tiny_all)

    return fused_kernel(
        11,
        "tail",
        common_greet,
        act,
        [],
        loads,
        far,
        [],
        [
            ((2, EDGE, C), BF16),
            ((G, m.D) + tiny.shape[2:], F32),
            ((T, m.cs, m.FL), BF16),
            ((T, m.mp, m.HW), BF16),
            (g_out.shape, BF16),
        ],
        [
            pltpu.VMEM((T, m.cs, m.FL), BF16),
            pltpu.VMEM((T, m.mp, m.HW), BF16),
            pltpu.VMEM(tiny.shape, BF16),
            pltpu.VMEM((G, m.D) + tiny.shape[2:], F32),
        ],
        2 + 3 * (T - 1) + 2 * (G - 1),
        5,
    )


def pad_rows(values, rows):
    return jnp.pad(values, ((0, rows - values.shape[0]),) + ((0, 0),) * (values.ndim - 1))


def body(
    latents,
    clip_tokens,
    time_embed,
    bucket_ids,
    heights,
    widths,
    text_mask,
    conv_weight,
    conv_bias,
    in_weight,
    in_bias,
    grn_gain,
    grn_bias,
    out_weight,
    out_bias,
    time_weight,
    time_bias,
    map_weight,
    map_bias,
    qkv_weight,
    qv_bias,
    proj_weight,
    proj_bias,
    cotangent,
):
    m = Sizes(latents, clip_tokens, in_weight, in_bias, conv_bias, map_weight)
    G, D, R, T, N, C = m.G, m.D, m.R, m.T, m.N, m.C
    pixels, texts, FFS, FL, FF, HW = m.pixels, m.texts, m.FFS, m.FL, m.FF, m.HW
    cs, ms, mp, sp, even, Q = m.cs, m.ms, m.mp, m.sp, m.even, m.Q
    q, c, z = (lax.axis_index(axis) for axis in AXES)
    head_slice = D * z + c

    vectors = [conv_bias, out_bias, map_bias, proj_bias, qv_bias]
    fvectors = [in_bias, grn_gain, grn_bias]
    in_cut, qkv_cut, map_cut, clip_pad, masked, grad_result, small, fvec = cut_kernel(
        m,
        [heights, widths, bucket_ids, in_weight, qkv_weight, map_weight, clip_tokens, latents]
        + [cotangent, conv_weight]
        + vectors
        + [time_embed, text_mask]
        + fvectors,
    )
    latents = latents[0]
    cotangent = cotangent[0]

    def swap_edges(plan, src, dst):
        p = plan.p
        for block, to, sends, lands in (
            (src.at[pl.ds(src.shape[0] - EDGE, EDGE)], p.z + 1, p.z < R - 1, p.z > 0),
            (src.at[pl.ds(0, EDGE)], p.z - 1, p.z > 0, p.z < R - 1),
        ):
            slot = jnp.where(to > p.z, 0, 1)
            plan.add(block, dst.at[slot], {"rows": to}, when=sends, lands=lands)

    outs = front_kernel(
        m,
        time_weight,
        time_bias[None],
        masked,
        small,
        fvec,
        in_cut,
        out_weight,
        map_cut,
        qkv_cut,
        clip_pad,
        proj_weight,
    )
    norms, total, silu, mapped_s = outs[:4]
    norm_hat, norm_inv, vec, fv, key_keep, keep, bias, embed, edges, _ = outs[4:14]
    normed_all, in_full, active, slope, out_full, qkv_rows, _, mod_all = outs[14:22]
    proj_part = outs[22].reshape(HW, C // G) if even else None
    normed_all = normed_all.reshape(D * pixels, C)
    in_full = in_full.reshape(C, FL)
    out_full = out_full.reshape(FL, C)
    outs = branch_kernel(
        m,
        active,
        norms,
        total,
        out_full,
        fv,
        latents,
        keep,
        vec,
        mod_all,
        qkv_rows.reshape(T * cs, 3 * HW),
        mapped_s,
        grad_result,
        proj_part,
    )
    grn_out, after_res, two_hat, two_inv, _, ratio, means, mods, two_all, mapped = outs[:10]
    qkv_full, gres_near = outs[10].reshape(C, 3 * HW), outs[11]
    if even:
        proj_s = outs[12]
    else:
        proj_whole = lax.all_gather(proj_weight, AXES, axis=0, tiled=True)
        proj_s = lax.dynamic_slice_in_dim(proj_whole, head_slice * HW, HW, axis=0)[None]
    result, mapped_part, grad_qkv, grad_proj, qv_grads, two_part = attention_kernel(
        m,
        two_all.reshape(D, pixels, C),
        grad_result,
        gres_near,
        mapped.reshape(T, D, texts, HW),
        qkv_full,
        proj_s,
        bias,
        key_keep,
    )
    outs = attended_kernel(
        m,
        two_part.reshape(D, R, N, C),
        mapped_part.reshape(D, R, D * texts, HW),
        result,
        cotangent,
        grad_result,
        two_hat,
        two_inv,
        after_res,
        mods,
        keep,
        vec,
        grad_qkv.reshape(G, T * cs, 3 * HW),
        grad_proj,
    )
    output, grad_after, _, grad_modulate, vec_sums, grad_mapped, gb_all, qkv_parts = outs[:8]
    if even:
        proj_parts = outs[8]
    else:
        proj_parts = None
        spread = jnp.zeros((C, C), F32)
        spread = lax.dynamic_update_slice_in_dim(
            spread, grad_proj[0].astype(F32), head_slice * HW, axis=0
        )
        proj_team = lax.psum_scatter(spread, AXES, scatter_dimension=0, tiled=True)[None]
    grad_map, map_bias_grad = text_back_kernel(m, silu, grad_mapped)
    outs = back_kernel(
        m,
        gb_all.reshape(D * pixels, C),
        out_full,
        active,
        slope,
        grn_out,
        normed_all,
        in_full,
        norms,
        ratio,
        means,
        fv,
        key_keep,
        qkv_parts,
        proj_parts,
        grad_map,
    )
    grad_conv_in, in_parts, f_sum, map_parts, qkv_team = outs[:5]
    grad_out = outs[-1]
    if even:
        proj_team = outs[5]

    grad_conv, conv_low, tiny = conv_back_kernel(
        m,
        bucket_ids,
        grad_conv_in,
        norm_hat,
        norm_inv,
        edges,
        masked,
        vec_sums,
        map_bias_grad,
        qv_grads,
        grad_modulate,
    )
    conv_edges, tiny_all, in_team, map_team, out_parts = tail_kernel(
        m, conv_low, tiny, grad_out, in_parts, map_parts
    )
    outs = finish_kernel(
        m,
        bucket_ids,
        conv_edges,
        conv_low,
        grad_after,
        keep,
        vec,
        in_team,
        qkv_team,
        map_team,
        proj_team,
        out_parts,
        tiny_all,
        f_sum,
        embed,
        time_embed.shape[1],
    )
    grad_latents, grad_in_shard, grad_qkv_shard, grad_map_shard, grad_proj_shard = outs[:5]
    grad_out_shard, grad_kernel, grad_time = outs[5:8]
    conv_b, out_b, proj_b, map_b, qv_b, time_b, in_b, gain_g, grn_b = outs[8:17]
    return (
        output[None],
        grad_latents,
        grad_kernel,
        conv_b,
        grad_in_shard,
        in_b,
        gain_g,
        grn_b,
        grad_out_shard,
        out_b,
        grad_time,
        time_b,
        grad_map_shard,
        map_b,
        grad_qkv_shard,
        qv_b,
        grad_proj_shard,
        proj_b,
    )


def solution(mesh):
    items, rows = mesh.devices.shape
    fine = Mesh(mesh.devices.reshape(items // 2, 2, rows), AXES)
    item = ("grp", "duo")
    full = AXES
    ins = (
        P(item, "rows", None),
        P(item, "rows", None),
        P(item, None),
        P(item),
        P(item),
        P(item),
        P(item, None),
        P(None, full),
        P(full),
        P(full, None),
        P(full),
        P(full),
        P(full),
        P(full, None),
        P(full),
        P(None, full),
        P(full),
        P(full, None),
        P(full),
        P(full, None),
        P(full),
        P(full, None),
        P(full),
        P(item, "rows", None),
    )
    outs = (
        P(item, "rows", None),
        P(item, "rows", None),
        P(None, full),
        P(full),
        P(full, None),
        P(full),
        P(full),
        P(full),
        P(full, None),
        P(full),
        P(None, full),
        P(full),
        P(full, None),
        P(full),
        P(full, None),
        P(full),
        P(full, None),
        P(full),
    )
    return jax.shard_map(body, mesh=fine, in_specs=ins, out_specs=outs, check_vma=False)
```
